32 devices in a mesh: dp: 8 (over z, x), tensor: 4 (over y, core).
Axes of the slice: x: 2, y: 2, z: 4, core: 2. Of those that a mesh axis runs over, the one named last changes fastest.
Arguments:
- tokens: bfloat16 [8192, 2048], P('dp'), may hold values from -6 to 6
- attn_gain: bfloat16 [2048], P('dp'), may hold values from 0.3984375 to 1.59375
- qkv_weight: bfloat16 [2048, 3, 2048], P('dp', None, 'tensor'), may hold values from -0.125 to 0.125
- out_weight: bfloat16 [2048, 2048], P('dp', 'tensor'), may hold values from -2 to 2
- moe_gain: bfloat16 [2048], P('dp'), may hold values from 0.3984375 to 1.59375
- router_weight: bfloat16 [2048, 4], P('dp'), may hold values from -0.09375 to 0.09375
- expert_weight: bfloat16 [3, 8192, 5632], P(None, 'dp', 'tensor'), may hold values from -0.125 to 0.125
- routes: int32 [8192, 2], P('dp'), may hold values from 0 to 3, all different within a row; in each aligned block of 1024 rows (0 to 1023, 1024 to 2047, ...) at most 768 rows name the same one
- cotangent: bfloat16 [8192, 2048], P('dp'), may hold values from -6 to 6
Outputs:
- layer_out: float32 [8192, 2048], P('dp')
- input_grad: float32 [8192, 2048], P('dp')
- attn_gain_grad: float32 [2048], P('dp')
- qkv_grad: float32 [2048, 3, 2048], P('dp', None, 'tensor')
- out_weight_grad: float32 [2048, 2048], P('dp', 'tensor')
- moe_gain_grad: float32 [2048], P('dp')
- router_grad: float32 [2048, 4], P('dp')
- expert_grad: float32 [3, 8192, 5632], P(None, 'dp', 'tensor')
The draws below stay inside these ranges and needn't reach their ends.
Inputs may be any that keep to these rules, and one draw needn't show every extreme that they name: `routes`: each row names two different experts; among the rows of one index of dp no expert is named more than 768 times.
All inputs are finite; a program needn't handle non-finite values.
Results may differ from the reference program's by a relative error of at most 0.023.
Values may be sent and summed in bfloat16 or wider, within the bound.
No kernel may reach another device: no remote copies, remote signals or barrier semaphores. Data moves between devices by JAX's collectives and lax.ppermute only.
A program may use at most 384 MiB of HBM per device.

```python
import math
import jax
import jax.numpy as jnp
import numpy as np
from jax import lax

D = 2048
HEADS = 16
HEAD = 128
FF = 5632
EXPERTS = 4
SEQ = 1024
BLOCK = 256
TOK_DEV = 1024
TOKENS = 8192
MOST = 768


def block_levels(key, extent, split, low, largest):
    def one(dim, shards_of):
        draws = jax.random.uniform(jax.random.fold_in(jax.random.fold_in(key, 6), dim), (shards_of,), jnp.float32, low / len(split), largest / len(split))
        return jnp.repeat(jnp.exp(draws), extent[dim] // shards_of).reshape((-1,) + (1,) * (len(extent) - dim - 1))

    loudness = one(*split[0])
    for cut in split[1:]:
        loudness = loudness * one(*cut)
    return loudness


def deal_out(own_key, own, number, rows, amount, top, bound, slope):
    sequence = jax.random.permutation(own_key, amount)
    packed, common = load_shares(amount, rows * top, bound, slope, True), load_shares(amount, rows * top, bound, slope, False)
    places = jnp.arange(amount)

    def named(sizes, offset_by):
        used = int((sizes > 0).sum())
        fixed = max(1, used // 4)
        passed = fixed + (places - fixed + offset_by * (used - fixed)) % max(1, amount - fixed)
        return jnp.zeros((amount,), jnp.int32).at[sequence[jnp.where(places < fixed, places, passed)]].set(jnp.asarray(sizes, jnp.int32))

    sizes = jnp.where(number % 4 == 0, named(packed, number // 4), named(common, number - number // 4 - 1))
    mixed = jax.random.permutation(jax.random.fold_in(own, 3), amount)
    donor, taker = mixed[0:amount // 2 * 2:2], mixed[1:amount // 2 * 2:2]
    margin = jnp.minimum(sizes[donor] - 1, bound - sizes[taker]) // 2
    margin = jnp.where((donor == sequence[0]) | (taker == sequence[0]) | (sizes[taker] == 0), 0, jnp.maximum(margin, 0))
    passed = jax.random.randint(jax.random.fold_in(own, 4), (amount // 2,), 0, 1 << 20) % (margin + 1)
    sizes = sizes.at[donor].add(-passed).at[taker].add(passed)
    labels = jnp.searchsorted(jnp.cumsum(sizes), jnp.arange(rows * top), side="right").astype(jnp.int32)
    listing = labels.reshape(top, rows).T
    listing = listing[jax.random.permutation(jax.random.fold_in(own, 1), rows)]
    offset_by = jax.random.randint(jax.random.fold_in(own, 2), (rows, 1), 0, top)
    return jnp.take_along_axis(listing, (jnp.arange(top)[None, :] + offset_by) % top, axis=1)


def load_shares(number_of, total, bound, lean, full):
    portions = [(1 << 20) // math.isqrt(rank ** lean) + 1 for rank in range(1, number_of + 1)]
    largest = bound if full else min(bound, max(-(-total // number_of), total * portions[0] // sum(portions)))
    least = 1 if total - largest >= number_of - 1 else 0
    holding, rest = [largest] + [least] * (number_of - 1), total - largest - least * (number_of - 1)
    while rest > 0:
        candidates = [i for i in range(1, number_of) if holding[i] < largest] or [i for i in range(1, number_of) if holding[i] < bound]
        whole, remaining = sum([portions[i] for i in candidates]), rest
        for i in candidates:
            extra = min(bound - holding[i], max(1, remaining * portions[i] // whole), rest)
            holding[i] = holding[i] + extra
            rest = rest - extra
    return np.array(holding)


def scatter_about(key, dims, scale, bound, pieces=(), held_as=jnp.bfloat16):
    loudness = block_levels(key, dims, pieces, -0.22, 0.18) if pieces else 1.0
    array = jax.random.normal(key, dims, jnp.float32) * scale * loudness
    return jnp.minimum(jnp.maximum(array, -bound), bound).astype(held_as)


def setup_inputs(seed: int = 0) -> dict:
    arg_keys = jax.random.split(jax.random.key(seed), 10)
    tokens = scatter_about(arg_keys[0], (TOKENS, D), 1.0, 6.0, ((0, 8),))
    attn_gain = jnp.clip(1.0 + 0.12 * jax.random.normal(arg_keys[1], (D,), jnp.float32), 0.3984375, 1.59375).astype(jnp.bfloat16)
    qkv_weight = scatter_about(arg_keys[2], (D, 3, D), D ** -0.5, 0.125, ((0, 8), (2, 4)))
    out_weight = scatter_about(arg_keys[3], (D, D), (4 * D // SEQ) ** -0.5, 2.0, ((0, 8), (1, 4)))
    moe_gain = jnp.clip(1.0 + 0.12 * jax.random.normal(arg_keys[4], (D,), jnp.float32), 0.3984375, 1.59375).astype(jnp.bfloat16)
    router_weight = scatter_about(arg_keys[5], (D, EXPERTS), (2 * D) ** -0.5, 0.09375, ((0, 8),))
    expert_weight = scatter_about(arg_keys[6], (3, EXPERTS * D, FF), D ** -0.5, 0.125, ((1, 8), (2, 4)))
    routes_keys = jax.random.split(jax.random.fold_in(arg_keys[7], 1), TOKENS // TOK_DEV)
    routes_turns = jax.random.permutation(jax.random.fold_in(arg_keys[7], 3), TOKENS // TOK_DEV)
    routes = jax.vmap(lambda own, number: deal_out(jax.random.fold_in(arg_keys[7], 2), own, number, TOK_DEV, EXPERTS, 2, MOST, 1))(routes_keys, routes_turns).reshape((TOKENS, 2))
    cotangent = scatter_about(arg_keys[8], (TOKENS, D), 1.0, 6.0, ((0, 8),))
    return {"tokens": tokens, "attn_gain": attn_gain, "qkv_weight": qkv_weight, "out_weight": out_weight, "moe_gain": moe_gain, "router_weight": router_weight, "expert_weight": expert_weight, "routes": routes, "cotangent": cotangent}


@jax.custom_vjp
def low(v):
    return lax.optimization_barrier(v.astype(jnp.bfloat16)).astype(jnp.float32)

@jax.custom_vjp
def low_back(v):
    return v

def low_keep(v):
    return (low(v), None)

def low_pass(kept, grad):
    return (grad,)

def back_keep(v):
    return (v, None)

def back_low(kept, grad):
    return (low(grad),)
low.defvjp(low_keep, low_pass)
low_back.defvjp(back_keep, back_low)
epsilon = 1e-05
theta_base = 10000.0
masked_out = -1e+30

def rotary_tables(length, width):
    half_width = width // 2
    freqs = theta_base ** (-(jnp.arange(half_width, dtype=jnp.float32) * 2.0 / width))
    angles = jnp.arange(length, dtype=jnp.float32)[:, None] * freqs[None, :]
    cosine = jnp.cos(angles)
    sine = jnp.sin(angles)
    return (jnp.concatenate([cosine, cosine], 1), jnp.concatenate([sine, sine], 1))

def rotate(vectors, cosine, sine):
    half_width = vectors.shape[-1] // 2
    turned = jnp.concatenate([-vectors[..., half_width:], vectors[..., :half_width]], -1)
    return vectors * cosine + turned * sine

def block_mask(length):
    blocks = jnp.arange(length, dtype=jnp.int32) // BLOCK
    return blocks[None, :] <= blocks[:, None]

def reference(tokens, attn_gain, qkv_weight, out_weight, moe_gain, router_weight, expert_weight, routes, cotangent):
    highest = lax.Precision.HIGHEST
    total_rows = tokens.shape[0]
    sequences = total_rows // SEQ
    picked = (routes[:, :, None] == jnp.arange(EXPERTS, dtype=jnp.int32)[None, None, :]).astype(jnp.float32)
    cosine, sine = rotary_tables(SEQ, HEAD)
    allowed = block_mask(SEQ)
    scale = 1.0 / math.sqrt(HEAD)

    def attend(operands):
        query, keys, values = operands
        query = low(rotate(query.transpose(1, 0, 2), cosine, sine))
        keys = low(rotate(keys.transpose(1, 0, 2), cosine, sine))
        values = values.transpose(1, 0, 2)
        scores = low_back(jnp.einsum('hqd,hkd->hqk', query, keys, precision=highest) * scale)
        scores = jnp.where(allowed[None], scores, masked_out)
        probs = jax.nn.softmax(scores, axis=-1)
        context = jnp.einsum('hqk,hkd->hqd', low(probs), values, precision=highest)
        return context.transpose(1, 0, 2).reshape(SEQ, D)

    def forward(inputs, gain_one, qkv_all, out_all, gain_two, router_all, experts_all):
        scale_one = lax.rsqrt(lax.optimization_barrier(jnp.mean(inputs * inputs, axis=1, keepdims=True)) + epsilon)
        normed_in = low(inputs * scale_one * gain_one)
        qkv = jnp.dot(normed_in, qkv_all.reshape(D, 3 * D), precision=highest, preferred_element_type=jnp.float32)
        query_lin = low_back(qkv[:, :D]).reshape(sequences, SEQ, HEADS, HEAD)
        key_lin = low_back(qkv[:, D:2 * D]).reshape(sequences, SEQ, HEADS, HEAD)
        value_lin = low(low_back(qkv[:, 2 * D:])).reshape(sequences, SEQ, HEADS, HEAD)
        context = lax.map(jax.checkpoint(attend), (query_lin, key_lin, value_lin)).reshape(total_rows, D)
        context = low(low_back(context))
        attn = low_back(jnp.dot(context, out_all.T, precision=highest, preferred_element_type=jnp.float32))
        hidden = inputs + attn
        scale_two = lax.rsqrt(lax.optimization_barrier(jnp.mean(hidden * hidden, axis=1, keepdims=True)) + epsilon)
        moe_in = low(hidden * scale_two * gain_two)
        logits = low_back(jnp.dot(moe_in, router_all, precision=highest, preferred_element_type=jnp.float32))
        chosen = lax.optimization_barrier(jnp.sum(picked * logits[:, None, :], axis=2))
        gates = jax.nn.softmax(chosen, axis=1)
        mixing = lax.optimization_barrier(jnp.sum(picked * gates[:, :, None], axis=1))

        def expert(weights):
            expert_in = low_back(moe_in)
            pre_gate = low_back(jnp.dot(expert_in, weights[0], precision=highest, preferred_element_type=jnp.float32))
            pre_up = low_back(jnp.dot(expert_in, weights[1], precision=highest, preferred_element_type=jnp.float32))
            activation = low(jax.nn.silu(pre_gate) * pre_up)
            return low(low_back(jnp.dot(activation, weights[2].T, precision=highest, preferred_element_type=jnp.float32)))
        stacked = experts_all.reshape(3, EXPERTS, D, FF).transpose(1, 0, 2, 3)
        outputs = lax.map(jax.checkpoint(expert), stacked)
        mixed = jnp.einsum('te,etd->td', mixing, outputs, precision=highest)
        return hidden + mixed
    params = (tokens.astype(jnp.float32), attn_gain.astype(jnp.float32), qkv_weight.astype(jnp.float32), out_weight.astype(jnp.float32), moe_gain.astype(jnp.float32), router_weight.astype(jnp.float32), expert_weight.astype(jnp.float32))
    layer_out, pull = jax.vjp(forward, *params)
    grads = pull(cotangent.astype(jnp.float32))
    return (layer_out, grads[0], grads[1], grads[2], grads[3], grads[4], grads[5], grads[6])
```

```python
import math

import jax
import jax.numpy as jnp
from jax import lax
from jax.sharding import PartitionSpec as P

HEAD = 128
EXPERTS = 4
SEQ = 1024
BLOCK = 256
MOST = 768


epsilon = 1e-05
theta_base = 10000.0
masked_out = -1e30
low = jnp.bfloat16
full = jnp.float32


def swap(value, axis, distance):
    return lax.ppermute(value, axis, [(i, i ^ distance) for i in range(lax.axis_size(axis))])


def rotary_tables(length, width):
    half_width = width // 2
    freqs = theta_base ** (-(jnp.arange(half_width, dtype=jnp.float32) * 2.0 / width))
    angles = jnp.arange(length, dtype=jnp.float32)[:, None] * freqs[None, :]
    cosine = jnp.cos(angles)
    sine = jnp.sin(angles)
    return (jnp.concatenate([cosine, cosine], 1), jnp.concatenate([sine, sine], 1))


def rotate(vectors, cosine, sine):
    half_width = vectors.shape[-1] // 2
    turned = jnp.concatenate([-vectors[..., half_width:], vectors[..., :half_width]], -1)
    return vectors * cosine + turned * sine


def block_mask(length):
    blocks = jnp.arange(length, dtype=jnp.int32) // BLOCK
    return blocks[None, :] <= blocks[:, None]


def contract(left, right, left_dim, right_dim):
    return lax.dot_general(
        left, right, (((left_dim,), (right_dim,)), ((), ())), preferred_element_type=jnp.float32
    )


def levels_of(count):
    return count.bit_length() - 1


def side_of(index, bit):
    return (index >> bit) & 1 == 1


def tensor_sum(value):
    for bit in range(levels_of(lax.axis_size("tensor"))):
        value = value + swap(value, "tensor", 1 << bit)
    return value


def all_sum(value):
    for axis in ("tensor", "dp"):
        for bit in range(levels_of(lax.axis_size(axis))):
            value = value + swap(value, axis, 1 << bit)
    return value


def tensor_reduce(part):
    count = lax.axis_size("tensor")
    place = lax.axis_index("tensor")
    size = part.shape[1] // count
    blocks = [part[:, i * size : (i + 1) * size] for i in range(count)]
    for bit in range(levels_of(count)):
        upper = side_of(place, bit)
        kept = [jnp.where(upper, b, a) for a, b in zip(blocks[::2], blocks[1::2])]
        given = [jnp.where(upper, a, b) for a, b in zip(blocks[::2], blocks[1::2])]
        sent = jnp.concatenate([v.astype(low) for v in given], 1)
        came = swap(sent, "tensor", 1 << bit)
        blocks = [
            v.astype(full) + came[:, i * size : (i + 1) * size].astype(full)
            for i, v in enumerate(kept)
        ]
    return blocks[0]


def tensor_gather(own):
    count = lax.axis_size("tensor")
    place = lax.axis_index("tensor")
    size = own.shape[1]
    held = own
    order = list(range(levels_of(count)))[::-1]
    for bit in order:
        came = swap(held, "tensor", 1 << bit)
        upper = side_of(place, bit)
        number = held.shape[1] // size
        mine = [held[:, i * size : (i + 1) * size] for i in range(number)]
        theirs = [came[:, i * size : (i + 1) * size] for i in range(number)]
        pairs = []
        for a, b in zip(mine, theirs):
            pairs.append((jnp.where(upper, b, a), jnp.where(upper, a, b)))
        held = jnp.concatenate([v for pair in pairs for v in pair], 1)
    return held


def near_gather(own):
    held = [own]
    count = lax.axis_size("tensor")
    for bit in range(levels_of(count))[::-1]:
        came = swap(jnp.concatenate(held, 1) if len(held) > 1 else held[0], "tensor", 1 << bit)
        size = own.shape[1]
        theirs = [came[:, i * size : (i + 1) * size] for i in range(len(held))]
        held = [v for pair in zip(held, theirs) for v in pair]
    return jnp.concatenate(held, 1)


def near_reduce(part):
    count = lax.axis_size("tensor")
    size = part.shape[1] // count
    blocks = [part[:, i * size : (i + 1) * size] for i in range(count)]
    for bit in range(levels_of(count)):
        sent = jnp.concatenate([v.astype(low) for v in blocks[1::2]], 1)
        came = swap(sent, "tensor", 1 << bit)
        blocks = [
            v.astype(full) + came[:, i * size : (i + 1) * size].astype(full)
            for i, v in enumerate(blocks[::2])
        ]
    return blocks[0]


def turn_blocks(value, index, number):
    size = value.shape[0] // number
    blocks = [value[i * size : (i + 1) * size] for i in range(number)]
    for bit in range(levels_of(number)):
        upper = side_of(index, bit)
        blocks = [jnp.where(upper, blocks[i ^ (1 << bit)], blocks[i]) for i in range(number)]
    return jnp.concatenate(blocks, 0) if number > 1 else value


def group_gather(local, position, group_count):
    held = local
    for bit in range(levels_of(group_count)):
        partner = swap(held, "dp", 1 << bit)
        upper = side_of(position, bit)
        held = jnp.concatenate(
            [jnp.where(upper, partner, held), jnp.where(upper, held, partner)], axis=0
        )
    return held


def group_reduce(value, position, group_count):
    current = value
    for bit in range(levels_of(group_count))[::-1]:
        middle = current.shape[0] // 2
        upper = side_of(position, bit)
        kept = jnp.where(upper, current[middle:], current[:middle])
        given = jnp.where(upper, current[:middle], current[middle:])
        current = kept.astype(full) + swap(given.astype(low), "dp", 1 << bit).astype(full)
    return current


def body(
    tokens,
    attn_gain,
    qkv_weight,
    out_weight,
    moe_gain,
    router_weight,
    expert_weight,
    routes,
    cotangent,
):
    rows = tokens.shape[0]
    width = tokens.shape[1]
    tensor_count = lax.axis_size("tensor")
    dp_count = lax.axis_size("dp")
    group_count = dp_count // EXPERTS
    size = width // tensor_count
    hidden_size = expert_weight.shape[2]
    head_count = size // HEAD
    scale = 1.0 / math.sqrt(HEAD)
    place = lax.axis_index("tensor")
    index = lax.axis_index("dp")
    expert = index // group_count
    inner = tensor_count // group_count
    position = (index % group_count) ^ (place // inner)
    turn = place % inner

    def own_columns(value):
        return lax.dynamic_slice_in_dim(value, place * size, size, 1)

    extras = jnp.concatenate([router_weight, attn_gain[:, None], moe_gain[:, None]], 1)
    extras = jnp.pad(extras, ((0, 0), (0, 128 - extras.shape[1])))
    first = lax.all_gather(
        jnp.concatenate([qkv_weight.reshape(-1, 3 * size), extras], 1), "dp", axis=0, tiled=True
    )
    qkv_flat = first[:, : 3 * size]
    small = first[:, 3 * size :].T
    router_full = small[:EXPERTS]
    gain_first = small[EXPERTS : EXPERTS + 1].astype(full)
    gain_second = small[EXPERTS + 1 : EXPERTS + 2].astype(full)
    gain_first_own = own_columns(gain_first)
    gain_second_own = own_columns(gain_second)
    router_own = own_columns(router_full)
    out_full = lax.all_gather(out_weight, "dp", axis=0, tiled=True)

    near = jnp.arange(EXPERTS, dtype=jnp.int32) ^ expert
    routes_t = routes.T
    names = jnp.arange(EXPERTS, dtype=jnp.int32)
    hits = jnp.sum((routes_t[None] == names[:, None, None]).astype(jnp.int32), 1)
    rank = jnp.cumsum(hits, axis=1) - hits
    slot = jnp.where(hits > 0, rank, -1)
    slot_near = jnp.take(slot, near, axis=0)
    chosen = (
        jnp.arange(MOST, dtype=jnp.int32)[None, :, None] == slot_near[:, None, :]
    ).astype(low).reshape(EXPERTS * MOST, rows)

    def to_experts(own):
        packed = jnp.dot(chosen, own, preferred_element_type=full).astype(low)
        parts = [packed[s * MOST : (s + 1) * MOST] for s in range(EXPERTS)]
        parts = [parts[0]] + [
            swap(parts[s], "dp", s * group_count) for s in range(1, EXPERTS)
        ]
        return jnp.concatenate([near_gather(v) for v in parts], 0)

    def to_tokens(part):
        parts = []
        for s in range(EXPERTS):
            own = near_reduce(part[s * MOST : (s + 1) * MOST]).astype(low)
            parts.append(own if s == 0 else swap(own, "dp", s * group_count))
        return contract(chosen, jnp.concatenate(parts, 0), 0, 0)

    grad_own = own_columns(cotangent)
    grad_rows = to_experts(grad_own)

    down_local = turn_blocks(expert_weight[2], turn, inner)
    pair_local = turn_blocks(
        jnp.concatenate([expert_weight[0], expert_weight[1]], 1), turn, inner
    )
    down_weight = group_gather(down_local, position, group_count)
    pair_weight = group_gather(pair_local, position, group_count)

    inputs = tokens.astype(full)
    scale_one = lax.rsqrt(jnp.mean(inputs * inputs, axis=1, keepdims=True) + epsilon)
    normed_in = (inputs * scale_one * gain_first).astype(low)
    inputs_own = own_columns(tokens).astype(full)
    qkv = jnp.dot(normed_in, qkv_flat, preferred_element_type=full)
    cosine, sine = rotary_tables(SEQ, HEAD)
    cosine = cosine[:, None, :]
    sine = sine[:, None, :]
    allowed = block_mask(SEQ)

    def heads_of(block):
        return block.reshape(-1, SEQ, head_count, HEAD)

    query = rotate(heads_of(qkv[:, :size]), cosine, sine).astype(low)
    keys = rotate(heads_of(qkv[:, size : 2 * size]), cosine, sine).astype(low)
    values = heads_of(qkv[:, 2 * size :]).astype(low)

    def scores_of(query_seq, key_seq):
        scores = jnp.einsum("qhd,khd->hqk", query_seq, key_seq, preferred_element_type=full) * scale
        return jnp.where(allowed[None], scores, masked_out)

    def forward_sequence(operands):
        query_seq, key_seq, value_seq = operands
        scores = scores_of(query_seq, key_seq)
        peak = jnp.max(scores, axis=2, keepdims=True)
        expo = jnp.exp(scores - peak)
        totals = jnp.sum(expo, axis=2, keepdims=True)
        probs = (expo / totals).astype(low)
        context_seq = jnp.einsum("hqk,khd->qhd", probs, value_seq, preferred_element_type=full)
        return (context_seq.astype(low), (peak + jnp.log(totals))[:, :, 0])

    context, logsum = lax.map(forward_sequence, (query, keys, values))
    context_rows = context.reshape(rows, size)
    attn_part = contract(context_rows, out_full, 1, 1).astype(low)
    hidden = inputs_own + tensor_reduce(attn_part)

    scaled_hidden = (hidden * gain_second_own).astype(low)
    sums = tensor_sum(
        jnp.concatenate(
            [contract(router_own, scaled_hidden, 1, 1), jnp.sum(hidden * hidden, 1)[None]], 0
        )
    )
    scale_two_row = lax.rsqrt(sums[EXPERTS:] / width + epsilon)
    scale_two = scale_two_row.reshape(rows, 1)
    logits = sums[:EXPERTS] * scale_two_row
    normed_two = hidden * scale_two
    moe_in = (normed_two * gain_second_own).astype(low)
    named = hits > 0
    top = jnp.max(jnp.where(named, logits, masked_out), axis=0, keepdims=True)
    weight = jnp.where(named, jnp.exp(logits - top), 0.0)
    gates = weight / jnp.sum(weight, axis=0, keepdims=True)

    def three_parts(value):
        a = value.astype(low)
        b = (value - a.astype(full)).astype(low)
        return [a, b, (value - a.astype(full) - b.astype(full)).astype(low)]

    gates_near = jnp.take(gates, near, axis=0)
    chosen_blocks = chosen.reshape(EXPERTS, MOST, rows)
    gate_parts = jnp.stack(three_parts(gates_near), 1)
    gate_packed = jnp.sum(
        lax.dot_general(
            gate_parts, chosen_blocks, (((2,), (2,)), ((0,), (0,))), preferred_element_type=full
        ),
        1,
    )
    gate_rows = jnp.concatenate(
        [gate_packed[0]]
        + [swap(gate_packed[s], "dp", s * group_count) for s in range(1, EXPERTS)],
        0,
    )[:, None]

    arrived = to_experts(moe_in)

    raw_grad = jnp.dot(grad_rows, down_weight, preferred_element_type=full)
    both = jnp.dot(arrived, pair_weight, preferred_element_type=full)
    pre_gate = both[:, :hidden_size]
    pre_up = both[:, hidden_size:]
    sigma = jax.nn.sigmoid(pre_gate)
    silu = pre_gate * sigma
    act = silu * pre_up
    gate_grad_part = jnp.sum(act * raw_grad, 1)
    activation = (act * gate_rows).astype(low)
    act_grad = raw_grad * gate_rows
    gate_pre_grad = (act_grad * pre_up * sigma * (1.0 + pre_gate * (1.0 - sigma))).astype(low)
    up_pre_grad = (act_grad * silu).astype(low)
    pre_grad = jnp.concatenate([gate_pre_grad, up_pre_grad], 1)

    input_part = contract(pre_grad, pair_weight, 1, 1).astype(low)
    back = to_tokens(input_part)
    gate_grad_rows = tensor_sum(gate_grad_part.reshape(EXPERTS, MOST))
    gate_grad_near = jnp.stack(
        [gate_grad_rows[0]]
        + [swap(gate_grad_rows[s], "dp", s * group_count) for s in range(1, EXPERTS)],
        0,
    )
    expert_part = contract(activation, down_weight, 1, 1).astype(low)
    mixed = to_tokens(expert_part)
    layer_own = hidden + mixed
    layer_out = tensor_gather(layer_own.astype(low)).astype(full)

    pair_terms = contract(arrived, pre_grad, 0, 0).astype(low)
    down_terms = contract(grad_rows, activation, 0, 0).astype(low)
    pair_grad = turn_blocks(group_reduce(pair_terms, position, group_count), turn, inner)
    down_grad = turn_blocks(group_reduce(down_terms, position, group_count), turn, inner)
    expert_grad = jnp.stack([pair_grad[:, :hidden_size], pair_grad[:, hidden_size:], down_grad])

    gate_grad_parts = jnp.stack(three_parts(gate_grad_near), 1)
    gate_grad = jnp.sum(
        lax.dot_general(
            gate_grad_parts, chosen_blocks, (((2,), (1,)), ((0,), (0,))), preferred_element_type=full
        ),
        1,
    )
    gate_grad = jnp.take(gate_grad, near, axis=0)
    weighted = jnp.sum(gates * gate_grad, axis=0, keepdims=True)
    logit_grad = (gates * (gate_grad - weighted)).astype(low)
    router_grad = jnp.dot(logit_grad, moe_in, preferred_element_type=full)
    moe_grad = contract(logit_grad, router_own, 0, 0) + back

    grad_out = grad_own.astype(full)
    scaled_grad = moe_grad * gain_second_own
    moe_gain_grad = jnp.sum(moe_grad * normed_two, axis=0)
    mean_two = tensor_sum(jnp.sum(scaled_grad * normed_two, axis=1)[None]) / width
    hidden_grad = grad_out + scale_two * (scaled_grad - normed_two * mean_two.reshape(rows, 1))
    attn_grad = tensor_gather(hidden_grad.astype(low))
    out_grad = contract(attn_grad, context_rows, 0, 0)
    out_shard = lax.psum_scatter(
        out_grad.astype(low), "dp", scatter_dimension=0, tiled=True
    ).astype(full)
    context_grad = heads_of(jnp.dot(attn_grad, out_full, preferred_element_type=full).astype(low))

    def backward_sequence(operands):
        query_seq, key_seq, value_seq, logsum_seq, grad_seq = operands
        scores = scores_of(query_seq, key_seq)
        probs = jnp.exp(scores - logsum_seq[:, :, None])
        rounded = probs.astype(low)
        prob_grad = jnp.einsum("qhd,khd->hqk", grad_seq, value_seq, preferred_element_type=full)
        score_grad = (
            probs * (prob_grad - jnp.sum(probs * prob_grad, axis=2, keepdims=True))
        ).astype(low)
        query_grad = (
            jnp.einsum("hqk,khd->qhd", score_grad, key_seq, preferred_element_type=full) * scale
        )
        key_grad = (
            jnp.einsum("hqk,qhd->khd", score_grad, query_seq, preferred_element_type=full) * scale
        )
        value_grad = jnp.einsum("hqk,qhd->khd", rounded, grad_seq, preferred_element_type=full)
        return (
            rotate(query_grad, cosine, -sine).astype(low),
            rotate(key_grad, cosine, -sine).astype(low),
            value_grad.astype(low),
        )

    query_back, key_back, value_back = lax.map(
        backward_sequence, (query, keys, values, logsum, context_grad)
    )
    qkv_grad_rows = jnp.concatenate(
        [v.reshape(rows, size) for v in (query_back, key_back, value_back)], axis=1
    )
    qkv_grad = contract(normed_in, qkv_grad_rows, 0, 0).astype(low)
    qkv_shard = lax.psum_scatter(qkv_grad, "dp", scatter_dimension=0, tiled=True).astype(full)
    normed_grad = tensor_reduce(contract(qkv_grad_rows, qkv_flat, 1, 1).astype(low))
    normed_one = inputs_own * scale_one
    scaled_in = normed_grad * gain_first_own
    attn_gain_grad = jnp.sum(normed_grad * normed_one, axis=0)
    mean_one = tensor_sum(jnp.sum(scaled_in * normed_one, axis=1)[None]) / width
    input_own = hidden_grad + scale_one * (scaled_in - normed_one * mean_one.reshape(rows, 1))
    input_grad = tensor_gather(input_own.astype(low)).astype(full)

    mine = jnp.concatenate(
        [router_grad, attn_gain_grad[None], moe_gain_grad[None]], 0
    )
    mine = lax.dynamic_update_slice_in_dim(
        jnp.zeros((mine.shape[0], width), full), mine, place * size, 1
    )
    share = width // dp_count
    mine = lax.dynamic_slice_in_dim(all_sum(mine), index * share, share, 1)
    return (
        layer_out,
        input_grad,
        mine[EXPERTS],
        qkv_shard.reshape(share, 3, size),
        out_shard,
        mine[EXPERTS + 1],
        mine[:EXPERTS].T,
        expert_grad,
    )


def solution(mesh):
    placed = (
        P("dp", None),
        P("dp"),
        P("dp", None, "tensor"),
        P("dp", "tensor"),
        P("dp"),
        P("dp", None),
        P(None, "dp", "tensor"),
        P("dp", None),
        P("dp", None),
    )
    return jax.shard_map(
        body,
        mesh=mesh,
        in_specs=placed,
        out_specs=(
            P("dp", None),
            P("dp", None),
            P("dp"),
            P("dp", None, "tensor"),
            P("dp", "tensor"),
            P("dp"),
            P("dp", None),
            P(None, "dp", "tensor"),
        ),
        check_vma=False,
    )
```

```python
import functools
import math

import jax
import jax.numpy as jnp
from jax import lax
from jax.experimental import pallas as pl
from jax.experimental.pallas import tpu as pltpu
from jax.sharding import PartitionSpec as P

HEAD = 128
EXPERTS = 4
SEQ = 1024
BLOCK = 256
MOST = 768


epsilon = 1e-05
theta_base = 10000.0
masked_out = -1e30
low = jnp.bfloat16
full = jnp.float32


def swap(value, axis, distance):
    return lax.ppermute(value, axis, [(i, i ^ distance) for i in range(lax.axis_size(axis))])


def contract(left, right, left_dim, right_dim):
    return lax.dot_general(
        left, right, (((left_dim,), (right_dim,)), ((), ())), preferred_element_type=jnp.float32
    )


def levels_of(count):
    return count.bit_length() - 1


def side_of(index, bit):
    return (index >> bit) & 1 == 1


def tensor_sum(value):
    for bit in range(levels_of(lax.axis_size("tensor"))):
        value = value + swap(value, "tensor", 1 << bit)
    return value


def all_sum(value):
    for axis in ("tensor", "dp"):
        for bit in range(levels_of(lax.axis_size(axis))):
            value = value + swap(value, axis, 1 << bit)
    return value


def tensor_reduce(part):
    count = lax.axis_size("tensor")
    place = lax.axis_index("tensor")
    size = part.shape[1] // count
    blocks = [part[:, i * size : (i + 1) * size] for i in range(count)]
    for bit in range(levels_of(count)):
        upper = side_of(place, bit)
        kept = [jnp.where(upper, b, a) for a, b in zip(blocks[::2], blocks[1::2])]
        given = [jnp.where(upper, a, b) for a, b in zip(blocks[::2], blocks[1::2])]
        sent = jnp.concatenate([v.astype(low) for v in given], 1)
        came = swap(sent, "tensor", 1 << bit)
        blocks = [
            v.astype(full) + came[:, i * size : (i + 1) * size].astype(full)
            for i, v in enumerate(kept)
        ]
    return blocks[0]


def tensor_gather(own):
    count = lax.axis_size("tensor")
    place = lax.axis_index("tensor")
    size = own.shape[1]
    held = own
    order = list(range(levels_of(count)))[::-1]
    for bit in order:
        came = swap(held, "tensor", 1 << bit)
        upper = side_of(place, bit)
        number = held.shape[1] // size
        mine = [held[:, i * size : (i + 1) * size] for i in range(number)]
        theirs = [came[:, i * size : (i + 1) * size] for i in range(number)]
        pairs = []
        for a, b in zip(mine, theirs):
            pairs.append((jnp.where(upper, b, a), jnp.where(upper, a, b)))
        held = jnp.concatenate([v for pair in pairs for v in pair], 1)
    return held


def after(value, *others):
    return lax.optimization_barrier((value, *others))[0]


def rotary_tables():
    half = HEAD // 2
    freqs = theta_base ** (-(jnp.arange(half, dtype=full) * 2.0 / HEAD))
    angles = jnp.arange(SEQ, dtype=full)[:, None] * freqs[None, :]
    cosine = jnp.cos(angles)
    sine = jnp.sin(angles)
    return (jnp.concatenate([cosine, cosine], 1), jnp.concatenate([-sine, sine], 1))


def limits(mib):
    return pltpu.CompilerParams(vmem_limit_bytes=mib << 20)


def cost(flops, moved, powers=0):
    return pl.CostEstimate(flops=int(flops), bytes_accessed=int(moved), transcendentals=int(powers))


def dot_cols(a, b):
    return lax.dot_general(a, b, (((1,), (1,)), ((), ())), preferred_element_type=full)


def dot_rows(a, b):
    return lax.dot_general(a, b, (((0,), (0,)), ((), ())), preferred_element_type=full)


def attention_kernel(scale, q_in, k_in, v_in, cos, sin, out, q_out, k_out, v_out, logs):
    def turned(ref):
        x = ref[...]
        return (x * cos[...] + pltpu.roll(x, HEAD // 2, 1) * sin[...]).astype(low)

    q_out[...] = turned(q_in)
    k_out[...] = turned(k_in)
    v_out[...] = v_in[...].astype(low)
    for block in range(SEQ // BLOCK):
        mine = pl.ds(block * BLOCK, BLOCK)
        seen = pl.ds(0, (block + 1) * BLOCK)
        scores = dot_cols(q_out[mine, :], k_out[seen, :]) * scale
        peak = jnp.max(scores, axis=1, keepdims=True)
        expo = jnp.exp(scores - peak)
        total = jnp.sum(expo, axis=1, keepdims=True)
        probs = (expo / total).astype(low)
        out[mine, :] = jnp.dot(probs, v_out[seen, :], preferred_element_type=full).astype(low)
        logs[0, mine, :] = peak + jnp.log(total)


def attention(qkv, cosine, sine, scale):
    rows = qkv.shape[0]
    size = qkv.shape[1] // 3
    heads = size // HEAD
    block = (SEQ, HEAD)
    table = pl.BlockSpec(block, lambda s, h: (0, 0))
    spec = pl.BlockSpec(block, lambda s, h: (s, h))
    shape = jax.ShapeDtypeStruct((rows, size), low)
    pairs = rows * heads * SEQ * 5 // 8
    return pl.pallas_call(
        functools.partial(attention_kernel, scale),
        grid=(rows // SEQ, heads),
        in_specs=[
            pl.BlockSpec(block, lambda s, h: (s, h)),
            pl.BlockSpec(block, lambda s, h: (s, heads + h)),
            pl.BlockSpec(block, lambda s, h: (s, 2 * heads + h)),
            table,
            table,
        ],
        out_specs=[spec] * 4 + [pl.BlockSpec((1, SEQ, 1), lambda s, h: (h, s, 0))],
        out_shape=[shape] * 4 + [jax.ShapeDtypeStruct((heads, rows, 1), full)],
        compiler_params=limits(48),
        cost_estimate=cost(4 * pairs * HEAD, rows * size * 20, pairs),
        name="attention",
    )(qkv, qkv, qkv, cosine, sine)


def attention_back_kernel(scale, heads, q_in, k_in, v_in, logs, grad, cos, sin, out, dk, dv):
    head = pl.program_id(1)
    dk[...] = jnp.zeros_like(dk)
    dv[...] = jnp.zeros_like(dv)

    def columns(which):
        return pl.ds(pl.multiple_of((which * heads + head) * HEAD, HEAD), HEAD)

    def turned(x, at):
        return (x * cos[at, :] - pltpu.roll(x, HEAD // 2, 1) * sin[at, :]).astype(low)

    for block in range(SEQ // BLOCK):
        mine = pl.ds(block * BLOCK, BLOCK)
        seen = pl.ds(0, (block + 1) * BLOCK)
        query, keys, values, given = q_in[mine, :], k_in[seen, :], v_in[seen, :], grad[mine, :]
        probs = jnp.exp(dot_cols(query, keys) * scale - logs[0, mine, :])
        prob_grad = dot_cols(given, values)
        inner = jnp.sum(probs * prob_grad, axis=1, keepdims=True)
        score_grad = (probs * (prob_grad - inner)).astype(low)
        query_grad = jnp.dot(score_grad, keys, preferred_element_type=full) * scale
        out[mine, columns(0)] = turned(query_grad, mine)
        dk[seen, :] += dot_rows(score_grad, query)
        dv[seen, :] += dot_rows(probs.astype(low), given)
    whole = pl.ds(0, SEQ)
    out[:, columns(1)] = turned(dk[...] * scale, whole)
    out[:, columns(2)] = dv[...].astype(low)


def attention_back(query, keys, values, logs, grad, cosine, sine, scale):
    rows, size = query.shape
    heads = size // HEAD
    block = (SEQ, HEAD)
    table = pl.BlockSpec(block, lambda s, h: (0, 0))
    spec = pl.BlockSpec(block, lambda s, h: (s, h))
    pairs = rows * heads * SEQ * 5 // 8
    return pl.pallas_call(
        functools.partial(attention_back_kernel, scale, heads),
        grid=(rows // SEQ, heads),
        in_specs=[spec] * 3
        + [pl.BlockSpec((1, SEQ, 1), lambda s, h: (h, s, 0)), spec, table, table],
        out_specs=pl.BlockSpec((SEQ, 3 * size), lambda s, h: (s, 0)),
        out_shape=jax.ShapeDtypeStruct((rows, 3 * size), low),
        scratch_shapes=[pltpu.VMEM(block, full)] * 2,
        compiler_params=limits(48),
        cost_estimate=cost(10 * pairs * HEAD, rows * size * 16, pairs),
        name="attention_back",
    )(query, keys, values, logs, grad, cosine, sine)


def expert_kernel(count, carried, *refs):
    blocks, refs = refs[:count], refs[count:]
    pair, raw, gate = refs[:3]
    rows_out, act_out, grad_out, even, odd, gate_grad, held = refs[3 + carried :]
    size = blocks[0].shape[1]
    hidden = raw.shape[1]
    for i, ref in enumerate(blocks):
        held[:, i * size : (i + 1) * size] = ref[...]
    rows_out[...] = held[...]
    both = jnp.dot(held[...], pair[...], preferred_element_type=full)
    pre_gate = both[:, :hidden]
    pre_up = both[:, hidden:]
    sigma = 1.0 / (1.0 + jnp.exp(-pre_gate))
    silu = pre_gate * sigma
    act = silu * pre_up
    back = raw[...].astype(full)
    gate_grad[...] = jnp.sum(act * back, axis=1, keepdims=True)
    act_out[...] = (act * gate[...]).astype(low)
    back = back * gate[...]
    grad_out[:, :hidden] = (back * pre_up * sigma * (1.0 + pre_gate * (1.0 - sigma))).astype(low)
    grad_out[:, hidden:] = (back * silu).astype(low)
    part = dot_cols(grad_out[...], pair[...]).astype(low)
    for i in range(count):
        (odd if i % 2 else even)[:, i // 2 * size : (i // 2 + 1) * size] = part[
            :, i * size : (i + 1) * size
        ]


def expert_pass(step, blocks, pair, raw, gate, carried):
    count = len(blocks)
    size = blocks[0].shape[1]
    width, both = pair.shape
    hidden = both // 2
    total = raw.shape[0]
    tile = 256
    steps = MOST // tile
    here = lambda i: (step * steps + i, 0)
    near = lambda i: (i, 0)
    near_spec = lambda columns: pl.BlockSpec((tile, columns), near)
    here_spec = lambda columns: pl.BlockSpec((tile, columns), here)
    shape = lambda r, c, t=low: jax.ShapeDtypeStruct((r, c), t)
    inputs = [*blocks, pair, raw, gate, *carried]
    return pl.pallas_call(
        functools.partial(expert_kernel, count, len(carried)),
        grid=(steps,),
        in_specs=[near_spec(size)] * count
        + [
            pl.BlockSpec((width, both), lambda i: (0, 0), pipeline_mode=pl.Buffered(1)),
            here_spec(hidden),
            near_spec(1),
        ]
        + [pl.BlockSpec(memory_space=pl.ANY)] * len(carried),
        out_specs=[
            here_spec(width),
            here_spec(hidden),
            here_spec(both),
            near_spec(width // 2),
            near_spec(width // 2),
            near_spec(1),
        ],
        out_shape=[
            shape(total, width),
            shape(total, hidden),
            shape(total, both),
            shape(MOST, width // 2),
            shape(MOST, width // 2),
            shape(MOST, 1, full),
        ],
        scratch_shapes=[pltpu.VMEM((tile, width), low)],
        input_output_aliases={count + 3 + i: i for i in range(len(carried))},
        compiler_params=limits(60),
        cost_estimate=cost(
            4 * MOST * width * both, width * both * 2 + MOST * (width * 8 + hidden * 8), MOST * hidden
        ),
        name="expert",
    )(*inputs)


def expert_grad_kernel(hidden, turn, pair_a, pair_b, down_a, down_b, out):
    which = pl.program_id(0)

    @pl.when(which < 2)
    def _():
        out[0] = (pair_a[...].astype(full) + pair_b[...].astype(full))[:, :hidden]

    @pl.when(which == 2)
    def _():
        out[0] = (down_a[...].astype(full) + down_b[...].astype(full))[:, :hidden]


def expert_grad_sum(turn, pair_a, pair_b, down_a, down_b, hidden, inner):
    rows = pair_a.shape[0]
    padded = pair_a.shape[1] // 2
    tile = 256
    per = rows // inner // tile
    pair_spec = pl.BlockSpec(
        (tile, padded), lambda w, i, turn: (i ^ (turn[0] * per), jnp.minimum(w, 1))
    )
    down_spec = pl.BlockSpec((tile, padded), lambda w, i, turn: (jnp.where(w == 2, i, 0), 0))
    return pl.pallas_call(
        functools.partial(expert_grad_kernel, hidden),
        grid_spec=pltpu.PrefetchScalarGridSpec(
            num_scalar_prefetch=1,
            grid=(3, rows // tile),
            in_specs=[pair_spec, pair_spec, down_spec, down_spec],
            out_specs=pl.BlockSpec((1, tile, hidden), lambda w, i, turn: (w, i, 0)),
        ),
        out_shape=jax.ShapeDtypeStruct((3, rows, hidden), full),
        compiler_params=limits(32),
        cost_estimate=cost(rows * padded * 3, rows * padded * 24),
        name="expert_grad_sum",
    )(turn, pair_a, pair_b, down_a, down_b)


def near_blocks(own):
    held = [own]
    for bit in range(levels_of(lax.axis_size("tensor")))[::-1]:
        theirs = [swap(v, "tensor", 1 << bit) for v in held]
        held = [v for pair in zip(held, theirs) for v in pair]
    return held


def near_reduce(even, odd):
    count = lax.axis_size("tensor")
    number = count // 2
    size = even.shape[1] // number
    came = swap(odd, "tensor", 1)
    for bit in range(1, levels_of(count)):
        blocks = [
            even[:, i * size : (i + 1) * size].astype(full)
            + came[:, i * size : (i + 1) * size].astype(full)
            for i in range(number)
        ]
        sent = [v.astype(low) for v in blocks[1::2]]
        even = jnp.concatenate(blocks[::2], 1)
        came = swap(jnp.concatenate(sent, 1), "tensor", 1 << bit)
        number //= 2
    return (even.astype(full) + came.astype(full)).astype(low)

def turn_blocks(value, index, number):
    size = value.shape[0] // number
    blocks = [value[i * size : (i + 1) * size] for i in range(number)]
    for bit in range(levels_of(number)):
        upper = side_of(index, bit)
        blocks = [jnp.where(upper, blocks[i ^ (1 << bit)], blocks[i]) for i in range(number)]
    return jnp.concatenate(blocks, 0) if number > 1 else value


def group_gather(local, position, group_count):
    held = local
    for bit in range(levels_of(group_count)):
        partner = swap(held, "dp", 1 << bit)
        upper = side_of(position, bit)
        held = jnp.concatenate(
            [jnp.where(upper, partner, held), jnp.where(upper, held, partner)], axis=0
        )
    return held


def group_sum(term, width, position, group_count):
    top = levels_of(group_count) - 1
    half = width // 2
    upper = (position >> top) & 1
    given = term((1 - upper) * half, half)
    came = swap(given, "dp", 1 << top)
    kept = functools.partial(term, upper * half, half)
    return given, came, kept


def group_finish(kept, came, position, group_count):
    for bit in range(levels_of(group_count) - 1)[::-1]:
        current = kept.astype(full) + came.astype(full)
        middle = current.shape[0] // 2
        upper = (position >> bit) & 1
        kept = lax.dynamic_slice_in_dim(current, upper * middle, middle, 0)
        given = lax.dynamic_slice_in_dim(current, (1 - upper) * middle, middle, 0)
        came = swap(given.astype(low), "dp", 1 << bit)
    return kept, came


def body(
    tokens,
    attn_gain,
    qkv_weight,
    out_weight,
    moe_gain,
    router_weight,
    expert_weight,
    routes,
    cotangent,
):
    rows = tokens.shape[0]
    width = tokens.shape[1]
    tensor_count = lax.axis_size("tensor")
    dp_count = lax.axis_size("dp")
    group_count = dp_count // EXPERTS
    size = width // tensor_count
    hidden_size = expert_weight.shape[2]
    padded = -(-hidden_size // 128) * 128
    scale = 1.0 / math.sqrt(HEAD)
    place = lax.axis_index("tensor")
    index = lax.axis_index("dp")
    expert = index // group_count
    member = index % group_count
    inner = tensor_count // group_count
    position = member ^ (place // inner)
    turn = place % inner

    def own_columns(value):
        return lax.dynamic_slice_in_dim(value, place * size, size, 1)

    extras = jnp.concatenate([router_weight, attn_gain[:, None], moe_gain[:, None]], 1)
    extras = jnp.pad(extras, ((0, 0), (0, 128 - extras.shape[1])))
    first = lax.all_gather(
        jnp.concatenate([qkv_weight.reshape(-1, 3 * size), extras], 1), "dp", axis=0, tiled=True
    )
    qkv_flat = first[:, : 3 * size]
    small = first[:, 3 * size :].T
    router_full = small[:EXPERTS]
    gain_first = small[EXPERTS : EXPERTS + 1].astype(full)
    gain_second = small[EXPERTS + 1 : EXPERTS + 2].astype(full)
    gain_first_own = own_columns(gain_first)
    gain_second_own = own_columns(gain_second)
    router_own = own_columns(router_full)
    out_full = lax.all_gather(out_weight, "dp", axis=0, tiled=True)

    near = jnp.arange(EXPERTS, dtype=jnp.int32) ^ expert
    names = jnp.arange(EXPERTS, dtype=jnp.int32)
    hits = jnp.sum((routes.T[None] == names[:, None, None]).astype(jnp.int32), 1)
    rank = jnp.cumsum(hits, axis=1) - hits
    slot_near = jnp.take(jnp.where(hits > 0, rank, -1), near, axis=0)
    places = jnp.arange(MOST, dtype=jnp.int32)[:, None]
    chosen = [(places == slot_near[s][None, :]).astype(low) for s in range(EXPERTS)]

    def packed(own):
        return [jnp.dot(c, own, preferred_element_type=full).astype(low) for c in chosen]

    def exchange(parts):
        return [parts[0]] + [swap(parts[s], "dp", s * group_count) for s in range(1, EXPERTS)]

    def unpacked(parts):
        total = contract(chosen[0], parts[0], 0, 0)
        for c, part in zip(chosen[1:], parts[1:]):
            total = total + contract(c, part, 0, 0)
        return total

    def widened(value):
        return jnp.pad(value, ((0, 0), (0, padded - hidden_size)))

    down_local = widened(expert_weight[2])
    pair_local = turn_blocks(
        jnp.concatenate([widened(expert_weight[0]), widened(expert_weight[1])], 1), turn, inner
    )
    down_weight = lax.optimization_barrier(
        group_gather(after(down_local, first), member, group_count)
    )
    pair_weight = group_gather(after(pair_local, down_weight), position, group_count)

    grad_own = own_columns(cotangent)
    grad_packed = [after(v, first) for v in packed(grad_own)]
    grad_rows = lax.all_gather(
        jnp.concatenate(exchange(grad_packed), 0), "tensor", axis=1, tiled=True
    )

    inputs = tokens.astype(full)
    scale_one = lax.rsqrt(jnp.mean(inputs * inputs, axis=1, keepdims=True) + epsilon)
    normed_in = (inputs * scale_one * gain_first).astype(low)
    inputs_own = own_columns(tokens).astype(full)
    qkv = jnp.dot(normed_in, qkv_flat, preferred_element_type=full)
    cosine, sine = rotary_tables()
    context, query, keys, values, logs = attention(qkv, cosine, sine, scale)
    attn_part = contract(context, out_full, 1, 1).astype(low)
    hidden = after(inputs_own + tensor_reduce(attn_part), down_weight)

    scaled_hidden = (hidden * gain_second_own).astype(low)
    sums = tensor_sum(
        jnp.concatenate(
            [contract(router_own, scaled_hidden, 1, 1), jnp.sum(hidden * hidden, 1)[None]], 0
        )
    )
    scale_two_row = lax.rsqrt(sums[EXPERTS:] / width + epsilon)
    scale_two = scale_two_row.reshape(rows, 1)
    logits = sums[:EXPERTS] * scale_two_row
    normed_two = hidden * scale_two
    moe_in = (normed_two * gain_second_own).astype(low)
    named = hits > 0
    top = jnp.max(jnp.where(named, logits, masked_out), axis=0, keepdims=True)
    weight = jnp.where(named, jnp.exp(logits - top), 0.0)
    gates = weight / jnp.sum(weight, axis=0, keepdims=True)

    def three_parts(value):
        a = value.astype(low)
        b = (value - a.astype(full)).astype(low)
        return jnp.stack([a, b, (value - a.astype(full) - b.astype(full)).astype(low)])

    moe_packed = packed(moe_in)
    arrived = [near_blocks(v) for v in exchange(moe_packed)]

    gates_near = jnp.take(gates, near, axis=0)
    gate_rows = exchange(
        [
            jnp.sum(contract(three_parts(gates_near[s]), chosen[s], 1, 1), 0)
            for s in range(EXPERTS)
        ]
    )

    grad_rows = after(grad_rows, *moe_packed)
    raw = jnp.dot(grad_rows, down_weight, preferred_element_type=full).astype(low)
    carried = ()
    returned = []
    gate_grads = []
    for step in range(EXPERTS):
        moe_rows, activation, pre_grad, even, odd, gate_grad = expert_pass(
            step, arrived[step], pair_weight, raw, gate_rows[step][:, None], carried
        )
        carried = (moe_rows, activation, pre_grad)
        returned.append(near_reduce(even, odd))
        gate_grads.append(gate_grad)
    back = unpacked(exchange(returned))
    gate_grad_rows = tensor_sum(jnp.concatenate(gate_grads, 1).T)
    gate_grad_near = jnp.stack(exchange([gate_grad_rows[s] for s in range(EXPERTS)]))

    def down_term(start, number):
        part = lax.dynamic_slice_in_dim(grad_rows, start, number, 1)
        return contract(part, activation, 0, 0).astype(low)

    def pair_term(start, number):
        part = lax.dynamic_slice_in_dim(moe_rows, start, number, 1)
        return contract(part, pre_grad, 0, 0).astype(low)

    down_given, down_came, down_kept = group_sum(down_term, width, member, group_count)
    pair_given, pair_came, pair_kept = group_sum(pair_term, width, position, group_count)
    expert_part = contract(
        after(activation, down_given, pair_given), down_weight, 1, 1
    ).astype(low)
    expert_own = lax.psum_scatter(expert_part, "tensor", scatter_dimension=1, tiled=True)
    mixed = unpacked(exchange([expert_own[s * MOST : (s + 1) * MOST] for s in range(EXPERTS)]))
    layer_own = hidden + mixed
    layer_out = tensor_gather(layer_own.astype(low)).astype(full)
    down_a, down_b = group_finish(down_kept(), down_came, member, group_count)
    pair_a, pair_b = group_finish(pair_kept(), pair_came, position, group_count)
    expert_grad = expert_grad_sum(
        turn[None].astype(jnp.int32), pair_a, pair_b, down_a, down_b, hidden_size, inner
    )

    gate_grad = jnp.stack(
        [
            jnp.sum(contract(three_parts(gate_grad_near[s]), chosen[s], 1, 0), 0)
            for s in range(EXPERTS)
        ]
    )
    gate_grad = jnp.take(gate_grad, near, axis=0)
    weighted = jnp.sum(gates * gate_grad, axis=0, keepdims=True)
    logit_grad = (gates * (gate_grad - weighted)).astype(low)
    router_grad = jnp.dot(logit_grad, moe_in, preferred_element_type=full)
    moe_grad = contract(logit_grad, router_own, 0, 0) + back

    grad_out = grad_own.astype(full)
    scaled_grad = moe_grad * gain_second_own
    moe_gain_grad = jnp.sum(moe_grad * normed_two, axis=0)
    mean_two = tensor_sum(jnp.sum(scaled_grad * normed_two, axis=1)[None]) / width
    hidden_grad = grad_out + scale_two * (scaled_grad - normed_two * mean_two.reshape(rows, 1))
    attn_grad = tensor_gather(hidden_grad.astype(low))
    out_grad = contract(attn_grad, context, 0, 0)
    out_shard = lax.psum_scatter(
        out_grad.astype(low), "dp", scatter_dimension=0, tiled=True
    ).astype(full)
    context_grad = jnp.dot(attn_grad, out_full, preferred_element_type=full).astype(low)
    qkv_grad_rows = attention_back(query, keys, values, logs, context_grad, cosine, sine, scale)
    qkv_grad = contract(normed_in, qkv_grad_rows, 0, 0).astype(low)
    qkv_shard = lax.psum_scatter(qkv_grad, "dp", scatter_dimension=0, tiled=True).astype(full)
    normed_grad = tensor_reduce(contract(qkv_grad_rows, qkv_flat, 1, 1).astype(low))
    normed_one = inputs_own * scale_one
    scaled_in = normed_grad * gain_first_own
    attn_gain_grad = jnp.sum(normed_grad * normed_one, axis=0)
    mean_one = tensor_sum(jnp.sum(scaled_in * normed_one, axis=1)[None]) / width
    input_own = hidden_grad + scale_one * (scaled_in - normed_one * mean_one.reshape(rows, 1))
    input_grad = tensor_gather(input_own.astype(low)).astype(full)

    mine = jnp.concatenate([router_grad, attn_gain_grad[None], moe_gain_grad[None]], 0)
    mine = lax.dynamic_update_slice_in_dim(
        jnp.zeros((mine.shape[0], width), full), mine, place * size, 1
    )
    share = width // dp_count
    mine = lax.dynamic_slice_in_dim(all_sum(mine), index * share, share, 1)
    return (
        layer_out,
        input_grad,
        mine[EXPERTS],
        qkv_shard.reshape(share, 3, size),
        out_shard,
        mine[EXPERTS + 1],
        mine[:EXPERTS].T,
        expert_grad,
    )


def solution(mesh):
    placed = (
        P("dp", None),
        P("dp"),
        P("dp", None, "tensor"),
        P("dp", "tensor"),
        P("dp"),
        P("dp", None),
        P(None, "dp", "tensor"),
        P("dp", None),
        P("dp", None),
    )
    return jax.shard_map(
        body,
        mesh=mesh,
        in_specs=placed,
        out_specs=(
            P("dp", None),
            P("dp", None),
            P("dp"),
            P("dp", None, "tensor"),
            P("dp", "tensor"),
            P("dp"),
            P("dp", None),
            P(None, "dp", "tensor"),
        ),
        check_vma=False,
    )
```

```python
import functools
import math

import jax
import jax.numpy as jnp
from jax import lax
from jax.experimental import pallas as pl
from jax.experimental.pallas import tpu as pltpu
from jax.sharding import PartitionSpec as P

HEAD = 128
EXPERTS = 4
SEQ = 1024
BLOCK = 256
MOST = 768


epsilon = 1e-05
theta_base = 10000.0
masked_out = -1e30
low = jnp.bfloat16
full = jnp.float32


def swap(value, axis, distance):
    return lax.ppermute(value, axis, [(i, i ^ distance) for i in range(lax.axis_size(axis))])


def contract(left, right, left_dim, right_dim):
    return lax.dot_general(
        left, right, (((left_dim,), (right_dim,)), ((), ())), preferred_element_type=jnp.float32
    )


def levels_of(count):
    return count.bit_length() - 1


def side_of(index, bit):
    return (index >> bit) & 1 == 1


def tensor_sum(value):
    for bit in range(levels_of(lax.axis_size("tensor"))):
        value = value + swap(value, "tensor", 1 << bit)
    return value


def all_sum(value):
    for axis in ("tensor", "dp"):
        for bit in range(levels_of(lax.axis_size(axis))):
            value = value + swap(value, axis, 1 << bit)
    return value


def tensor_reduce(part, filler=None):
    count = lax.axis_size("tensor")
    place = lax.axis_index("tensor")
    size = part.shape[1] // count
    blocks = [part[:, i * size : (i + 1) * size] for i in range(count)]
    for bit in range(levels_of(count)):
        upper = side_of(place, bit)
        kept = [jnp.where(upper, b, a) for a, b in zip(blocks[::2], blocks[1::2])]
        given = [jnp.where(upper, a, b) for a, b in zip(blocks[::2], blocks[1::2])]
        sent = jnp.concatenate([v.astype(low) for v in given], 1)
        came = swap(sent, "tensor", 1 << bit)
        if filler is not None and bit == levels_of(count) - 1:
            came = after(came, *filler(sent))
        blocks = [
            v.astype(full) + came[:, i * size : (i + 1) * size].astype(full)
            for i, v in enumerate(kept)
        ]
    return blocks[0]


def tensor_gather(own, filler=None):
    count = lax.axis_size("tensor")
    place = lax.axis_index("tensor")
    size = own.shape[1]
    held = own
    order = list(range(levels_of(count)))[::-1]
    for bit in order:
        came = swap(held, "tensor", 1 << bit)
        if filler is not None and bit == order[0]:
            came = after(came, *filler(held))
        upper = side_of(place, bit)
        number = held.shape[1] // size
        mine = [held[:, i * size : (i + 1) * size] for i in range(number)]
        theirs = [came[:, i * size : (i + 1) * size] for i in range(number)]
        pairs = []
        for a, b in zip(mine, theirs):
            pairs.append((jnp.where(upper, b, a), jnp.where(upper, a, b)))
        held = jnp.concatenate([v for pair in pairs for v in pair], 1)
    return held


def after(value, *others):
    return lax.optimization_barrier((value, *others))[0]


def rotary_tables():
    half = HEAD // 2
    freqs = theta_base ** (-(jnp.arange(half, dtype=full) * 2.0 / HEAD))
    angles = jnp.arange(SEQ, dtype=full)[:, None] * freqs[None, :]
    cosine = jnp.cos(angles)
    sine = jnp.sin(angles)
    return (jnp.concatenate([cosine, cosine], 1), jnp.concatenate([-sine, sine], 1))


def limits(mib):
    return pltpu.CompilerParams(vmem_limit_bytes=mib << 20)


def cost(flops, moved, powers=0):
    return pl.CostEstimate(flops=int(flops), bytes_accessed=int(moved), transcendentals=int(powers))


def dot_cols(a, b):
    return lax.dot_general(a, b, (((1,), (1,)), ((), ())), preferred_element_type=full)


def dot_rows(a, b):
    return lax.dot_general(a, b, (((0,), (0,)), ((), ())), preferred_element_type=full)


def attention_kernel(scale, q_in, k_in, v_in, cos, sin, out, q_out, k_out, v_out, logs):
    def turned(ref):
        x = ref[...]
        return (x * cos[...] + pltpu.roll(x, HEAD // 2, 1) * sin[...]).astype(low)

    q_out[...] = turned(q_in)
    k_out[...] = turned(k_in)
    v_out[...] = v_in[...].astype(low)
    for block in range(SEQ // BLOCK):
        mine = pl.ds(block * BLOCK, BLOCK)
        seen = pl.ds(0, (block + 1) * BLOCK)
        scores = dot_cols(q_out[mine, :], k_out[seen, :]) * scale
        peak = jnp.max(scores, axis=1, keepdims=True)
        expo = jnp.exp(scores - peak)
        total = jnp.sum(expo, axis=1, keepdims=True)
        probs = (expo / total).astype(low)
        out[mine, :] = jnp.dot(probs, v_out[seen, :], preferred_element_type=full).astype(low)
        logs[0, mine, :] = peak + jnp.log(total)


def attention(qkv, cosine, sine, scale):
    rows = qkv.shape[0]
    size = qkv.shape[1] // 3
    heads = size // HEAD
    block = (SEQ, HEAD)
    table = pl.BlockSpec(block, lambda s, h: (0, 0))
    spec = pl.BlockSpec(block, lambda s, h: (s, h))
    shape = jax.ShapeDtypeStruct((rows, size), low)
    pairs = rows * heads * SEQ * 5 // 8
    return pl.pallas_call(
        functools.partial(attention_kernel, scale),
        grid=(rows // SEQ, heads),
        in_specs=[
            pl.BlockSpec(block, lambda s, h: (s, h)),
            pl.BlockSpec(block, lambda s, h: (s, heads + h)),
            pl.BlockSpec(block, lambda s, h: (s, 2 * heads + h)),
            table,
            table,
        ],
        out_specs=[spec] * 4 + [pl.BlockSpec((1, SEQ, 1), lambda s, h: (h, s, 0))],
        out_shape=[shape] * 4 + [jax.ShapeDtypeStruct((heads, rows, 1), full)],
        compiler_params=limits(48),
        cost_estimate=cost(4 * pairs * HEAD, rows * size * 20, pairs),
        name="attention",
    )(qkv, qkv, qkv, cosine, sine)


def attention_back_kernel(scale, heads, q_in, k_in, v_in, logs, grad, cos, sin, out, dk, dv):
    head = pl.program_id(1)
    dk[...] = jnp.zeros_like(dk)
    dv[...] = jnp.zeros_like(dv)

    def columns(which):
        return pl.ds(pl.multiple_of((which * heads + head) * HEAD, HEAD), HEAD)

    def turned(x, at):
        return (x * cos[at, :] - pltpu.roll(x, HEAD // 2, 1) * sin[at, :]).astype(low)

    for block in range(SEQ // BLOCK):
        mine = pl.ds(block * BLOCK, BLOCK)
        seen = pl.ds(0, (block + 1) * BLOCK)
        query, keys, values, given = q_in[mine, :], k_in[seen, :], v_in[seen, :], grad[mine, :]
        probs = jnp.exp(dot_cols(query, keys) * scale - logs[0, mine, :])
        prob_grad = dot_cols(given, values)
        inner = jnp.sum(probs * prob_grad, axis=1, keepdims=True)
        score_grad = (probs * (prob_grad - inner)).astype(low)
        query_grad = jnp.dot(score_grad, keys, preferred_element_type=full) * scale
        out[mine, columns(0)] = turned(query_grad, mine)
        dk[seen, :] += dot_rows(score_grad, query)
        dv[seen, :] += dot_rows(probs.astype(low), given)
    whole = pl.ds(0, SEQ)
    out[:, columns(1)] = turned(dk[...] * scale, whole)
    out[:, columns(2)] = dv[...].astype(low)


def attention_back(query, keys, values, logs, grad, cosine, sine, scale):
    rows, size = query.shape
    heads = size // HEAD
    block = (SEQ, HEAD)
    table = pl.BlockSpec(block, lambda s, h: (0, 0))
    spec = pl.BlockSpec(block, lambda s, h: (s, h))
    pairs = rows * heads * SEQ * 5 // 8
    return pl.pallas_call(
        functools.partial(attention_back_kernel, scale, heads),
        grid=(rows // SEQ, heads),
        in_specs=[spec] * 3
        + [pl.BlockSpec((1, SEQ, 1), lambda s, h: (h, s, 0)), spec, table, table],
        out_specs=pl.BlockSpec((SEQ, 3 * size), lambda s, h: (s, 0)),
        out_shape=jax.ShapeDtypeStruct((rows, 3 * size), low),
        scratch_shapes=[pltpu.VMEM(block, full)] * 2,
        compiler_params=limits(48),
        cost_estimate=cost(10 * pairs * HEAD, rows * size * 16, pairs),
        name="attention_back",
    )(query, keys, values, logs, grad, cosine, sine)


def place_rows(pieces, held, sems, upper, first):
    copies = []
    for ref, start, number, mine, there, column in pieces:
        half = held.shape[0] // 2
        columns = ref.shape[1]
        side = upper if mine else 1 - upper
        copies.append(
            pltpu.make_async_copy(
                ref.at[pl.ds(start, number), :],
                held.at[
                    pl.ds(pl.multiple_of(side * half + there, 64), number),
                    pl.ds(column * columns, columns),
                ],
                sems.at[len(copies)],
            )
        )

    @pl.when(first)
    def _():
        for copy in copies:
            copy.start()
        for copy in copies:
            copy.wait()


def down_pieces(own, came):
    half = own.shape[0]
    return [(own, 0, half, True, 0, 0), (came, 0, half, False, 0, 0)]


def pair_pieces(own_gate, own_up, came, rest):
    half, less = own_gate.shape[0], rest.shape[0]
    more = half - less
    return [
        (own_gate, 0, half, True, 0, 0),
        (own_up, 0, half, True, 0, 1),
        (came, 0, half, False, 0, 0),
        (came, half, more, False, 0, 1),
        (rest, 0, less, False, more, 1),
    ]


def column_block(where, i, size):
    return pl.ds(pl.multiple_of((i ^ where[0]) * size, size), size)


def down_kernel(split, where, mine, rest, own, came, rows_out, raw, held, sems):
    step = pl.program_id(0)
    place_rows(down_pieces(own, came), held, sems, where[1], step == 0)

    @pl.when(step < split)
    def _():
        rows_out[...] = mine[...]

    @pl.when(step >= split)
    def _():
        rows_out[...] = rest[...]

    raw[...] = jnp.dot(rows_out[...], held[...], preferred_element_type=full).astype(low)


def down_pass(where, mine, rest, own, came):
    total = mine.shape[0] + rest.shape[0]
    width, hidden = 2 * own.shape[0], own.shape[1]
    tile = 256
    split = mine.shape[0] // tile
    spec = lambda columns: pl.BlockSpec((tile, columns), lambda i, where: (i, 0))
    return pl.pallas_call(
        functools.partial(down_kernel, split),
        grid_spec=pltpu.PrefetchScalarGridSpec(
            num_scalar_prefetch=1,
            grid=(total // tile,),
            in_specs=[
                pl.BlockSpec((tile, width), lambda i, where: (jnp.minimum(i, split - 1), 0)),
                pl.BlockSpec((tile, width), lambda i, where: (jnp.maximum(i - split, 0), 0)),
            ]
            + [pl.BlockSpec(memory_space=pl.ANY)] * 2,
            out_specs=[spec(width), spec(hidden)],
            scratch_shapes=[pltpu.VMEM((width, hidden), low), pltpu.SemaphoreType.DMA((2,))],
        ),
        out_shape=[
            jax.ShapeDtypeStruct((total, width), low),
            jax.ShapeDtypeStruct((total, hidden), low),
        ],
        compiler_params=limits(48),
        cost_estimate=cost(
            2 * total * width * hidden, (total * (2 * width + hidden) + width * hidden) * 2
        ),
        name="down",
    )(where, mine, rest, own, came)


def up_kernel(where, act, own, came, out, held, sems):
    place_rows(down_pieces(own, came), held, sems, where[1], pl.program_id(0) == 0)
    out[...] = dot_cols(act[...], held[...]).astype(low)


def up_pass(where, act, own, came):
    total, hidden = act.shape
    width = 2 * own.shape[0]
    tile = 256
    spec = lambda columns: pl.BlockSpec((tile, columns), lambda i, where: (i, 0))
    return pl.pallas_call(
        up_kernel,
        grid_spec=pltpu.PrefetchScalarGridSpec(
            num_scalar_prefetch=1,
            grid=(total // tile,),
            in_specs=[spec(hidden)] + [pl.BlockSpec(memory_space=pl.ANY)] * 2,
            out_specs=spec(width),
            scratch_shapes=[pltpu.VMEM((width, hidden), low), pltpu.SemaphoreType.DMA((2,))],
        ),
        out_shape=jax.ShapeDtypeStruct((total, width), low),
        compiler_params=limits(48),
        cost_estimate=cost(
            2 * total * width * hidden, (total * (width + hidden) + width * hidden) * 2
        ),
        name="up",
    )(where, act, own, came)


def expert_kernel(count, carried, where, *refs):
    blocks, refs = refs[:count], refs[count:]
    weights, raw, gate = refs[:4], refs[4], refs[5]
    rows_out, act_out, grad_out, even, odd, gate_grad, pair, part, sems = refs[6 + carried :]
    size = blocks[0].shape[1]
    hidden = raw.shape[1]
    place_rows(pair_pieces(*weights), pair, sems, where[1], pl.program_id(0) == 0)
    for i, ref in enumerate(blocks):
        rows_out[:, column_block(where, i, size)] = ref[...]
    both = jnp.dot(rows_out[...], pair[...], preferred_element_type=full)
    pre_gate = both[:, :hidden]
    pre_up = both[:, hidden:]
    sigma = 1.0 / (1.0 + jnp.exp(-pre_gate))
    silu = pre_gate * sigma
    act = silu * pre_up
    back = raw[...].astype(full)
    gate_grad[...] = jnp.sum(act * back, axis=1, keepdims=True)
    act_out[...] = (act * gate[...]).astype(low)
    back = back * gate[...]
    grad_out[:, :hidden] = (back * pre_up * sigma * (1.0 + pre_gate * (1.0 - sigma))).astype(low)
    grad_out[:, hidden:] = (back * silu).astype(low)
    part[...] = dot_cols(grad_out[...], pair[...]).astype(low)
    for i in range(count):
        (odd if i % 2 else even)[:, i // 2 * size : (i // 2 + 1) * size] = part[
            :, column_block(where, i, size)
        ]


def expert_pass(step, where, blocks, weights, raw, gate, carried):
    count = len(blocks)
    size = blocks[0].shape[1]
    width, hidden = 2 * weights[0].shape[0], weights[0].shape[1]
    both = 2 * hidden
    total = raw.shape[0]
    tile = 256
    steps = MOST // tile
    here = lambda i, where: (step * steps + i, 0)
    near = lambda i, where: (i, 0)
    near_spec = lambda columns: pl.BlockSpec((tile, columns), near)
    here_spec = lambda columns: pl.BlockSpec((tile, columns), here)
    anywhere = pl.BlockSpec(memory_space=pl.ANY)
    shape = lambda r, c, t=low: jax.ShapeDtypeStruct((r, c), t)
    return pl.pallas_call(
        functools.partial(expert_kernel, count, len(carried)),
        grid_spec=pltpu.PrefetchScalarGridSpec(
            num_scalar_prefetch=1,
            grid=(steps,),
            in_specs=[near_spec(size)] * count
            + [anywhere] * 4
            + [here_spec(hidden), near_spec(1)]
            + [anywhere] * len(carried),
            out_specs=[
                here_spec(width),
                here_spec(hidden),
                here_spec(both),
                near_spec(width // 2),
                near_spec(width // 2),
                near_spec(1),
            ],
            scratch_shapes=[
                pltpu.VMEM((width, both), low),
                pltpu.VMEM((tile, width), low),
                pltpu.SemaphoreType.DMA((5,)),
            ],
        ),
        out_shape=[
            shape(total, width),
            shape(total, hidden),
            shape(total, both),
            shape(MOST, width // 2),
            shape(MOST, width // 2),
            shape(MOST, 1, full),
        ],
        input_output_aliases={count + 7 + i: i for i in range(len(carried))},
        compiler_params=limits(60),
        cost_estimate=cost(
            4 * MOST * width * both, width * both * 2 + MOST * (width * 8 + hidden * 8), MOST * hidden
        ),
        name="expert",
    )(where, *blocks, *weights, raw, gate, *carried)


def expert_grad_kernel(hidden, *refs):
    out = refs[-1]
    for k in range(3):

        @pl.when(pl.program_id(0) == k)
        def _():
            out[0] = (refs[2 * k][...].astype(full) + refs[2 * k + 1][...].astype(full))[:, :hidden]


def expert_grad_sum(terms, hidden):
    rows, padded = terms[0].shape
    tile = 256
    last = rows // tile - 1

    def spec(k):
        return pl.BlockSpec(
            (tile, padded), lambda w, i: (jnp.where(w == k, i, jnp.where(w < k, 0, last)), 0)
        )

    return pl.pallas_call(
        functools.partial(expert_grad_kernel, hidden),
        grid=(3, rows // tile),
        in_specs=[spec(k // 2) for k in range(6)],
        out_specs=pl.BlockSpec((1, tile, hidden), lambda w, i: (w, i, 0)),
        out_shape=jax.ShapeDtypeStruct((3, rows, hidden), full),
        compiler_params=limits(32),
        cost_estimate=cost(rows * padded * 3, rows * padded * 24),
        name="expert_grad_sum",
    )(*terms)


def near_blocks(own, *others):
    held = [own]
    for bit in range(levels_of(lax.axis_size("tensor")))[::-1]:
        theirs = [swap(v, "tensor", 1 << bit) for v in held]
        if bit and others:
            theirs = [after(v, *others) for v in theirs]
        held = [v for pair in zip(held, theirs) for v in pair]
    return held


def near_reduce(even, odd, meet, *others):
    count = lax.axis_size("tensor")
    number = count // 2
    size = even.shape[1] // number
    came = swap(odd, "tensor", 1)
    for bit in range(1, levels_of(count)):
        blocks = [
            even[:, i * size : (i + 1) * size].astype(full)
            + came[:, i * size : (i + 1) * size].astype(full)
            for i in range(number)
        ]
        sent = jnp.concatenate([v.astype(low) for v in blocks[1::2]], 1)
        if bit == levels_of(count) - 1:
            sent = after(sent, *others)
            meet.append(sent)
        even = jnp.concatenate(blocks[::2], 1)
        came = swap(sent, "tensor", 1 << bit)
        number //= 2
    return (even.astype(full) + came.astype(full)).astype(low)


def half_gather(local, group_count):
    held = local
    place = lax.axis_index("dp") % group_count
    for bit in range(levels_of(group_count) - 1):
        came = swap(held, "dp", 1 << bit)
        upper = side_of(place, bit)
        held = jnp.concatenate([jnp.where(upper, came, held), jnp.where(upper, held, came)], 0)
    return held


def dp_scatter(value):
    index = lax.axis_index("dp")
    for bit in range(levels_of(lax.axis_size("dp")))[::-1]:
        middle = value.shape[0] // 2
        upper = (index >> bit) & 1
        kept = lax.dynamic_slice_in_dim(value, upper * middle, middle, 0)
        given = lax.dynamic_slice_in_dim(value, (1 - upper) * middle, middle, 0)
        value = kept.astype(full) + swap(given.astype(low), "dp", 1 << bit).astype(full)
    return value


def group_finish(kept, came, position, group_count):
    for bit in range(levels_of(group_count) - 1)[::-1]:
        current = kept.astype(full) + came.astype(full)
        middle = current.shape[0] // 2
        upper = (position >> bit) & 1
        kept = lax.dynamic_slice_in_dim(current, upper * middle, middle, 0)
        given = lax.dynamic_slice_in_dim(current, (1 - upper) * middle, middle, 0)
        came = swap(given.astype(low), "dp", 1 << bit)
    return kept, came


def body(
    tokens,
    attn_gain,
    qkv_weight,
    out_weight,
    moe_gain,
    router_weight,
    expert_weight,
    routes,
    cotangent,
):
    rows = tokens.shape[0]
    width = tokens.shape[1]
    tensor_count = lax.axis_size("tensor")
    dp_count = lax.axis_size("dp")
    group_count = dp_count // EXPERTS
    size = width // tensor_count
    hidden_size = expert_weight.shape[2]
    padded = -(-hidden_size // 128) * 128
    scale = 1.0 / math.sqrt(HEAD)
    place = lax.axis_index("tensor")
    index = lax.axis_index("dp")
    expert = index // group_count
    member = index % group_count
    top_half = member >> (levels_of(group_count) - 1)
    where = jnp.stack([place, top_half]).astype(jnp.int32)

    def own_columns(value):
        return lax.dynamic_slice_in_dim(value, place * size, size, 1)

    extras = jnp.concatenate([router_weight, attn_gain[:, None], moe_gain[:, None]], 1)
    extras = jnp.pad(extras, ((0, 0), (0, 128 - extras.shape[1])))
    first = lax.all_gather(
        jnp.concatenate([qkv_weight.reshape(-1, 3 * size), out_weight, extras], 1),
        "dp",
        axis=0,
        tiled=True,
    )
    qkv_flat = first[:, : 3 * size]
    out_full = first[:, 3 * size : 4 * size]
    small = first[:, 4 * size :].T
    router_full = small[:EXPERTS]
    gain_first = small[EXPERTS : EXPERTS + 1].astype(full)
    gain_second = small[EXPERTS + 1 : EXPERTS + 2].astype(full)
    gain_first_own = own_columns(gain_first)
    gain_second_own = own_columns(gain_second)
    router_own = own_columns(router_full)

    near = jnp.arange(EXPERTS, dtype=jnp.int32) ^ expert
    names = jnp.arange(EXPERTS, dtype=jnp.int32)
    hits = jnp.sum((routes.T[None] == names[:, None, None]).astype(jnp.int32), 1)
    rank = jnp.cumsum(hits, axis=1) - hits
    slot_near = jnp.take(jnp.where(hits > 0, rank, -1), near, axis=0)
    places = jnp.arange(MOST, dtype=jnp.int32)[:, None]
    chosen = [(places == slot_near[s][None, :]).astype(low) for s in range(EXPERTS)]

    def packed(own):
        return [jnp.dot(c, own, preferred_element_type=full).astype(low) for c in chosen]

    def exchange(parts):
        return [parts[0]] + [swap(parts[s], "dp", s * group_count) for s in range(1, EXPERTS)]

    def unpacked(parts):
        total = contract(chosen[0], parts[0], 0, 0)
        for c, part in zip(chosen[1:], parts[1:]):
            total = total + contract(c, part, 0, 0)
        return total

    def widened(value):
        return jnp.pad(value, ((0, 0), (0, padded - hidden_size)))

    gate_mine, up_mine, down_mine = [
        half_gather(widened(expert_weight[k]), group_count) for k in range(3)
    ]
    half = width // 2
    mine_at, given_at = top_half * half, (1 - top_half) * half
    reach = group_count // 2

    def group_send(given, *others):
        return swap(after(given, *others), "dp", reach)

    cut = half // 2
    down = (down_mine, group_send(down_mine))
    pair_came = group_send(jnp.concatenate([gate_mine, up_mine[:cut]], 0), down[1])
    pair_rest = group_send(up_mine[cut:], pair_came)
    pair = (gate_mine, up_mine, pair_came, pair_rest)

    grad_own = own_columns(cotangent)
    grad_mine = jnp.dot(chosen[0], cotangent, preferred_element_type=full).astype(low)
    grad_came = exchange([after(v, down[1]) for v in packed(grad_own)])[1:]
    grad_rest = lax.all_gather(
        after(jnp.concatenate(grad_came, 0), pair_came), "tensor", axis=1, tiled=True
    )

    inputs = tokens.astype(full)
    scale_one = lax.rsqrt(jnp.mean(inputs * inputs, axis=1, keepdims=True) + epsilon)
    normed_in = (inputs * scale_one * gain_first).astype(low)
    inputs_own = own_columns(tokens).astype(full)
    qkv_flat = after(qkv_flat, *grad_came)
    qkv = jnp.dot(normed_in, qkv_flat, preferred_element_type=full)
    cosine, sine = rotary_tables()
    context, query, keys, values, logs = attention(qkv, cosine, sine, scale)
    attn_part = contract(context, out_full, 1, 1).astype(low)
    hidden = after(inputs_own + tensor_reduce(attn_part), pair_rest)

    scaled_hidden = (hidden * gain_second_own).astype(low)
    sums = tensor_sum(
        jnp.concatenate(
            [contract(router_own, scaled_hidden, 1, 1), jnp.sum(hidden * hidden, 1)[None]], 0
        )
    )
    scale_two_row = lax.rsqrt(sums[EXPERTS:] / width + epsilon)
    scale_two = scale_two_row.reshape(rows, 1)
    logits = sums[:EXPERTS] * scale_two_row
    normed_two = hidden * scale_two
    moe_in = (normed_two * gain_second_own).astype(low)
    named = hits > 0
    top = jnp.max(jnp.where(named, logits, masked_out), axis=0, keepdims=True)
    weight = jnp.where(named, jnp.exp(logits - top), 0.0)
    gates = weight / jnp.sum(weight, axis=0, keepdims=True)

    def three_parts(value):
        a = value.astype(low)
        b = (value - a.astype(full)).astype(low)
        return jnp.stack([a, b, (value - a.astype(full) - b.astype(full)).astype(low)])

    moe_packed = packed(moe_in)
    crossed = [moe_packed[0]] + [
        swap(moe_packed[s], "dp", s * group_count) for s in range(1, EXPERTS - 1)
    ]
    arrived = [near_blocks(moe_packed[0])]

    gates_near = after(jnp.take(gates, near, axis=0), crossed[1])
    gate_rows = exchange(
        [
            jnp.sum(contract(three_parts(gates_near[s]), chosen[s], 1, 1), 0)
            for s in range(EXPERTS)
        ]
    )

    grad_rows, raw = down_pass(where, after(grad_mine, *moe_packed), grad_rest, *down)
    carried = ()
    sums_sent = []
    returned = []
    gate_grads = []
    for step in range(EXPERTS):
        gate = gate_rows[step][:, None]
        if step == 2:
            gate = after(gate, sums_sent[0])
        if step == 3:
            gate = after(gate, sums_sent[1], returned[0])
        moe_rows, activation, pre_grad, even, odd, gate_grad = expert_pass(
            step, where, arrived[step], pair, raw, gate, carried
        )
        carried = (moe_rows, activation, pre_grad)
        if step == 0:
            arrived.append(near_blocks(crossed[1], even))
            crossed[2] = after(crossed[2], even)
            crossed.append(swap(after(moe_packed[3], crossed[2]), "dp", 3 * group_count))
        if step == 1:
            arrived.append(near_blocks(crossed[2], even))
            crossed[3] = after(crossed[3], even)
        if step == 2:
            arrived.append(near_blocks(crossed[3], even))
        returned.append(near_reduce(even, odd, sums_sent, *returned[2:]))
        gate_grads.append(gate_grad)
    own_returned = returned
    returned = exchange(returned)
    gate_grad_rows = tensor_sum(jnp.concatenate(gate_grads, 1).T)
    gate_grad_near = exchange([gate_grad_rows[s] for s in range(EXPERTS)])

    def term(left, right):
        def part(start, number):
            taken = lax.dynamic_slice_in_dim(left, start, number, 1)
            return contract(taken, right, 0, 0).astype(low)

        return part

    down_term = term(grad_rows, after(activation, sums_sent[2], own_returned[1]))
    down_given = down_term(given_at, half)
    gate_term = term(moe_rows, after(pre_grad[:, :padded], down_given, sums_sent[3]))
    gate_given = gate_term(given_at, half)
    up_term = term(moe_rows, after(pre_grad[:, padded:], gate_given, own_returned[3]))
    up_given = up_term(given_at, half)
    down_came = group_send(down_given)
    gate_came = group_send(gate_given, down_came)
    up_came = group_send(up_given, gate_came)
    expert_part = up_pass(
        where, after(activation, up_given, returned[1], *gate_grad_near), *down
    )
    expert_part = after(expert_part, down_came, returned[2])
    expert_own = lax.psum_scatter(expert_part, "tensor", scatter_dimension=1, tiled=True)
    mixed = unpacked(exchange([expert_own[s * MOST : (s + 1) * MOST] for s in range(EXPERTS)]))
    layer_own = hidden + mixed
    layer_out = tensor_gather(layer_own.astype(low)).astype(full)
    back = unpacked(returned)

    gate_grad = jnp.stack(
        [
            jnp.sum(contract(three_parts(gate_grad_near[s]), chosen[s], 1, 0), 0)
            for s in range(EXPERTS)
        ]
    )
    gate_grad = jnp.take(gate_grad, near, axis=0)
    weighted = jnp.sum(gates * gate_grad, axis=0, keepdims=True)
    logit_grad = (gates * (gate_grad - weighted)).astype(low)
    router_grad = jnp.dot(logit_grad, moe_in, preferred_element_type=full)
    moe_grad = contract(logit_grad, router_own, 0, 0) + back

    grad_out = grad_own.astype(full)
    scaled_grad = moe_grad * gain_second_own
    moe_gain_grad = jnp.sum(moe_grad * normed_two, axis=0)
    mean_two = tensor_sum(jnp.sum(scaled_grad * normed_two, axis=1)[None]) / width
    hidden_grad = grad_out + scale_two * (scaled_grad - normed_two * mean_two.reshape(rows, 1))
    kept = []

    def first_kept(sent):
        kept.append(term(grad_rows, after(activation, sent))(mine_at, half))
        kept.append(term(moe_rows, after(pre_grad[:, :padded], sent))(mine_at, half))
        return kept

    def last_kept(sent):
        kept.append(term(moe_rows, after(pre_grad[:, padded:], sent))(mine_at, half))
        return kept[2:]

    attn_grad = tensor_gather(hidden_grad.astype(low), first_kept)
    context_grad = jnp.dot(attn_grad, out_full, preferred_element_type=full).astype(low)
    qkv_grad_rows = attention_back(query, keys, values, logs, context_grad, cosine, sine, scale)
    qkv_grad_rows = after(qkv_grad_rows, gate_came)
    qkv_grad = contract(normed_in, qkv_grad_rows, 0, 0).astype(low)
    qkv_shard = lax.psum_scatter(qkv_grad, "dp", scatter_dimension=0, tiled=True).astype(full)
    normed_grad = tensor_reduce(
        contract(after(qkv_grad_rows, qkv_grad), qkv_flat, 1, 1).astype(low), last_kept
    )
    out_shard = dp_scatter(contract(attn_grad, context, 0, 0).astype(low))
    normed_one = inputs_own * scale_one
    scaled_in = normed_grad * gain_first_own
    attn_gain_grad = jnp.sum(normed_grad * normed_one, axis=0)
    mean_one = tensor_sum(jnp.sum(scaled_in * normed_one, axis=1)[None]) / width
    input_own = hidden_grad + scale_one * (scaled_in - normed_one * mean_one.reshape(rows, 1))
    input_own = after(input_own, up_came)
    input_grad = tensor_gather(input_own.astype(low)).astype(full)
    terms = []
    for mine_part, came in zip(
        (kept[1], kept[2], kept[0]), (gate_came, up_came, down_came)
    ):
        terms += group_finish(mine_part, came, member, group_count)
    expert_grad = expert_grad_sum(terms, hidden_size)

    mine = jnp.concatenate([router_grad, attn_gain_grad[None], moe_gain_grad[None]], 0)
    mine = lax.dynamic_update_slice_in_dim(
        jnp.zeros((mine.shape[0], width), full), mine, place * size, 1
    )
    share = width // dp_count
    mine = lax.dynamic_slice_in_dim(all_sum(mine), index * share, share, 1)
    return (
        layer_out,
        input_grad,
        mine[EXPERTS],
        qkv_shard.reshape(share, 3, size),
        out_shard,
        mine[EXPERTS + 1],
        mine[:EXPERTS].T,
        expert_grad,
    )


def solution(mesh):
    placed = (
        P("dp", None),
        P("dp"),
        P("dp", None, "tensor"),
        P("dp", "tensor"),
        P("dp"),
        P("dp", None),
        P(None, "dp", "tensor"),
        P("dp", None),
        P("dp", None),
    )
    return jax.shard_map(
        body,
        mesh=mesh,
        in_specs=placed,
        out_specs=(
            P("dp", None),
            P("dp", None),
            P("dp"),
            P("dp", None, "tensor"),
            P("dp", "tensor"),
            P("dp"),
            P("dp", None),
            P(None, "dp", "tensor"),
        ),
        check_vma=False,
    )
```

```python
import functools
import math

import jax
import jax.numpy as jnp
from jax import lax
from jax.experimental import pallas as pl
from jax.experimental.pallas import tpu as pltpu
from jax.sharding import PartitionSpec as P

HEAD = 128
EXPERTS = 4
SEQ = 1024
BLOCK = 256
MOST = 768


epsilon = 1e-05
theta_base = 10000.0
masked_out = -1e30
low = jnp.bfloat16
full = jnp.float32


def swap(value, axis, distance):
    return lax.ppermute(value, axis, [(i, i ^ distance) for i in range(lax.axis_size(axis))])


def contract(left, right, left_dim, right_dim):
    return lax.dot_general(
        left, right, (((left_dim,), (right_dim,)), ((), ())), preferred_element_type=jnp.float32
    )


def levels_of(count):
    return count.bit_length() - 1


def side_of(index, bit):
    return (index >> bit) & 1 == 1


def tensor_sum(value):
    for bit in range(levels_of(lax.axis_size("tensor"))):
        value = value + swap(value, "tensor", 1 << bit)
    return value


def all_sum(value):
    for axis in ("tensor", "dp"):
        for bit in range(levels_of(lax.axis_size(axis))):
            value = value + swap(value, axis, 1 << bit)
    return value


def tensor_reduce(part, filler=None):
    count = lax.axis_size("tensor")
    place = lax.axis_index("tensor")
    size = part.shape[1] // count
    blocks = [part[:, i * size : (i + 1) * size] for i in range(count)]
    for bit in range(levels_of(count)):
        upper = side_of(place, bit)
        kept = [jnp.where(upper, b, a) for a, b in zip(blocks[::2], blocks[1::2])]
        given = [jnp.where(upper, a, b) for a, b in zip(blocks[::2], blocks[1::2])]
        sent = jnp.concatenate([v.astype(low) for v in given], 1)
        came = swap(sent, "tensor", 1 << bit)
        if filler is not None and bit == levels_of(count) - 1:
            came = after(came, *filler(sent))
        blocks = [
            v.astype(full) + came[:, i * size : (i + 1) * size].astype(full)
            for i, v in enumerate(kept)
        ]
    return blocks[0]


def tensor_gather(own, filler=None):
    count = lax.axis_size("tensor")
    place = lax.axis_index("tensor")
    size = own.shape[1]
    held = own
    order = list(range(levels_of(count)))[::-1]
    for bit in order:
        came = swap(held, "tensor", 1 << bit)
        if filler is not None and bit == order[0]:
            came = after(came, *filler(held))
        upper = side_of(place, bit)
        number = held.shape[1] // size
        mine = [held[:, i * size : (i + 1) * size] for i in range(number)]
        theirs = [came[:, i * size : (i + 1) * size] for i in range(number)]
        pairs = []
        for a, b in zip(mine, theirs):
            pairs.append((jnp.where(upper, b, a), jnp.where(upper, a, b)))
        held = jnp.concatenate([v for pair in pairs for v in pair], 1)
    return held


def after(value, *others):
    return lax.optimization_barrier((value, *others))[0]


def rotary_tables():
    half = HEAD // 2
    freqs = theta_base ** (-(jnp.arange(half, dtype=full) * 2.0 / HEAD))
    angles = jnp.arange(SEQ, dtype=full)[:, None] * freqs[None, :]
    cosine = jnp.cos(angles)
    sine = jnp.sin(angles)
    return (jnp.concatenate([cosine, cosine], 1), jnp.concatenate([-sine, sine], 1))


def limits(mib):
    return pltpu.CompilerParams(vmem_limit_bytes=mib << 20)


def cost(flops, moved, powers=0):
    return pl.CostEstimate(flops=int(flops), bytes_accessed=int(moved), transcendentals=int(powers))


def dot_cols(a, b):
    return lax.dot_general(a, b, (((1,), (1,)), ((), ())), preferred_element_type=full)


def dot_rows(a, b):
    return lax.dot_general(a, b, (((0,), (0,)), ((), ())), preferred_element_type=full)


def attention_kernel(scale, q_in, k_in, v_in, cos, sin, out, q_out, k_out, v_out, logs):
    def turned(ref):
        x = ref[...]
        return (x * cos[...] + pltpu.roll(x, HEAD // 2, 1) * sin[...]).astype(low)

    q_out[...] = turned(q_in)
    k_out[...] = turned(k_in)
    v_out[...] = v_in[...].astype(low)
    for block in range(SEQ // BLOCK):
        mine = pl.ds(block * BLOCK, BLOCK)
        seen = pl.ds(0, (block + 1) * BLOCK)
        scores = dot_cols(q_out[mine, :], k_out[seen, :]) * scale
        peak = jnp.max(scores, axis=1, keepdims=True)
        expo = jnp.exp(scores - peak)
        total = jnp.sum(expo, axis=1, keepdims=True)
        probs = (expo / total).astype(low)
        out[mine, :] = jnp.dot(probs, v_out[seen, :], preferred_element_type=full).astype(low)
        logs[0, mine, :] = peak + jnp.log(total)


def attention(qkv, cosine, sine, scale):
    rows = qkv.shape[0]
    size = qkv.shape[1] // 3
    heads = size // HEAD
    block = (SEQ, HEAD)
    table = pl.BlockSpec(block, lambda s, h: (0, 0))
    spec = pl.BlockSpec(block, lambda s, h: (s, h))
    shape = jax.ShapeDtypeStruct((rows, size), low)
    pairs = rows * heads * SEQ * 5 // 8
    return pl.pallas_call(
        functools.partial(attention_kernel, scale),
        grid=(rows // SEQ, heads),
        in_specs=[
            pl.BlockSpec(block, lambda s, h: (s, h)),
            pl.BlockSpec(block, lambda s, h: (s, heads + h)),
            pl.BlockSpec(block, lambda s, h: (s, 2 * heads + h)),
            table,
            table,
        ],
        out_specs=[spec] * 4 + [pl.BlockSpec((1, SEQ, 1), lambda s, h: (h, s, 0))],
        out_shape=[shape] * 4 + [jax.ShapeDtypeStruct((heads, rows, 1), full)],
        compiler_params=limits(48),
        cost_estimate=cost(4 * pairs * HEAD, rows * size * 20, pairs),
        name="attention",
    )(qkv, qkv, qkv, cosine, sine)


def attention_back_kernel(scale, heads, q_in, k_in, v_in, logs, grad, cos, sin, out, dk, dv):
    head = pl.program_id(1)
    dk[...] = jnp.zeros_like(dk)
    dv[...] = jnp.zeros_like(dv)

    def columns(which):
        return pl.ds(pl.multiple_of((which * heads + head) * HEAD, HEAD), HEAD)

    def turned(x, at):
        return (x * cos[at, :] - pltpu.roll(x, HEAD // 2, 1) * sin[at, :]).astype(low)

    for block in range(SEQ // BLOCK):
        mine = pl.ds(block * BLOCK, BLOCK)
        seen = pl.ds(0, (block + 1) * BLOCK)
        query, keys, values, given = q_in[mine, :], k_in[seen, :], v_in[seen, :], grad[mine, :]
        probs = jnp.exp(dot_cols(query, keys) * scale - logs[0, mine, :])
        prob_grad = dot_cols(given, values)
        inner = jnp.sum(probs * prob_grad, axis=1, keepdims=True)
        score_grad = (probs * (prob_grad - inner)).astype(low)
        query_grad = jnp.dot(score_grad, keys, preferred_element_type=full) * scale
        out[mine, columns(0)] = turned(query_grad, mine)
        dk[seen, :] += dot_rows(score_grad, query)
        dv[seen, :] += dot_rows(probs.astype(low), given)
    whole = pl.ds(0, SEQ)
    out[:, columns(1)] = turned(dk[...] * scale, whole)
    out[:, columns(2)] = dv[...].astype(low)


def attention_back(query, keys, values, logs, grad, cosine, sine, scale):
    rows, size = query.shape
    heads = size // HEAD
    block = (SEQ, HEAD)
    table = pl.BlockSpec(block, lambda s, h: (0, 0))
    spec = pl.BlockSpec(block, lambda s, h: (s, h))
    pairs = rows * heads * SEQ * 5 // 8
    return pl.pallas_call(
        functools.partial(attention_back_kernel, scale, heads),
        grid=(rows // SEQ, heads),
        in_specs=[spec] * 3
        + [pl.BlockSpec((1, SEQ, 1), lambda s, h: (h, s, 0)), spec, table, table],
        out_specs=pl.BlockSpec((SEQ, 3 * size), lambda s, h: (s, 0)),
        out_shape=jax.ShapeDtypeStruct((rows, 3 * size), low),
        scratch_shapes=[pltpu.VMEM(block, full)] * 2,
        compiler_params=limits(48),
        cost_estimate=cost(10 * pairs * HEAD, rows * size * 16, pairs),
        name="attention_back",
    )(query, keys, values, logs, grad, cosine, sine)


def place_rows(pieces, held, sems, upper, first):
    copies = []
    for ref, start, number, mine, there, column in pieces:
        half = held.shape[0] // 2
        columns = ref.shape[1]
        side = upper if mine else 1 - upper
        copies.append(
            pltpu.make_async_copy(
                ref.at[pl.ds(start, number), :],
                held.at[
                    pl.ds(pl.multiple_of(side * half + there, 64), number),
                    pl.ds(column * columns, columns),
                ],
                sems.at[len(copies)],
            )
        )

    @pl.when(first)
    def _():
        for copy in copies:
            copy.start()
        for copy in copies:
            copy.wait()


def down_pieces(own, came):
    half = own.shape[0]
    return [(own, 0, half, True, 0, 0), (came, 0, half, False, 0, 0)]


def pair_pieces(own_gate, own_up, came, near, far):
    half, more = own_gate.shape[0], near.shape[0]
    return [
        (own_gate, 0, half, True, 0, 0),
        (own_up, 0, half, True, 0, 1),
        (came, 0, half, False, 0, 0),
        (near, 0, more, False, 0, 1),
        (far, 0, half - more, False, more, 1),
    ]


def column_block(where, i, size):
    return pl.ds(pl.multiple_of((i ^ where[0]) * size, size), size)


def down_kernel(count, split, where, mine, *refs):
    blocks = refs[:count]
    own, came, rows_out, raw, held, sems = refs[count:]
    step = pl.program_id(0)
    size = blocks[0].shape[1]
    place_rows(down_pieces(own, came), held, sems, where[1], step == 0)

    @pl.when(step < split)
    def _():
        rows_out[...] = mine[...]

    @pl.when(step >= split)
    def _():
        for i, ref in enumerate(blocks):
            rows_out[:, column_block(where, i, size)] = ref[...]

    raw[...] = jnp.dot(rows_out[...], held[...], preferred_element_type=full).astype(low)


def down_pass(where, mine, blocks, own, came):
    count = len(blocks)
    size = blocks[0].shape[1]
    width, hidden = 2 * own.shape[0], own.shape[1]
    total = mine.shape[0] + blocks[0].shape[0]
    tile = 256
    split = mine.shape[0] // tile
    anywhere = pl.BlockSpec(memory_space=pl.ANY)
    spec = lambda columns: pl.BlockSpec((tile, columns), lambda i, where: (i, 0))
    late = pl.BlockSpec((tile, size), lambda i, where: (jnp.maximum(i - split, 0), 0))
    return pl.pallas_call(
        functools.partial(down_kernel, count, split),
        grid_spec=pltpu.PrefetchScalarGridSpec(
            num_scalar_prefetch=1,
            grid=(total // tile,),
            in_specs=[
                pl.BlockSpec((tile, width), lambda i, where: (jnp.minimum(i, split - 1), 0))
            ]
            + [late] * count
            + [anywhere] * 2,
            out_specs=[spec(width), spec(hidden)],
            scratch_shapes=[pltpu.VMEM((width, hidden), low), pltpu.SemaphoreType.DMA((2,))],
        ),
        out_shape=[
            jax.ShapeDtypeStruct((total, width), low),
            jax.ShapeDtypeStruct((total, hidden), low),
        ],
        compiler_params=limits(48),
        cost_estimate=cost(
            2 * total * width * hidden, (total * (2 * width + hidden) + width * hidden) * 2
        ),
        name="down",
    )(where, mine, *blocks, own, came)


def up_kernel(where, act, own, came, out, held, sems):
    place_rows(down_pieces(own, came), held, sems, where[1], pl.program_id(0) == 0)
    out[...] = dot_cols(act[...], held[...]).astype(low)


def up_pass(where, act, own, came):
    total, hidden = act.shape
    width = 2 * own.shape[0]
    tile = 256
    spec = lambda columns: pl.BlockSpec((tile, columns), lambda i, where: (i, 0))
    return pl.pallas_call(
        up_kernel,
        grid_spec=pltpu.PrefetchScalarGridSpec(
            num_scalar_prefetch=1,
            grid=(total // tile,),
            in_specs=[spec(hidden)] + [pl.BlockSpec(memory_space=pl.ANY)] * 2,
            out_specs=spec(width),
            scratch_shapes=[pltpu.VMEM((width, hidden), low), pltpu.SemaphoreType.DMA((2,))],
        ),
        out_shape=jax.ShapeDtypeStruct((total, width), low),
        compiler_params=limits(48),
        cost_estimate=cost(
            2 * total * width * hidden, (total * (width + hidden) + width * hidden) * 2
        ),
        name="up",
    )(where, act, own, came)


def expert_kernel(count, carried, where, *refs):
    blocks, refs = refs[:count], refs[count:]
    weights, raw, routed, router = refs[:5], refs[5], refs[6], refs[7]
    rows_out, act_out, grad_out, even, odd, gate_grad, pair, part, sems = refs[8 + carried :]
    size = blocks[0].shape[1]
    hidden = raw.shape[1]
    place_rows(pair_pieces(*weights), pair, sems, where[1], pl.program_id(0) == 0)
    for i, ref in enumerate(blocks):
        rows_out[:, column_block(where, i, size)] = ref[...]
    both = jnp.dot(rows_out[...], pair[...], preferred_element_type=full)
    pre_gate = both[:, :hidden]
    pre_up = both[:, hidden:]
    sigma = 1.0 / (1.0 + jnp.exp(-pre_gate))
    silu = pre_gate * sigma
    act = silu * pre_up
    back = raw[...].astype(full)
    tile = back.shape[0]
    own = where[2].astype(full)
    other = jnp.broadcast_to(routed[...], (128, tile)).T - own
    logits = jnp.dot(rows_out[...], router[...], preferred_element_type=full)
    lane = lax.broadcasted_iota(jnp.int32, (tile, 128), 1).astype(full)
    ahead = jnp.where(lane == other, logits, 0.0) - jnp.where(lane == own, logits, 0.0)
    gate = 1.0 / (1.0 + jnp.exp(jnp.sum(ahead, axis=1, keepdims=True)))
    gate_sum = jnp.sum(act * back, axis=1, keepdims=True)
    gate_grad[...] = jnp.broadcast_to(gate_sum, (tile, 128)).T[:1]
    act_out[...] = (act * gate).astype(low)
    back = back * gate
    grad_out[:, :hidden] = (back * pre_up * sigma * (1.0 + pre_gate * (1.0 - sigma))).astype(low)
    grad_out[:, hidden:] = (back * silu).astype(low)
    part[...] = dot_cols(grad_out[...], pair[...]).astype(low)
    for i in range(count):
        (odd if i % 2 else even)[:, i // 2 * size : (i // 2 + 1) * size] = part[
            :, column_block(where, i, size)
        ]


def expert_pass(step, where, blocks, weights, raw, routed, router, carried):
    count = len(blocks)
    size = blocks[0].shape[1]
    width, hidden = 2 * weights[0].shape[0], weights[0].shape[1]
    both = 2 * hidden
    total = raw.shape[0]
    tile = 256
    steps = MOST // tile
    here = lambda i, where: (step * steps + i, 0)
    near = lambda i, where: (i, 0)
    near_spec = lambda columns: pl.BlockSpec((tile, columns), near)
    here_spec = lambda columns: pl.BlockSpec((tile, columns), here)
    row_spec = pl.BlockSpec((1, tile), lambda i, where: (0, i))
    anywhere = pl.BlockSpec(memory_space=pl.ANY)
    shape = lambda r, c, t=low: jax.ShapeDtypeStruct((r, c), t)
    return pl.pallas_call(
        functools.partial(expert_kernel, count, len(carried)),
        grid_spec=pltpu.PrefetchScalarGridSpec(
            num_scalar_prefetch=1,
            grid=(steps,),
            in_specs=[near_spec(size)] * count
            + [anywhere] * 5
            + [
                here_spec(hidden),
                row_spec,
                pl.BlockSpec((width, 128), lambda i, where: (0, 0)),
            ]
            + [anywhere] * len(carried),
            out_specs=[
                here_spec(width),
                here_spec(hidden),
                here_spec(both),
                near_spec(width // 2),
                near_spec(width // 2),
                row_spec,
            ],
            scratch_shapes=[
                pltpu.VMEM((width, both), low),
                pltpu.VMEM((tile, width), low),
                pltpu.SemaphoreType.DMA((5,)),
            ],
        ),
        out_shape=[
            shape(total, width),
            shape(total, hidden),
            shape(total, both),
            shape(MOST, width // 2),
            shape(MOST, width // 2),
            shape(1, MOST, full),
        ],
        input_output_aliases={count + 9 + i: i for i in range(len(carried))},
        compiler_params=limits(60),
        cost_estimate=cost(
            4 * MOST * width * both, width * both * 2 + MOST * (width * 8 + hidden * 8), MOST * hidden
        ),
        name="expert",
    )(where, *blocks, *weights, raw, routed, router, *carried)


def expert_grad_kernel(hidden, pieces, per, *refs):
    out = refs[-1]
    which, at = pl.program_id(0), pl.program_id(1)

    def add(ref, other):
        out[0] = (ref[...].astype(full) + other[...].astype(full))[:, :hidden]

    for k in range(pieces):

        @pl.when((which < 2) & (at // per == k))
        def _():
            add(refs[0], refs[1 + k])

    @pl.when(which == 2)
    def _():
        add(refs[1 + pieces], refs[2 + pieces])


def expert_grad_sum(pair, down, hidden):
    rows, padded = down[0].shape
    tile = min(256, rows)
    pieces = len(pair) - 1
    per = rows // tile // pieces
    last = rows // tile - 1

    def piece_spec(k):
        return pl.BlockSpec(
            (tile, padded),
            lambda w, i: (
                jnp.where(w == 2, per - 1, jnp.clip(i - k * per, 0, per - 1)),
                jnp.minimum(w, 1),
            ),
        )

    pair_spec = pl.BlockSpec(
        (tile, padded), lambda w, i: (jnp.where(w == 2, last, i), jnp.minimum(w, 1))
    )
    down_spec = pl.BlockSpec((tile, padded), lambda w, i: (jnp.where(w == 2, i, 0), 0))
    return pl.pallas_call(
        functools.partial(expert_grad_kernel, hidden, pieces, per),
        grid=(3, rows // tile),
        in_specs=[pair_spec] + [piece_spec(k) for k in range(pieces)] + [down_spec] * 2,
        out_specs=pl.BlockSpec((1, tile, hidden), lambda w, i: (w, i, 0)),
        out_shape=jax.ShapeDtypeStruct((3, rows, hidden), full),
        compiler_params=limits(40),
        cost_estimate=cost(rows * padded * 3, rows * padded * 24),
        name="expert_grad_sum",
    )(*pair, *down)


def near_blocks(own, *others):
    held = [own]
    for bit in range(levels_of(lax.axis_size("tensor")))[::-1]:
        theirs = [swap(v, "tensor", 1 << bit) for v in held]
        if bit and others:
            theirs = [after(v, *others) for v in theirs]
        held = [v for pair in zip(held, theirs) for v in pair]
    return held


def near_reduce(even, odd, meet, *others):
    count = lax.axis_size("tensor")
    number = count // 2
    size = even.shape[1] // number
    came = swap(odd, "tensor", 1)
    for bit in range(1, levels_of(count)):
        blocks = [
            even[:, i * size : (i + 1) * size].astype(full)
            + came[:, i * size : (i + 1) * size].astype(full)
            for i in range(number)
        ]
        sent = jnp.concatenate([v.astype(low) for v in blocks[1::2]], 1)
        if bit == levels_of(count) - 1:
            sent = after(sent, *others)
            meet.append(sent)
        even = jnp.concatenate(blocks[::2], 1)
        came = swap(sent, "tensor", 1 << bit)
        number //= 2
    return (even.astype(full) + came.astype(full)).astype(low)


def half_gather(local, group_count):
    held = local
    place = lax.axis_index("dp") % group_count
    for bit in range(levels_of(group_count) - 1):
        came = swap(held, "dp", 1 << bit)
        upper = side_of(place, bit)
        held = jnp.concatenate([jnp.where(upper, came, held), jnp.where(upper, held, came)], 0)
    return held


def group_finish(kept, came, position, group_count):
    if group_count > 2:
        came = jnp.concatenate(came, 0)
    for bit in range(levels_of(group_count) - 1)[::-1]:
        current = kept.astype(full) + came.astype(full)
        middle = current.shape[0] // 2
        upper = (position >> bit) & 1
        kept = lax.dynamic_slice_in_dim(current, upper * middle, middle, 0)
        given = lax.dynamic_slice_in_dim(current, (1 - upper) * middle, middle, 0)
        came = swap(given.astype(low), "dp", 1 << bit)
    return [kept, *came] if isinstance(came, list) else [kept, came]


def body(
    tokens,
    attn_gain,
    qkv_weight,
    out_weight,
    moe_gain,
    router_weight,
    expert_weight,
    routes,
    cotangent,
):
    rows = tokens.shape[0]
    width = tokens.shape[1]
    tensor_count = lax.axis_size("tensor")
    dp_count = lax.axis_size("dp")
    group_count = dp_count // EXPERTS
    size = width // tensor_count
    hidden_size = expert_weight.shape[2]
    padded = -(-hidden_size // 128) * 128
    scale = 1.0 / math.sqrt(HEAD)
    place = lax.axis_index("tensor")
    index = lax.axis_index("dp")
    expert = index // group_count
    member = index % group_count
    top_half = member >> (levels_of(group_count) - 1)
    where = jnp.stack([place, top_half, expert]).astype(jnp.int32)

    def own_columns(value):
        return lax.dynamic_slice_in_dim(value, place * size, size, 1)

    extras = jnp.concatenate([router_weight, attn_gain[:, None], moe_gain[:, None]], 1)
    extras = jnp.pad(extras, ((0, 0), (0, 128 - extras.shape[1])))
    first = lax.all_gather(
        jnp.concatenate([qkv_weight.reshape(-1, 3 * size), out_weight, extras], 1),
        "dp",
        axis=0,
        tiled=True,
    )
    qkv_flat = first[:, : 3 * size]
    out_full = first[:, 3 * size : 4 * size]
    small = first[:, 4 * size :].T
    router_full = small[:EXPERTS]
    gain_first = small[EXPERTS : EXPERTS + 1].astype(full)
    gain_second = small[EXPERTS + 1 : EXPERTS + 2].astype(full)
    gain_first_own = own_columns(gain_first)
    gain_second_own = own_columns(gain_second)
    router_own = own_columns(router_full)

    near = jnp.arange(EXPERTS, dtype=jnp.int32) ^ expert
    names = jnp.arange(EXPERTS, dtype=jnp.int32)
    hits = jnp.sum((routes.T[None] == names[:, None, None]).astype(jnp.int32), 1)
    rank = jnp.cumsum(hits, axis=1) - hits
    slot_near = jnp.take(jnp.where(hits > 0, rank, -1), near, axis=0)
    places = jnp.arange(MOST, dtype=jnp.int32)[:, None]
    chosen = [(places == slot_near[s][None, :]).astype(low) for s in range(EXPERTS)]

    def packed(own):
        return [jnp.dot(c, own, preferred_element_type=full).astype(low) for c in chosen]

    def exchange(parts):
        return [parts[0]] + [swap(parts[s], "dp", s * group_count) for s in range(1, EXPERTS)]

    def unpacked(parts):
        total = contract(chosen[0], parts[0], 0, 0)
        for c, part in zip(chosen[1:], parts[1:]):
            total = total + contract(c, part, 0, 0)
        return total

    def widened(value):
        return jnp.pad(value, ((0, 0), (0, padded - hidden_size)))

    gate_mine, up_mine, down_mine = [
        half_gather(widened(expert_weight[k]), group_count) for k in range(3)
    ]
    half = width // 2
    mine_at, given_at = top_half * half, (1 - top_half) * half
    reach = group_count // 2

    def group_send(given, *others):
        return swap(after(given, *others), "dp", reach)

    cut = half // 2
    down = (down_mine, group_send(down_mine))
    gate_came = group_send(gate_mine)
    up_near = group_send(up_mine[:cut], first)
    pair = (gate_mine, up_mine, gate_came, up_near, group_send(up_mine[cut:], up_near))

    grad_own = own_columns(cotangent)
    grad_mine = jnp.dot(chosen[0], cotangent, preferred_element_type=full).astype(low)
    grad_came = exchange(packed(grad_own))[1:]
    grad_blocks = near_blocks(after(jnp.concatenate(grad_came, 0), down[1]))
    route_sums = jnp.sum(routes, axis=1)[None].astype(low)
    routed = exchange([contract(route_sums, c, 1, 1) for c in chosen])

    inputs = tokens.astype(full)
    scale_one = lax.rsqrt(jnp.mean(inputs * inputs, axis=1, keepdims=True) + epsilon)
    normed_in = (inputs * scale_one * gain_first).astype(low)
    inputs_own = own_columns(tokens).astype(full)
    qkv_flat = after(qkv_flat, down[1], gate_came, *grad_blocks, *routed)
    qkv = jnp.dot(normed_in, qkv_flat, preferred_element_type=full)
    cosine, sine = rotary_tables()
    context, query, keys, values, logs = attention(qkv, cosine, sine, scale)
    attn_part = contract(context, out_full, 1, 1).astype(low)
    rows_raw = []

    def down_filler(sent):
        rows_raw.extend(down_pass(where, after(grad_mine, sent), grad_blocks, *down))
        return rows_raw

    hidden = after(inputs_own + tensor_reduce(attn_part, down_filler), up_near)

    scaled_hidden = (hidden * gain_second_own).astype(low)
    sums = tensor_sum(
        jnp.concatenate(
            [contract(router_own, scaled_hidden, 1, 1), jnp.sum(hidden * hidden, 1)[None]], 0
        )
    )
    scale_two_row = lax.rsqrt(sums[EXPERTS:] / width + epsilon)
    scale_two = scale_two_row.reshape(rows, 1)
    logits = sums[:EXPERTS] * scale_two_row
    normed_two = hidden * scale_two
    moe_in = (normed_two * gain_second_own).astype(low)
    named = hits > 0
    top = jnp.max(jnp.where(named, logits, masked_out), axis=0, keepdims=True)
    weight = jnp.where(named, jnp.exp(logits - top), 0.0)
    gates = weight / jnp.sum(weight, axis=0, keepdims=True)

    def three_parts(value):
        a = value.astype(low)
        b = (value - a.astype(full)).astype(low)
        return jnp.stack([a, b, (value - a.astype(full) - b.astype(full)).astype(low)])

    moe_packed = packed(moe_in)
    crossed = [moe_packed[0]] + [
        swap(moe_packed[s], "dp", s * group_count) for s in range(1, EXPERTS - 1)
    ]
    arrived = [near_blocks(moe_packed[0])]

    carried = ()
    sums_sent = []
    returned = []
    gate_grads = []
    router_block = first[:, 4 * size :]
    for step in range(EXPERTS):
        named_sum = routed[step]
        if step == 2:
            named_sum = after(named_sum, sums_sent[0])
        if step == 3:
            named_sum = after(named_sum, sums_sent[1], returned[0], gate_grads[1])
        moe_rows, activation, pre_grad, even, odd, gate_grad = expert_pass(
            step, where, arrived[step], pair, rows_raw[1], named_sum, router_block, carried
        )
        carried = (moe_rows, activation, pre_grad)
        if step == 0:
            arrived.append(near_blocks(crossed[1], even))
            crossed[2] = after(crossed[2], even)
            crossed.append(swap(after(moe_packed[3], crossed[2]), "dp", 3 * group_count))
        if step == 1:
            arrived.append(near_blocks(crossed[2], even))
            crossed[3] = after(crossed[3], even)
        if step == 2:
            arrived.append(near_blocks(crossed[3], even))
        returned.append(near_reduce(even, odd, sums_sent, *returned[2:]))
        gate_grads.append(swap(gate_grad, "dp", step * group_count) if step else gate_grad)
    own_returned = returned
    returned = exchange(returned)
    gate_grad_near = gate_grads
    grad_rows = rows_raw[0]

    def term(left, right):
        def part(start, number):
            taken = lax.dynamic_slice_in_dim(left, start, number, 1)
            return contract(taken, right, 0, 0).astype(low)

        return part

    expert_part = up_pass(where, after(activation, sums_sent[2], own_returned[1], gate_grads[2]), *down)
    expert_own = lax.psum_scatter(
        after(expert_part, sums_sent[3], gate_grads[3]), "tensor", scatter_dimension=1, tiled=True
    )
    down_given = term(grad_rows, after(activation, expert_part, sums_sent[3], own_returned[2]))(
        given_at, half
    )
    down_sum = group_send(down_given)
    pair_term = term(moe_rows, after(pre_grad, down_given, own_returned[3]))
    quarter = half // 2
    pair_given = [pair_term(given_at + k * quarter, quarter) for k in range(2)]
    pair_sum = [group_send(pair_given[0], down_sum)]
    pair_sum.append(group_send(pair_given[1], pair_sum[0]))
    mixed = unpacked(exchange([expert_own[s * MOST : (s + 1) * MOST] for s in range(EXPERTS)]))
    layer_own = hidden + mixed
    layer_out = tensor_gather(layer_own.astype(low)).astype(full)
    returned = [after(v, *pair_given) for v in returned]
    returned[3] = after(returned[3], down_sum)
    back = unpacked(returned)

    gate_grad = jnp.concatenate(
        [
            jnp.sum(contract(three_parts(gate_grad_near[s][0]), chosen[s], 1, 0), 0, keepdims=True)
            for s in range(EXPERTS)
        ],
        0,
    )
    scaled_back = back * gain_second_own
    sums = tensor_sum(
        jnp.concatenate([gate_grad, jnp.sum(scaled_back * normed_two, axis=1)[None]], 0)
    )
    gate_grad = jnp.take(sums[:EXPERTS], near, axis=0)
    weighted = jnp.sum(gates * gate_grad, axis=0, keepdims=True)
    logit_grad = (gates * (gate_grad - weighted)).astype(low)
    mean_two = (
        sums[EXPERTS:] + jnp.sum(logit_grad.astype(full) * logits, axis=0, keepdims=True)
    ) / width
    moe_grad = contract(logit_grad, router_own, 0, 0) + back

    grad_out = grad_own.astype(full)
    hidden_grad = grad_out + scale_two * (
        moe_grad * gain_second_own - normed_two * mean_two.reshape(rows, 1)
    )
    router_grad = jnp.dot(logit_grad, moe_in, preferred_element_type=full)
    moe_gain_grad = jnp.sum(moe_grad * normed_two, axis=0)
    kept = []

    def keep(sent):
        kept.append(term(grad_rows, after(activation, sent))(mine_at, half))
        return kept[:1]

    def keep_pair(sent):
        kept.append(term(moe_rows, after(pre_grad, sent))(mine_at, half))
        return kept[1:]

    attn_grad = tensor_gather(hidden_grad.astype(low), keep)
    context_grad = jnp.dot(attn_grad, out_full, preferred_element_type=full).astype(low)
    out_shard = lax.psum_scatter(
        contract(after(attn_grad, context_grad), context, 0, 0).astype(low), "dp", scatter_dimension=0, tiled=True
    ).astype(full)
    qkv_grad_rows = attention_back(query, keys, values, logs, context_grad, cosine, sine, scale)
    qkv_grad_rows = after(qkv_grad_rows, pair_sum[0])
    qkv_grad = contract(normed_in, qkv_grad_rows, 0, 0).astype(low)
    qkv_shard = lax.psum_scatter(qkv_grad, "dp", scatter_dimension=0, tiled=True).astype(full)
    normed_grad = tensor_reduce(
        contract(after(qkv_grad_rows, qkv_grad), qkv_flat, 1, 1).astype(low), keep_pair
    )
    normed_one = inputs_own * scale_one
    scaled_in = normed_grad * gain_first_own
    attn_gain_grad = jnp.sum(normed_grad * normed_one, axis=0)
    mean_one = tensor_sum(jnp.sum(scaled_in * normed_one, axis=1)[None]) / width
    input_own = hidden_grad + scale_one * (scaled_in - normed_one * mean_one.reshape(rows, 1))
    input_own = after(input_own, pair_sum[1])
    input_grad = tensor_gather(input_own.astype(low)).astype(full)
    expert_grad = expert_grad_sum(
        group_finish(kept[1], pair_sum, member, group_count),
        group_finish(kept[0], [down_sum], member, group_count),
        hidden_size,
    )

    mine = jnp.concatenate([router_grad, attn_gain_grad[None], moe_gain_grad[None]], 0)
    mine = lax.dynamic_update_slice_in_dim(
        jnp.zeros((mine.shape[0], width), full), mine, place * size, 1
    )
    share = width // dp_count
    mine = lax.dynamic_slice_in_dim(all_sum(mine), index * share, share, 1)
    return (
        layer_out,
        input_grad,
        mine[EXPERTS],
        qkv_shard.reshape(share, 3, size),
        out_shard,
        mine[EXPERTS + 1],
        mine[:EXPERTS].T,
        expert_grad,
    )


def solution(mesh):
    placed = (
        P("dp", None),
        P("dp"),
        P("dp", None, "tensor"),
        P("dp", "tensor"),
        P("dp"),
        P("dp", None),
        P(None, "dp", "tensor"),
        P("dp", None),
        P("dp", None),
    )
    return jax.shard_map(
        body,
        mesh=mesh,
        in_specs=placed,
        out_specs=(
            P("dp", None),
            P("dp", None),
            P("dp"),
            P("dp", None, "tensor"),
            P("dp", "tensor"),
            P("dp"),
            P("dp", None),
            P(None, "dp", "tensor"),
        ),
        check_vma=False,
    )
```

```python
import functools
import math

import jax
import jax.numpy as jnp
from jax import lax
from jax.experimental import pallas as pl
from jax.experimental.pallas import tpu as pltpu
from jax.sharding import PartitionSpec as P

HEAD = 128
EXPERTS = 4
SEQ = 1024
BLOCK = 256
MOST = 768


epsilon = 1e-05
theta_base = 10000.0
masked_out = -1e30
low = jnp.bfloat16
full = jnp.float32


def swap(value, axis, distance):
    return lax.ppermute(value, axis, [(i, i ^ distance) for i in range(lax.axis_size(axis))])


def contract(left, right, left_dim, right_dim):
    return lax.dot_general(
        left, right, (((left_dim,), (right_dim,)), ((), ())), preferred_element_type=jnp.float32
    )


def levels_of(count):
    return count.bit_length() - 1


def side_of(index, bit):
    return (index >> bit) & 1 == 1


def tensor_sum(value):
    for bit in range(levels_of(lax.axis_size("tensor"))):
        value = value + swap(value, "tensor", 1 << bit)
    return value


def all_sum(value):
    for axis in ("tensor", "dp"):
        for bit in range(levels_of(lax.axis_size(axis))):
            value = value + swap(value, axis, 1 << bit)
    return value


def tensor_reduce(part, filler=None, others=()):
    count = lax.axis_size("tensor")
    place = lax.axis_index("tensor")
    size = part.shape[1] // count
    blocks = [part[:, i * size : (i + 1) * size] for i in range(count)]
    for bit in range(levels_of(count)):
        upper = side_of(place, bit)
        kept = [jnp.where(upper, b, a) for a, b in zip(blocks[::2], blocks[1::2])]
        given = [jnp.where(upper, a, b) for a, b in zip(blocks[::2], blocks[1::2])]
        sent = jnp.concatenate([v.astype(low) for v in given], 1)
        if others and bit == levels_of(count) - 1:
            sent = after(sent, *others)
        came = swap(sent, "tensor", 1 << bit)
        if filler is not None and bit == levels_of(count) - 1:
            came = after(came, *filler(sent))
        blocks = [
            v.astype(full) + came[:, i * size : (i + 1) * size].astype(full)
            for i, v in enumerate(kept)
        ]
    return blocks[0]


def tensor_gather(own, filler=None):
    count = lax.axis_size("tensor")
    place = lax.axis_index("tensor")
    size = own.shape[1]
    held = own
    order = list(range(levels_of(count)))[::-1]
    for bit in order:
        came = swap(held, "tensor", 1 << bit)
        if filler is not None and bit == order[0]:
            came = after(came, *filler(held))
        upper = side_of(place, bit)
        number = held.shape[1] // size
        mine = [held[:, i * size : (i + 1) * size] for i in range(number)]
        theirs = [came[:, i * size : (i + 1) * size] for i in range(number)]
        pairs = []
        for a, b in zip(mine, theirs):
            pairs.append((jnp.where(upper, b, a), jnp.where(upper, a, b)))
        held = jnp.concatenate([v for pair in pairs for v in pair], 1)
    return held


def after(value, *others):
    return lax.optimization_barrier((value, *others))[0]


def rotary_tables():
    half = HEAD // 2
    freqs = theta_base ** (-(jnp.arange(half, dtype=full) * 2.0 / HEAD))
    angles = jnp.arange(SEQ, dtype=full)[:, None] * freqs[None, :]
    cosine = jnp.cos(angles)
    sine = jnp.sin(angles)
    return (jnp.concatenate([cosine, cosine], 1), jnp.concatenate([-sine, sine], 1))


def limits(mib):
    return pltpu.CompilerParams(vmem_limit_bytes=mib << 20)


def cost(flops, moved, powers=0):
    return pl.CostEstimate(flops=int(flops), bytes_accessed=int(moved), transcendentals=int(powers))


def dot_cols(a, b):
    return lax.dot_general(a, b, (((1,), (1,)), ((), ())), preferred_element_type=full)


def dot_rows(a, b):
    return lax.dot_general(a, b, (((0,), (0,)), ((), ())), preferred_element_type=full)


def attention_kernel(scale, q_in, k_in, v_in, cos, sin, out, q_out, k_out, v_out, logs):
    def turned(ref):
        x = ref[...]
        return (x * cos[...] + pltpu.roll(x, HEAD // 2, 1) * sin[...]).astype(low)

    q_out[...] = turned(q_in)
    k_out[...] = turned(k_in)
    v_out[...] = v_in[...].astype(low)
    for block in range(SEQ // BLOCK):
        mine = pl.ds(block * BLOCK, BLOCK)
        seen = pl.ds(0, (block + 1) * BLOCK)
        scores = dot_cols(q_out[mine, :], k_out[seen, :]) * scale
        peak = jnp.max(scores, axis=1, keepdims=True)
        expo = jnp.exp(scores - peak)
        total = jnp.sum(expo, axis=1, keepdims=True)
        probs = (expo / total).astype(low)
        out[mine, :] = jnp.dot(probs, v_out[seen, :], preferred_element_type=full).astype(low)
        logs[0, mine, :] = peak + jnp.log(total)


def attention(qkv, cosine, sine, scale):
    rows = qkv.shape[0]
    size = qkv.shape[1] // 3
    heads = size // HEAD
    block = (SEQ, HEAD)
    table = pl.BlockSpec(block, lambda s, h: (0, 0))
    spec = pl.BlockSpec(block, lambda s, h: (s, h))
    shape = jax.ShapeDtypeStruct((rows, size), low)
    pairs = rows * heads * SEQ * 5 // 8
    return pl.pallas_call(
        functools.partial(attention_kernel, scale),
        grid=(rows // SEQ, heads),
        in_specs=[
            pl.BlockSpec(block, lambda s, h: (s, h)),
            pl.BlockSpec(block, lambda s, h: (s, heads + h)),
            pl.BlockSpec(block, lambda s, h: (s, 2 * heads + h)),
            table,
            table,
        ],
        out_specs=[spec] * 4 + [pl.BlockSpec((1, SEQ, 1), lambda s, h: (h, s, 0))],
        out_shape=[shape] * 4 + [jax.ShapeDtypeStruct((heads, rows, 1), full)],
        compiler_params=limits(48),
        cost_estimate=cost(4 * pairs * HEAD, rows * size * 20, pairs),
        name="attention",
    )(qkv, qkv, qkv, cosine, sine)


def attention_back_kernel(scale, heads, q_in, k_in, v_in, logs, grad, cos, sin, out, dk, dv):
    head = pl.program_id(1)
    dk[...] = jnp.zeros_like(dk)
    dv[...] = jnp.zeros_like(dv)

    def columns(which):
        return pl.ds(pl.multiple_of((which * heads + head) * HEAD, HEAD), HEAD)

    def turned(x, at):
        return (x * cos[at, :] - pltpu.roll(x, HEAD // 2, 1) * sin[at, :]).astype(low)

    for block in range(SEQ // BLOCK):
        mine = pl.ds(block * BLOCK, BLOCK)
        seen = pl.ds(0, (block + 1) * BLOCK)
        query, keys, values, given = q_in[mine, :], k_in[seen, :], v_in[seen, :], grad[mine, :]
        probs = jnp.exp(dot_cols(query, keys) * scale - logs[0, mine, :])
        prob_grad = dot_cols(given, values)
        inner = jnp.sum(probs * prob_grad, axis=1, keepdims=True)
        score_grad = (probs * (prob_grad - inner)).astype(low)
        query_grad = jnp.dot(score_grad, keys, preferred_element_type=full) * scale
        out[mine, columns(0)] = turned(query_grad, mine)
        dk[seen, :] += dot_rows(score_grad, query)
        dv[seen, :] += dot_rows(probs.astype(low), given)
    whole = pl.ds(0, SEQ)
    out[:, columns(1)] = turned(dk[...] * scale, whole)
    out[:, columns(2)] = dv[...].astype(low)


def attention_back(query, keys, values, logs, grad, cosine, sine, scale):
    rows, size = query.shape
    heads = size // HEAD
    block = (SEQ, HEAD)
    table = pl.BlockSpec(block, lambda s, h: (0, 0))
    spec = pl.BlockSpec(block, lambda s, h: (s, h))
    pairs = rows * heads * SEQ * 5 // 8
    return pl.pallas_call(
        functools.partial(attention_back_kernel, scale, heads),
        grid=(rows // SEQ, heads),
        in_specs=[spec] * 3
        + [pl.BlockSpec((1, SEQ, 1), lambda s, h: (h, s, 0)), spec, table, table],
        out_specs=pl.BlockSpec((SEQ, 3 * size), lambda s, h: (s, 0)),
        out_shape=jax.ShapeDtypeStruct((rows, 3 * size), low),
        scratch_shapes=[pltpu.VMEM(block, full)] * 2,
        compiler_params=limits(48),
        cost_estimate=cost(10 * pairs * HEAD, rows * size * 16, pairs),
        name="attention_back",
    )(query, keys, values, logs, grad, cosine, sine)


def place_rows(pieces, held, sems, upper, first):
    copies = []
    for ref, start, number, mine, there, column in pieces:
        half = held.shape[0] // 2
        columns = ref.shape[1]
        side = upper if mine else 1 - upper
        copies.append(
            pltpu.make_async_copy(
                ref.at[pl.ds(start, number), :],
                held.at[
                    pl.ds(pl.multiple_of(side * half + there, 64), number),
                    pl.ds(column * columns, columns),
                ],
                sems.at[len(copies)],
            )
        )

    @pl.when(first)
    def _():
        for copy in copies:
            copy.start()
        for copy in copies:
            copy.wait()


def down_pieces(own, came):
    half = own.shape[0]
    return [(own, 0, half, True, 0, 0), (came, 0, half, False, 0, 0)]


cuts = (
    ((0, 0, 48),),
    ((0, 48, 64),),
    ((0, 64, 88),),
    ((0, 88, 100),),
    ((0, 100, 128), (1, 0, 28)),
    ((1, 28, 128),),
)


def pair_pieces(own_gate, own_up, *came):
    half = own_gate.shape[0]
    pieces = [(own_gate, 0, half, True, 0, 0), (own_up, 0, half, True, 0, 1)]
    for cut, ref in zip(cuts, came):
        at = 0
        for which, start, stop in cut:
            number = (stop - start) * half // 128
            pieces.append((ref, at, number, False, start * half // 128, which))
            at += number
    return pieces


def column_block(where, i, size):
    return pl.ds(pl.multiple_of((i ^ where[0]) * size, size), size)


def down_kernel(count, split, where, mine, *refs):
    blocks = refs[:count]
    own, came, rows_out, raw, held, sems = refs[count:]
    step = pl.program_id(0)
    size = blocks[0].shape[1]
    place_rows(down_pieces(own, came), held, sems, where[1], step == 0)

    @pl.when(step < split)
    def _():
        rows_out[...] = mine[...]

    @pl.when(step >= split)
    def _():
        for i, ref in enumerate(blocks):
            rows_out[:, column_block(where, i, size)] = ref[...]

    raw[...] = jnp.dot(rows_out[...], held[...], preferred_element_type=full).astype(low)


def down_pass(where, mine, blocks, own, came):
    count = len(blocks)
    size = blocks[0].shape[1]
    width, hidden = 2 * own.shape[0], own.shape[1]
    total = mine.shape[0] + blocks[0].shape[0]
    tile = 256
    split = mine.shape[0] // tile
    anywhere = pl.BlockSpec(memory_space=pl.ANY)
    spec = lambda columns: pl.BlockSpec((tile, columns), lambda i, where: (i, 0))
    late = pl.BlockSpec((tile, size), lambda i, where: (jnp.maximum(i - split, 0), 0))
    return pl.pallas_call(
        functools.partial(down_kernel, count, split),
        grid_spec=pltpu.PrefetchScalarGridSpec(
            num_scalar_prefetch=1,
            grid=(total // tile,),
            in_specs=[
                pl.BlockSpec((tile, width), lambda i, where: (jnp.minimum(i, split - 1), 0))
            ]
            + [late] * count
            + [anywhere] * 2,
            out_specs=[spec(width), spec(hidden)],
            scratch_shapes=[pltpu.VMEM((width, hidden), low), pltpu.SemaphoreType.DMA((2,))],
        ),
        out_shape=[
            jax.ShapeDtypeStruct((total, width), low),
            jax.ShapeDtypeStruct((total, hidden), low),
        ],
        compiler_params=limits(48),
        cost_estimate=cost(
            2 * total * width * hidden, (total * (2 * width + hidden) + width * hidden) * 2
        ),
        name="down",
    )(where, mine, *blocks, own, came)


def up_kernel(where, act, own, came, out, held, sems):
    place_rows(down_pieces(own, came), held, sems, where[1], pl.program_id(0) == 0)
    out[...] = dot_cols(act[...], held[...]).astype(low)


def up_pass(where, act, own, came):
    total, hidden = act.shape
    width = 2 * own.shape[0]
    tile = 256
    spec = lambda columns: pl.BlockSpec((tile, columns), lambda i, where: (i, 0))
    return pl.pallas_call(
        up_kernel,
        grid_spec=pltpu.PrefetchScalarGridSpec(
            num_scalar_prefetch=1,
            grid=(total // tile,),
            in_specs=[spec(hidden)] + [pl.BlockSpec(memory_space=pl.ANY)] * 2,
            out_specs=spec(width),
            scratch_shapes=[pltpu.VMEM((width, hidden), low), pltpu.SemaphoreType.DMA((2,))],
        ),
        out_shape=jax.ShapeDtypeStruct((total, width), low),
        compiler_params=limits(48),
        cost_estimate=cost(
            2 * total * width * hidden, (total * (width + hidden) + width * hidden) * 2
        ),
        name="up",
    )(where, act, own, came)


def expert_kernel(count, carried, where, *refs):
    blocks, refs = refs[:count], refs[count:]
    number = 2 + len(cuts)
    weights, (raw, routed, router) = refs[:number], refs[number : number + 3]
    rows_out, act_out, grad_out, even, odd, gate_grad, pair, part, sems = refs[
        number + 3 + carried :
    ]
    size = blocks[0].shape[1]
    hidden = raw.shape[1]
    place_rows(pair_pieces(*weights), pair, sems, where[1], pl.program_id(0) == 0)
    for i, ref in enumerate(blocks):
        rows_out[:, column_block(where, i, size)] = ref[...]
    both = jnp.dot(rows_out[...], pair[...], preferred_element_type=full)
    pre_gate = both[:, :hidden]
    pre_up = both[:, hidden:]
    sigma = 1.0 / (1.0 + jnp.exp(-pre_gate))
    silu = pre_gate * sigma
    act = silu * pre_up
    back = raw[...].astype(full)
    tile = back.shape[0]
    own = where[2].astype(full)
    other = jnp.broadcast_to(routed[...], (128, tile)).T - own
    logits = jnp.dot(rows_out[...], router[...], preferred_element_type=full)
    lane = lax.broadcasted_iota(jnp.int32, (tile, 128), 1).astype(full)
    ahead = jnp.where(lane == other, logits, 0.0) - jnp.where(lane == own, logits, 0.0)
    gate = 1.0 / (1.0 + jnp.exp(jnp.sum(ahead, axis=1, keepdims=True)))
    gate_sum = jnp.sum(act * back, axis=1, keepdims=True)
    gate_grad[...] = jnp.broadcast_to(gate_sum, (tile, 128)).T[:1]
    act_out[...] = (act * gate).astype(low)
    back = back * gate
    grad_out[:, :hidden] = (back * pre_up * sigma * (1.0 + pre_gate * (1.0 - sigma))).astype(low)
    grad_out[:, hidden:] = (back * silu).astype(low)
    part[...] = dot_cols(grad_out[...], pair[...]).astype(low)
    for i in range(count):
        (odd if i % 2 else even)[:, i // 2 * size : (i // 2 + 1) * size] = part[
            :, column_block(where, i, size)
        ]


def expert_pass(step, where, blocks, weights, raw, routed, router, carried):
    count = len(blocks)
    size = blocks[0].shape[1]
    width, hidden = 2 * weights[0].shape[0], weights[0].shape[1]
    both = 2 * hidden
    total = raw.shape[0]
    tile = 256
    steps = MOST // tile
    here = lambda i, where: (step * steps + i, 0)
    near = lambda i, where: (i, 0)
    near_spec = lambda columns: pl.BlockSpec((tile, columns), near)
    here_spec = lambda columns: pl.BlockSpec((tile, columns), here)
    row_spec = pl.BlockSpec((1, tile), lambda i, where: (0, i))
    anywhere = pl.BlockSpec(memory_space=pl.ANY)
    shape = lambda r, c, t=low: jax.ShapeDtypeStruct((r, c), t)
    return pl.pallas_call(
        functools.partial(expert_kernel, count, len(carried)),
        grid_spec=pltpu.PrefetchScalarGridSpec(
            num_scalar_prefetch=1,
            grid=(steps,),
            in_specs=[near_spec(size)] * count
            + [anywhere] * len(weights)
            + [
                here_spec(hidden),
                row_spec,
                pl.BlockSpec((width, 128), lambda i, where: (0, 0)),
            ]
            + [anywhere] * len(carried),
            out_specs=[
                here_spec(width),
                here_spec(hidden),
                here_spec(both),
                near_spec(width // 2),
                near_spec(width // 2),
                row_spec,
            ],
            scratch_shapes=[
                pltpu.VMEM((width, both), low),
                pltpu.VMEM((tile, width), low),
                pltpu.SemaphoreType.DMA((2 + sum(len(cut) for cut in cuts),)),
            ],
        ),
        out_shape=[
            shape(total, width),
            shape(total, hidden),
            shape(total, both),
            shape(MOST, width // 2),
            shape(MOST, width // 2),
            shape(1, MOST, full),
        ],
        input_output_aliases={
            count + len(weights) + 4 + i: i for i in range(len(carried))
        },
        compiler_params=limits(60),
        cost_estimate=cost(
            4 * MOST * width * both, width * both * 2 + MOST * (width * 8 + hidden * 8), MOST * hidden
        ),
        name="expert",
    )(where, *blocks, *weights, raw, routed, router, *carried)


def expert_grad_kernel(hidden, pieces, per, *refs):
    out = refs[-1]
    which, at = pl.program_id(0), pl.program_id(1)

    def add(ref, other):
        out[0] = (ref[...].astype(full) + other[...].astype(full))[:, :hidden]

    for k in range(pieces):

        @pl.when((which < 2) & (at // per == k))
        def _():
            add(refs[0], refs[1 + k])

    @pl.when(which == 2)
    def _():
        add(refs[1 + pieces], refs[2 + pieces])


def expert_grad_sum(pair, down, hidden):
    rows, padded = down[0].shape
    tile = min(256, rows)
    pieces = len(pair) - 1
    per = rows // tile // pieces
    last = rows // tile - 1

    def piece_spec(k):
        return pl.BlockSpec(
            (tile, padded),
            lambda w, i: (
                jnp.where(w == 2, per - 1, jnp.clip(i - k * per, 0, per - 1)),
                jnp.minimum(w, 1),
            ),
        )

    pair_spec = pl.BlockSpec(
        (tile, padded), lambda w, i: (jnp.where(w == 2, last, i), jnp.minimum(w, 1))
    )
    down_spec = pl.BlockSpec((tile, padded), lambda w, i: (jnp.where(w == 2, i, 0), 0))
    return pl.pallas_call(
        functools.partial(expert_grad_kernel, hidden, pieces, per),
        grid=(3, rows // tile),
        in_specs=[pair_spec] + [piece_spec(k) for k in range(pieces)] + [down_spec] * 2,
        out_specs=pl.BlockSpec((1, tile, hidden), lambda w, i: (w, i, 0)),
        out_shape=jax.ShapeDtypeStruct((3, rows, hidden), full),
        compiler_params=limits(40),
        cost_estimate=cost(rows * padded * 3, rows * padded * 24),
        name="expert_grad_sum",
    )(*pair, *down)


def near_blocks(own, *others):
    held = [own]
    for bit in range(levels_of(lax.axis_size("tensor")))[::-1]:
        theirs = [swap(v, "tensor", 1 << bit) for v in held]
        if bit and others:
            theirs = [after(v, *others) for v in theirs]
        held = [v for pair in zip(held, theirs) for v in pair]
    return held


def near_reduce(even, odd, meet, *others):
    count = lax.axis_size("tensor")
    number = count // 2
    size = even.shape[1] // number
    came = swap(odd, "tensor", 1)
    for bit in range(1, levels_of(count)):
        blocks = [
            even[:, i * size : (i + 1) * size].astype(full)
            + came[:, i * size : (i + 1) * size].astype(full)
            for i in range(number)
        ]
        sent = jnp.concatenate([v.astype(low) for v in blocks[1::2]], 1)
        if bit == levels_of(count) - 1:
            sent = after(sent, *others)
            meet.append(sent)
        even = jnp.concatenate(blocks[::2], 1)
        came = swap(sent, "tensor", 1 << bit)
        number //= 2
    return (even.astype(full) + came.astype(full)).astype(low)


def half_gather(local, group_count):
    held = local
    place = lax.axis_index("dp") % group_count
    for bit in range(levels_of(group_count) - 1):
        came = swap(held, "dp", 1 << bit)
        upper = side_of(place, bit)
        held = jnp.concatenate([jnp.where(upper, came, held), jnp.where(upper, held, came)], 0)
    return held


def group_finish(kept, came, position, group_count):
    if group_count > 2:
        came = jnp.concatenate(came, 0)
    for bit in range(levels_of(group_count) - 1)[::-1]:
        current = kept.astype(full) + came.astype(full)
        middle = current.shape[0] // 2
        upper = (position >> bit) & 1
        kept = lax.dynamic_slice_in_dim(current, upper * middle, middle, 0)
        given = lax.dynamic_slice_in_dim(current, (1 - upper) * middle, middle, 0)
        came = swap(given.astype(low), "dp", 1 << bit)
    return [kept, *came] if isinstance(came, list) else [kept, came]


def body(
    tokens,
    attn_gain,
    qkv_weight,
    out_weight,
    moe_gain,
    router_weight,
    expert_weight,
    routes,
    cotangent,
):
    rows = tokens.shape[0]
    width = tokens.shape[1]
    tensor_count = lax.axis_size("tensor")
    dp_count = lax.axis_size("dp")
    group_count = dp_count // EXPERTS
    size = width // tensor_count
    hidden_size = expert_weight.shape[2]
    padded = -(-hidden_size // 128) * 128
    scale = 1.0 / math.sqrt(HEAD)
    place = lax.axis_index("tensor")
    index = lax.axis_index("dp")
    expert = index // group_count
    member = index % group_count
    top_half = member >> (levels_of(group_count) - 1)
    where = jnp.stack([place, top_half, expert]).astype(jnp.int32)

    def own_columns(value):
        return lax.dynamic_slice_in_dim(value, place * size, size, 1)

    extras = jnp.concatenate([router_weight, attn_gain[:, None], moe_gain[:, None]], 1)
    extras = jnp.pad(extras, ((0, 0), (0, 128 - extras.shape[1])))
    first = lax.all_gather(
        jnp.concatenate([qkv_weight.reshape(-1, 3 * size), out_weight, extras], 1),
        "dp",
        axis=0,
        tiled=True,
    )
    qkv_flat = first[:, : 3 * size]
    out_full = first[:, 3 * size : 4 * size]
    small = first[:, 4 * size :].T
    router_full = small[:EXPERTS]
    gain_first = small[EXPERTS : EXPERTS + 1].astype(full)
    gain_second = small[EXPERTS + 1 : EXPERTS + 2].astype(full)
    gain_first_own = own_columns(gain_first)
    gain_second_own = own_columns(gain_second)
    router_own = own_columns(router_full)

    near = jnp.arange(EXPERTS, dtype=jnp.int32) ^ expert
    names = jnp.arange(EXPERTS, dtype=jnp.int32)
    hits = jnp.sum((routes.T[None] == names[:, None, None]).astype(jnp.int32), 1)
    rank = jnp.cumsum(hits, axis=1) - hits
    slot_near = jnp.take(jnp.where(hits > 0, rank, -1), near, axis=0)
    places = jnp.arange(MOST, dtype=jnp.int32)[:, None]
    chosen = [(places == slot_near[s][None, :]).astype(low) for s in range(EXPERTS)]

    def packed(own):
        return [jnp.dot(c, own, preferred_element_type=full).astype(low) for c in chosen]

    def exchange(parts):
        return [parts[0]] + [swap(parts[s], "dp", s * group_count) for s in range(1, EXPERTS)]

    def unpacked(parts):
        total = contract(chosen[0], parts[0], 0, 0)
        for c, part in zip(chosen[1:], parts[1:]):
            total = total + contract(c, part, 0, 0)
        return total

    def widened(value):
        return jnp.pad(value, ((0, 0), (0, padded - hidden_size)))

    gate_mine, up_mine, down_mine = [
        half_gather(widened(expert_weight[k]), group_count) for k in range(3)
    ]
    half = width // 2
    mine_at, given_at = top_half * half, (1 - top_half) * half
    reach = group_count // 2

    def group_send(given, *others):
        return swap(after(given, *others), "dp", reach)

    down = (down_mine, group_send(down_mine))
    crossing = []

    def cross(*others):
        pieces = [
            (gate_mine, up_mine)[which][start * half // 128 : stop * half // 128]
            for which, start, stop in cuts[len(crossing)]
        ]
        crossing.append(group_send(jnp.concatenate(pieces, 0), *crossing[-1:], *others))

    cross(down[1])
    cross(first)

    grad_own = own_columns(cotangent)
    grad_mine = jnp.dot(chosen[0], cotangent, preferred_element_type=full).astype(low)
    grad_came = exchange(packed(grad_own))[1:]
    grad_blocks = near_blocks(after(jnp.concatenate(grad_came, 0), down[1]))
    route_sums = jnp.sum(routes, axis=1)[None].astype(low)
    routed = exchange([contract(route_sums, c, 1, 1) for c in chosen])

    inputs = tokens.astype(full)
    scale_one = lax.rsqrt(jnp.mean(inputs * inputs, axis=1, keepdims=True) + epsilon)
    normed_in = (inputs * scale_one * gain_first).astype(low)
    inputs_own = own_columns(tokens).astype(full)
    normed_in = after(normed_in, crossing[0], grad_mine, *grad_blocks, *routed)
    qkv = jnp.dot(normed_in, qkv_flat, preferred_element_type=full)
    cross(qkv)
    cosine, sine = rotary_tables()
    context, query, keys, values, logs = attention(qkv, cosine, sine, scale)
    context = after(context, crossing[2])
    cross(context)
    attn_part = contract(context, out_full, 1, 1).astype(low)
    rows_raw = []

    def down_filler(sent):
        cross(sent)
        rows_raw.extend(down_pass(where, after(grad_mine, sent), grad_blocks, *down))
        return (*rows_raw, crossing[4])

    hidden = inputs_own + tensor_reduce(attn_part, down_filler, (crossing[3],))
    cross(rows_raw[1])

    scaled_hidden = (hidden * gain_second_own).astype(low)
    sums = tensor_sum(
        jnp.concatenate(
            [contract(router_own, scaled_hidden, 1, 1), jnp.sum(hidden * hidden, 1)[None]], 0
        )
    )
    scale_two_row = lax.rsqrt(sums[EXPERTS:] / width + epsilon)
    scale_two = scale_two_row.reshape(rows, 1)
    logits = sums[:EXPERTS] * scale_two_row
    normed_two = hidden * scale_two
    moe_in = (normed_two * gain_second_own).astype(low)
    named = hits > 0
    top = jnp.max(jnp.where(named, logits, masked_out), axis=0, keepdims=True)
    weight = jnp.where(named, jnp.exp(logits - top), 0.0)
    gates = weight / jnp.sum(weight, axis=0, keepdims=True)

    def three_parts(value):
        a = value.astype(low)
        b = (value - a.astype(full)).astype(low)
        return jnp.stack([a, b, (value - a.astype(full) - b.astype(full)).astype(low)])

    moe_packed = packed(moe_in)
    pair = (gate_mine, up_mine, *crossing)
    crossed = [moe_packed[0]] + [
        swap(moe_packed[s], "dp", s * group_count) for s in range(1, EXPERTS - 1)
    ]
    arrived = [near_blocks(moe_packed[0])]

    carried = ()
    sums_sent = []
    returned = []
    gate_grads = []
    router_block = first[:, 4 * size :]
    for step in range(EXPERTS):
        named_sum = routed[step]
        if step == 2:
            named_sum = after(named_sum, sums_sent[0])
        if step == 3:
            named_sum = after(named_sum, sums_sent[1], returned[0])
        moe_rows, activation, pre_grad, even, odd, gate_grad = expert_pass(
            step, where, arrived[step], pair, rows_raw[1], named_sum, router_block, carried
        )
        carried = (moe_rows, activation, pre_grad)
        if step == 0:
            arrived.append(near_blocks(crossed[1], even))
            crossed[2] = after(crossed[2], even)
            crossed.append(swap(after(moe_packed[3], crossed[2]), "dp", 3 * group_count))
        if step == 1:
            arrived.append(near_blocks(crossed[2], even))
            crossed[3] = after(crossed[3], even)
        if step == 2:
            arrived.append(near_blocks(crossed[3], even))
        returned.append(near_reduce(even, odd, sums_sent, *returned[2:]))
        gate_grads.append(gate_grad)
    own_returned = returned
    returned = exchange(returned)
    gate_grad_near = exchange([gate_grads[0]] + [after(v, even) for v in gate_grads[1:]])
    grad_rows = rows_raw[0]

    def term(left, right):
        def part(start, number):
            taken = lax.dynamic_slice_in_dim(left, start, number, 1)
            return contract(taken, right, 0, 0).astype(low)

        return part

    down_given = term(grad_rows, after(activation, sums_sent[2], own_returned[1]))(given_at, half)
    down_sum = group_send(down_given)
    expert_part = up_pass(
        where, after(activation, down_given, sums_sent[3], own_returned[2], *gate_grad_near), *down
    )
    expert_own = lax.psum_scatter(expert_part, "tensor", scatter_dimension=1, tiled=True)
    pair_term = term(moe_rows, after(pre_grad, expert_part, own_returned[3]))
    quarter = half // 2
    pair_given = [pair_term(given_at + k * quarter, quarter) for k in range(2)]
    pair_sum = [group_send(pair_given[0], down_sum)]
    pair_sum.append(group_send(pair_given[1], pair_sum[0]))
    returned = [after(v, *pair_given) for v in returned]
    returned[3] = after(returned[3], down_sum)
    back = unpacked(returned)

    gate_grad = jnp.concatenate(
        [
            jnp.sum(contract(three_parts(gate_grad_near[s][0]), chosen[s], 1, 0), 0, keepdims=True)
            for s in range(EXPERTS)
        ],
        0,
    )
    scaled_back = back * gain_second_own
    sums = tensor_sum(
        jnp.concatenate([gate_grad, jnp.sum(scaled_back * normed_two, axis=1)[None]], 0)
    )
    gate_grad = jnp.take(sums[:EXPERTS], near, axis=0)
    weighted = jnp.sum(gates * gate_grad, axis=0, keepdims=True)
    logit_grad = (gates * (gate_grad - weighted)).astype(low)
    mean_two = (
        sums[EXPERTS:] + jnp.sum(logit_grad.astype(full) * logits, axis=0, keepdims=True)
    ) / width
    moe_grad = contract(logit_grad, router_own, 0, 0) + back

    grad_out = grad_own.astype(full)
    hidden_grad = grad_out + scale_two * (
        moe_grad * gain_second_own - normed_two * mean_two.reshape(rows, 1)
    )
    router_grad = jnp.dot(logit_grad, moe_in, preferred_element_type=full)
    moe_gain_grad = jnp.sum(moe_grad * normed_two, axis=0)
    kept = {}
    outputs = {0: expert_own[:MOST]}

    def keep_pair(sent):
        kept["pair"] = term(moe_rows, after(pre_grad, sent, expert_own))(mine_at, half)
        outputs[2] = swap(expert_own[2 * MOST : 3 * MOST], "dp", 2 * group_count)
        return (kept["pair"],)

    def keep_down(sent):
        kept["down"] = term(grad_rows, after(activation, sent))(mine_at, half)
        return (kept["down"],)

    attn_grad = tensor_gather(hidden_grad.astype(low), keep_pair)
    attn_grad = after(attn_grad, outputs[2])
    for s in (3, 1):
        part = after(expert_own[s * MOST : (s + 1) * MOST], outputs[2])
        outputs[s] = swap(part, "dp", s * group_count)
    context_grad = jnp.dot(attn_grad, out_full, preferred_element_type=full).astype(low)
    out_shard = lax.psum_scatter(
        contract(after(attn_grad, context_grad), context, 0, 0).astype(low), "dp", scatter_dimension=0, tiled=True
    ).astype(full)
    qkv_grad_rows = attention_back(query, keys, values, logs, context_grad, cosine, sine, scale)
    qkv_grad = contract(normed_in, qkv_grad_rows, 0, 0).astype(low)
    qkv_shard = lax.psum_scatter(qkv_grad, "dp", scatter_dimension=0, tiled=True).astype(full)
    normed_grad = tensor_reduce(
        contract(
            after(qkv_grad_rows, qkv_grad, pair_sum[0], outputs[1], outputs[3]), qkv_flat, 1, 1
        ).astype(low),
        keep_down,
    )
    normed_one = inputs_own * scale_one
    scaled_in = normed_grad * gain_first_own
    attn_gain_grad = jnp.sum(normed_grad * normed_one, axis=0)
    mean_one = tensor_sum(jnp.sum(scaled_in * normed_one, axis=1)[None]) / width
    input_own = hidden_grad + scale_one * (scaled_in - normed_one * mean_one.reshape(rows, 1))
    input_own = after(input_own, pair_sum[1])
    input_grad = tensor_gather(input_own.astype(low)).astype(full)
    layer_own = hidden + unpacked([outputs[s] for s in range(EXPERTS)])
    layer_out = tensor_gather(layer_own.astype(low)).astype(full)
    expert_grad = expert_grad_sum(
        group_finish(kept["pair"], pair_sum, member, group_count),
        group_finish(kept["down"], [down_sum], member, group_count),
        hidden_size,
    )

    mine = jnp.concatenate([router_grad, attn_gain_grad[None], moe_gain_grad[None]], 0)
    mine = lax.dynamic_update_slice_in_dim(
        jnp.zeros((mine.shape[0], width), full), mine, place * size, 1
    )
    share = width // dp_count
    mine = lax.dynamic_slice_in_dim(all_sum(mine), index * share, share, 1)
    return (
        layer_out,
        input_grad,
        mine[EXPERTS],
        qkv_shard.reshape(share, 3, size),
        out_shard,
        mine[EXPERTS + 1],
        mine[:EXPERTS].T,
        expert_grad,
    )


def solution(mesh):
    placed = (
        P("dp", None),
        P("dp"),
        P("dp", None, "tensor"),
        P("dp", "tensor"),
        P("dp"),
        P("dp", None),
        P(None, "dp", "tensor"),
        P("dp", None),
        P("dp", None),
    )
    return jax.shard_map(
        body,
        mesh=mesh,
        in_specs=placed,
        out_specs=(
            P("dp", None),
            P("dp", None),
            P("dp"),
            P("dp", None, "tensor"),
            P("dp", "tensor"),
            P("dp"),
            P("dp", None),
            P(None, "dp", "tensor"),
        ),
        check_vma=False,
    )
```

```python
import functools
import math

import jax
import jax.numpy as jnp
from jax import lax
from jax.experimental import pallas as pl
from jax.experimental.pallas import tpu as pltpu
from jax.sharding import PartitionSpec as P

HEAD = 128
EXPERTS = 4
SEQ = 1024
BLOCK = 256
MOST = 768


epsilon = 1e-05
theta_base = 10000.0
masked_out = -1e30
low = jnp.bfloat16
full = jnp.float32


def swap(value, axis, distance):
    return lax.ppermute(value, axis, [(i, i ^ distance) for i in range(lax.axis_size(axis))])


def contract(left, right, left_dim, right_dim):
    return lax.dot_general(
        left, right, (((left_dim,), (right_dim,)), ((), ())), preferred_element_type=jnp.float32
    )


def levels_of(count):
    return count.bit_length() - 1


def side_of(index, bit):
    return (index >> bit) & 1 == 1


def tensor_sum(value):
    for bit in range(levels_of(lax.axis_size("tensor"))):
        value = value + swap(value, "tensor", 1 << bit)
    return value


def all_sum(value):
    for axis in ("tensor", "dp"):
        for bit in range(levels_of(lax.axis_size(axis))):
            value = value + swap(value, axis, 1 << bit)
    return value


def tensor_reduce(part, filler=None, others=()):
    count = lax.axis_size("tensor")
    place = lax.axis_index("tensor")
    size = part.shape[1] // count
    blocks = [part[:, i * size : (i + 1) * size] for i in range(count)]
    for bit in range(levels_of(count)):
        upper = side_of(place, bit)
        kept = [jnp.where(upper, b, a) for a, b in zip(blocks[::2], blocks[1::2])]
        given = [jnp.where(upper, a, b) for a, b in zip(blocks[::2], blocks[1::2])]
        sent = jnp.concatenate([v.astype(low) for v in given], 1)
        if others and bit == levels_of(count) - 1:
            sent = after(sent, *others)
        came = swap(sent, "tensor", 1 << bit)
        if filler is not None and bit == levels_of(count) - 1:
            came = after(came, *filler(sent))
        blocks = [
            v.astype(full) + came[:, i * size : (i + 1) * size].astype(full)
            for i, v in enumerate(kept)
        ]
    return blocks[0]


def tensor_gather(own, filler=None):
    count = lax.axis_size("tensor")
    place = lax.axis_index("tensor")
    size = own.shape[1]
    held = own
    order = list(range(levels_of(count)))[::-1]
    for bit in order:
        came = swap(held, "tensor", 1 << bit)
        if filler is not None and bit == order[0]:
            came = after(came, *filler(held))
        upper = side_of(place, bit)
        number = held.shape[1] // size
        mine = [held[:, i * size : (i + 1) * size] for i in range(number)]
        theirs = [came[:, i * size : (i + 1) * size] for i in range(number)]
        pairs = []
        for a, b in zip(mine, theirs):
            pairs.append((jnp.where(upper, b, a), jnp.where(upper, a, b)))
        held = jnp.concatenate([v for pair in pairs for v in pair], 1)
    return held


def after(value, *others):
    return lax.optimization_barrier((value, *others))[0]


def rotary_tables():
    half = HEAD // 2
    freqs = theta_base ** (-(jnp.arange(half, dtype=full) * 2.0 / HEAD))
    angles = jnp.arange(SEQ, dtype=full)[:, None] * freqs[None, :]
    cosine = jnp.cos(angles)
    sine = jnp.sin(angles)
    return (jnp.concatenate([cosine, cosine], 1), jnp.concatenate([-sine, sine], 1))


def limits(mib):
    return pltpu.CompilerParams(vmem_limit_bytes=mib << 20)


def cost(flops, moved, powers=0):
    return pl.CostEstimate(flops=int(flops), bytes_accessed=int(moved), transcendentals=int(powers))


def dot_cols(a, b):
    return lax.dot_general(a, b, (((1,), (1,)), ((), ())), preferred_element_type=full)


def dot_rows(a, b):
    return lax.dot_general(a, b, (((0,), (0,)), ((), ())), preferred_element_type=full)


def attention_kernel(scale, q_in, k_in, v_in, cos, sin, out, q_out, k_out, v_out, logs):
    def turned(ref):
        x = ref[...]
        return (x * cos[...] + pltpu.roll(x, HEAD // 2, 1) * sin[...]).astype(low)

    q_out[...] = turned(q_in)
    k_out[...] = turned(k_in)
    v_out[...] = v_in[...].astype(low)
    for block in range(SEQ // BLOCK):
        mine = pl.ds(block * BLOCK, BLOCK)
        seen = pl.ds(0, (block + 1) * BLOCK)
        scores = dot_cols(q_out[mine, :], k_out[seen, :]) * scale
        peak = jnp.max(scores, axis=1, keepdims=True)
        expo = jnp.exp(scores - peak)
        total = jnp.sum(expo, axis=1, keepdims=True)
        probs = (expo / total).astype(low)
        out[mine, :] = jnp.dot(probs, v_out[seen, :], preferred_element_type=full).astype(low)
        logs[0, mine, :] = peak + jnp.log(total)


def attention(qkv, cosine, sine, scale):
    rows = qkv.shape[0]
    size = qkv.shape[1] // 3
    heads = size // HEAD
    block = (SEQ, HEAD)
    table = pl.BlockSpec(block, lambda s, h: (0, 0))
    spec = pl.BlockSpec(block, lambda s, h: (s, h))
    shape = jax.ShapeDtypeStruct((rows, size), low)
    pairs = rows * heads * SEQ * 5 // 8
    return pl.pallas_call(
        functools.partial(attention_kernel, scale),
        grid=(rows // SEQ, heads),
        in_specs=[
            pl.BlockSpec(block, lambda s, h: (s, h)),
            pl.BlockSpec(block, lambda s, h: (s, heads + h)),
            pl.BlockSpec(block, lambda s, h: (s, 2 * heads + h)),
            table,
            table,
        ],
        out_specs=[spec] * 4 + [pl.BlockSpec((1, SEQ, 1), lambda s, h: (h, s, 0))],
        out_shape=[shape] * 4 + [jax.ShapeDtypeStruct((heads, rows, 1), full)],
        compiler_params=limits(48),
        cost_estimate=cost(4 * pairs * HEAD, rows * size * 20, pairs),
        name="attention",
    )(qkv, qkv, qkv, cosine, sine)


def attention_back_kernel(scale, heads, q_in, k_in, v_in, logs, grad, cos, sin, out, dk, dv):
    head = pl.program_id(1)
    dk[...] = jnp.zeros_like(dk)
    dv[...] = jnp.zeros_like(dv)

    def columns(which):
        return pl.ds(pl.multiple_of((which * heads + head) * HEAD, HEAD), HEAD)

    def turned(x, at):
        return (x * cos[at, :] - pltpu.roll(x, HEAD // 2, 1) * sin[at, :]).astype(low)

    for block in range(SEQ // BLOCK):
        mine = pl.ds(block * BLOCK, BLOCK)
        seen = pl.ds(0, (block + 1) * BLOCK)
        query, keys, values, given = q_in[mine, :], k_in[seen, :], v_in[seen, :], grad[mine, :]
        probs = jnp.exp(dot_cols(query, keys) * scale - logs[0, mine, :])
        prob_grad = dot_cols(given, values)
        inner = jnp.sum(probs * prob_grad, axis=1, keepdims=True)
        score_grad = (probs * (prob_grad - inner)).astype(low)
        query_grad = jnp.dot(score_grad, keys, preferred_element_type=full) * scale
        out[mine, columns(0)] = turned(query_grad, mine)
        dk[seen, :] += dot_rows(score_grad, query)
        dv[seen, :] += dot_rows(probs.astype(low), given)
    whole = pl.ds(0, SEQ)
    out[:, columns(1)] = turned(dk[...] * scale, whole)
    out[:, columns(2)] = dv[...].astype(low)


def attention_back(query, keys, values, logs, grad, cosine, sine, scale):
    rows, size = query.shape
    heads = size // HEAD
    block = (SEQ, HEAD)
    table = pl.BlockSpec(block, lambda s, h: (0, 0))
    spec = pl.BlockSpec(block, lambda s, h: (s, h))
    pairs = rows * heads * SEQ * 5 // 8
    return pl.pallas_call(
        functools.partial(attention_back_kernel, scale, heads),
        grid=(rows // SEQ, heads),
        in_specs=[spec] * 3
        + [pl.BlockSpec((1, SEQ, 1), lambda s, h: (h, s, 0)), spec, table, table],
        out_specs=pl.BlockSpec((SEQ, 3 * size), lambda s, h: (s, 0)),
        out_shape=jax.ShapeDtypeStruct((rows, 3 * size), low),
        scratch_shapes=[pltpu.VMEM(block, full)] * 2,
        compiler_params=limits(48),
        cost_estimate=cost(10 * pairs * HEAD, rows * size * 16, pairs),
        name="attention_back",
    )(query, keys, values, logs, grad, cosine, sine)


def place_rows(pieces, held, sems, upper, first):
    copies = []
    for ref, start, number, mine, there, column in pieces:
        half = held.shape[0] // 2
        columns = ref.shape[1]
        side = upper if mine else 1 - upper
        copies.append(
            pltpu.make_async_copy(
                ref.at[pl.ds(start, number), :],
                held.at[
                    pl.ds(pl.multiple_of(side * half + there, 64), number),
                    pl.ds(column * columns, columns),
                ],
                sems.at[len(copies)],
            )
        )

    @pl.when(first)
    def _():
        for copy in copies:
            copy.start()
        for copy in copies:
            copy.wait()


def down_pieces(own, came):
    half = own.shape[0]
    return [(own, 0, half, True, 0, 0), (came, 0, half, False, 0, 0)]


cuts = (
    ((0, 0, 16),),
    ((0, 16, 40),),
    ((0, 40, 56),),
    ((0, 56, 108),),
    ((0, 108, 128), (1, 0, 128)),
)


def pair_pieces(own_gate, own_up, *came):
    half = own_gate.shape[0]
    pieces = [(own_gate, 0, half, True, 0, 0), (own_up, 0, half, True, 0, 1)]
    for cut, ref in zip(cuts, came):
        at = 0
        for which, start, stop in cut:
            number = (stop - start) * half // 128
            pieces.append((ref, at, number, False, start * half // 128, which))
            at += number
    return pieces


def column_block(where, i, size):
    return pl.ds(pl.multiple_of((i ^ where[0]) * size, size), size)


def down_kernel(carried, where, rows, own, came, *refs):
    rows_out, raw, held, sems = refs[carried:]
    place_rows(down_pieces(own, came), held, sems, where[1], pl.program_id(0) == 0)
    rows_out[...] = rows[...]
    raw[...] = jnp.dot(rows[...], held[...], preferred_element_type=full).astype(low)


def down_pass(where, rows, own, came, start, total, carried):
    number, width = rows.shape
    hidden = own.shape[1]
    tile = 256
    first = start // tile
    anywhere = pl.BlockSpec(memory_space=pl.ANY)
    here = lambda columns: pl.BlockSpec((tile, columns), lambda i, where: (first + i, 0))
    return pl.pallas_call(
        functools.partial(down_kernel, len(carried)),
        grid_spec=pltpu.PrefetchScalarGridSpec(
            num_scalar_prefetch=1,
            grid=(number // tile,),
            in_specs=[pl.BlockSpec((tile, width), lambda i, where: (i, 0))]
            + [anywhere] * (2 + len(carried)),
            out_specs=[here(width), here(hidden)],
            scratch_shapes=[pltpu.VMEM((width, hidden), low), pltpu.SemaphoreType.DMA((2,))],
        ),
        out_shape=[
            jax.ShapeDtypeStruct((total, width), low),
            jax.ShapeDtypeStruct((total, hidden), low),
        ],
        input_output_aliases={4 + i: i for i in range(len(carried))},
        compiler_params=limits(48),
        cost_estimate=cost(
            2 * number * width * hidden, (number * (2 * width + hidden) + width * hidden) * 2
        ),
        name="down",
    )(where, rows, own, came, *carried)


def up_kernel(where, act, own, came, out, held, sems):
    place_rows(down_pieces(own, came), held, sems, where[1], pl.program_id(0) == 0)
    out[...] = dot_cols(act[...], held[...]).astype(low)


def up_pass(where, act, own, came):
    total, hidden = act.shape
    width = 2 * own.shape[0]
    tile = 256
    spec = lambda columns: pl.BlockSpec((tile, columns), lambda i, where: (i, 0))
    return pl.pallas_call(
        up_kernel,
        grid_spec=pltpu.PrefetchScalarGridSpec(
            num_scalar_prefetch=1,
            grid=(total // tile,),
            in_specs=[spec(hidden)] + [pl.BlockSpec(memory_space=pl.ANY)] * 2,
            out_specs=spec(width),
            scratch_shapes=[pltpu.VMEM((width, hidden), low), pltpu.SemaphoreType.DMA((2,))],
        ),
        out_shape=jax.ShapeDtypeStruct((total, width), low),
        compiler_params=limits(48),
        cost_estimate=cost(
            2 * total * width * hidden, (total * (width + hidden) + width * hidden) * 2
        ),
        name="up",
    )(where, act, own, came)


def expert_kernel(count, carried, where, *refs):
    blocks, refs = refs[:count], refs[count:]
    number = 2 + len(cuts)
    weights, (raw, routed, router) = refs[:number], refs[number : number + 3]
    rows_out, act_out, grad_out, even, odd, gate_grad, pair, part, sems = refs[
        number + 3 + carried :
    ]
    size = blocks[0].shape[1]
    hidden = raw.shape[1]
    place_rows(pair_pieces(*weights), pair, sems, where[1], pl.program_id(0) == 0)
    for i, ref in enumerate(blocks):
        rows_out[:, column_block(where, i, size)] = ref[...]
    both = jnp.dot(rows_out[...], pair[...], preferred_element_type=full)
    pre_gate = both[:, :hidden]
    pre_up = both[:, hidden:]
    sigma = 1.0 / (1.0 + jnp.exp(-pre_gate))
    silu = pre_gate * sigma
    act = silu * pre_up
    back = raw[...].astype(full)
    tile = back.shape[0]
    own = where[2].astype(full)
    other = jnp.broadcast_to(routed[...], (128, tile)).T - own
    logits = jnp.dot(rows_out[...], router[...], preferred_element_type=full)
    lane = lax.broadcasted_iota(jnp.int32, (tile, 128), 1).astype(full)
    ahead = jnp.where(lane == other, logits, 0.0) - jnp.where(lane == own, logits, 0.0)
    gate = 1.0 / (1.0 + jnp.exp(jnp.sum(ahead, axis=1, keepdims=True)))
    gate_sum = jnp.sum(act * back, axis=1, keepdims=True)
    gate_grad[...] = jnp.broadcast_to(gate_sum, (tile, 128)).T[:1]
    act_out[...] = (act * gate).astype(low)
    back = back * gate
    grad_out[:, :hidden] = (back * pre_up * sigma * (1.0 + pre_gate * (1.0 - sigma))).astype(low)
    grad_out[:, hidden:] = (back * silu).astype(low)
    part[...] = dot_cols(grad_out[...], pair[...]).astype(low)
    for i in range(count):
        (odd if i % 2 else even)[:, i // 2 * size : (i // 2 + 1) * size] = part[
            :, column_block(where, i, size)
        ]


def expert_pass(step, where, blocks, weights, raw, routed, router, carried):
    count = len(blocks)
    size = blocks[0].shape[1]
    width, hidden = 2 * weights[0].shape[0], weights[0].shape[1]
    both = 2 * hidden
    total = raw.shape[0]
    tile = 256
    steps = MOST // tile
    here = lambda i, where: (step * steps + i, 0)
    near = lambda i, where: (i, 0)
    near_spec = lambda columns: pl.BlockSpec((tile, columns), near)
    here_spec = lambda columns: pl.BlockSpec((tile, columns), here)
    row_spec = pl.BlockSpec((1, tile), lambda i, where: (0, i))
    anywhere = pl.BlockSpec(memory_space=pl.ANY)
    shape = lambda r, c, t=low: jax.ShapeDtypeStruct((r, c), t)
    return pl.pallas_call(
        functools.partial(expert_kernel, count, len(carried)),
        grid_spec=pltpu.PrefetchScalarGridSpec(
            num_scalar_prefetch=1,
            grid=(steps,),
            in_specs=[near_spec(size)] * count
            + [anywhere] * len(weights)
            + [
                here_spec(hidden),
                row_spec,
                pl.BlockSpec((width, 128), lambda i, where: (0, 0)),
            ]
            + [anywhere] * len(carried),
            out_specs=[
                here_spec(width),
                here_spec(hidden),
                here_spec(both),
                near_spec(width // 2),
                near_spec(width // 2),
                row_spec,
            ],
            scratch_shapes=[
                pltpu.VMEM((width, both), low),
                pltpu.VMEM((tile, width), low),
                pltpu.SemaphoreType.DMA((2 + sum(len(cut) for cut in cuts),)),
            ],
        ),
        out_shape=[
            shape(total, width),
            shape(total, hidden),
            shape(total, both),
            shape(MOST, width // 2),
            shape(MOST, width // 2),
            shape(1, MOST, full),
        ],
        input_output_aliases={
            count + len(weights) + 4 + i: i for i in range(len(carried))
        },
        compiler_params=limits(60),
        cost_estimate=cost(
            4 * MOST * width * both, width * both * 2 + MOST * (width * 8 + hidden * 8), MOST * hidden
        ),
        name="expert",
    )(where, *blocks, *weights, raw, routed, router, *carried)


def expert_grad_kernel(hidden, pieces, per, *refs):
    out = refs[-1]
    which, at = pl.program_id(0), pl.program_id(1)

    def add(ref, other):
        out[0] = (ref[...].astype(full) + other[...].astype(full))[:, :hidden]

    for k in range(pieces):

        @pl.when((which < 2) & (at // per == k))
        def _():
            add(refs[0], refs[1 + k])

    @pl.when(which == 2)
    def _():
        add(refs[1 + pieces], refs[2 + pieces])


def expert_grad_sum(pair, down, hidden):
    rows, padded = down[0].shape
    tile = min(256, rows)
    pieces = len(pair) - 1
    per = rows // tile // pieces
    last = rows // tile - 1

    def piece_spec(k):
        return pl.BlockSpec(
            (tile, padded),
            lambda w, i: (
                jnp.where(w == 2, per - 1, jnp.clip(i - k * per, 0, per - 1)),
                jnp.minimum(w, 1),
            ),
        )

    pair_spec = pl.BlockSpec(
        (tile, padded), lambda w, i: (jnp.where(w == 2, last, i), jnp.minimum(w, 1))
    )
    down_spec = pl.BlockSpec((tile, padded), lambda w, i: (jnp.where(w == 2, i, 0), 0))
    return pl.pallas_call(
        functools.partial(expert_grad_kernel, hidden, pieces, per),
        grid=(3, rows // tile),
        in_specs=[pair_spec] + [piece_spec(k) for k in range(pieces)] + [down_spec] * 2,
        out_specs=pl.BlockSpec((1, tile, hidden), lambda w, i: (w, i, 0)),
        out_shape=jax.ShapeDtypeStruct((3, rows, hidden), full),
        compiler_params=limits(40),
        cost_estimate=cost(rows * padded * 3, rows * padded * 24),
        name="expert_grad_sum",
    )(*pair, *down)


def near_blocks(own, *others):
    held = [own]
    for bit in range(levels_of(lax.axis_size("tensor")))[::-1]:
        theirs = [swap(v, "tensor", 1 << bit) for v in held]
        if bit and others:
            theirs = [after(v, *others) for v in theirs]
        held = [v for pair in zip(held, theirs) for v in pair]
    return held


def near_reduce(even, odd, meet, *others):
    count = lax.axis_size("tensor")
    number = count // 2
    size = even.shape[1] // number
    came = swap(odd, "tensor", 1)
    for bit in range(1, levels_of(count)):
        blocks = [
            even[:, i * size : (i + 1) * size].astype(full)
            + came[:, i * size : (i + 1) * size].astype(full)
            for i in range(number)
        ]
        sent = jnp.concatenate([v.astype(low) for v in blocks[1::2]], 1)
        if bit == levels_of(count) - 1:
            sent = after(sent, *others)
            meet.append(sent)
        even = jnp.concatenate(blocks[::2], 1)
        came = swap(sent, "tensor", 1 << bit)
        number //= 2
    return (even.astype(full) + came.astype(full)).astype(low)


def half_gather(local, group_count):
    held = local
    place = lax.axis_index("dp") % group_count
    for bit in range(levels_of(group_count) - 1):
        came = swap(held, "dp", 1 << bit)
        upper = side_of(place, bit)
        held = jnp.concatenate([jnp.where(upper, came, held), jnp.where(upper, held, came)], 0)
    return held


def group_finish(kept, came, position, group_count):
    if group_count > 2:
        came = jnp.concatenate(came, 0)
    for bit in range(levels_of(group_count) - 1)[::-1]:
        current = kept.astype(full) + came.astype(full)
        middle = current.shape[0] // 2
        upper = (position >> bit) & 1
        kept = lax.dynamic_slice_in_dim(current, upper * middle, middle, 0)
        given = lax.dynamic_slice_in_dim(current, (1 - upper) * middle, middle, 0)
        came = swap(given.astype(low), "dp", 1 << bit)
    return [kept, *came] if isinstance(came, list) else [kept, came]


def body(
    tokens,
    attn_gain,
    qkv_weight,
    out_weight,
    moe_gain,
    router_weight,
    expert_weight,
    routes,
    cotangent,
):
    rows = tokens.shape[0]
    width = tokens.shape[1]
    tensor_count = lax.axis_size("tensor")
    dp_count = lax.axis_size("dp")
    group_count = dp_count // EXPERTS
    size = width // tensor_count
    hidden_size = expert_weight.shape[2]
    padded = -(-hidden_size // 128) * 128
    scale = 1.0 / math.sqrt(HEAD)
    place = lax.axis_index("tensor")
    index = lax.axis_index("dp")
    expert = index // group_count
    member = index % group_count
    top_half = member >> (levels_of(group_count) - 1)
    where = jnp.stack([place, top_half, expert]).astype(jnp.int32)

    def own_columns(value):
        return lax.dynamic_slice_in_dim(value, place * size, size, 1)

    extras = jnp.concatenate([router_weight, attn_gain[:, None], moe_gain[:, None]], 1)
    extras = jnp.pad(extras, ((0, 0), (0, 128 - extras.shape[1])))
    first = lax.all_gather(
        jnp.concatenate([qkv_weight.reshape(-1, 3 * size), out_weight, extras], 1),
        "dp",
        axis=0,
        tiled=True,
    )
    qkv_flat = first[:, : 3 * size]
    out_full = first[:, 3 * size : 4 * size]
    small = first[:, 4 * size :].T
    router_full = small[:EXPERTS]
    gain_first = small[EXPERTS : EXPERTS + 1].astype(full)
    gain_second = small[EXPERTS + 1 : EXPERTS + 2].astype(full)
    gain_first_own = own_columns(gain_first)
    gain_second_own = own_columns(gain_second)
    router_own = own_columns(router_full)

    near = jnp.arange(EXPERTS, dtype=jnp.int32) ^ expert
    names = jnp.arange(EXPERTS, dtype=jnp.int32)
    hits = jnp.sum((routes.T[None] == names[:, None, None]).astype(jnp.int32), 1)
    rank = jnp.cumsum(hits, axis=1) - hits
    slot_near = jnp.take(jnp.where(hits > 0, rank, -1), near, axis=0)
    places = jnp.arange(MOST, dtype=jnp.int32)[:, None]
    chosen = [(places == slot_near[s][None, :]).astype(low) for s in range(EXPERTS)]

    def packed(own):
        return [jnp.dot(c, own, preferred_element_type=full).astype(low) for c in chosen]

    def exchange(parts):
        return [parts[0]] + [swap(parts[s], "dp", s * group_count) for s in range(1, EXPERTS)]

    def unpacked(parts):
        total = contract(chosen[0], parts[0], 0, 0)
        for c, part in zip(chosen[1:], parts[1:]):
            total = total + contract(c, part, 0, 0)
        return total

    def widened(value):
        return jnp.pad(value, ((0, 0), (0, padded - hidden_size)))

    gate_mine, up_mine, down_mine = [
        half_gather(widened(expert_weight[k]), group_count) for k in range(3)
    ]
    half = width // 2
    mine_at, given_at = top_half * half, (1 - top_half) * half
    reach = group_count // 2

    def group_send(given, *others):
        return swap(after(given, *others), "dp", reach)

    down = (down_mine, group_send(down_mine))
    crossing = []

    def cross(*others):
        pieces = [
            (gate_mine, up_mine)[which][start * half // 128 : stop * half // 128]
            for which, start, stop in cuts[len(crossing)]
        ]
        crossing.append(group_send(jnp.concatenate(pieces, 0), *crossing[-1:], *others))

    cross(first)

    grad_own = own_columns(cotangent)
    grad_mine = jnp.dot(chosen[0], cotangent, preferred_element_type=full).astype(low)
    planes = [
        [m + g * group_count for g in range(EXPERTS)] for m in range(group_count)
    ]
    grad_planes = lax.all_gather(
        after(grad_own, first), "dp", axis=0, tiled=True, axis_index_groups=planes
    )
    slots_came = exchange([slot_near[s][None].astype(full) for s in range(EXPERTS)])
    route_sums = jnp.sum(routes, axis=1)[None].astype(low)
    routed = exchange([contract(route_sums, c, 1, 1) for c in chosen])

    inputs = tokens.astype(full)
    scale_one = lax.rsqrt(jnp.mean(inputs * inputs, axis=1, keepdims=True) + epsilon)
    normed_in = (inputs * scale_one * gain_first).astype(low)
    inputs_own = own_columns(tokens).astype(full)
    normed_in = after(normed_in, down[1], grad_mine, *slots_came, *routed)
    qkv = jnp.dot(normed_in, qkv_flat, preferred_element_type=full)
    cross(qkv)
    cosine, sine = rotary_tables()
    context, query, keys, values, logs = attention(qkv, cosine, sine, scale)
    context = after(context, crossing[1])
    cross(context)
    attn_part = contract(context, out_full, 1, 1).astype(low)
    rows_raw = []

    total = EXPERTS * MOST

    def down_filler(sent):
        cross(sent)
        rows_raw.extend(down_pass(where, after(grad_mine, sent), *down, 0, total, ()))
        return (rows_raw[1], crossing[3])

    hidden = inputs_own + tensor_reduce(attn_part, down_filler, (crossing[2],))
    cross(rows_raw[1])
    grad_planes = after(grad_planes, hidden)
    grad_packed = []
    for s in range(1, EXPERTS):
        source = lax.dynamic_slice_in_dim(grad_planes, (expert ^ s) * rows, rows, 0)
        taken = (places.astype(full) == slots_came[s]).astype(low)
        grad_packed.append(jnp.dot(taken, source, preferred_element_type=full).astype(low))
    grad_rest = lax.all_gather(jnp.concatenate(grad_packed, 0), "tensor", axis=1, tiled=True)

    scaled_hidden = (hidden * gain_second_own).astype(low)
    sums = tensor_sum(
        jnp.concatenate(
            [contract(router_own, scaled_hidden, 1, 1), jnp.sum(hidden * hidden, 1)[None]], 0
        )
    )
    scale_two_row = lax.rsqrt(sums[EXPERTS:] / width + epsilon)
    scale_two = scale_two_row.reshape(rows, 1)
    logits = sums[:EXPERTS] * scale_two_row
    normed_two = hidden * scale_two
    moe_in = (normed_two * gain_second_own).astype(low)
    named = hits > 0
    top = jnp.max(jnp.where(named, logits, masked_out), axis=0, keepdims=True)
    weight = jnp.where(named, jnp.exp(logits - top), 0.0)
    gates = weight / jnp.sum(weight, axis=0, keepdims=True)

    def three_parts(value):
        a = value.astype(low)
        b = (value - a.astype(full)).astype(low)
        return jnp.stack([a, b, (value - a.astype(full) - b.astype(full)).astype(low)])

    moe_packed = packed(moe_in)
    pair = (gate_mine, up_mine, *crossing)
    crossed = [moe_packed[0]] + [
        swap(moe_packed[s], "dp", s * group_count) for s in range(1, EXPERTS - 1)
    ]
    arrived = [near_blocks(moe_packed[0])]

    carried = ()
    sums_sent = []
    returned = []
    gate_grads = []
    router_block = first[:, 4 * size :]
    for step in range(EXPERTS):
        named_sum = routed[step]
        if step == 1:
            rows_raw = down_pass(where, after(grad_rest, even), *down, MOST, total, rows_raw)
        if step == 2:
            named_sum = after(named_sum, sums_sent[0])
        if step == 3:
            named_sum = after(named_sum, sums_sent[1], returned[0])
        moe_rows, activation, pre_grad, even, odd, gate_grad = expert_pass(
            step, where, arrived[step], pair, rows_raw[1], named_sum, router_block, carried
        )
        carried = (moe_rows, activation, pre_grad)
        if step == 0:
            arrived.append(near_blocks(crossed[1], even))
            crossed[2] = after(crossed[2], even)
            crossed.append(swap(after(moe_packed[3], crossed[2]), "dp", 3 * group_count))
        if step == 1:
            arrived.append(near_blocks(crossed[2], even))
            crossed[3] = after(crossed[3], even)
        if step == 2:
            arrived.append(near_blocks(crossed[3], even))
        returned.append(near_reduce(even, odd, sums_sent, *returned[2:]))
        gate_grads.append(gate_grad)
    own_returned = returned
    returned = exchange(returned)
    gate_grad_near = exchange([gate_grads[0]] + [after(v, even) for v in gate_grads[1:]])
    grad_rows = rows_raw[0]

    def term(left, right):
        def part(start, number):
            taken = lax.dynamic_slice_in_dim(left, start, number, 1)
            return contract(taken, right, 0, 0).astype(low)

        return part

    unit = half // 128
    down_given = term(grad_rows, after(activation, sums_sent[2], own_returned[1]))(given_at, half)
    down_sums = [group_send(down_given[: 52 * unit])]
    expert_part = up_pass(
        where, after(activation, down_given, sums_sent[3], own_returned[2], *gate_grad_near), *down
    )
    expert_part = after(expert_part, down_sums[0])
    expert_own = lax.psum_scatter(expert_part, "tensor", scatter_dimension=1, tiled=True)
    pair_term = term(moe_rows, after(pre_grad, expert_part, own_returned[3]))
    down_sums.append(group_send(down_given[52 * unit : 108 * unit], down_sums[0], expert_part))
    quarter = half // 2
    pair_given = [pair_term(given_at + k * quarter, quarter) for k in range(2)]
    returned = [after(v, *pair_given) for v in returned]
    returned[3] = after(returned[3], down_sums[1])
    down_sums.append(group_send(down_given[108 * unit :], down_sums[1]))
    pair_sums = [group_send(pair_given[0][: 26 * unit], down_sums[1])]
    back = unpacked(returned)

    gate_grad = jnp.concatenate(
        [
            jnp.sum(contract(three_parts(gate_grad_near[s][0]), chosen[s], 1, 0), 0, keepdims=True)
            for s in range(EXPERTS)
        ],
        0,
    )
    scaled_back = back * gain_second_own
    sums = tensor_sum(
        jnp.concatenate([gate_grad, jnp.sum(scaled_back * normed_two, axis=1)[None]], 0)
    )
    gate_grad = jnp.take(sums[:EXPERTS], near, axis=0)
    weighted = jnp.sum(gates * gate_grad, axis=0, keepdims=True)
    logit_grad = (gates * (gate_grad - weighted)).astype(low)
    mean_two = (
        sums[EXPERTS:] + jnp.sum(logit_grad.astype(full) * logits, axis=0, keepdims=True)
    ) / width
    moe_grad = contract(logit_grad, router_own, 0, 0) + back

    grad_out = grad_own.astype(full)
    hidden_grad = grad_out + scale_two * (
        moe_grad * gain_second_own - normed_two * mean_two.reshape(rows, 1)
    )
    router_grad = jnp.dot(logit_grad, moe_in, preferred_element_type=full)
    moe_gain_grad = jnp.sum(moe_grad * normed_two, axis=0)
    kept = {}
    outputs = {0: expert_own[:MOST]}

    def keep_pair(sent):
        kept["pair"] = term(moe_rows, after(pre_grad, sent))(mine_at, half)
        return (kept["pair"], down_sums[2], pair_sums[0])

    def keep_down(sent):
        kept["down"] = term(grad_rows, after(activation, sent))(mine_at, half)
        return (kept["down"], outputs[1])

    attn_grad = tensor_gather(hidden_grad.astype(low), keep_pair)
    attn_grad = after(attn_grad, expert_own)
    pair_sums.append(
        group_send(pair_given[0][26 * unit : 42 * unit], pair_sums[0], down_sums[2], kept["pair"])
    )
    context_grad = jnp.dot(attn_grad, out_full, preferred_element_type=full).astype(low)
    for s in (2, 3, 1):
        part = after(expert_own[s * MOST : (s + 1) * MOST], context_grad, *list(outputs.values())[1:])
        outputs[s] = swap(part, "dp", s * group_count)
    out_shard = lax.psum_scatter(
        contract(after(attn_grad, context_grad), context, 0, 0).astype(low), "dp", scatter_dimension=0, tiled=True
    ).astype(full)
    qkv_grad_rows = attention_back(query, keys, values, logs, context_grad, cosine, sine, scale)
    qkv_grad_rows = after(qkv_grad_rows, pair_sums[1])
    qkv_grad = contract(normed_in, qkv_grad_rows, 0, 0).astype(low)
    pair_sums.append(group_send(pair_given[0][42 * unit :], pair_sums[1], qkv_grad))
    pair_last = group_send(pair_given[1], pair_sums[1], qkv_grad)
    qkv_shard = lax.psum_scatter(qkv_grad, "dp", scatter_dimension=0, tiled=True).astype(full)
    normed_grad = tensor_reduce(
        contract(
            after(qkv_grad_rows, qkv_grad, outputs[2]), qkv_flat, 1, 1
        ).astype(low),
        keep_down,
        (outputs[3],),
    )
    normed_one = inputs_own * scale_one
    scaled_in = normed_grad * gain_first_own
    attn_gain_grad = jnp.sum(normed_grad * normed_one, axis=0)
    mean_one = tensor_sum(jnp.sum(scaled_in * normed_one, axis=1)[None]) / width
    input_own = hidden_grad + scale_one * (scaled_in - normed_one * mean_one.reshape(rows, 1))
    input_own = after(input_own, pair_last, pair_sums[2])
    input_grad = tensor_gather(input_own.astype(low)).astype(full)
    layer_own = hidden + unpacked([outputs[s] for s in range(EXPERTS)])
    layer_out = tensor_gather(layer_own.astype(low)).astype(full)
    expert_grad = expert_grad_sum(
        group_finish(
            kept["pair"], [jnp.concatenate(pair_sums, 0), pair_last], member, group_count
        ),
        group_finish(kept["down"], [jnp.concatenate(down_sums, 0)], member, group_count),
        hidden_size,
    )

    mine = jnp.concatenate([router_grad, attn_gain_grad[None], moe_gain_grad[None]], 0)
    mine = lax.dynamic_update_slice_in_dim(
        jnp.zeros((mine.shape[0], width), full), mine, place * size, 1
    )
    share = width // dp_count
    mine = lax.dynamic_slice_in_dim(all_sum(mine), index * share, share, 1)
    return (
        layer_out,
        input_grad,
        mine[EXPERTS],
        qkv_shard.reshape(share, 3, size),
        out_shard,
        mine[EXPERTS + 1],
        mine[:EXPERTS].T,
        expert_grad,
    )


def solution(mesh):
    placed = (
        P("dp", None),
        P("dp"),
        P("dp", None, "tensor"),
        P("dp", "tensor"),
        P("dp"),
        P("dp", None),
        P(None, "dp", "tensor"),
        P("dp", None),
        P("dp", None),
    )
    return jax.shard_map(
        body,
        mesh=mesh,
        in_specs=placed,
        out_specs=(
            P("dp", None),
            P("dp", None),
            P("dp"),
            P("dp", None, "tensor"),
            P("dp", "tensor"),
            P("dp"),
            P("dp", None),
            P(None, "dp", "tensor"),
        ),
        check_vma=False,
    )
```

```python
import functools
import math

import jax
import jax.numpy as jnp
from jax import lax
from jax.experimental import pallas as pl
from jax.experimental.pallas import tpu as pltpu
from jax.sharding import PartitionSpec as P

HEAD = 128
EXPERTS = 4
SEQ = 1024
BLOCK = 256
MOST = 768


epsilon = 1e-05
theta_base = 10000.0
masked_out = -1e30
low = jnp.bfloat16
full = jnp.float32


def swap(value, axis, distance):
    return lax.ppermute(value, axis, [(i, i ^ distance) for i in range(lax.axis_size(axis))])


def contract(left, right, left_dim, right_dim):
    return lax.dot_general(
        left, right, (((left_dim,), (right_dim,)), ((), ())), preferred_element_type=jnp.float32
    )


def levels_of(count):
    return count.bit_length() - 1


def side_of(index, bit):
    return (index >> bit) & 1 == 1


def tensor_sum(value):
    for bit in range(levels_of(lax.axis_size("tensor"))):
        value = value + swap(value, "tensor", 1 << bit)
    return value


def all_sum(value):
    for axis in ("tensor", "dp"):
        for bit in range(levels_of(lax.axis_size(axis))):
            value = value + swap(value, axis, 1 << bit)
    return value


def tensor_gather(own, filler=None):
    count = lax.axis_size("tensor")
    place = lax.axis_index("tensor")
    size = own.shape[1]
    held = own
    order = list(range(levels_of(count)))[::-1]
    for bit in order:
        came = swap(held, "tensor", 1 << bit)
        if filler is not None and bit == order[0]:
            came = after(came, *filler(held))
        upper = side_of(place, bit)
        number = held.shape[1] // size
        mine = [held[:, i * size : (i + 1) * size] for i in range(number)]
        theirs = [came[:, i * size : (i + 1) * size] for i in range(number)]
        pairs = []
        for a, b in zip(mine, theirs):
            pairs.append((jnp.where(upper, b, a), jnp.where(upper, a, b)))
        held = jnp.concatenate([v for pair in pairs for v in pair], 1)
    return held


def after(value, *others):
    return lax.optimization_barrier((value, *others))[0]


def rotary_tables():
    half = HEAD // 2
    freqs = theta_base ** (-(jnp.arange(half, dtype=full) * 2.0 / HEAD))
    angles = jnp.arange(SEQ, dtype=full)[:, None] * freqs[None, :]
    cosine = jnp.cos(angles)
    sine = jnp.sin(angles)
    return (jnp.concatenate([cosine, cosine], 1), jnp.concatenate([-sine, sine], 1))


def limits(mib):
    return pltpu.CompilerParams(vmem_limit_bytes=mib << 20)


def cost(flops, moved, powers=0):
    return pl.CostEstimate(flops=int(flops), bytes_accessed=int(moved), transcendentals=int(powers))


def dot_cols(a, b):
    return lax.dot_general(a, b, (((1,), (1,)), ((), ())), preferred_element_type=full)


def dot_rows(a, b):
    return lax.dot_general(a, b, (((0,), (0,)), ((), ())), preferred_element_type=full)


def attention_kernel(scale, q_in, k_in, v_in, cos, sin, out, q_out, k_out, v_out, logs):
    def turned(ref):
        x = ref[...]
        return (x * cos[...] + pltpu.roll(x, HEAD // 2, 1) * sin[...]).astype(low)

    q_out[...] = turned(q_in)
    k_out[...] = turned(k_in)
    v_out[...] = v_in[...].astype(low)
    for block in range(SEQ // BLOCK):
        mine = pl.ds(block * BLOCK, BLOCK)
        seen = pl.ds(0, (block + 1) * BLOCK)
        scores = dot_cols(q_out[mine, :], k_out[seen, :]) * scale
        peak = jnp.max(scores, axis=1, keepdims=True)
        expo = jnp.exp(scores - peak)
        total = jnp.sum(expo, axis=1, keepdims=True)
        probs = (expo / total).astype(low)
        out[mine, :] = jnp.dot(probs, v_out[seen, :], preferred_element_type=full).astype(low)
        logs[0, mine, :] = peak + jnp.log(total)


def attention(qkv, cosine, sine, scale):
    rows = qkv.shape[0]
    size = qkv.shape[1] // 3
    heads = size // HEAD
    block = (SEQ, HEAD)
    table = pl.BlockSpec(block, lambda s, h: (0, 0))
    spec = pl.BlockSpec(block, lambda s, h: (s, h))
    shape = jax.ShapeDtypeStruct((rows, size), low)
    pairs = rows * heads * SEQ * 5 // 8
    return pl.pallas_call(
        functools.partial(attention_kernel, scale),
        grid=(rows // SEQ, heads),
        in_specs=[
            pl.BlockSpec(block, lambda s, h: (s, h)),
            pl.BlockSpec(block, lambda s, h: (s, heads + h)),
            pl.BlockSpec(block, lambda s, h: (s, 2 * heads + h)),
            table,
            table,
        ],
        out_specs=[spec] * 4 + [pl.BlockSpec((1, SEQ, 1), lambda s, h: (h, s, 0))],
        out_shape=[shape] * 4 + [jax.ShapeDtypeStruct((heads, rows, 1), full)],
        compiler_params=limits(48),
        cost_estimate=cost(4 * pairs * HEAD, rows * size * 20, pairs),
        name="attention",
    )(qkv, qkv, qkv, cosine, sine)


def attention_back_kernel(scale, heads, q_in, k_in, v_in, logs, grad, cos, sin, out, dk, dv):
    head = pl.program_id(1)
    dk[...] = jnp.zeros_like(dk)
    dv[...] = jnp.zeros_like(dv)

    def columns(which):
        return pl.ds(pl.multiple_of((which * heads + head) * HEAD, HEAD), HEAD)

    def turned(x, at):
        return (x * cos[at, :] - pltpu.roll(x, HEAD // 2, 1) * sin[at, :]).astype(low)

    for block in range(SEQ // BLOCK):
        mine = pl.ds(block * BLOCK, BLOCK)
        seen = pl.ds(0, (block + 1) * BLOCK)
        query, keys, values, given = q_in[mine, :], k_in[seen, :], v_in[seen, :], grad[mine, :]
        probs = jnp.exp(dot_cols(query, keys) * scale - logs[0, mine, :])
        prob_grad = dot_cols(given, values)
        inner = jnp.sum(probs * prob_grad, axis=1, keepdims=True)
        score_grad = (probs * (prob_grad - inner)).astype(low)
        query_grad = jnp.dot(score_grad, keys, preferred_element_type=full) * scale
        out[mine, columns(0)] = turned(query_grad, mine)
        dk[seen, :] += dot_rows(score_grad, query)
        dv[seen, :] += dot_rows(probs.astype(low), given)
    whole = pl.ds(0, SEQ)
    out[:, columns(1)] = turned(dk[...] * scale, whole)
    out[:, columns(2)] = dv[...].astype(low)


def attention_back(query, keys, values, logs, grad, cosine, sine, scale):
    rows, size = query.shape
    heads = size // HEAD
    block = (SEQ, HEAD)
    table = pl.BlockSpec(block, lambda s, h: (0, 0))
    spec = pl.BlockSpec(block, lambda s, h: (s, h))
    pairs = rows * heads * SEQ * 5 // 8
    return pl.pallas_call(
        functools.partial(attention_back_kernel, scale, heads),
        grid=(rows // SEQ, heads),
        in_specs=[spec] * 3
        + [pl.BlockSpec((1, SEQ, 1), lambda s, h: (h, s, 0)), spec, table, table],
        out_specs=pl.BlockSpec((SEQ, 3 * size), lambda s, h: (s, 0)),
        out_shape=jax.ShapeDtypeStruct((rows, 3 * size), low),
        scratch_shapes=[pltpu.VMEM(block, full)] * 2,
        compiler_params=limits(48),
        cost_estimate=cost(10 * pairs * HEAD, rows * size * 16, pairs),
        name="attention_back",
    )(query, keys, values, logs, grad, cosine, sine)


def place_rows(pieces, held, sems, upper, first):
    copies = []
    for ref, start, number, mine, there, column in pieces:
        half = held.shape[0] // 2
        columns = ref.shape[1]
        side = upper if mine else 1 - upper
        copies.append(
            pltpu.make_async_copy(
                ref.at[pl.ds(start, number), :],
                held.at[
                    pl.ds(pl.multiple_of(side * half + there, 64), number),
                    pl.ds(column * columns, columns),
                ],
                sems.at[len(copies)],
            )
        )

    @pl.when(first)
    def _():
        for copy in copies:
            copy.start()
        for copy in copies:
            copy.wait()


def down_pieces(own, came):
    half = own.shape[0]
    return [(own, 0, half, True, 0, 0), (came, 0, half, False, 0, 0)]


cuts = (
    ((0, 0, 40),),
    ((0, 40, 56),),
    ((0, 56, 80),),
    ((0, 80, 96),),
    ((0, 96, 128), (1, 0, 20)),
    ((1, 20, 46),),
    ((1, 46, 128),),
)


def pair_pieces(own_gate, own_up, *came):
    half = own_gate.shape[0]
    pieces = [(own_gate, 0, half, True, 0, 0), (own_up, 0, half, True, 0, 1)]
    for cut, ref in zip(cuts, came):
        at = 0
        for which, start, stop in cut:
            number = (stop - start) * half // 128
            pieces.append((ref, at, number, False, start * half // 128, which))
            at += number
    return pieces


def column_block(where, i, size):
    return pl.ds(pl.multiple_of((i ^ where[0]) * size, size), size)


def down_kernel(carried, where, rows, own, came, *refs):
    rows_out, raw, held, sems = refs[carried:]
    place_rows(down_pieces(own, came), held, sems, where[1], pl.program_id(0) == 0)
    rows_out[...] = rows[...]
    raw[...] = jnp.dot(rows[...], held[...], preferred_element_type=full).astype(low)


def down_pass(where, rows, own, came, start, total, carried):
    number, width = rows.shape
    hidden = own.shape[1]
    tile = 256
    first = start // tile
    anywhere = pl.BlockSpec(memory_space=pl.ANY)
    here = lambda columns: pl.BlockSpec((tile, columns), lambda i, where: (first + i, 0))
    return pl.pallas_call(
        functools.partial(down_kernel, len(carried)),
        grid_spec=pltpu.PrefetchScalarGridSpec(
            num_scalar_prefetch=1,
            grid=(number // tile,),
            in_specs=[pl.BlockSpec((tile, width), lambda i, where: (i, 0))]
            + [anywhere] * (2 + len(carried)),
            out_specs=[here(width), here(hidden)],
            scratch_shapes=[pltpu.VMEM((width, hidden), low), pltpu.SemaphoreType.DMA((2,))],
        ),
        out_shape=[
            jax.ShapeDtypeStruct((total, width), low),
            jax.ShapeDtypeStruct((total, hidden), low),
        ],
        input_output_aliases={4 + i: i for i in range(len(carried))},
        compiler_params=limits(48),
        cost_estimate=cost(
            2 * number * width * hidden, (number * (2 * width + hidden) + width * hidden) * 2
        ),
        name="down",
    )(where, rows, own, came, *carried)


def spread_kernel(count, where, left, right, even, odd, part):
    size = part.shape[1] // count
    part[...] = dot_cols(left[...], right[...]).astype(low)
    for i in range(count):
        (odd if i % 2 else even)[:, i // 2 * size : (i // 2 + 1) * size] = part[
            :, column_block(where, i, size)
        ]


def spread_dot(where, left, right, column, count):
    rows, depth = left.shape
    width = right.shape[0]
    tile = 256
    spec = lambda columns: pl.BlockSpec((tile, columns), lambda i, where: (i, 0))
    half = jax.ShapeDtypeStruct((rows, width // 2), low)
    return pl.pallas_call(
        functools.partial(spread_kernel, count),
        grid_spec=pltpu.PrefetchScalarGridSpec(
            num_scalar_prefetch=1,
            grid=(rows // tile,),
            in_specs=[
                spec(depth),
                pl.BlockSpec((width, depth), lambda i, where: (0, column)),
            ],
            out_specs=[spec(width // 2)] * 2,
            scratch_shapes=[pltpu.VMEM((tile, width), low)],
        ),
        out_shape=[half, half],
        compiler_params=limits(48),
        cost_estimate=cost(2 * rows * width * depth, (rows * (width + depth) + width * depth) * 2),
        name="spread",
    )(where, left, right)


def up_kernel(where, act, own, came, out, held, sems):
    place_rows(down_pieces(own, came), held, sems, where[1], pl.program_id(0) == 0)
    out[...] = dot_cols(act[...], held[...]).astype(low)


def up_pass(where, act, own, came):
    total, hidden = act.shape
    width = 2 * own.shape[0]
    tile = 256
    spec = lambda columns: pl.BlockSpec((tile, columns), lambda i, where: (i, 0))
    return pl.pallas_call(
        up_kernel,
        grid_spec=pltpu.PrefetchScalarGridSpec(
            num_scalar_prefetch=1,
            grid=(total // tile,),
            in_specs=[spec(hidden)] + [pl.BlockSpec(memory_space=pl.ANY)] * 2,
            out_specs=spec(width),
            scratch_shapes=[pltpu.VMEM((width, hidden), low), pltpu.SemaphoreType.DMA((2,))],
        ),
        out_shape=jax.ShapeDtypeStruct((total, width), low),
        compiler_params=limits(48),
        cost_estimate=cost(
            2 * total * width * hidden, (total * (width + hidden) + width * hidden) * 2
        ),
        name="up",
    )(where, act, own, came)


def expert_kernel(count, carried, where, *refs):
    blocks, refs = refs[:count], refs[count:]
    number = 2 + len(cuts)
    weights, (raw, routed, router) = refs[:number], refs[number : number + 3]
    rows_out, act_out, grad_out, even, odd, gate_grad, pair, part, sems = refs[
        number + 3 + carried :
    ]
    size = blocks[0].shape[1]
    hidden = raw.shape[1]
    place_rows(pair_pieces(*weights), pair, sems, where[1], pl.program_id(0) == 0)
    for i, ref in enumerate(blocks):
        rows_out[:, column_block(where, i, size)] = ref[...]
    both = jnp.dot(rows_out[...], pair[...], preferred_element_type=full)
    pre_gate = both[:, :hidden]
    pre_up = both[:, hidden:]
    sigma = 1.0 / (1.0 + jnp.exp(-pre_gate))
    silu = pre_gate * sigma
    act = silu * pre_up
    back = raw[...].astype(full)
    tile = back.shape[0]
    own = where[2].astype(full)
    other = jnp.broadcast_to(routed[...], (128, tile)).T - own
    logits = jnp.dot(rows_out[...], router[...], preferred_element_type=full)
    lane = lax.broadcasted_iota(jnp.int32, (tile, 128), 1).astype(full)
    ahead = jnp.where(lane == other, logits, 0.0) - jnp.where(lane == own, logits, 0.0)
    gate = 1.0 / (1.0 + jnp.exp(jnp.sum(ahead, axis=1, keepdims=True)))
    gate_sum = jnp.sum(act * back, axis=1, keepdims=True)
    gate_grad[...] = jnp.broadcast_to(gate_sum, (tile, 128)).T[:1]
    act_out[...] = (act * gate).astype(low)
    back = back * gate
    grad_out[:, :hidden] = (back * pre_up * sigma * (1.0 + pre_gate * (1.0 - sigma))).astype(low)
    grad_out[:, hidden:] = (back * silu).astype(low)
    part[...] = dot_cols(grad_out[...], pair[...]).astype(low)
    for i in range(count):
        (odd if i % 2 else even)[:, i // 2 * size : (i // 2 + 1) * size] = part[
            :, column_block(where, i, size)
        ]


def expert_pass(step, where, blocks, weights, raw, routed, router, carried):
    count = len(blocks)
    size = blocks[0].shape[1]
    width, hidden = 2 * weights[0].shape[0], weights[0].shape[1]
    both = 2 * hidden
    total = raw.shape[0]
    tile = 256
    steps = MOST // tile
    here = lambda i, where: (step * steps + i, 0)
    near = lambda i, where: (i, 0)
    near_spec = lambda columns: pl.BlockSpec((tile, columns), near)
    here_spec = lambda columns: pl.BlockSpec((tile, columns), here)
    row_spec = pl.BlockSpec((1, tile), lambda i, where: (0, i))
    anywhere = pl.BlockSpec(memory_space=pl.ANY)
    shape = lambda r, c, t=low: jax.ShapeDtypeStruct((r, c), t)
    return pl.pallas_call(
        functools.partial(expert_kernel, count, len(carried)),
        grid_spec=pltpu.PrefetchScalarGridSpec(
            num_scalar_prefetch=1,
            grid=(steps,),
            in_specs=[near_spec(size)] * count
            + [anywhere] * len(weights)
            + [
                here_spec(hidden),
                row_spec,
                pl.BlockSpec((width, 128), lambda i, where: (0, 0)),
            ]
            + [anywhere] * len(carried),
            out_specs=[
                here_spec(width),
                here_spec(hidden),
                here_spec(both),
                near_spec(width // 2),
                near_spec(width // 2),
                row_spec,
            ],
            scratch_shapes=[
                pltpu.VMEM((width, both), low),
                pltpu.VMEM((tile, width), low),
                pltpu.SemaphoreType.DMA((2 + sum(len(cut) for cut in cuts),)),
            ],
        ),
        out_shape=[
            shape(total, width),
            shape(total, hidden),
            shape(total, both),
            shape(MOST, width // 2),
            shape(MOST, width // 2),
            shape(1, MOST, full),
        ],
        input_output_aliases={
            count + len(weights) + 4 + i: i for i in range(len(carried))
        },
        compiler_params=limits(60),
        cost_estimate=cost(
            4 * MOST * width * both, width * both * 2 + MOST * (width * 8 + hidden * 8), MOST * hidden
        ),
        name="expert",
    )(where, *blocks, *weights, raw, routed, router, *carried)


def expert_grad_kernel(hidden, pieces, per, *refs):
    out = refs[-1]
    which, at = pl.program_id(0), pl.program_id(1)

    def add(ref, other):
        out[0] = (ref[...].astype(full) + other[...].astype(full))[:, :hidden]

    for k in range(pieces):

        @pl.when((which < 2) & (at // per == k))
        def _():
            add(refs[0], refs[1 + k])

    @pl.when(which == 2)
    def _():
        add(refs[1 + pieces], refs[2 + pieces])


def expert_grad_sum(pair, down, hidden):
    rows, padded = down[0].shape
    tile = min(256, rows)
    pieces = len(pair) - 1
    per = rows // tile // pieces
    last = rows // tile - 1

    def piece_spec(k):
        return pl.BlockSpec(
            (tile, padded),
            lambda w, i: (
                jnp.where(w == 2, per - 1, jnp.clip(i - k * per, 0, per - 1)),
                jnp.minimum(w, 1),
            ),
        )

    pair_spec = pl.BlockSpec(
        (tile, padded), lambda w, i: (jnp.where(w == 2, last, i), jnp.minimum(w, 1))
    )
    down_spec = pl.BlockSpec((tile, padded), lambda w, i: (jnp.where(w == 2, i, 0), 0))
    return pl.pallas_call(
        functools.partial(expert_grad_kernel, hidden, pieces, per),
        grid=(3, rows // tile),
        in_specs=[pair_spec] + [piece_spec(k) for k in range(pieces)] + [down_spec] * 2,
        out_specs=pl.BlockSpec((1, tile, hidden), lambda w, i: (w, i, 0)),
        out_shape=jax.ShapeDtypeStruct((3, rows, hidden), full),
        compiler_params=limits(40),
        cost_estimate=cost(rows * padded * 3, rows * padded * 24),
        name="expert_grad_sum",
    )(*pair, *down)


def near_blocks(own, *others):
    held = [own]
    for bit in range(levels_of(lax.axis_size("tensor")))[::-1]:
        theirs = [swap(v, "tensor", 1 << bit) for v in held]
        if bit and others:
            theirs = [after(v, *others) for v in theirs]
        held = [v for pair in zip(held, theirs) for v in pair]
    return held


def near_reduce(even, odd, meet, *others, filler=None):
    count = lax.axis_size("tensor")
    number = count // 2
    size = even.shape[1] // number
    came = swap(odd, "tensor", 1)
    for bit in range(1, levels_of(count)):
        blocks = [
            even[:, i * size : (i + 1) * size].astype(full)
            + came[:, i * size : (i + 1) * size].astype(full)
            for i in range(number)
        ]
        sent = jnp.concatenate([v.astype(low) for v in blocks[1::2]], 1)
        if bit == levels_of(count) - 1:
            sent = after(sent, *others)
            meet.append(sent)
        even = jnp.concatenate(blocks[::2], 1)
        came = swap(sent, "tensor", 1 << bit)
        if filler is not None and bit == levels_of(count) - 1:
            came = after(came, *filler(sent))
        number //= 2
    return even.astype(full) + came.astype(full)


def half_gather(local, group_count):
    held = local
    place = lax.axis_index("dp") % group_count
    for bit in range(levels_of(group_count) - 1):
        came = swap(held, "dp", 1 << bit)
        upper = side_of(place, bit)
        held = jnp.concatenate([jnp.where(upper, came, held), jnp.where(upper, held, came)], 0)
    return held


def group_finish(kept, came, position, group_count):
    if group_count > 2:
        came = jnp.concatenate(came, 0)
    for bit in range(levels_of(group_count) - 1)[::-1]:
        current = kept.astype(full) + came.astype(full)
        middle = current.shape[0] // 2
        upper = (position >> bit) & 1
        kept = lax.dynamic_slice_in_dim(current, upper * middle, middle, 0)
        given = lax.dynamic_slice_in_dim(current, (1 - upper) * middle, middle, 0)
        came = swap(given.astype(low), "dp", 1 << bit)
    return [kept, *came] if isinstance(came, list) else [kept, came]


def body(
    tokens,
    attn_gain,
    qkv_weight,
    out_weight,
    moe_gain,
    router_weight,
    expert_weight,
    routes,
    cotangent,
):
    rows = tokens.shape[0]
    width = tokens.shape[1]
    tensor_count = lax.axis_size("tensor")
    dp_count = lax.axis_size("dp")
    group_count = dp_count // EXPERTS
    size = width // tensor_count
    hidden_size = expert_weight.shape[2]
    padded = -(-hidden_size // 128) * 128
    scale = 1.0 / math.sqrt(HEAD)
    place = lax.axis_index("tensor")
    index = lax.axis_index("dp")
    expert = index // group_count
    member = index % group_count
    top_half = member >> (levels_of(group_count) - 1)
    where = jnp.stack([place, top_half, expert]).astype(jnp.int32)

    def own_columns(value):
        return lax.dynamic_slice_in_dim(value, place * size, size, 1)

    extras = jnp.concatenate([router_weight, attn_gain[:, None], moe_gain[:, None]], 1)
    extras = jnp.pad(extras, ((0, 0), (0, 128 - extras.shape[1])))
    first = lax.all_gather(
        jnp.concatenate([qkv_weight.reshape(-1, 3 * size), out_weight, extras], 1),
        "dp",
        axis=0,
        tiled=True,
    )
    qkv_flat = first[:, : 3 * size]
    out_full = first[:, 3 * size : 4 * size]
    small = first[:, 4 * size :].T
    router_full = small[:EXPERTS]
    gain_first = small[EXPERTS : EXPERTS + 1].astype(full)
    gain_second = small[EXPERTS + 1 : EXPERTS + 2].astype(full)
    gain_first_own = own_columns(gain_first)
    gain_second_own = own_columns(gain_second)
    router_own = own_columns(router_full)

    near = jnp.arange(EXPERTS, dtype=jnp.int32) ^ expert
    names = jnp.arange(EXPERTS, dtype=jnp.int32)
    hits = jnp.sum((routes.T[None] == names[:, None, None]).astype(jnp.int32), 1)
    rank = jnp.cumsum(hits, axis=1) - hits
    slot_near = jnp.take(jnp.where(hits > 0, rank, -1), near, axis=0)
    places = jnp.arange(MOST, dtype=jnp.int32)[:, None]
    chosen = [(places == slot_near[s][None, :]).astype(low) for s in range(EXPERTS)]

    def packed(own):
        return [jnp.dot(c, own, preferred_element_type=full).astype(low) for c in chosen]

    def exchange(parts):
        return [parts[0]] + [swap(parts[s], "dp", s * group_count) for s in range(1, EXPERTS)]

    def unpacked(parts):
        total = contract(chosen[0], parts[0], 0, 0)
        for c, part in zip(chosen[1:], parts[1:]):
            total = total + contract(c, part, 0, 0)
        return total

    def widened(value):
        return jnp.pad(value, ((0, 0), (0, padded - hidden_size)))

    gate_mine, up_mine, down_mine = [
        half_gather(widened(expert_weight[k]), group_count) for k in range(3)
    ]
    half = width // 2
    mine_at, given_at = top_half * half, (1 - top_half) * half
    reach = group_count // 2

    def group_send(given, *others):
        return swap(after(given, *others), "dp", reach)

    down = (down_mine, group_send(down_mine))
    crossing = []

    def cross(*others):
        pieces = [
            (gate_mine, up_mine)[which][start * half // 128 : stop * half // 128]
            for which, start, stop in cuts[len(crossing)]
        ]
        crossing.append(group_send(jnp.concatenate(pieces, 0), *crossing[-1:], *others))

    cross(down[1])
    cross(first)

    grad_own = own_columns(cotangent)
    grad_mine = jnp.dot(chosen[0], cotangent, preferred_element_type=full).astype(low)
    planes = [
        [m + g * group_count for g in range(EXPERTS)] for m in range(group_count)
    ]
    grad_planes = lax.all_gather(
        after(grad_own, first), "dp", axis=0, tiled=True, axis_index_groups=planes
    )
    slots_came = exchange([slot_near[s][None].astype(full) for s in range(EXPERTS)])
    route_sums = jnp.sum(routes, axis=1)[None].astype(low)
    routed = exchange([contract(route_sums, c, 1, 1) for c in chosen])

    inputs = tokens.astype(full)
    scale_one = lax.rsqrt(jnp.mean(inputs * inputs, axis=1, keepdims=True) + epsilon)
    normed_in = (inputs * scale_one * gain_first).astype(low)
    inputs_own = own_columns(tokens).astype(full)
    normed_in = after(normed_in, crossing[0], grad_mine, *slots_came, *routed)
    qkv = jnp.dot(normed_in, qkv_flat, preferred_element_type=full)
    cross(qkv)
    cosine, sine = rotary_tables()
    context, query, keys, values, logs = attention(qkv, cosine, sine, scale)
    context = after(context, crossing[2])
    cross(context)
    attn_parts = spread_dot(where, context, first, 3, tensor_count)
    rows_raw = []

    total = EXPERTS * MOST

    def down_filler(sent):
        cross(sent)
        rows_raw.extend(down_pass(where, after(grad_mine, sent), *down, 0, total, ()))
        return (rows_raw[1], crossing[4])

    hidden = inputs_own + near_reduce(*attn_parts, [], crossing[3], filler=down_filler)
    cross(rows_raw[1])
    grad_planes = after(grad_planes, hidden)
    grad_packed = []
    for s in range(1, EXPERTS):
        source = lax.dynamic_slice_in_dim(grad_planes, (expert ^ s) * rows, rows, 0)
        taken = (places.astype(full) == slots_came[s]).astype(low)
        grad_packed.append(jnp.dot(taken, source, preferred_element_type=full).astype(low))
    grad_rest = lax.all_gather(jnp.concatenate(grad_packed, 0), "tensor", axis=1, tiled=True)

    scaled_hidden = (hidden * gain_second_own).astype(low)
    sums = tensor_sum(
        jnp.concatenate(
            [contract(router_own, scaled_hidden, 1, 1), jnp.sum(hidden * hidden, 1)[None]], 0
        )
    )
    scale_two_row = lax.rsqrt(sums[EXPERTS:] / width + epsilon)
    scale_two = scale_two_row.reshape(rows, 1)
    logits = sums[:EXPERTS] * scale_two_row
    normed_two = hidden * scale_two
    moe_in = (normed_two * gain_second_own).astype(low)
    named = hits > 0
    top = jnp.max(jnp.where(named, logits, masked_out), axis=0, keepdims=True)
    weight = jnp.where(named, jnp.exp(logits - top), 0.0)
    gates = weight / jnp.sum(weight, axis=0, keepdims=True)

    def three_parts(value):
        a = value.astype(low)
        b = (value - a.astype(full)).astype(low)
        return jnp.stack([a, b, (value - a.astype(full) - b.astype(full)).astype(low)])

    moe_packed = packed(after(moe_in, crossing[5]))
    cross(moe_packed[0])
    pair = (gate_mine, up_mine, *crossing)
    crossed = [moe_packed[0]] + [
        swap(moe_packed[s], "dp", s * group_count) for s in range(1, EXPERTS - 1)
    ]
    arrived = [near_blocks(moe_packed[0])]

    carried = ()
    sums_sent = []
    returned = []
    gate_grads = []
    router_block = first[:, 4 * size :]
    for step in range(EXPERTS):
        named_sum = routed[step]
        if step == 1:
            rows_raw = down_pass(where, after(grad_rest, even), *down, MOST, total, rows_raw)
        if step == 2:
            named_sum = after(named_sum, sums_sent[0])
        if step == 3:
            named_sum = after(named_sum, sums_sent[1], returned[0])
        moe_rows, activation, pre_grad, even, odd, gate_grad = expert_pass(
            step, where, arrived[step], pair, rows_raw[1], named_sum, router_block, carried
        )
        carried = (moe_rows, activation, pre_grad)
        if step == 0:
            arrived.append(near_blocks(crossed[1], even))
            crossed[2] = after(crossed[2], even)
            crossed.append(swap(after(moe_packed[3], crossed[2]), "dp", 3 * group_count))
        if step == 1:
            arrived.append(near_blocks(crossed[2], even))
            crossed[3] = after(crossed[3], even)
        if step == 2:
            arrived.append(near_blocks(crossed[3], even))
        returned.append(near_reduce(even, odd, sums_sent, *returned[2:]).astype(low))
        gate_grads.append(gate_grad)
    own_returned = returned
    returned = exchange(returned)
    gate_grad_near = exchange([gate_grads[0]] + [after(v, even) for v in gate_grads[1:]])
    grad_rows = rows_raw[0]

    def term(left, right):
        def part(start, number):
            taken = lax.dynamic_slice_in_dim(left, start, number, 1)
            return contract(taken, right, 0, 0).astype(low)

        return part

    unit = half // 128
    expert_part = up_pass(where, after(activation, sums_sent[2], own_returned[1]), *down)
    expert_part = after(expert_part, sums_sent[3], own_returned[2])
    expert_own = lax.psum_scatter(expert_part, "tensor", scatter_dimension=1, tiled=True)
    act_late = after(activation, expert_part)
    down_given = term(grad_rows, act_late)(given_at, half)
    down_sums = [group_send(down_given[: 40 * unit])]
    pair_term = term(
        moe_rows, after(pre_grad, down_given, own_returned[3], returned[1], *gate_grad_near)
    )
    quarter = half // 2
    pair_given = [pair_term(given_at, quarter)]
    down_sums.append(group_send(down_given[40 * unit : 80 * unit], down_sums[0], pair_given[0]))
    pair_term = term(moe_rows, after(pre_grad, pair_given[0], down_sums[0], returned[2]))
    pair_given.append(pair_term(given_at + quarter, quarter))
    returned = [after(v, *pair_given) for v in returned]
    returned[3] = after(returned[3], down_sums[1])
    down_sums.append(group_send(down_given[80 * unit :], down_sums[1]))
    pair_sums = [group_send(pair_given[0][: 16 * unit], down_sums[1])]
    back = unpacked(returned)

    gate_grad = jnp.concatenate(
        [
            jnp.sum(contract(three_parts(gate_grad_near[s][0]), chosen[s], 1, 0), 0, keepdims=True)
            for s in range(EXPERTS)
        ],
        0,
    )
    scaled_back = back * gain_second_own
    sums = tensor_sum(
        jnp.concatenate([gate_grad, jnp.sum(scaled_back * normed_two, axis=1)[None]], 0)
    )
    gate_grad = jnp.take(sums[:EXPERTS], near, axis=0)
    weighted = jnp.sum(gates * gate_grad, axis=0, keepdims=True)
    logit_grad = (gates * (gate_grad - weighted)).astype(low)
    mean_two = (
        sums[EXPERTS:] + jnp.sum(logit_grad.astype(full) * logits, axis=0, keepdims=True)
    ) / width
    moe_grad = contract(logit_grad, router_own, 0, 0) + back

    grad_out = grad_own.astype(full)
    hidden_grad = grad_out + scale_two * (
        moe_grad * gain_second_own - normed_two * mean_two.reshape(rows, 1)
    )
    router_grad = jnp.dot(logit_grad, moe_in, preferred_element_type=full)
    moe_gain_grad = jnp.sum(moe_grad * normed_two, axis=0)
    kept = {}
    outputs = {0: expert_own[:MOST]}

    def keep_pair(sent):
        kept["pair"] = term(moe_rows, after(pre_grad, sent, expert_own))(mine_at, half)
        outputs[2] = swap(expert_own[2 * MOST : 3 * MOST], "dp", 2 * group_count)
        return (kept["pair"], down_sums[2], pair_sums[0], outputs[2])

    def keep_down(sent):
        kept["down"] = term(grad_rows, after(activation, sent))(mine_at, half)
        return (kept["down"], outputs[1])

    attn_grad = tensor_gather(hidden_grad.astype(low), keep_pair)
    pair_sums.append(
        group_send(pair_given[0][16 * unit : 34 * unit], pair_sums[0], down_sums[2], kept["pair"])
    )
    context_grad = jnp.dot(attn_grad, out_full, preferred_element_type=full).astype(low)
    for s in (3, 1):
        part = after(expert_own[s * MOST : (s + 1) * MOST], context_grad, *list(outputs.values())[1:])
        outputs[s] = swap(part, "dp", s * group_count)
    out_shard = lax.psum_scatter(
        contract(after(attn_grad, context_grad), context, 0, 0).astype(low), "dp", scatter_dimension=0, tiled=True
    ).astype(full)
    qkv_grad_rows = attention_back(query, keys, values, logs, context_grad, cosine, sine, scale)
    qkv_grad_rows = after(qkv_grad_rows, pair_sums[1])
    qkv_grad = contract(normed_in, qkv_grad_rows, 0, 0).astype(low)
    pair_sums.append(group_send(pair_given[0][34 * unit :], pair_sums[1], qkv_grad))
    pair_last = group_send(pair_given[1], pair_sums[1], qkv_grad)
    qkv_shard = lax.psum_scatter(qkv_grad, "dp", scatter_dimension=0, tiled=True).astype(full)
    parts = spread_dot(where, after(qkv_grad_rows, qkv_grad, outputs[3]), first, 0, tensor_count)
    normed_grad = near_reduce(*parts, [], filler=keep_down)
    normed_one = inputs_own * scale_one
    scaled_in = normed_grad * gain_first_own
    attn_gain_grad = jnp.sum(normed_grad * normed_one, axis=0)
    mean_one = tensor_sum(jnp.sum(scaled_in * normed_one, axis=1)[None]) / width
    input_own = hidden_grad + scale_one * (scaled_in - normed_one * mean_one.reshape(rows, 1))
    mine = jnp.concatenate([router_grad, attn_gain_grad[None], moe_gain_grad[None]], 0)
    mine = lax.dynamic_update_slice_in_dim(
        jnp.zeros((mine.shape[0], width), full), mine, place * size, 1
    )
    mine = all_sum(mine)
    input_own = after(input_own, pair_last, pair_sums[2])
    expert_grad = expert_grad_sum(
        group_finish(
            kept["pair"], [jnp.concatenate(pair_sums, 0), pair_last], member, group_count
        ),
        group_finish(kept["down"], [jnp.concatenate(down_sums, 0)], member, group_count),
        hidden_size,
    )
    input_grad = tensor_gather(input_own.astype(low), lambda sent: (expert_grad, mine))
    input_grad = input_grad.astype(full)
    layer_own = hidden + unpacked([outputs[s] for s in range(EXPERTS)])
    layer_out = tensor_gather(layer_own.astype(low)).astype(full)
    share = width // dp_count
    mine = lax.dynamic_slice_in_dim(mine, index * share, share, 1)
    return (
        layer_out,
        input_grad,
        mine[EXPERTS],
        qkv_shard.reshape(share, 3, size),
        out_shard,
        mine[EXPERTS + 1],
        mine[:EXPERTS].T,
        expert_grad,
    )


def solution(mesh):
    placed = (
        P("dp", None),
        P("dp"),
        P("dp", None, "tensor"),
        P("dp", "tensor"),
        P("dp"),
        P("dp", None),
        P(None, "dp", "tensor"),
        P("dp", None),
        P("dp", None),
    )
    return jax.shard_map(
        body,
        mesh=mesh,
        in_specs=placed,
        out_specs=(
            P("dp", None),
            P("dp", None),
            P("dp"),
            P("dp", None, "tensor"),
            P("dp", "tensor"),
            P("dp"),
            P("dp", None),
            P(None, "dp", "tensor"),
        ),
        check_vma=False,
    )
```

```python
import functools
import math

import jax
import jax.numpy as jnp
from jax import lax
from jax.experimental import pallas as pl
from jax.experimental.pallas import tpu as pltpu
from jax.sharding import PartitionSpec as P

HEAD = 128
EXPERTS = 4
SEQ = 1024
BLOCK = 256
MOST = 768


epsilon = 1e-05
theta_base = 10000.0
masked_out = -1e30
low = jnp.bfloat16
full = jnp.float32


def swap(value, axis, distance):
    return lax.ppermute(value, axis, [(i, i ^ distance) for i in range(lax.axis_size(axis))])


def contract(left, right, left_dim, right_dim):
    return lax.dot_general(
        left, right, (((left_dim,), (right_dim,)), ((), ())), preferred_element_type=jnp.float32
    )


def levels_of(count):
    return count.bit_length() - 1


def side_of(index, bit):
    return (index >> bit) & 1 == 1


def tensor_sum(value):
    for bit in range(levels_of(lax.axis_size("tensor"))):
        value = value + swap(value, "tensor", 1 << bit)
    return value


def all_sum(value):
    for axis in ("tensor", "dp"):
        for bit in range(levels_of(lax.axis_size(axis))):
            value = value + swap(value, axis, 1 << bit)
    return value


def tensor_gather(own, filler=None):
    count = lax.axis_size("tensor")
    place = lax.axis_index("tensor")
    size = own.shape[1]
    held = own
    order = list(range(levels_of(count)))[::-1]
    for bit in order:
        came = swap(held, "tensor", 1 << bit)
        if filler is not None and bit == order[0]:
            came = after(came, *filler(held))
        upper = side_of(place, bit)
        number = held.shape[1] // size
        mine = [held[:, i * size : (i + 1) * size] for i in range(number)]
        theirs = [came[:, i * size : (i + 1) * size] for i in range(number)]
        pairs = []
        for a, b in zip(mine, theirs):
            pairs.append((jnp.where(upper, b, a), jnp.where(upper, a, b)))
        held = jnp.concatenate([v for pair in pairs for v in pair], 1)
    return held


def after(value, *others):
    return lax.optimization_barrier((value, *others))[0]


def rotary_tables():
    half = HEAD // 2
    freqs = theta_base ** (-(jnp.arange(half, dtype=full) * 2.0 / HEAD))
    angles = jnp.arange(SEQ, dtype=full)[:, None] * freqs[None, :]
    cosine = jnp.cos(angles)
    sine = jnp.sin(angles)
    return (jnp.concatenate([cosine, cosine], 1), jnp.concatenate([-sine, sine], 1))


def limits(mib):
    return pltpu.CompilerParams(vmem_limit_bytes=mib << 20)


def cost(flops, moved, powers=0):
    return pl.CostEstimate(flops=int(flops), bytes_accessed=int(moved), transcendentals=int(powers))


def dot_cols(a, b):
    return lax.dot_general(a, b, (((1,), (1,)), ((), ())), preferred_element_type=full)


def dot_rows(a, b):
    return lax.dot_general(a, b, (((0,), (0,)), ((), ())), preferred_element_type=full)


def attention_kernel(scale, q_in, k_in, v_in, cos, sin, out, q_out, k_out, v_out, logs):
    def turned(ref):
        x = ref[...]
        return (x * cos[...] + pltpu.roll(x, HEAD // 2, 1) * sin[...]).astype(low)

    q_out[...] = turned(q_in)
    k_out[...] = turned(k_in)
    v_out[...] = v_in[...].astype(low)
    for block in range(SEQ // BLOCK):
        mine = pl.ds(block * BLOCK, BLOCK)
        seen = pl.ds(0, (block + 1) * BLOCK)
        scores = dot_cols(q_out[mine, :], k_out[seen, :]) * scale
        peak = jnp.max(scores, axis=1, keepdims=True)
        expo = jnp.exp(scores - peak)
        total = jnp.sum(expo, axis=1, keepdims=True)
        probs = (expo / total).astype(low)
        out[mine, :] = jnp.dot(probs, v_out[seen, :], preferred_element_type=full).astype(low)
        logs[0, mine, :] = peak + jnp.log(total)


def attention(qkv, cosine, sine, scale):
    rows = qkv.shape[0]
    size = qkv.shape[1] // 3
    heads = size // HEAD
    block = (SEQ, HEAD)
    table = pl.BlockSpec(block, lambda s, h: (0, 0))
    spec = pl.BlockSpec(block, lambda s, h: (s, h))
    shape = jax.ShapeDtypeStruct((rows, size), low)
    pairs = rows * heads * SEQ * 5 // 8
    return pl.pallas_call(
        functools.partial(attention_kernel, scale),
        grid=(rows // SEQ, heads),
        in_specs=[
            pl.BlockSpec(block, lambda s, h: (s, h)),
            pl.BlockSpec(block, lambda s, h: (s, heads + h)),
            pl.BlockSpec(block, lambda s, h: (s, 2 * heads + h)),
            table,
            table,
        ],
        out_specs=[spec] * 4 + [pl.BlockSpec((1, SEQ, 1), lambda s, h: (h, s, 0))],
        out_shape=[shape] * 4 + [jax.ShapeDtypeStruct((heads, rows, 1), full)],
        compiler_params=limits(48),
        cost_estimate=cost(4 * pairs * HEAD, rows * size * 20, pairs),
        name="attention",
    )(qkv, qkv, qkv, cosine, sine)


def attention_back_kernel(scale, heads, q_in, k_in, v_in, logs, grad, cos, sin, out, dk, dv):
    head = pl.program_id(1)
    dk[...] = jnp.zeros_like(dk)
    dv[...] = jnp.zeros_like(dv)

    def columns(which):
        return pl.ds(pl.multiple_of((which * heads + head) * HEAD, HEAD), HEAD)

    def turned(x, at):
        return (x * cos[at, :] - pltpu.roll(x, HEAD // 2, 1) * sin[at, :]).astype(low)

    for block in range(SEQ // BLOCK):
        mine = pl.ds(block * BLOCK, BLOCK)
        seen = pl.ds(0, (block + 1) * BLOCK)
        query, keys, values, given = q_in[mine, :], k_in[seen, :], v_in[seen, :], grad[mine, :]
        probs = jnp.exp(dot_cols(query, keys) * scale - logs[0, mine, :])
        prob_grad = dot_cols(given, values)
        inner = jnp.sum(probs * prob_grad, axis=1, keepdims=True)
        score_grad = (probs * (prob_grad - inner)).astype(low)
        query_grad = jnp.dot(score_grad, keys, preferred_element_type=full) * scale
        out[mine, columns(0)] = turned(query_grad, mine)
        dk[seen, :] += dot_rows(score_grad, query)
        dv[seen, :] += dot_rows(probs.astype(low), given)
    whole = pl.ds(0, SEQ)
    out[:, columns(1)] = turned(dk[...] * scale, whole)
    out[:, columns(2)] = dv[...].astype(low)


def attention_back(query, keys, values, logs, grad, cosine, sine, scale):
    rows, size = query.shape
    heads = size // HEAD
    block = (SEQ, HEAD)
    table = pl.BlockSpec(block, lambda s, h: (0, 0))
    spec = pl.BlockSpec(block, lambda s, h: (s, h))
    pairs = rows * heads * SEQ * 5 // 8
    return pl.pallas_call(
        functools.partial(attention_back_kernel, scale, heads),
        grid=(rows // SEQ, heads),
        in_specs=[spec] * 3
        + [pl.BlockSpec((1, SEQ, 1), lambda s, h: (h, s, 0)), spec, table, table],
        out_specs=pl.BlockSpec((SEQ, 3 * size), lambda s, h: (s, 0)),
        out_shape=jax.ShapeDtypeStruct((rows, 3 * size), low),
        scratch_shapes=[pltpu.VMEM(block, full)] * 2,
        compiler_params=limits(48),
        cost_estimate=cost(10 * pairs * HEAD, rows * size * 16, pairs),
        name="attention_back",
    )(query, keys, values, logs, grad, cosine, sine)


def place_rows(pieces, held, sems, upper, first):
    copies = []
    for ref, start, number, mine, there, column in pieces:
        half = held.shape[0] // 2
        columns = ref.shape[1]
        side = upper if mine else 1 - upper
        copies.append(
            pltpu.make_async_copy(
                ref.at[pl.ds(start, number), :],
                held.at[
                    pl.ds(pl.multiple_of(side * half + there, 64), number),
                    pl.ds(column * columns, columns),
                ],
                sems.at[len(copies)],
            )
        )

    @pl.when(first)
    def _():
        for copy in copies:
            copy.start()
        for copy in copies:
            copy.wait()


def down_pieces(own, came):
    half = own.shape[0]
    return [(own, 0, half, True, 0, 0), (came, 0, half, False, 0, 0)]


cuts = (
    ((0, 0, 16),),
    ((0, 16, 40),),
    ((0, 40, 56),),
    ((0, 56, 108),),
    ((0, 108, 128), (1, 0, 128)),
)
order = (0, 2, 3, 1)


def pair_pieces(own_gate, own_up, *came):
    half = own_gate.shape[0]
    pieces = [(own_gate, 0, half, True, 0, 0), (own_up, 0, half, True, 0, 1)]
    for cut, ref in zip(cuts, came):
        at = 0
        for which, start, stop in cut:
            number = (stop - start) * half // 128
            pieces.append((ref, at, number, False, start * half // 128, which))
            at += number
    return pieces


def column_block(where, i, size):
    return pl.ds(pl.multiple_of((i ^ where[0]) * size, size), size)


def down_kernel(carried, where, rows, own, came, *refs):
    rows_out, raw, held, sems = refs[carried:]
    place_rows(down_pieces(own, came), held, sems, where[1], pl.program_id(0) == 0)
    rows_out[...] = rows[...]
    raw[...] = jnp.dot(rows[...], held[...], preferred_element_type=full).astype(low)


def down_pass(where, rows, own, came, start, total, carried):
    number, width = rows.shape
    hidden = own.shape[1]
    tile = 256
    first = start // tile
    anywhere = pl.BlockSpec(memory_space=pl.ANY)
    here = lambda columns: pl.BlockSpec((tile, columns), lambda i, where: (first + i, 0))
    return pl.pallas_call(
        functools.partial(down_kernel, len(carried)),
        grid_spec=pltpu.PrefetchScalarGridSpec(
            num_scalar_prefetch=1,
            grid=(number // tile,),
            in_specs=[pl.BlockSpec((tile, width), lambda i, where: (i, 0))]
            + [anywhere] * (2 + len(carried)),
            out_specs=[here(width), here(hidden)],
            scratch_shapes=[pltpu.VMEM((width, hidden), low), pltpu.SemaphoreType.DMA((2,))],
        ),
        out_shape=[
            jax.ShapeDtypeStruct((total, width), low),
            jax.ShapeDtypeStruct((total, hidden), low),
        ],
        input_output_aliases={4 + i: i for i in range(len(carried))},
        compiler_params=limits(48),
        cost_estimate=cost(
            2 * number * width * hidden, (number * (2 * width + hidden) + width * hidden) * 2
        ),
        name="down",
    )(where, rows, own, came, *carried)


def spread_kernel(count, where, left, right, even, odd, part):
    size = part.shape[1] // count
    part[...] = dot_cols(left[...], right[...]).astype(low)
    for i in range(count):
        (odd if i % 2 else even)[:, i // 2 * size : (i // 2 + 1) * size] = part[
            :, column_block(where, i, size)
        ]


def spread_dot(where, left, right, column, count):
    rows, depth = left.shape
    width = right.shape[0]
    tile = 256
    spec = lambda columns: pl.BlockSpec((tile, columns), lambda i, where: (i, 0))
    half = jax.ShapeDtypeStruct((rows, width // 2), low)
    return pl.pallas_call(
        functools.partial(spread_kernel, count),
        grid_spec=pltpu.PrefetchScalarGridSpec(
            num_scalar_prefetch=1,
            grid=(rows // tile,),
            in_specs=[
                spec(depth),
                pl.BlockSpec((width, depth), lambda i, where: (0, column)),
            ],
            out_specs=[spec(width // 2)] * 2,
            scratch_shapes=[pltpu.VMEM((tile, width), low)],
        ),
        out_shape=[half, half],
        compiler_params=limits(48),
        cost_estimate=cost(2 * rows * width * depth, (rows * (width + depth) + width * depth) * 2),
        name="spread",
    )(where, left, right)


def up_kernel(where, act, own, came, out, held, sems):
    place_rows(down_pieces(own, came), held, sems, where[1], pl.program_id(0) == 0)
    out[...] = dot_cols(act[...], held[...]).astype(low)


def up_pass(where, act, own, came):
    total, hidden = act.shape
    width = 2 * own.shape[0]
    tile = 256
    spec = lambda columns: pl.BlockSpec((tile, columns), lambda i, where: (i, 0))
    return pl.pallas_call(
        up_kernel,
        grid_spec=pltpu.PrefetchScalarGridSpec(
            num_scalar_prefetch=1,
            grid=(total // tile,),
            in_specs=[spec(hidden)] + [pl.BlockSpec(memory_space=pl.ANY)] * 2,
            out_specs=spec(width),
            scratch_shapes=[pltpu.VMEM((width, hidden), low), pltpu.SemaphoreType.DMA((2,))],
        ),
        out_shape=jax.ShapeDtypeStruct((total, width), low),
        compiler_params=limits(48),
        cost_estimate=cost(
            2 * total * width * hidden, (total * (width + hidden) + width * hidden) * 2
        ),
        name="up",
    )(where, act, own, came)


def expert_kernel(count, carried, where, *refs):
    blocks, refs = refs[:count], refs[count:]
    number = 2 + len(cuts)
    weights, (raw, routed, router) = refs[:number], refs[number : number + 3]
    rows_out, act_out, grad_out, even, odd, gate_grad, pair, part, sems = refs[
        number + 3 + carried :
    ]
    size = blocks[0].shape[1]
    hidden = raw.shape[1]
    place_rows(pair_pieces(*weights), pair, sems, where[1], pl.program_id(0) == 0)
    for i, ref in enumerate(blocks):
        rows_out[:, column_block(where, i, size)] = ref[...]
    both = jnp.dot(rows_out[...], pair[...], preferred_element_type=full)
    pre_gate = both[:, :hidden]
    pre_up = both[:, hidden:]
    sigma = 1.0 / (1.0 + jnp.exp(-pre_gate))
    silu = pre_gate * sigma
    act = silu * pre_up
    back = raw[...].astype(full)
    tile = back.shape[0]
    own = where[2].astype(full)
    other = jnp.broadcast_to(routed[...], (128, tile)).T - own
    logits = jnp.dot(rows_out[...], router[...], preferred_element_type=full)
    lane = lax.broadcasted_iota(jnp.int32, (tile, 128), 1).astype(full)
    ahead = jnp.where(lane == other, logits, 0.0) - jnp.where(lane == own, logits, 0.0)
    gate = 1.0 / (1.0 + jnp.exp(jnp.sum(ahead, axis=1, keepdims=True)))
    gate_sum = jnp.sum(act * back, axis=1, keepdims=True)
    gate_grad[...] = jnp.broadcast_to(gate_sum, (tile, 128)).T[:1]
    act_out[...] = (act * gate).astype(low)
    back = back * gate
    grad_out[:, :hidden] = (back * pre_up * sigma * (1.0 + pre_gate * (1.0 - sigma))).astype(low)
    grad_out[:, hidden:] = (back * silu).astype(low)
    part[...] = dot_cols(grad_out[...], pair[...]).astype(low)
    for i in range(count):
        (odd if i % 2 else even)[:, i // 2 * size : (i // 2 + 1) * size] = part[
            :, column_block(where, i, size)
        ]


def expert_pass(step, where, blocks, weights, raw, routed, router, carried):
    count = len(blocks)
    size = blocks[0].shape[1]
    width, hidden = 2 * weights[0].shape[0], weights[0].shape[1]
    both = 2 * hidden
    total = raw.shape[0]
    tile = 256
    steps = MOST // tile
    here = lambda i, where: (step * steps + i, 0)
    near = lambda i, where: (i, 0)
    near_spec = lambda columns: pl.BlockSpec((tile, columns), near)
    here_spec = lambda columns: pl.BlockSpec((tile, columns), here)
    row_spec = pl.BlockSpec((1, tile), lambda i, where: (0, i))
    anywhere = pl.BlockSpec(memory_space=pl.ANY)
    shape = lambda r, c, t=low: jax.ShapeDtypeStruct((r, c), t)
    return pl.pallas_call(
        functools.partial(expert_kernel, count, len(carried)),
        grid_spec=pltpu.PrefetchScalarGridSpec(
            num_scalar_prefetch=1,
            grid=(steps,),
            in_specs=[near_spec(size)] * count
            + [anywhere] * len(weights)
            + [
                here_spec(hidden),
                row_spec,
                pl.BlockSpec((width, 128), lambda i, where: (0, 0)),
            ]
            + [anywhere] * len(carried),
            out_specs=[
                here_spec(width),
                here_spec(hidden),
                here_spec(both),
                near_spec(width // 2),
                near_spec(width // 2),
                row_spec,
            ],
            scratch_shapes=[
                pltpu.VMEM((width, both), low),
                pltpu.VMEM((tile, width), low),
                pltpu.SemaphoreType.DMA((2 + sum(len(cut) for cut in cuts),)),
            ],
        ),
        out_shape=[
            shape(total, width),
            shape(total, hidden),
            shape(total, both),
            shape(MOST, width // 2),
            shape(MOST, width // 2),
            shape(1, MOST, full),
        ],
        input_output_aliases={
            count + len(weights) + 4 + i: i for i in range(len(carried))
        },
        compiler_params=limits(60),
        cost_estimate=cost(
            4 * MOST * width * both, width * both * 2 + MOST * (width * 8 + hidden * 8), MOST * hidden
        ),
        name="expert",
    )(where, *blocks, *weights, raw, routed, router, *carried)


def expert_grad_kernel(hidden, pieces, per, *refs):
    out = refs[-1]
    which, at = pl.program_id(0), pl.program_id(1)

    def add(ref, other):
        out[0] = (ref[...].astype(full) + other[...].astype(full))[:, :hidden]

    for k in range(pieces):

        @pl.when((which < 2) & (at // per == k))
        def _():
            add(refs[0], refs[1 + k])

    @pl.when(which == 2)
    def _():
        add(refs[1 + pieces], refs[2 + pieces])


def expert_grad_sum(pair, down, hidden):
    rows, padded = down[0].shape
    tile = min(256, rows)
    pieces = len(pair) - 1
    per = rows // tile // pieces
    last = rows // tile - 1

    def piece_spec(k):
        return pl.BlockSpec(
            (tile, padded),
            lambda w, i: (
                jnp.where(w == 2, per - 1, jnp.clip(i - k * per, 0, per - 1)),
                jnp.minimum(w, 1),
            ),
        )

    pair_spec = pl.BlockSpec(
        (tile, padded), lambda w, i: (jnp.where(w == 2, last, i), jnp.minimum(w, 1))
    )
    down_spec = pl.BlockSpec((tile, padded), lambda w, i: (jnp.where(w == 2, i, 0), 0))
    return pl.pallas_call(
        functools.partial(expert_grad_kernel, hidden, pieces, per),
        grid=(3, rows // tile),
        in_specs=[pair_spec] + [piece_spec(k) for k in range(pieces)] + [down_spec] * 2,
        out_specs=pl.BlockSpec((1, tile, hidden), lambda w, i: (w, i, 0)),
        out_shape=jax.ShapeDtypeStruct((3, rows, hidden), full),
        compiler_params=limits(40),
        cost_estimate=cost(rows * padded * 3, rows * padded * 24),
        name="expert_grad_sum",
    )(*pair, *down)


def near_blocks(own, *others):
    held = [own]
    for bit in range(levels_of(lax.axis_size("tensor")))[::-1]:
        theirs = [swap(v, "tensor", 1 << bit) for v in held]
        if bit and others:
            theirs = [after(v, *others) for v in theirs]
        held = [v for pair in zip(held, theirs) for v in pair]
    return held


def near_reduce(even, odd, meet, *others, filler=None):
    count = lax.axis_size("tensor")
    number = count // 2
    size = even.shape[1] // number
    came = swap(odd, "tensor", 1)
    for bit in range(1, levels_of(count)):
        blocks = [
            even[:, i * size : (i + 1) * size].astype(full)
            + came[:, i * size : (i + 1) * size].astype(full)
            for i in range(number)
        ]
        sent = jnp.concatenate([v.astype(low) for v in blocks[1::2]], 1)
        if bit == levels_of(count) - 1:
            sent = after(sent, *others)
            meet.append(sent)
        even = jnp.concatenate(blocks[::2], 1)
        came = swap(sent, "tensor", 1 << bit)
        if filler is not None and bit == levels_of(count) - 1:
            came = after(came, *filler(sent))
        number //= 2
    return even.astype(full) + came.astype(full)


def half_gather(local, group_count):
    held = local
    place = lax.axis_index("dp") % group_count
    for bit in range(levels_of(group_count) - 1):
        came = swap(held, "dp", 1 << bit)
        upper = side_of(place, bit)
        held = jnp.concatenate([jnp.where(upper, came, held), jnp.where(upper, held, came)], 0)
    return held


def group_finish(kept, came, position, group_count):
    if group_count > 2:
        came = jnp.concatenate(came, 0)
    for bit in range(levels_of(group_count) - 1)[::-1]:
        current = kept.astype(full) + came.astype(full)
        middle = current.shape[0] // 2
        upper = (position >> bit) & 1
        kept = lax.dynamic_slice_in_dim(current, upper * middle, middle, 0)
        given = lax.dynamic_slice_in_dim(current, (1 - upper) * middle, middle, 0)
        came = swap(given.astype(low), "dp", 1 << bit)
    return [kept, *came] if isinstance(came, list) else [kept, came]


def body(
    tokens,
    attn_gain,
    qkv_weight,
    out_weight,
    moe_gain,
    router_weight,
    expert_weight,
    routes,
    cotangent,
):
    rows = tokens.shape[0]
    width = tokens.shape[1]
    tensor_count = lax.axis_size("tensor")
    dp_count = lax.axis_size("dp")
    group_count = dp_count // EXPERTS
    size = width // tensor_count
    hidden_size = expert_weight.shape[2]
    padded = -(-hidden_size // 128) * 128
    scale = 1.0 / math.sqrt(HEAD)
    place = lax.axis_index("tensor")
    index = lax.axis_index("dp")
    expert = index // group_count
    member = index % group_count
    top_half = member >> (levels_of(group_count) - 1)
    where = jnp.stack([place, top_half, expert]).astype(jnp.int32)

    def own_columns(value):
        return lax.dynamic_slice_in_dim(value, place * size, size, 1)

    extras = jnp.concatenate([router_weight, attn_gain[:, None], moe_gain[:, None]], 1)
    extras = jnp.pad(extras, ((0, 0), (0, 128 - extras.shape[1])))
    first = lax.all_gather(
        jnp.concatenate([qkv_weight.reshape(-1, 3 * size), out_weight, extras], 1),
        "dp",
        axis=0,
        tiled=True,
    )
    qkv_flat = first[:, : 3 * size]
    out_full = first[:, 3 * size : 4 * size]
    small = first[:, 4 * size :].T
    router_full = small[:EXPERTS]
    gain_first = small[EXPERTS : EXPERTS + 1].astype(full)
    gain_second = small[EXPERTS + 1 : EXPERTS + 2].astype(full)
    gain_first_own = own_columns(gain_first)
    gain_second_own = own_columns(gain_second)
    router_own = own_columns(router_full)

    near = jnp.arange(EXPERTS, dtype=jnp.int32) ^ expert
    names = jnp.arange(EXPERTS, dtype=jnp.int32)
    hits = jnp.sum((routes.T[None] == names[:, None, None]).astype(jnp.int32), 1)
    rank = jnp.cumsum(hits, axis=1) - hits
    slot_near = jnp.take(jnp.where(hits > 0, rank, -1), near, axis=0)
    places = jnp.arange(MOST, dtype=jnp.int32)[:, None]
    chosen = [(places == slot_near[s][None, :]).astype(low) for s in range(EXPERTS)]

    def packed(own):
        return [jnp.dot(c, own, preferred_element_type=full).astype(low) for c in chosen]

    def exchange(parts):
        return [parts[0]] + [swap(parts[s], "dp", s * group_count) for s in range(1, EXPERTS)]

    def unpacked(parts):
        total = contract(chosen[0], parts[0], 0, 0)
        for c, part in zip(chosen[1:], parts[1:]):
            total = total + contract(c, part, 0, 0)
        return total

    def widened(value):
        return jnp.pad(value, ((0, 0), (0, padded - hidden_size)))

    gate_mine, up_mine, down_mine = [
        half_gather(widened(expert_weight[k]), group_count) for k in range(3)
    ]
    half = width // 2
    mine_at, given_at = top_half * half, (1 - top_half) * half
    reach = group_count // 2

    def group_send(given, *others):
        return swap(after(given, *others), "dp", reach)

    down = (down_mine, group_send(down_mine))
    crossing = []

    def cross(*others):
        pieces = [
            (gate_mine, up_mine)[which][start * half // 128 : stop * half // 128]
            for which, start, stop in cuts[len(crossing)]
        ]
        crossing.append(group_send(jnp.concatenate(pieces, 0), *crossing[-1:], *others))

    cross(first)

    grad_own = own_columns(cotangent)
    grad_mine = jnp.dot(chosen[0], cotangent, preferred_element_type=full).astype(low)
    planes = [
        [m + g * group_count for g in range(EXPERTS)] for m in range(group_count)
    ]
    grad_planes = lax.all_gather(
        after(grad_own, first), "dp", axis=0, tiled=True, axis_index_groups=planes
    )
    slots_came = exchange([slot_near[s][None].astype(full) for s in range(EXPERTS)])
    route_sums = jnp.sum(routes, axis=1)[None].astype(low)
    routed = exchange([contract(route_sums, c, 1, 1) for c in chosen])

    inputs = tokens.astype(full)
    scale_one = lax.rsqrt(jnp.mean(inputs * inputs, axis=1, keepdims=True) + epsilon)
    normed_in = (inputs * scale_one * gain_first).astype(low)
    inputs_own = own_columns(tokens).astype(full)
    normed_in = after(normed_in, down[1], grad_mine, *slots_came, *routed)
    qkv = jnp.dot(normed_in, qkv_flat, preferred_element_type=full)
    cross(qkv)
    cosine, sine = rotary_tables()
    context, query, keys, values, logs = attention(qkv, cosine, sine, scale)
    context = after(context, crossing[1])
    cross(context)
    attn_parts = spread_dot(where, context, first, 3, tensor_count)
    rows_raw = []

    total = EXPERTS * MOST

    def down_filler(sent):
        cross(sent)
        rows_raw.extend(down_pass(where, after(grad_mine, sent), *down, 0, total, ()))
        return (rows_raw[1], crossing[3])

    hidden = inputs_own + near_reduce(*attn_parts, [], crossing[2], filler=down_filler)
    cross(rows_raw[1])
    grad_planes = after(grad_planes, hidden)
    grad_packed = []
    for s in order[1:]:
        source = lax.dynamic_slice_in_dim(grad_planes, (expert ^ s) * rows, rows, 0)
        taken = (places.astype(full) == slots_came[s]).astype(low)
        grad_packed.append(jnp.dot(taken, source, preferred_element_type=full).astype(low))
    grad_rest = lax.all_gather(jnp.concatenate(grad_packed, 0), "tensor", axis=1, tiled=True)

    scaled_hidden = (hidden * gain_second_own).astype(low)
    sums = tensor_sum(
        jnp.concatenate(
            [contract(router_own, scaled_hidden, 1, 1), jnp.sum(hidden * hidden, 1)[None]], 0
        )
    )
    scale_two_row = lax.rsqrt(sums[EXPERTS:] / width + epsilon)
    scale_two = scale_two_row.reshape(rows, 1)
    logits = sums[:EXPERTS] * scale_two_row
    normed_two = hidden * scale_two
    moe_in = (normed_two * gain_second_own).astype(low)
    named = hits > 0
    top = jnp.max(jnp.where(named, logits, masked_out), axis=0, keepdims=True)
    weight = jnp.where(named, jnp.exp(logits - top), 0.0)
    gates = weight / jnp.sum(weight, axis=0, keepdims=True)

    def three_parts(value):
        a = value.astype(low)
        b = (value - a.astype(full)).astype(low)
        return jnp.stack([a, b, (value - a.astype(full) - b.astype(full)).astype(low)])

    moe_packed = packed(moe_in)
    pair = (gate_mine, up_mine, *crossing)
    crossed = {2: swap(moe_packed[2], "dp", 2 * group_count)}
    crossed[3] = swap(after(moe_packed[3], crossed[2]), "dp", 3 * group_count)
    arrived = [near_blocks(moe_packed[0])]

    carried = ()
    sums_sent = []
    came_home = {}
    returned = []
    gate_grads = []
    router_block = first[:, 4 * size :]
    for step in range(EXPERTS):
        named_sum = routed[order[step]]
        if step == 1:
            rows_raw = down_pass(where, after(grad_rest, even), *down, MOST, total, rows_raw)
            named_sum = after(named_sum, crossed[3])
        if step == 2:
            named_sum = after(named_sum, crossed[1], *sums_sent)
        if step == 3:
            named_sum = after(named_sum, sums_sent[2])
        moe_rows, activation, pre_grad, even, odd, gate_grad = expert_pass(
            step, where, arrived[step], pair, rows_raw[1], named_sum, router_block, carried
        )
        carried = (moe_rows, activation, pre_grad)
        if step == 0:
            arrived.append(near_blocks(crossed[2], even))
            crossed[3] = after(crossed[3], even)
            crossed[1] = swap(after(moe_packed[1], crossed[3]), "dp", group_count)
        if step == 1:
            arrived.append(near_blocks(crossed[3], even))
            odd = after(odd, crossed[1], arrived[2][tensor_count // 2])
        if step == 2:
            arrived.append(near_blocks(crossed[1], even))
        if step == 2:
            odd = after(odd, *returned, arrived[3][tensor_count // 2])
        if step == 3:
            came_home[2] = swap(returned[1], "dp", 2 * group_count)
            odd = after(odd, returned[2], came_home[2])
        returned.append(near_reduce(even, odd, sums_sent).astype(low))
        gate_grads.append(gate_grad)

    def home(parts):
        return {
            s: swap(v, "dp", s * group_count) if s else v for s, v in zip(order, parts)
        }

    came_home[0] = returned[0]
    came_home[3] = swap(returned[2], "dp", 3 * group_count)
    came_home[1] = swap(returned[3], "dp", group_count)
    gate_grad_near = home([gate_grads[0]] + [after(v, even) for v in gate_grads[1:]])
    grad_rows = rows_raw[0]

    def term(left, right):
        def part(start, number):
            taken = lax.dynamic_slice_in_dim(left, start, number, 1)
            return contract(taken, right, 0, 0).astype(low)

        return part

    unit = half // 128
    quarter = half // 2
    act_late = after(activation, sums_sent[3], returned[2])
    down_given = term(grad_rows, act_late)(given_at, half)
    down_sums = [group_send(down_given[: 40 * unit])]
    expert_part = up_pass(
        where, after(activation, down_given, returned[3], *gate_grad_near.values()), *down
    )
    expert_part = after(expert_part, down_sums[0], came_home[3], came_home[1])
    expert_own = lax.psum_scatter(expert_part, "tensor", scatter_dimension=1, tiled=True)
    down_sums.append(group_send(down_given[40 * unit : 80 * unit], down_sums[0]))
    came_home = {s: after(v, expert_part) for s, v in came_home.items()}
    back = unpacked([came_home[s] for s in range(EXPERTS)])

    gate_grad = jnp.concatenate(
        [
            jnp.sum(contract(three_parts(gate_grad_near[s][0]), chosen[s], 1, 0), 0, keepdims=True)
            for s in range(EXPERTS)
        ],
        0,
    )
    scaled_back = back * gain_second_own
    sums = tensor_sum(
        jnp.concatenate([gate_grad, jnp.sum(scaled_back * normed_two, axis=1)[None]], 0)
    )
    gate_grad = jnp.take(sums[:EXPERTS], near, axis=0)
    weighted = jnp.sum(gates * gate_grad, axis=0, keepdims=True)
    logit_grad = (gates * (gate_grad - weighted)).astype(low)
    mean_two = (
        sums[EXPERTS:] + jnp.sum(logit_grad.astype(full) * logits, axis=0, keepdims=True)
    ) / width
    moe_grad = contract(logit_grad, router_own, 0, 0) + back

    grad_out = grad_own.astype(full)
    hidden_grad = grad_out + scale_two * (
        moe_grad * gain_second_own - normed_two * mean_two.reshape(rows, 1)
    )
    router_grad = jnp.dot(logit_grad, moe_in, preferred_element_type=full)
    moe_gain_grad = jnp.sum(moe_grad * normed_two, axis=0)
    pair_given = []
    kept = []

    def give_pair(sent):
        down_sums.append(group_send(down_given[80 * unit :], down_sums[1], sent))
        pair_term = term(moe_rows, after(pre_grad, sent, down_sums[1]))
        pair_given.extend(pair_term(given_at + k * quarter, quarter) for k in range(2))
        return (*pair_given, down_sums[2])

    attn_grad = tensor_gather(hidden_grad.astype(low), give_pair)
    pair_sums = [group_send(pair_given[0][: 16 * unit], down_sums[2])]
    context_grad = jnp.dot(attn_grad, out_full, preferred_element_type=full).astype(low)
    out_grad = contract(after(attn_grad, context_grad), context, 0, 0).astype(low)
    qkv_grad_rows = attention_back(query, keys, values, logs, context_grad, cosine, sine, scale)
    qkv_grad_rows = after(qkv_grad_rows, pair_sums[0], out_grad)
    qkv_grad = contract(normed_in, qkv_grad_rows, 0, 0).astype(low)
    grads_both = jnp.concatenate([qkv_grad, out_grad], 1)
    shards = lax.psum_scatter(grads_both, "dp", scatter_dimension=0, tiled=True)
    pair_sums.append(group_send(pair_given[0][16 * unit : 32 * unit], pair_sums[0], grads_both))
    pair_sums.append(group_send(pair_given[0][32 * unit :], pair_sums[1]))
    pair_last = group_send(pair_given[1], pair_sums[2])
    outputs = {}

    def keep(sent):
        part = after(expert_own[MOST : 2 * MOST], sent)
        outputs[2] = swap(part, "dp", 2 * group_count)
        late = after(pre_grad, sent, expert_own)
        kept.append(term(moe_rows, late)(mine_at, half))
        kept.append(term(grad_rows, after(activation, kept[0]))(mine_at, half))
        return (*kept, outputs[2], pair_sums[1])

    parts = spread_dot(where, after(qkv_grad_rows, grads_both), first, 0, tensor_count)
    normed_grad = near_reduce(*parts, [], filler=keep)
    outputs[0] = expert_own[:MOST]
    for k in (2, 3):
        part = after(expert_own[k * MOST : (k + 1) * MOST], outputs[2])
        outputs[order[k]] = swap(part, "dp", order[k] * group_count)
    normed_one = inputs_own * scale_one
    scaled_in = normed_grad * gain_first_own
    attn_gain_grad = jnp.sum(normed_grad * normed_one, axis=0)
    mean_one = tensor_sum(jnp.sum(scaled_in * normed_one, axis=1)[None]) / width
    input_own = hidden_grad + scale_one * (scaled_in - normed_one * mean_one.reshape(rows, 1))
    mine = jnp.concatenate([router_grad, attn_gain_grad[None], moe_gain_grad[None]], 0)
    mine = lax.dynamic_update_slice_in_dim(
        jnp.zeros((mine.shape[0], width), full), mine, place * size, 1
    )
    mine = all_sum(mine)
    input_own = after(input_own, outputs[3], outputs[1], pair_sums[2])
    expert_grad = expert_grad_sum(
        group_finish(kept[0], [jnp.concatenate(pair_sums, 0), pair_last], member, group_count),
        group_finish(kept[1], [jnp.concatenate(down_sums, 0)], member, group_count),
        hidden_size,
    )
    input_grad = tensor_gather(input_own.astype(low), lambda sent: (mine,))
    input_grad = input_grad.astype(full)
    layer_own = hidden + unpacked([outputs[s] for s in range(EXPERTS)])
    layer_out = tensor_gather(layer_own.astype(low)).astype(full)
    share = width // dp_count
    mine = lax.dynamic_slice_in_dim(mine, index * share, share, 1)
    shards = after(shards, layer_out, input_grad, expert_grad).astype(full)
    qkv_shard, out_shard = shards[:, : 3 * size], shards[:, 3 * size :]
    return (
        layer_out,
        input_grad,
        mine[EXPERTS],
        qkv_shard.reshape(share, 3, size),
        out_shard,
        mine[EXPERTS + 1],
        mine[:EXPERTS].T,
        expert_grad,
    )


def solution(mesh):
    placed = (
        P("dp", None),
        P("dp"),
        P("dp", None, "tensor"),
        P("dp", "tensor"),
        P("dp"),
        P("dp", None),
        P(None, "dp", "tensor"),
        P("dp", None),
        P("dp", None),
    )
    return jax.shard_map(
        body,
        mesh=mesh,
        in_specs=placed,
        out_specs=(
            P("dp", None),
            P("dp", None),
            P("dp"),
            P("dp", None, "tensor"),
            P("dp", "tensor"),
            P("dp"),
            P("dp", None),
            P(None, "dp", "tensor"),
        ),
        check_vma=False,
    )
```

```python
import functools
import math

import jax
import jax.numpy as jnp
from jax import lax
from jax.experimental import pallas as pl
from jax.experimental.pallas import tpu as pltpu
from jax.sharding import PartitionSpec as P

HEAD = 128
EXPERTS = 4
SEQ = 1024
BLOCK = 256
MOST = 768


epsilon = 1e-05
theta_base = 10000.0
masked_out = -1e30
low = jnp.bfloat16
full = jnp.float32


def swap(value, axis, distance):
    return lax.ppermute(value, axis, [(i, i ^ distance) for i in range(lax.axis_size(axis))])


def contract(left, right, left_dim, right_dim):
    return lax.dot_general(
        left, right, (((left_dim,), (right_dim,)), ((), ())), preferred_element_type=jnp.float32
    )


def levels_of(count):
    return count.bit_length() - 1


def side_of(index, bit):
    return (index >> bit) & 1 == 1


def tensor_sum(value):
    for bit in range(levels_of(lax.axis_size("tensor"))):
        value = value + swap(value, "tensor", 1 << bit)
    return value


def all_sum(value):
    for axis in ("tensor", "dp"):
        for bit in range(levels_of(lax.axis_size(axis))):
            value = value + swap(value, axis, 1 << bit)
    return value


def tensor_gather(own, filler=None):
    count = lax.axis_size("tensor")
    place = lax.axis_index("tensor")
    size = own.shape[1]
    held = own
    order = list(range(levels_of(count)))[::-1]
    for bit in order:
        came = swap(held, "tensor", 1 << bit)
        if filler is not None and bit == order[0]:
            came = after(came, *filler(held))
        upper = side_of(place, bit)
        number = held.shape[1] // size
        mine = [held[:, i * size : (i + 1) * size] for i in range(number)]
        theirs = [came[:, i * size : (i + 1) * size] for i in range(number)]
        pairs = []
        for a, b in zip(mine, theirs):
            pairs.append((jnp.where(upper, b, a), jnp.where(upper, a, b)))
        held = jnp.concatenate([v for pair in pairs for v in pair], 1)
    return held


def after(value, *others):
    return lax.optimization_barrier((value, *others))[0]


def rotary_tables():
    half = HEAD // 2
    freqs = theta_base ** (-(jnp.arange(half, dtype=full) * 2.0 / HEAD))
    angles = jnp.arange(SEQ, dtype=full)[:, None] * freqs[None, :]
    cosine = jnp.cos(angles)
    sine = jnp.sin(angles)
    return (jnp.concatenate([cosine, cosine], 1), jnp.concatenate([-sine, sine], 1))


def limits(mib):
    return pltpu.CompilerParams(vmem_limit_bytes=mib << 20)


def cost(flops, moved, powers=0):
    return pl.CostEstimate(flops=int(flops), bytes_accessed=int(moved), transcendentals=int(powers))


def dot_cols(a, b):
    return lax.dot_general(a, b, (((1,), (1,)), ((), ())), preferred_element_type=full)


def dot_rows(a, b):
    return lax.dot_general(a, b, (((0,), (0,)), ((), ())), preferred_element_type=full)


def attention_kernel(scale, q_in, k_in, v_in, cos, sin, out, q_out, k_out, v_out, logs):
    def turned(ref):
        x = ref[...]
        return (x * cos[...] + pltpu.roll(x, HEAD // 2, 1) * sin[...]).astype(low)

    q_out[...] = turned(q_in)
    k_out[...] = turned(k_in)
    v_out[...] = v_in[...].astype(low)
    for block in range(SEQ // BLOCK):
        mine = pl.ds(block * BLOCK, BLOCK)
        seen = pl.ds(0, (block + 1) * BLOCK)
        scores = dot_cols(q_out[mine, :], k_out[seen, :]) * scale
        peak = jnp.max(scores, axis=1, keepdims=True)
        expo = jnp.exp(scores - peak)
        total = jnp.sum(expo, axis=1, keepdims=True)
        probs = (expo / total).astype(low)
        out[mine, :] = jnp.dot(probs, v_out[seen, :], preferred_element_type=full).astype(low)
        logs[0, mine, :] = peak + jnp.log(total)


def attention(qkv, cosine, sine, scale):
    rows = qkv.shape[0]
    size = qkv.shape[1] // 3
    heads = size // HEAD
    block = (SEQ, HEAD)
    table = pl.BlockSpec(block, lambda s, h: (0, 0))
    spec = pl.BlockSpec(block, lambda s, h: (s, h))
    shape = jax.ShapeDtypeStruct((rows, size), low)
    pairs = rows * heads * SEQ * 5 // 8
    return pl.pallas_call(
        functools.partial(attention_kernel, scale),
        grid=(rows // SEQ, heads),
        in_specs=[
            pl.BlockSpec(block, lambda s, h: (s, h)),
            pl.BlockSpec(block, lambda s, h: (s, heads + h)),
            pl.BlockSpec(block, lambda s, h: (s, 2 * heads + h)),
            table,
            table,
        ],
        out_specs=[spec] * 4 + [pl.BlockSpec((1, SEQ, 1), lambda s, h: (h, s, 0))],
        out_shape=[shape] * 4 + [jax.ShapeDtypeStruct((heads, rows, 1), full)],
        compiler_params=limits(48),
        cost_estimate=cost(4 * pairs * HEAD, rows * size * 20, pairs),
        name="attention",
    )(qkv, qkv, qkv, cosine, sine)


def attention_back_kernel(scale, heads, q_in, k_in, v_in, logs, grad, cos, sin, out, dk, dv):
    head = pl.program_id(1)
    dk[...] = jnp.zeros_like(dk)
    dv[...] = jnp.zeros_like(dv)

    def columns(which):
        return pl.ds(pl.multiple_of((which * heads + head) * HEAD, HEAD), HEAD)

    def turned(x, at):
        return (x * cos[at, :] - pltpu.roll(x, HEAD // 2, 1) * sin[at, :]).astype(low)

    for block in range(SEQ // BLOCK):
        mine = pl.ds(block * BLOCK, BLOCK)
        seen = pl.ds(0, (block + 1) * BLOCK)
        query, keys, values, given = q_in[mine, :], k_in[seen, :], v_in[seen, :], grad[mine, :]
        probs = jnp.exp(dot_cols(query, keys) * scale - logs[0, mine, :])
        prob_grad = dot_cols(given, values)
        inner = jnp.sum(probs * prob_grad, axis=1, keepdims=True)
        score_grad = (probs * (prob_grad - inner)).astype(low)
        query_grad = jnp.dot(score_grad, keys, preferred_element_type=full) * scale
        out[mine, columns(0)] = turned(query_grad, mine)
        dk[seen, :] += dot_rows(score_grad, query)
        dv[seen, :] += dot_rows(probs.astype(low), given)
    whole = pl.ds(0, SEQ)
    out[:, columns(1)] = turned(dk[...] * scale, whole)
    out[:, columns(2)] = dv[...].astype(low)


def attention_back(query, keys, values, logs, grad, cosine, sine, scale):
    rows, size = query.shape
    heads = size // HEAD
    block = (SEQ, HEAD)
    table = pl.BlockSpec(block, lambda s, h: (0, 0))
    spec = pl.BlockSpec(block, lambda s, h: (s, h))
    pairs = rows * heads * SEQ * 5 // 8
    return pl.pallas_call(
        functools.partial(attention_back_kernel, scale, heads),
        grid=(rows // SEQ, heads),
        in_specs=[spec] * 3
        + [pl.BlockSpec((1, SEQ, 1), lambda s, h: (h, s, 0)), spec, table, table],
        out_specs=pl.BlockSpec((SEQ, 3 * size), lambda s, h: (s, 0)),
        out_shape=jax.ShapeDtypeStruct((rows, 3 * size), low),
        scratch_shapes=[pltpu.VMEM(block, full)] * 2,
        compiler_params=limits(48),
        cost_estimate=cost(10 * pairs * HEAD, rows * size * 16, pairs),
        name="attention_back",
    )(query, keys, values, logs, grad, cosine, sine)


def place_rows(pieces, held, sems, upper, first):
    copies = []
    for ref, start, number, mine, there, column in pieces:
        half = held.shape[0] // 2
        columns = ref.shape[1]
        side = upper if mine else 1 - upper
        copies.append(
            pltpu.make_async_copy(
                ref.at[pl.ds(start, number), :],
                held.at[
                    pl.ds(pl.multiple_of(side * half + there, 64), number),
                    pl.ds(column * columns, columns),
                ],
                sems.at[len(copies)],
            )
        )

    @pl.when(first)
    def _():
        for copy in copies:
            copy.start()
        for copy in copies:
            copy.wait()


def down_pieces(own, came):
    half = own.shape[0]
    return [(own, 0, half, True, 0, 0), (came, 0, half, False, 0, 0)]


cuts = (
    ((0, 0, 16),),
    ((0, 16, 40),),
    ((0, 40, 56),),
    ((0, 56, 108),),
    ((0, 108, 128), (1, 0, 128)),
)
order = (0, 2, 3, 1)


def pair_pieces(own_gate, own_up, *came):
    half = own_gate.shape[0]
    pieces = [(own_gate, 0, half, True, 0, 0), (own_up, 0, half, True, 0, 1)]
    for cut, ref in zip(cuts, came):
        at = 0
        for which, start, stop in cut:
            number = (stop - start) * half // 128
            pieces.append((ref, at, number, False, start * half // 128, which))
            at += number
    return pieces


def column_block(where, i, size):
    return pl.ds(pl.multiple_of((i ^ where[0]) * size, size), size)


def down_kernel(carried, where, rows, own, came, *refs):
    rows_out, raw, held, sems = refs[carried:]
    place_rows(down_pieces(own, came), held, sems, where[1], pl.program_id(0) == 0)
    rows_out[...] = rows[...]
    raw[...] = jnp.dot(rows[...], held[...], preferred_element_type=full).astype(low)


def down_pass(where, rows, own, came, start, total, carried):
    number, width = rows.shape
    hidden = own.shape[1]
    tile = 256
    first = start // tile
    anywhere = pl.BlockSpec(memory_space=pl.ANY)
    here = lambda columns: pl.BlockSpec((tile, columns), lambda i, where: (first + i, 0))
    return pl.pallas_call(
        functools.partial(down_kernel, len(carried)),
        grid_spec=pltpu.PrefetchScalarGridSpec(
            num_scalar_prefetch=1,
            grid=(number // tile,),
            in_specs=[pl.BlockSpec((tile, width), lambda i, where: (i, 0))]
            + [anywhere] * (2 + len(carried)),
            out_specs=[here(width), here(hidden)],
            scratch_shapes=[pltpu.VMEM((width, hidden), low), pltpu.SemaphoreType.DMA((2,))],
        ),
        out_shape=[
            jax.ShapeDtypeStruct((total, width), low),
            jax.ShapeDtypeStruct((total, hidden), low),
        ],
        input_output_aliases={4 + i: i for i in range(len(carried))},
        compiler_params=limits(48),
        cost_estimate=cost(
            2 * number * width * hidden, (number * (2 * width + hidden) + width * hidden) * 2
        ),
        name="down",
    )(where, rows, own, came, *carried)


def spread_kernel(count, where, left, right, even, odd, part):
    size = part.shape[1] // count
    part[...] = dot_cols(left[...], right[...]).astype(low)
    for i in range(count):
        (odd if i % 2 else even)[:, i // 2 * size : (i // 2 + 1) * size] = part[
            :, column_block(where, i, size)
        ]


def spread_dot(where, left, right, column, count):
    rows, depth = left.shape
    width = right.shape[0]
    tile = 256
    spec = lambda columns: pl.BlockSpec((tile, columns), lambda i, where: (i, 0))
    half = jax.ShapeDtypeStruct((rows, width // 2), low)
    return pl.pallas_call(
        functools.partial(spread_kernel, count),
        grid_spec=pltpu.PrefetchScalarGridSpec(
            num_scalar_prefetch=1,
            grid=(rows // tile,),
            in_specs=[
                spec(depth),
                pl.BlockSpec((width, depth), lambda i, where: (0, column)),
            ],
            out_specs=[spec(width // 2)] * 2,
            scratch_shapes=[pltpu.VMEM((tile, width), low)],
        ),
        out_shape=[half, half],
        compiler_params=limits(48),
        cost_estimate=cost(2 * rows * width * depth, (rows * (width + depth) + width * depth) * 2),
        name="spread",
    )(where, left, right)


def up_kernel(where, act, own, came, out, held, sems):
    place_rows(down_pieces(own, came), held, sems, where[1], pl.program_id(0) == 0)
    out[...] = dot_cols(act[...], held[...]).astype(low)


def up_pass(where, act, own, came):
    total, hidden = act.shape
    width = 2 * own.shape[0]
    tile = 256
    spec = lambda columns: pl.BlockSpec((tile, columns), lambda i, where: (i, 0))
    return pl.pallas_call(
        up_kernel,
        grid_spec=pltpu.PrefetchScalarGridSpec(
            num_scalar_prefetch=1,
            grid=(total // tile,),
            in_specs=[spec(hidden)] + [pl.BlockSpec(memory_space=pl.ANY)] * 2,
            out_specs=spec(width),
            scratch_shapes=[pltpu.VMEM((width, hidden), low), pltpu.SemaphoreType.DMA((2,))],
        ),
        out_shape=jax.ShapeDtypeStruct((total, width), low),
        compiler_params=limits(48),
        cost_estimate=cost(
            2 * total * width * hidden, (total * (width + hidden) + width * hidden) * 2
        ),
        name="up",
    )(where, act, own, came)


def expert_kernel(count, carried, where, *refs):
    blocks, refs = refs[:count], refs[count:]
    number = 2 + len(cuts)
    weights, (raw, routed, router) = refs[:number], refs[number : number + 3]
    rows_out, act_out, grad_out, even, odd, gate_grad, pair, part, sems = refs[
        number + 3 + carried :
    ]
    size = blocks[0].shape[1]
    hidden = raw.shape[1]
    place_rows(pair_pieces(*weights), pair, sems, where[1], pl.program_id(0) == 0)
    for i, ref in enumerate(blocks):
        rows_out[:, column_block(where, i, size)] = ref[...]
    both = jnp.dot(rows_out[...], pair[...], preferred_element_type=full)
    pre_gate = both[:, :hidden]
    pre_up = both[:, hidden:]
    sigma = 1.0 / (1.0 + jnp.exp(-pre_gate))
    silu = pre_gate * sigma
    act = silu * pre_up
    back = raw[...].astype(full)
    tile = back.shape[0]
    own = where[2].astype(full)
    other = jnp.broadcast_to(routed[...], (128, tile)).T - own
    logits = jnp.dot(rows_out[...], router[...], preferred_element_type=full)
    lane = lax.broadcasted_iota(jnp.int32, (tile, 128), 1).astype(full)
    ahead = jnp.where(lane == other, logits, 0.0) - jnp.where(lane == own, logits, 0.0)
    gate = 1.0 / (1.0 + jnp.exp(jnp.sum(ahead, axis=1, keepdims=True)))
    gate_sum = jnp.sum(act * back, axis=1, keepdims=True)
    gate_grad[...] = jnp.broadcast_to(gate_sum, (tile, 128)).T[:1]
    act_out[...] = (act * gate).astype(low)
    back = back * gate
    grad_out[:, :hidden] = (back * pre_up * sigma * (1.0 + pre_gate * (1.0 - sigma))).astype(low)
    grad_out[:, hidden:] = (back * silu).astype(low)
    part[...] = dot_cols(grad_out[...], pair[...]).astype(low)
    for i in range(count):
        (odd if i % 2 else even)[:, i // 2 * size : (i // 2 + 1) * size] = part[
            :, column_block(where, i, size)
        ]


def expert_pass(step, where, blocks, weights, raw, routed, router, carried):
    count = len(blocks)
    size = blocks[0].shape[1]
    width, hidden = 2 * weights[0].shape[0], weights[0].shape[1]
    both = 2 * hidden
    total = raw.shape[0]
    tile = 256
    steps = MOST // tile
    here = lambda i, where: (step * steps + i, 0)
    near = lambda i, where: (i, 0)
    near_spec = lambda columns: pl.BlockSpec((tile, columns), near)
    here_spec = lambda columns: pl.BlockSpec((tile, columns), here)
    row_spec = pl.BlockSpec((1, tile), lambda i, where: (0, i))
    anywhere = pl.BlockSpec(memory_space=pl.ANY)
    shape = lambda r, c, t=low: jax.ShapeDtypeStruct((r, c), t)
    return pl.pallas_call(
        functools.partial(expert_kernel, count, len(carried)),
        grid_spec=pltpu.PrefetchScalarGridSpec(
            num_scalar_prefetch=1,
            grid=(steps,),
            in_specs=[near_spec(size)] * count
            + [anywhere] * len(weights)
            + [
                here_spec(hidden),
                row_spec,
                pl.BlockSpec((width, 128), lambda i, where: (0, 0)),
            ]
            + [anywhere] * len(carried),
            out_specs=[
                here_spec(width),
                here_spec(hidden),
                here_spec(both),
                near_spec(width // 2),
                near_spec(width // 2),
                row_spec,
            ],
            scratch_shapes=[
                pltpu.VMEM((width, both), low),
                pltpu.VMEM((tile, width), low),
                pltpu.SemaphoreType.DMA((2 + sum(len(cut) for cut in cuts),)),
            ],
        ),
        out_shape=[
            shape(total, width),
            shape(total, hidden),
            shape(total, both),
            shape(MOST, width // 2),
            shape(MOST, width // 2),
            shape(1, MOST, full),
        ],
        input_output_aliases={
            count + len(weights) + 4 + i: i for i in range(len(carried))
        },
        compiler_params=limits(60),
        cost_estimate=cost(
            4 * MOST * width * both, width * both * 2 + MOST * (width * 8 + hidden * 8), MOST * hidden
        ),
        name="expert",
    )(where, *blocks, *weights, raw, routed, router, *carried)


def expert_grad_kernel(hidden, pieces, per, *refs):
    out = refs[-1]
    which, at = pl.program_id(0), pl.program_id(1)

    def add(ref, other):
        out[0] = (ref[...].astype(full) + other[...].astype(full))[:, :hidden]

    for k in range(pieces):

        @pl.when((which < 2) & (at // per == k))
        def _():
            add(refs[0], refs[1 + k])

    @pl.when(which == 2)
    def _():
        add(refs[1 + pieces], refs[2 + pieces])


def expert_grad_sum(pair, down, hidden):
    rows, padded = down[0].shape
    tile = min(256, rows)
    pieces = len(pair) - 1
    per = rows // tile // pieces
    last = rows // tile - 1

    def piece_spec(k):
        return pl.BlockSpec(
            (tile, padded),
            lambda w, i: (
                jnp.where(w == 2, per - 1, jnp.clip(i - k * per, 0, per - 1)),
                jnp.minimum(w, 1),
            ),
        )

    pair_spec = pl.BlockSpec(
        (tile, padded), lambda w, i: (jnp.where(w == 2, last, i), jnp.minimum(w, 1))
    )
    down_spec = pl.BlockSpec((tile, padded), lambda w, i: (jnp.where(w == 2, i, 0), 0))
    return pl.pallas_call(
        functools.partial(expert_grad_kernel, hidden, pieces, per),
        grid=(3, rows // tile),
        in_specs=[pair_spec] + [piece_spec(k) for k in range(pieces)] + [down_spec] * 2,
        out_specs=pl.BlockSpec((1, tile, hidden), lambda w, i: (w, i, 0)),
        out_shape=jax.ShapeDtypeStruct((3, rows, hidden), full),
        compiler_params=limits(40),
        cost_estimate=cost(rows * padded * 3, rows * padded * 24),
        name="expert_grad_sum",
    )(*pair, *down)


def near_blocks(own, *others):
    held = [own]
    for bit in range(levels_of(lax.axis_size("tensor")))[::-1]:
        theirs = [swap(v, "tensor", 1 << bit) for v in held]
        if bit and others:
            theirs = [after(v, *others) for v in theirs]
        held = [v for pair in zip(held, theirs) for v in pair]
    return held


def near_reduce(even, odd, meet, *others, filler=None):
    count = lax.axis_size("tensor")
    number = count // 2
    size = even.shape[1] // number
    came = swap(odd, "tensor", 1)
    for bit in range(1, levels_of(count)):
        blocks = [
            even[:, i * size : (i + 1) * size].astype(full)
            + came[:, i * size : (i + 1) * size].astype(full)
            for i in range(number)
        ]
        sent = jnp.concatenate([v.astype(low) for v in blocks[1::2]], 1)
        if bit == levels_of(count) - 1:
            sent = after(sent, *others)
            meet.append(sent)
        even = jnp.concatenate(blocks[::2], 1)
        came = swap(sent, "tensor", 1 << bit)
        if filler is not None and bit == levels_of(count) - 1:
            came = after(came, *filler(sent))
        number //= 2
    return even.astype(full) + came.astype(full)


def half_gather(local, group_count):
    held = local
    place = lax.axis_index("dp") % group_count
    for bit in range(levels_of(group_count) - 1):
        came = swap(held, "dp", 1 << bit)
        upper = side_of(place, bit)
        held = jnp.concatenate([jnp.where(upper, came, held), jnp.where(upper, held, came)], 0)
    return held


def group_finish(kept, came, position, group_count):
    if group_count > 2:
        came = jnp.concatenate(came, 0)
    for bit in range(levels_of(group_count) - 1)[::-1]:
        current = kept.astype(full) + came.astype(full)
        middle = current.shape[0] // 2
        upper = (position >> bit) & 1
        kept = lax.dynamic_slice_in_dim(current, upper * middle, middle, 0)
        given = lax.dynamic_slice_in_dim(current, (1 - upper) * middle, middle, 0)
        came = swap(given.astype(low), "dp", 1 << bit)
    return [kept, *came] if isinstance(came, list) else [kept, came]


def body(
    tokens,
    attn_gain,
    qkv_weight,
    out_weight,
    moe_gain,
    router_weight,
    expert_weight,
    routes,
    cotangent,
):
    rows = tokens.shape[0]
    width = tokens.shape[1]
    tensor_count = lax.axis_size("tensor")
    dp_count = lax.axis_size("dp")
    group_count = dp_count // EXPERTS
    size = width // tensor_count
    hidden_size = expert_weight.shape[2]
    padded = -(-hidden_size // 128) * 128
    scale = 1.0 / math.sqrt(HEAD)
    place = lax.axis_index("tensor")
    index = lax.axis_index("dp")
    expert = index // group_count
    member = index % group_count
    top_half = member >> (levels_of(group_count) - 1)
    where = jnp.stack([place, top_half, expert]).astype(jnp.int32)

    def own_columns(value):
        return lax.dynamic_slice_in_dim(value, place * size, size, 1)

    extras = jnp.concatenate([router_weight, attn_gain[:, None], moe_gain[:, None]], 1)
    extras = jnp.pad(extras, ((0, 0), (0, 128 - extras.shape[1])))
    first = lax.all_gather(
        jnp.concatenate([qkv_weight.reshape(-1, 3 * size), out_weight, extras], 1),
        "dp",
        axis=0,
        tiled=True,
    )
    qkv_flat = first[:, : 3 * size]
    out_full = first[:, 3 * size : 4 * size]
    small = first[:, 4 * size :].T
    router_full = small[:EXPERTS]
    gain_first = small[EXPERTS : EXPERTS + 1].astype(full)
    gain_second = small[EXPERTS + 1 : EXPERTS + 2].astype(full)
    gain_first_own = own_columns(gain_first)
    gain_second_own = own_columns(gain_second)
    router_own = own_columns(router_full)

    near = jnp.arange(EXPERTS, dtype=jnp.int32) ^ expert
    names = jnp.arange(EXPERTS, dtype=jnp.int32)
    hits = jnp.sum((routes.T[None] == names[:, None, None]).astype(jnp.int32), 1)
    rank = jnp.cumsum(hits, axis=1) - hits
    slot_near = jnp.take(jnp.where(hits > 0, rank, -1), near, axis=0)
    places = jnp.arange(MOST, dtype=jnp.int32)[:, None]
    chosen = [(places == slot_near[s][None, :]).astype(low) for s in range(EXPERTS)]

    def packed(own):
        return [jnp.dot(c, own, preferred_element_type=full).astype(low) for c in chosen]

    def exchange(parts):
        return [parts[0]] + [swap(parts[s], "dp", s * group_count) for s in range(1, EXPERTS)]

    def unpacked(parts):
        total = contract(chosen[0], parts[0], 0, 0)
        for c, part in zip(chosen[1:], parts[1:]):
            total = total + contract(c, part, 0, 0)
        return total

    def widened(value):
        return jnp.pad(value, ((0, 0), (0, padded - hidden_size)))

    gate_mine, up_mine, down_mine = [
        half_gather(widened(expert_weight[k]), group_count) for k in range(3)
    ]
    half = width // 2
    mine_at, given_at = top_half * half, (1 - top_half) * half
    reach = group_count // 2

    def group_send(given, *others):
        return swap(after(given, *others), "dp", reach)

    down = (down_mine, group_send(down_mine))
    crossing = []

    def cross(*others):
        pieces = [
            (gate_mine, up_mine)[which][start * half // 128 : stop * half // 128]
            for which, start, stop in cuts[len(crossing)]
        ]
        crossing.append(group_send(jnp.concatenate(pieces, 0), *crossing[-1:], *others))

    cross(first)

    grad_own = own_columns(cotangent)
    grad_mine = jnp.dot(chosen[0], cotangent, preferred_element_type=full).astype(low)
    planes = [
        [m + g * group_count for g in range(EXPERTS)] for m in range(group_count)
    ]
    grad_planes = lax.all_gather(
        after(grad_own, first), "dp", axis=0, tiled=True, axis_index_groups=planes
    )
    slots_came = exchange([slot_near[s][None].astype(full) for s in range(EXPERTS)])
    route_sums = jnp.sum(routes, axis=1)[None].astype(low)
    routed = exchange([contract(route_sums, c, 1, 1) for c in chosen])

    inputs = tokens.astype(full)
    scale_one = lax.rsqrt(jnp.mean(inputs * inputs, axis=1, keepdims=True) + epsilon)
    normed_in = (inputs * scale_one * gain_first).astype(low)
    inputs_own = own_columns(tokens).astype(full)
    normed_in = after(normed_in, down[1], grad_mine, *slots_came, *routed)
    qkv = jnp.dot(normed_in, qkv_flat, preferred_element_type=full)
    cross(qkv)
    cosine, sine = rotary_tables()
    context, query, keys, values, logs = attention(qkv, cosine, sine, scale)
    context = after(context, crossing[1])
    cross(context)
    attn_parts = spread_dot(where, context, first, 3, tensor_count)
    rows_raw = []

    total = EXPERTS * MOST

    def down_filler(sent):
        cross(sent)
        rows_raw.extend(down_pass(where, after(grad_mine, sent), *down, 0, total, ()))
        return (rows_raw[1], crossing[3])

    hidden = inputs_own + near_reduce(*attn_parts, [], crossing[2], filler=down_filler)
    cross(rows_raw[1])
    grad_planes = after(grad_planes, hidden)
    grad_packed = []
    for s in order[1:]:
        source = lax.dynamic_slice_in_dim(grad_planes, (expert ^ s) * rows, rows, 0)
        taken = (places.astype(full) == slots_came[s]).astype(low)
        grad_packed.append(jnp.dot(taken, source, preferred_element_type=full).astype(low))
    grad_rest = lax.all_gather(jnp.concatenate(grad_packed, 0), "tensor", axis=1, tiled=True)

    scaled_hidden = (hidden * gain_second_own).astype(low)
    sums = tensor_sum(
        jnp.concatenate(
            [contract(router_own, scaled_hidden, 1, 1), jnp.sum(hidden * hidden, 1)[None]], 0
        )
    )
    scale_two_row = lax.rsqrt(sums[EXPERTS:] / width + epsilon)
    scale_two = scale_two_row.reshape(rows, 1)
    logits = sums[:EXPERTS] * scale_two_row
    normed_two = hidden * scale_two
    moe_in = (normed_two * gain_second_own).astype(low)
    named = hits > 0
    top = jnp.max(jnp.where(named, logits, masked_out), axis=0, keepdims=True)
    weight = jnp.where(named, jnp.exp(logits - top), 0.0)
    gates = weight / jnp.sum(weight, axis=0, keepdims=True)

    def three_parts(value):
        a = value.astype(low)
        b = (value - a.astype(full)).astype(low)
        return jnp.stack([a, b, (value - a.astype(full) - b.astype(full)).astype(low)])

    moe_packed = packed(moe_in)
    pair = (gate_mine, up_mine, *crossing)
    crossed = {2: swap(moe_packed[2], "dp", 2 * group_count)}
    crossed[3] = swap(after(moe_packed[3], crossed[2]), "dp", 3 * group_count)
    arrived = [near_blocks(moe_packed[0])]

    carried = ()
    sums_sent = []
    came_home = {}
    returned = []
    gate_grads = []
    router_block = first[:, 4 * size :]
    for step in range(EXPERTS):
        named_sum = routed[order[step]]
        if step == 1:
            rows_raw = down_pass(where, after(grad_rest, even), *down, MOST, total, rows_raw)
            named_sum = after(named_sum, crossed[3])
        if step == 2:
            named_sum = after(named_sum, crossed[1], sums_sent[0])
        if step == 3:
            named_sum = after(named_sum, sums_sent[1])
        moe_rows, activation, pre_grad, even, odd, gate_grad = expert_pass(
            step, where, arrived[step], pair, rows_raw[1], named_sum, router_block, carried
        )
        carried = (moe_rows, activation, pre_grad)
        if step == 0:
            arrived.append(near_blocks(crossed[2], even))
            crossed[3] = after(crossed[3], even)
            crossed[1] = swap(after(moe_packed[1], crossed[3]), "dp", group_count)
        if step == 1:
            arrived.append(near_blocks(crossed[3], even))
            odd = after(odd, crossed[1], arrived[2][tensor_count // 2])
        if step == 2:
            arrived.append(near_blocks(crossed[1], even))
        if step == 2:
            odd = after(odd, *returned, arrived[3][tensor_count // 2])
        if step == 3:
            came_home[2] = swap(returned[0], "dp", 2 * group_count)
            odd = after(odd, returned[1], came_home[2])
        if step == 0:
            own_parts = (even, odd)
        else:
            returned.append(near_reduce(even, odd, sums_sent).astype(low))
        gate_grads.append(gate_grad)

    def home(parts):
        return {
            s: swap(v, "dp", s * group_count) if s else v for s, v in zip(order, parts)
        }

    came_home[3] = swap(returned[1], "dp", 3 * group_count)
    came_home[1] = swap(returned[2], "dp", group_count)
    own_even, own_odd = own_parts
    came_home[0] = near_reduce(own_even, after(own_odd, sums_sent[2]), []).astype(low)
    gate_grad_near = home([gate_grads[0]] + [after(v, even) for v in gate_grads[1:]])
    grad_rows = rows_raw[0]

    def term(left, right):
        def part(start, number):
            taken = lax.dynamic_slice_in_dim(left, start, number, 1)
            return contract(taken, right, 0, 0).astype(low)

        return part

    unit = half // 128
    quarter = half // 2
    expert_part = up_pass(where, after(activation, sums_sent[2], returned[1]), *down)
    expert_part = after(expert_part, returned[2], came_home[3])
    expert_own = lax.psum_scatter(expert_part, "tensor", scatter_dimension=1, tiled=True)
    act_late = after(activation, expert_part, *gate_grad_near.values())
    down_given = term(grad_rows, act_late)(given_at, half)
    came_home = {s: after(v, down_given) for s, v in came_home.items()}
    back = unpacked([came_home[s] for s in range(EXPERTS)])

    gate_grad = jnp.concatenate(
        [
            jnp.sum(contract(three_parts(gate_grad_near[s][0]), chosen[s], 1, 0), 0, keepdims=True)
            for s in range(EXPERTS)
        ],
        0,
    )
    scaled_back = back * gain_second_own
    sums = tensor_sum(
        jnp.concatenate([gate_grad, jnp.sum(scaled_back * normed_two, axis=1)[None]], 0)
    )
    gate_grad = jnp.take(sums[:EXPERTS], near, axis=0)
    weighted = jnp.sum(gates * gate_grad, axis=0, keepdims=True)
    logit_grad = (gates * (gate_grad - weighted)).astype(low)
    mean_two = (
        sums[EXPERTS:] + jnp.sum(logit_grad.astype(full) * logits, axis=0, keepdims=True)
    ) / width
    moe_grad = contract(logit_grad, router_own, 0, 0) + back

    grad_out = grad_own.astype(full)
    hidden_grad = grad_out + scale_two * (
        moe_grad * gain_second_own - normed_two * mean_two.reshape(rows, 1)
    )
    router_grad = jnp.dot(logit_grad, moe_in, preferred_element_type=full)
    moe_gain_grad = jnp.sum(moe_grad * normed_two, axis=0)
    pair_given = []
    down_sums = []
    kept = []

    def give_pair(sent):
        down_sums.append(group_send(down_given[: 56 * unit], sent))
        pair_term = term(moe_rows, after(pre_grad, sent))
        pair_given.extend(pair_term(given_at + k * quarter, quarter) for k in range(2))
        return (*pair_given, down_sums[0])

    attn_grad = tensor_gather(hidden_grad.astype(low), give_pair)
    down_sums.append(group_send(down_given[56 * unit : 96 * unit], down_sums[0], *pair_given))
    context_grad = jnp.dot(attn_grad, out_full, preferred_element_type=full).astype(low)
    out_grad = contract(after(attn_grad, context_grad), context, 0, 0).astype(low)
    out_shard = lax.psum_scatter(out_grad, "dp", scatter_dimension=0, tiled=True).astype(full)
    outputs = {0: expert_own[:MOST]}
    part = after(expert_own[MOST : 2 * MOST], context_grad)
    outputs[2] = swap(part, "dp", 2 * group_count)
    context_grad = after(context_grad, out_grad)
    qkv_grad_rows = attention_back(query, keys, values, logs, context_grad, cosine, sine, scale)
    qkv_grad_rows = after(qkv_grad_rows, down_sums[1])
    qkv_grad = contract(normed_in, qkv_grad_rows, 0, 0).astype(low)
    qkv_shard = lax.psum_scatter(qkv_grad, "dp", scatter_dimension=0, tiled=True).astype(full)
    down_sums.append(group_send(down_given[96 * unit :], down_sums[1], qkv_grad))
    pair_sums = [group_send(v, down_sums[2]) for v in pair_given]
    for k in (2, 3):
        part = after(expert_own[k * MOST : (k + 1) * MOST], outputs[2])
        outputs[order[k]] = swap(part, "dp", order[k] * group_count)

    def keep(sent):
        kept.append(term(moe_rows, after(pre_grad, sent))(mine_at, half))
        kept.append(term(grad_rows, after(activation, kept[0]))(mine_at, half))
        return (*kept, outputs[3], outputs[1])

    parts = spread_dot(
        where, after(qkv_grad_rows, qkv_grad, outputs[2]), first, 0, tensor_count
    )
    normed_grad = near_reduce(*parts, [], filler=keep)
    normed_one = inputs_own * scale_one
    scaled_in = normed_grad * gain_first_own
    attn_gain_grad = jnp.sum(normed_grad * normed_one, axis=0)
    mean_one = tensor_sum(jnp.sum(scaled_in * normed_one, axis=1)[None]) / width
    input_own = hidden_grad + scale_one * (scaled_in - normed_one * mean_one.reshape(rows, 1))
    mine = jnp.concatenate([router_grad, attn_gain_grad[None], moe_gain_grad[None]], 0)
    mine = lax.dynamic_update_slice_in_dim(
        jnp.zeros((mine.shape[0], width), full), mine, place * size, 1
    )
    mine = all_sum(mine)
    expert_grad = expert_grad_sum(
        group_finish(kept[0], pair_sums, member, group_count),
        group_finish(kept[1], [jnp.concatenate(down_sums, 0)], member, group_count),
        hidden_size,
    )
    input_grad = tensor_gather(input_own.astype(low), lambda sent: (mine,))
    input_grad = input_grad.astype(full)
    layer_own = hidden + unpacked([outputs[s] for s in range(EXPERTS)])
    layer_out = tensor_gather(layer_own.astype(low)).astype(full)
    share = width // dp_count
    mine = lax.dynamic_slice_in_dim(mine, index * share, share, 1)
    return (
        layer_out,
        input_grad,
        mine[EXPERTS],
        qkv_shard.reshape(share, 3, size),
        out_shard,
        mine[EXPERTS + 1],
        mine[:EXPERTS].T,
        expert_grad,
    )


def solution(mesh):
    placed = (
        P("dp", None),
        P("dp"),
        P("dp", None, "tensor"),
        P("dp", "tensor"),
        P("dp"),
        P("dp", None),
        P(None, "dp", "tensor"),
        P("dp", None),
        P("dp", None),
    )
    return jax.shard_map(
        body,
        mesh=mesh,
        in_specs=placed,
        out_specs=(
            P("dp", None),
            P("dp", None),
            P("dp"),
            P("dp", None, "tensor"),
            P("dp", "tensor"),
            P("dp"),
            P("dp", None),
            P(None, "dp", "tensor"),
        ),
        check_vma=False,
    )
```

```python
import functools
import math

import jax
import jax.numpy as jnp
from jax import lax
from jax.experimental import pallas as pl
from jax.experimental.pallas import tpu as pltpu
from jax.sharding import PartitionSpec as P

HEAD = 128
EXPERTS = 4
SEQ = 1024
BLOCK = 256
MOST = 768


epsilon = 1e-05
theta_base = 10000.0
masked_out = -1e30
low = jnp.bfloat16
full = jnp.float32


def swap(value, axis, distance):
    return lax.ppermute(value, axis, [(i, i ^ distance) for i in range(lax.axis_size(axis))])


def contract(left, right, left_dim, right_dim):
    return lax.dot_general(
        left, right, (((left_dim,), (right_dim,)), ((), ())), preferred_element_type=jnp.float32
    )


def levels_of(count):
    return count.bit_length() - 1


def side_of(index, bit):
    return (index >> bit) & 1 == 1


def tensor_sum(value):
    for bit in range(levels_of(lax.axis_size("tensor"))):
        value = value + swap(value, "tensor", 1 << bit)
    return value


def all_sum(value):
    for axis in ("tensor", "dp"):
        for bit in range(levels_of(lax.axis_size(axis))):
            value = value + swap(value, axis, 1 << bit)
    return value


def tensor_gather(own, filler=None):
    count = lax.axis_size("tensor")
    place = lax.axis_index("tensor")
    size = own.shape[1]
    held = own
    order = list(range(levels_of(count)))[::-1]
    for bit in order:
        came = swap(held, "tensor", 1 << bit)
        if filler is not None and bit == order[0]:
            came = after(came, *filler(held))
        upper = side_of(place, bit)
        number = held.shape[1] // size
        mine = [held[:, i * size : (i + 1) * size] for i in range(number)]
        theirs = [came[:, i * size : (i + 1) * size] for i in range(number)]
        pairs = []
        for a, b in zip(mine, theirs):
            pairs.append((jnp.where(upper, b, a), jnp.where(upper, a, b)))
        held = jnp.concatenate([v for pair in pairs for v in pair], 1)
    return held


def after(value, *others):
    return lax.optimization_barrier((value, *others))[0]


def rotary_tables():
    half = HEAD // 2
    freqs = theta_base ** (-(jnp.arange(half, dtype=full) * 2.0 / HEAD))
    angles = jnp.arange(SEQ, dtype=full)[:, None] * freqs[None, :]
    cosine = jnp.cos(angles)
    sine = jnp.sin(angles)
    return (jnp.concatenate([cosine, cosine], 1), jnp.concatenate([-sine, sine], 1))


def limits(mib):
    return pltpu.CompilerParams(vmem_limit_bytes=mib << 20)


def cost(flops, moved, powers=0):
    return pl.CostEstimate(flops=int(flops), bytes_accessed=int(moved), transcendentals=int(powers))


def dot_cols(a, b):
    return lax.dot_general(a, b, (((1,), (1,)), ((), ())), preferred_element_type=full)


def dot_rows(a, b):
    return lax.dot_general(a, b, (((0,), (0,)), ((), ())), preferred_element_type=full)


def attention_kernel(scale, q_in, k_in, v_in, cos, sin, out, q_out, k_out, v_out, logs):
    def turned(ref):
        x = ref[...]
        return (x * cos[...] + pltpu.roll(x, HEAD // 2, 1) * sin[...]).astype(low)

    q_out[...] = turned(q_in)
    k_out[...] = turned(k_in)
    v_out[...] = v_in[...].astype(low)
    for block in range(SEQ // BLOCK):
        mine = pl.ds(block * BLOCK, BLOCK)
        seen = pl.ds(0, (block + 1) * BLOCK)
        scores = dot_cols(q_out[mine, :], k_out[seen, :]) * scale
        peak = jnp.max(scores, axis=1, keepdims=True)
        expo = jnp.exp(scores - peak)
        total = jnp.sum(expo, axis=1, keepdims=True)
        probs = (expo / total).astype(low)
        out[mine, :] = jnp.dot(probs, v_out[seen, :], preferred_element_type=full).astype(low)
        logs[0, mine, :] = peak + jnp.log(total)


def attention(qkv, cosine, sine, scale):
    rows = qkv.shape[0]
    size = qkv.shape[1] // 3
    heads = size // HEAD
    block = (SEQ, HEAD)
    table = pl.BlockSpec(block, lambda s, h: (0, 0))
    spec = pl.BlockSpec(block, lambda s, h: (s, h))
    shape = jax.ShapeDtypeStruct((rows, size), low)
    pairs = rows * heads * SEQ * 5 // 8
    return pl.pallas_call(
        functools.partial(attention_kernel, scale),
        grid=(rows // SEQ, heads),
        in_specs=[
            pl.BlockSpec(block, lambda s, h: (s, h)),
            pl.BlockSpec(block, lambda s, h: (s, heads + h)),
            pl.BlockSpec(block, lambda s, h: (s, 2 * heads + h)),
            table,
            table,
        ],
        out_specs=[spec] * 4 + [pl.BlockSpec((1, SEQ, 1), lambda s, h: (h, s, 0))],
        out_shape=[shape] * 4 + [jax.ShapeDtypeStruct((heads, rows, 1), full)],
        compiler_params=limits(48),
        cost_estimate=cost(4 * pairs * HEAD, rows * size * 20, pairs),
        name="attention",
    )(qkv, qkv, qkv, cosine, sine)


def attention_back_kernel(scale, heads, q_in, k_in, v_in, logs, grad, cos, sin, out, dk, dv):
    head = pl.program_id(1)
    dk[...] = jnp.zeros_like(dk)
    dv[...] = jnp.zeros_like(dv)

    def columns(which):
        return pl.ds(pl.multiple_of((which * heads + head) * HEAD, HEAD), HEAD)

    def turned(x, at):
        return (x * cos[at, :] - pltpu.roll(x, HEAD // 2, 1) * sin[at, :]).astype(low)

    for block in range(SEQ // BLOCK):
        mine = pl.ds(block * BLOCK, BLOCK)
        seen = pl.ds(0, (block + 1) * BLOCK)
        query, keys, values, given = q_in[mine, :], k_in[seen, :], v_in[seen, :], grad[mine, :]
        probs = jnp.exp(dot_cols(query, keys) * scale - logs[0, mine, :])
        prob_grad = dot_cols(given, values)
        inner = jnp.sum(probs * prob_grad, axis=1, keepdims=True)
        score_grad = (probs * (prob_grad - inner)).astype(low)
        query_grad = jnp.dot(score_grad, keys, preferred_element_type=full) * scale
        out[mine, columns(0)] = turned(query_grad, mine)
        dk[seen, :] += dot_rows(score_grad, query)
        dv[seen, :] += dot_rows(probs.astype(low), given)
    whole = pl.ds(0, SEQ)
    out[:, columns(1)] = turned(dk[...] * scale, whole)
    out[:, columns(2)] = dv[...].astype(low)


def attention_back(query, keys, values, logs, grad, cosine, sine, scale):
    rows, size = query.shape
    heads = size // HEAD
    block = (SEQ, HEAD)
    table = pl.BlockSpec(block, lambda s, h: (0, 0))
    spec = pl.BlockSpec(block, lambda s, h: (s, h))
    pairs = rows * heads * SEQ * 5 // 8
    return pl.pallas_call(
        functools.partial(attention_back_kernel, scale, heads),
        grid=(rows // SEQ, heads),
        in_specs=[spec] * 3
        + [pl.BlockSpec((1, SEQ, 1), lambda s, h: (h, s, 0)), spec, table, table],
        out_specs=pl.BlockSpec((SEQ, 3 * size), lambda s, h: (s, 0)),
        out_shape=jax.ShapeDtypeStruct((rows, 3 * size), low),
        scratch_shapes=[pltpu.VMEM(block, full)] * 2,
        compiler_params=limits(48),
        cost_estimate=cost(10 * pairs * HEAD, rows * size * 16, pairs),
        name="attention_back",
    )(query, keys, values, logs, grad, cosine, sine)


def place_rows(pieces, held, sems, upper, first):
    copies = []
    for ref, start, number, mine, there, column in pieces:
        half = held.shape[0] // 2
        columns = ref.shape[1]
        side = upper if mine else 1 - upper
        copies.append(
            pltpu.make_async_copy(
                ref.at[pl.ds(start, number), :],
                held.at[
                    pl.ds(pl.multiple_of(side * half + there, 64), number),
                    pl.ds(column * columns, columns),
                ],
                sems.at[len(copies)],
            )
        )

    @pl.when(first)
    def _():
        for copy in copies:
            copy.start()
        for copy in copies:
            copy.wait()


def down_pieces(own, came):
    half = own.shape[0]
    return [(own, 0, half, True, 0, 0), (came, 0, half, False, 0, 0)]


cuts = (
    ((0, 0, 16),),
    ((0, 16, 40),),
    ((0, 40, 56),),
    ((0, 56, 108),),
    ((0, 108, 128), (1, 0, 128)),
)
order = (0, 2, 3, 1)


def pair_pieces(own_gate, own_up, *came):
    half = own_gate.shape[0]
    pieces = [(own_gate, 0, half, True, 0, 0), (own_up, 0, half, True, 0, 1)]
    for cut, ref in zip(cuts, came):
        at = 0
        for which, start, stop in cut:
            number = (stop - start) * half // 128
            pieces.append((ref, at, number, False, start * half // 128, which))
            at += number
    return pieces


def column_block(where, i, size):
    return pl.ds(pl.multiple_of((i ^ where[0]) * size, size), size)


def down_kernel(carried, where, rows, own, came, *refs):
    rows_out, raw, held, sems = refs[carried:]
    place_rows(down_pieces(own, came), held, sems, where[1], pl.program_id(0) == 0)
    rows_out[...] = rows[...]
    raw[...] = jnp.dot(rows[...], held[...], preferred_element_type=full).astype(low)


def down_pass(where, rows, own, came, start, total, carried):
    number, width = rows.shape
    hidden = own.shape[1]
    tile = 256
    first = start // tile
    anywhere = pl.BlockSpec(memory_space=pl.ANY)
    here = lambda columns: pl.BlockSpec((tile, columns), lambda i, where: (first + i, 0))
    return pl.pallas_call(
        functools.partial(down_kernel, len(carried)),
        grid_spec=pltpu.PrefetchScalarGridSpec(
            num_scalar_prefetch=1,
            grid=(number // tile,),
            in_specs=[pl.BlockSpec((tile, width), lambda i, where: (i, 0))]
            + [anywhere] * (2 + len(carried)),
            out_specs=[here(width), here(hidden)],
            scratch_shapes=[pltpu.VMEM((width, hidden), low), pltpu.SemaphoreType.DMA((2,))],
        ),
        out_shape=[
            jax.ShapeDtypeStruct((total, width), low),
            jax.ShapeDtypeStruct((total, hidden), low),
        ],
        input_output_aliases={4 + i: i for i in range(len(carried))},
        compiler_params=limits(48),
        cost_estimate=cost(
            2 * number * width * hidden, (number * (2 * width + hidden) + width * hidden) * 2
        ),
        name="down",
    )(where, rows, own, came, *carried)


def spread_kernel(count, where, left, right, even, odd, part):
    size = part.shape[1] // count
    part[...] = dot_cols(left[...], right[...]).astype(low)
    for i in range(count):
        (odd if i % 2 else even)[:, i // 2 * size : (i // 2 + 1) * size] = part[
            :, column_block(where, i, size)
        ]


def spread_dot(where, left, right, column, count):
    rows, depth = left.shape
    width = right.shape[0]
    tile = 256
    spec = lambda columns: pl.BlockSpec((tile, columns), lambda i, where: (i, 0))
    half = jax.ShapeDtypeStruct((rows, width // 2), low)
    return pl.pallas_call(
        functools.partial(spread_kernel, count),
        grid_spec=pltpu.PrefetchScalarGridSpec(
            num_scalar_prefetch=1,
            grid=(rows // tile,),
            in_specs=[
                spec(depth),
                pl.BlockSpec((width, depth), lambda i, where: (0, column)),
            ],
            out_specs=[spec(width // 2)] * 2,
            scratch_shapes=[pltpu.VMEM((tile, width), low)],
        ),
        out_shape=[half, half],
        compiler_params=limits(48),
        cost_estimate=cost(2 * rows * width * depth, (rows * (width + depth) + width * depth) * 2),
        name="spread",
    )(where, left, right)


def up_kernel(where, act, own, came, out, held, sems):
    place_rows(down_pieces(own, came), held, sems, where[1], pl.program_id(0) == 0)
    out[...] = dot_cols(act[...], held[...]).astype(low)


def up_pass(where, act, own, came):
    total, hidden = act.shape
    width = 2 * own.shape[0]
    tile = 256
    spec = lambda columns: pl.BlockSpec((tile, columns), lambda i, where: (i, 0))
    return pl.pallas_call(
        up_kernel,
        grid_spec=pltpu.PrefetchScalarGridSpec(
            num_scalar_prefetch=1,
            grid=(total // tile,),
            in_specs=[spec(hidden)] + [pl.BlockSpec(memory_space=pl.ANY)] * 2,
            out_specs=spec(width),
            scratch_shapes=[pltpu.VMEM((width, hidden), low), pltpu.SemaphoreType.DMA((2,))],
        ),
        out_shape=jax.ShapeDtypeStruct((total, width), low),
        compiler_params=limits(48),
        cost_estimate=cost(
            2 * total * width * hidden, (total * (width + hidden) + width * hidden) * 2
        ),
        name="up",
    )(where, act, own, came)


def expert_kernel(count, carried, where, *refs):
    blocks, refs = refs[:count], refs[count:]
    number = 2 + len(cuts)
    weights, (raw, routed, router) = refs[:number], refs[number : number + 3]
    rows_out, act_out, grad_out, even, odd, gate_grad, pair, part, sems = refs[
        number + 3 + carried :
    ]
    size = blocks[0].shape[1]
    hidden = raw.shape[1]
    place_rows(pair_pieces(*weights), pair, sems, where[1], pl.program_id(0) == 0)
    for i, ref in enumerate(blocks):
        rows_out[:, column_block(where, i, size)] = ref[...]
    both = jnp.dot(rows_out[...], pair[...], preferred_element_type=full)
    pre_gate = both[:, :hidden]
    pre_up = both[:, hidden:]
    sigma = 1.0 / (1.0 + jnp.exp(-pre_gate))
    silu = pre_gate * sigma
    act = silu * pre_up
    back = raw[...].astype(full)
    tile = back.shape[0]
    own = where[2].astype(full)
    other = jnp.broadcast_to(routed[...], (128, tile)).T - own
    logits = jnp.dot(rows_out[...], router[...], preferred_element_type=full)
    lane = lax.broadcasted_iota(jnp.int32, (tile, 128), 1).astype(full)
    ahead = jnp.where(lane == other, logits, 0.0) - jnp.where(lane == own, logits, 0.0)
    gate = 1.0 / (1.0 + jnp.exp(jnp.sum(ahead, axis=1, keepdims=True)))
    gate_sum = jnp.sum(act * back, axis=1, keepdims=True)
    gate_grad[...] = jnp.broadcast_to(gate_sum, (tile, 128)).T[:1]
    act_out[...] = (act * gate).astype(low)
    back = back * gate
    grad_out[:, :hidden] = (back * pre_up * sigma * (1.0 + pre_gate * (1.0 - sigma))).astype(low)
    grad_out[:, hidden:] = (back * silu).astype(low)
    part[...] = dot_cols(grad_out[...], pair[...]).astype(low)
    for i in range(count):
        (odd if i % 2 else even)[:, i // 2 * size : (i // 2 + 1) * size] = part[
            :, column_block(where, i, size)
        ]


def expert_pass(step, where, blocks, weights, raw, routed, router, carried):
    count = len(blocks)
    size = blocks[0].shape[1]
    width, hidden = 2 * weights[0].shape[0], weights[0].shape[1]
    both = 2 * hidden
    total = raw.shape[0]
    tile = 256
    steps = MOST // tile
    here = lambda i, where: (step * steps + i, 0)
    near = lambda i, where: (i, 0)
    near_spec = lambda columns: pl.BlockSpec((tile, columns), near)
    here_spec = lambda columns: pl.BlockSpec((tile, columns), here)
    row_spec = pl.BlockSpec((1, tile), lambda i, where: (0, i))
    anywhere = pl.BlockSpec(memory_space=pl.ANY)
    shape = lambda r, c, t=low: jax.ShapeDtypeStruct((r, c), t)
    return pl.pallas_call(
        functools.partial(expert_kernel, count, len(carried)),
        grid_spec=pltpu.PrefetchScalarGridSpec(
            num_scalar_prefetch=1,
            grid=(steps,),
            in_specs=[near_spec(size)] * count
            + [anywhere] * len(weights)
            + [
                here_spec(hidden),
                row_spec,
                pl.BlockSpec((width, 128), lambda i, where: (0, 0)),
            ]
            + [anywhere] * len(carried),
            out_specs=[
                here_spec(width),
                here_spec(hidden),
                here_spec(both),
                near_spec(width // 2),
                near_spec(width // 2),
                row_spec,
            ],
            scratch_shapes=[
                pltpu.VMEM((width, both), low),
                pltpu.VMEM((tile, width), low),
                pltpu.SemaphoreType.DMA((2 + sum(len(cut) for cut in cuts),)),
            ],
        ),
        out_shape=[
            shape(total, width),
            shape(total, hidden),
            shape(total, both),
            shape(MOST, width // 2),
            shape(MOST, width // 2),
            shape(1, MOST, full),
        ],
        input_output_aliases={
            count + len(weights) + 4 + i: i for i in range(len(carried))
        },
        compiler_params=limits(60),
        cost_estimate=cost(
            4 * MOST * width * both, width * both * 2 + MOST * (width * 8 + hidden * 8), MOST * hidden
        ),
        name="expert",
    )(where, *blocks, *weights, raw, routed, router, *carried)


def expert_grad_kernel(hidden, pieces, per, *refs):
    out = refs[-1]
    which, at = pl.program_id(0), pl.program_id(1)

    def add(ref, other):
        out[0] = (ref[...].astype(full) + other[...].astype(full))[:, :hidden]

    for k in range(pieces):

        @pl.when((which < 2) & (at // per == k))
        def _():
            add(refs[0], refs[1 + k])

    @pl.when(which == 2)
    def _():
        add(refs[1 + pieces], refs[2 + pieces])


def expert_grad_sum(pair, down, hidden):
    rows, padded = down[0].shape
    tile = min(256, rows)
    pieces = len(pair) - 1
    per = rows // tile // pieces
    last = rows // tile - 1

    def piece_spec(k):
        return pl.BlockSpec(
            (tile, padded),
            lambda w, i: (
                jnp.where(w == 2, per - 1, jnp.clip(i - k * per, 0, per - 1)),
                jnp.minimum(w, 1),
            ),
        )

    pair_spec = pl.BlockSpec(
        (tile, padded), lambda w, i: (jnp.where(w == 2, last, i), jnp.minimum(w, 1))
    )
    down_spec = pl.BlockSpec((tile, padded), lambda w, i: (jnp.where(w == 2, i, 0), 0))
    return pl.pallas_call(
        functools.partial(expert_grad_kernel, hidden, pieces, per),
        grid=(3, rows // tile),
        in_specs=[pair_spec] + [piece_spec(k) for k in range(pieces)] + [down_spec] * 2,
        out_specs=pl.BlockSpec((1, tile, hidden), lambda w, i: (w, i, 0)),
        out_shape=jax.ShapeDtypeStruct((3, rows, hidden), full),
        compiler_params=limits(40),
        cost_estimate=cost(rows * padded * 3, rows * padded * 24),
        name="expert_grad_sum",
    )(*pair, *down)


def near_blocks(own, *others):
    held = [own]
    for bit in range(levels_of(lax.axis_size("tensor")))[::-1]:
        theirs = [swap(v, "tensor", 1 << bit) for v in held]
        if bit and others:
            theirs = [after(v, *others) for v in theirs]
        held = [v for pair in zip(held, theirs) for v in pair]
    return held


def near_reduce(even, odd, meet, *others, filler=None):
    count = lax.axis_size("tensor")
    number = count // 2
    size = even.shape[1] // number
    came = swap(odd, "tensor", 1)
    for bit in range(1, levels_of(count)):
        blocks = [
            even[:, i * size : (i + 1) * size].astype(full)
            + came[:, i * size : (i + 1) * size].astype(full)
            for i in range(number)
        ]
        sent = jnp.concatenate([v.astype(low) for v in blocks[1::2]], 1)
        if bit == levels_of(count) - 1:
            sent = after(sent, *others)
            meet.append(sent)
        even = jnp.concatenate(blocks[::2], 1)
        came = swap(sent, "tensor", 1 << bit)
        if filler is not None and bit == levels_of(count) - 1:
            came = after(came, *filler(sent))
        number //= 2
    return even.astype(full) + came.astype(full)


def half_gather(local, group_count):
    held = local
    place = lax.axis_index("dp") % group_count
    for bit in range(levels_of(group_count) - 1):
        came = swap(held, "dp", 1 << bit)
        upper = side_of(place, bit)
        held = jnp.concatenate([jnp.where(upper, came, held), jnp.where(upper, held, came)], 0)
    return held


def group_finish(kept, came, position, group_count):
    if group_count > 2:
        came = jnp.concatenate(came, 0)
    for bit in range(levels_of(group_count) - 1)[::-1]:
        current = kept.astype(full) + came.astype(full)
        middle = current.shape[0] // 2
        upper = (position >> bit) & 1
        kept = lax.dynamic_slice_in_dim(current, upper * middle, middle, 0)
        given = lax.dynamic_slice_in_dim(current, (1 - upper) * middle, middle, 0)
        came = swap(given.astype(low), "dp", 1 << bit)
    return [kept, *came] if isinstance(came, list) else [kept, came]


def body(
    tokens,
    attn_gain,
    qkv_weight,
    out_weight,
    moe_gain,
    router_weight,
    expert_weight,
    routes,
    cotangent,
):
    rows = tokens.shape[0]
    width = tokens.shape[1]
    tensor_count = lax.axis_size("tensor")
    dp_count = lax.axis_size("dp")
    group_count = dp_count // EXPERTS
    size = width // tensor_count
    hidden_size = expert_weight.shape[2]
    padded = -(-hidden_size // 128) * 128
    scale = 1.0 / math.sqrt(HEAD)
    place = lax.axis_index("tensor")
    index = lax.axis_index("dp")
    expert = index // group_count
    member = index % group_count
    top_half = member >> (levels_of(group_count) - 1)
    where = jnp.stack([place, top_half, expert]).astype(jnp.int32)

    def own_columns(value):
        return lax.dynamic_slice_in_dim(value, place * size, size, 1)

    extras = jnp.concatenate([router_weight, attn_gain[:, None], moe_gain[:, None]], 1)
    extras = jnp.pad(extras, ((0, 0), (0, 128 - extras.shape[1])))
    first = lax.all_gather(
        jnp.concatenate([qkv_weight.reshape(-1, 3 * size), out_weight, extras], 1),
        "dp",
        axis=0,
        tiled=True,
    )
    qkv_flat = first[:, : 3 * size]
    out_full = first[:, 3 * size : 4 * size]
    small = first[:, 4 * size :].T
    router_full = small[:EXPERTS]
    gain_first = small[EXPERTS : EXPERTS + 1].astype(full)
    gain_second = small[EXPERTS + 1 : EXPERTS + 2].astype(full)
    gain_first_own = own_columns(gain_first)
    gain_second_own = own_columns(gain_second)
    router_own = own_columns(router_full)

    near = jnp.arange(EXPERTS, dtype=jnp.int32) ^ expert
    names = jnp.arange(EXPERTS, dtype=jnp.int32)
    hits = jnp.sum((routes.T[None] == names[:, None, None]).astype(jnp.int32), 1)
    rank = jnp.cumsum(hits, axis=1) - hits
    slot_near = jnp.take(jnp.where(hits > 0, rank, -1), near, axis=0)
    places = jnp.arange(MOST, dtype=jnp.int32)[:, None]
    chosen = [(places == slot_near[s][None, :]).astype(low) for s in range(EXPERTS)]

    def packed(own):
        return [jnp.dot(c, own, preferred_element_type=full).astype(low) for c in chosen]

    def exchange(parts):
        return [parts[0]] + [swap(parts[s], "dp", s * group_count) for s in range(1, EXPERTS)]

    def unpacked(parts):
        total = contract(chosen[0], parts[0], 0, 0)
        for c, part in zip(chosen[1:], parts[1:]):
            total = total + contract(c, part, 0, 0)
        return total

    def widened(value):
        return jnp.pad(value, ((0, 0), (0, padded - hidden_size)))

    gate_mine, up_mine, down_mine = [
        half_gather(widened(expert_weight[k]), group_count) for k in range(3)
    ]
    half = width // 2
    mine_at, given_at = top_half * half, (1 - top_half) * half
    reach = group_count // 2

    def group_send(given, *others):
        return swap(after(given, *others), "dp", reach)

    down = (down_mine, group_send(down_mine))
    crossing = []

    def cross(*others):
        pieces = [
            (gate_mine, up_mine)[which][start * half // 128 : stop * half // 128]
            for which, start, stop in cuts[len(crossing)]
        ]
        crossing.append(group_send(jnp.concatenate(pieces, 0), *crossing[-1:], *others))

    cross(first)

    grad_own = own_columns(cotangent)
    grad_mine = jnp.dot(chosen[0], cotangent, preferred_element_type=full).astype(low)
    planes = [
        [m + g * group_count for g in range(EXPERTS)] for m in range(group_count)
    ]
    grad_planes = lax.all_gather(
        after(grad_own, first), "dp", axis=0, tiled=True, axis_index_groups=planes
    )
    slots_came = exchange([slot_near[s][None].astype(full) for s in range(EXPERTS)])
    route_sums = jnp.sum(routes, axis=1)[None].astype(low)
    routed = exchange([contract(route_sums, c, 1, 1) for c in chosen])

    inputs = tokens.astype(full)
    scale_one = lax.rsqrt(jnp.mean(inputs * inputs, axis=1, keepdims=True) + epsilon)
    normed_in = (inputs * scale_one * gain_first).astype(low)
    inputs_own = own_columns(tokens).astype(full)
    normed_in = after(normed_in, down[1], grad_mine, *slots_came, *routed)
    qkv = jnp.dot(normed_in, qkv_flat, preferred_element_type=full)
    cross(qkv)
    cosine, sine = rotary_tables()
    context, query, keys, values, logs = attention(qkv, cosine, sine, scale)
    context = after(context, crossing[1])
    cross(context)
    attn_parts = spread_dot(where, context, first, 3, tensor_count)
    rows_raw = []

    total = EXPERTS * MOST

    def down_filler(sent):
        cross(sent)
        rows_raw.extend(down_pass(where, after(grad_mine, sent), *down, 0, total, ()))
        return (rows_raw[1], crossing[3])

    hidden = inputs_own + near_reduce(*attn_parts, [], crossing[2], filler=down_filler)
    cross(rows_raw[1])
    grad_planes = after(grad_planes, hidden)
    grad_packed = []
    for s in order[1:]:
        source = lax.dynamic_slice_in_dim(grad_planes, (expert ^ s) * rows, rows, 0)
        taken = (places.astype(full) == slots_came[s]).astype(low)
        grad_packed.append(jnp.dot(taken, source, preferred_element_type=full).astype(low))
    grad_rest = lax.all_gather(jnp.concatenate(grad_packed, 0), "tensor", axis=1, tiled=True)

    scaled_hidden = (hidden * gain_second_own).astype(low)
    sums = tensor_sum(
        jnp.concatenate(
            [contract(router_own, scaled_hidden, 1, 1), jnp.sum(hidden * hidden, 1)[None]], 0
        )
    )
    scale_two_row = lax.rsqrt(sums[EXPERTS:] / width + epsilon)
    scale_two = scale_two_row.reshape(rows, 1)
    logits = sums[:EXPERTS] * scale_two_row
    normed_two = hidden * scale_two
    moe_in = (normed_two * gain_second_own).astype(low)
    named = hits > 0
    top = jnp.max(jnp.where(named, logits, masked_out), axis=0, keepdims=True)
    weight = jnp.where(named, jnp.exp(logits - top), 0.0)
    gates = weight / jnp.sum(weight, axis=0, keepdims=True)

    def three_parts(value):
        a = value.astype(low)
        b = (value - a.astype(full)).astype(low)
        return jnp.stack([a, b, (value - a.astype(full) - b.astype(full)).astype(low)])

    moe_packed = packed(moe_in)
    pair = (gate_mine, up_mine, *crossing)
    crossed = {2: swap(moe_packed[2], "dp", 2 * group_count)}
    crossed[3] = swap(after(moe_packed[3], crossed[2]), "dp", 3 * group_count)
    arrived = [near_blocks(moe_packed[0])]

    carried = ()
    sums_sent = []
    came_home = {}
    returned = []
    gate_grads = []
    router_block = first[:, 4 * size :]
    for step in range(EXPERTS):
        named_sum = routed[order[step]]
        if step == 1:
            rows_raw = down_pass(where, after(grad_rest, even), *down, MOST, total, rows_raw)
            named_sum = after(named_sum, crossed[3])
        if step == 2:
            named_sum = after(named_sum, crossed[1], sums_sent[0])
        if step == 3:
            named_sum = after(named_sum, sums_sent[1])
        moe_rows, activation, pre_grad, even, odd, gate_grad = expert_pass(
            step, where, arrived[step], pair, rows_raw[1], named_sum, router_block, carried
        )
        carried = (moe_rows, activation, pre_grad)
        if step == 0:
            arrived.append(near_blocks(crossed[2], even))
            crossed[3] = after(crossed[3], even)
            crossed[1] = swap(after(moe_packed[1], crossed[3]), "dp", group_count)
        if step == 1:
            arrived.append(near_blocks(crossed[3], even))
            odd = after(odd, crossed[1], arrived[2][tensor_count // 2])
        if step == 2:
            arrived.append(near_blocks(crossed[1], even))
        if step == 2:
            odd = after(odd, *returned, arrived[3][tensor_count // 2])
        if step == 3:
            came_home[2] = swap(returned[0], "dp", 2 * group_count)
            odd = after(odd, returned[1], came_home[2])
        if step == 0:
            own_parts = (even, odd)
        else:
            returned.append(near_reduce(even, odd, sums_sent).astype(low))
        gate_grads.append(gate_grad)

    def home(parts):
        return {
            s: swap(v, "dp", s * group_count) if s else v for s, v in zip(order, parts)
        }

    came_home[3] = swap(returned[1], "dp", 3 * group_count)
    came_home[1] = swap(returned[2], "dp", group_count)
    own_even, own_odd = own_parts
    came_home[0] = near_reduce(own_even, after(own_odd, sums_sent[2]), []).astype(low)
    gate_grad_near = home([gate_grads[0]] + [after(v, even) for v in gate_grads[1:]])
    grad_rows = rows_raw[0]

    def term(left, right):
        def part(start, number):
            taken = lax.dynamic_slice_in_dim(left, start, number, 1)
            return contract(taken, right, 0, 0).astype(low)

        return part

    unit = half // 128
    quarter = half // 2
    act_late = after(activation, sums_sent[2], returned[1])
    down_given = term(grad_rows, act_late)(given_at, half)
    down_sums = [group_send(down_given[: 56 * unit])]
    expert_part = up_pass(
        where, after(activation, down_given, returned[2], *gate_grad_near.values()), *down
    )
    expert_part = after(expert_part, down_sums[0], came_home[3], came_home[1])
    expert_own = lax.psum_scatter(expert_part, "tensor", scatter_dimension=1, tiled=True)
    down_sums.append(group_send(down_given[56 * unit :], down_sums[0], expert_part))
    pair_term = term(moe_rows, after(pre_grad, expert_part, came_home[0]))
    pair_given = [pair_term(given_at + k * quarter, quarter) for k in range(2)]
    came_home = {s: after(v, down_sums[1], *pair_given) for s, v in came_home.items()}
    back = unpacked([came_home[s] for s in range(EXPERTS)])

    gate_grad = jnp.concatenate(
        [
            jnp.sum(contract(three_parts(gate_grad_near[s][0]), chosen[s], 1, 0), 0, keepdims=True)
            for s in range(EXPERTS)
        ],
        0,
    )
    scaled_back = back * gain_second_own
    sums = tensor_sum(
        jnp.concatenate([gate_grad, jnp.sum(scaled_back * normed_two, axis=1)[None]], 0)
    )
    gate_grad = jnp.take(sums[:EXPERTS], near, axis=0)
    weighted = jnp.sum(gates * gate_grad, axis=0, keepdims=True)
    logit_grad = (gates * (gate_grad - weighted)).astype(low)
    mean_two = (
        sums[EXPERTS:] + jnp.sum(logit_grad.astype(full) * logits, axis=0, keepdims=True)
    ) / width
    moe_grad = contract(logit_grad, router_own, 0, 0) + back

    grad_out = grad_own.astype(full)
    hidden_grad = grad_out + scale_two * (
        moe_grad * gain_second_own - normed_two * mean_two.reshape(rows, 1)
    )
    router_grad = jnp.dot(logit_grad, moe_in, preferred_element_type=full)
    moe_gain_grad = jnp.sum(moe_grad * normed_two, axis=0)
    kept = []
    pair_sums = []

    def keep_pair(sent):
        pair_sums.append(group_send(pair_given[0][: 27 * unit], down_sums[1], sent))
        kept.append(term(moe_rows, after(pre_grad, sent))(mine_at, half))
        return (kept[0], pair_sums[0])

    attn_grad = tensor_gather(hidden_grad.astype(low), keep_pair)
    pair_sums.append(group_send(pair_given[0][27 * unit : 48 * unit], pair_sums[0], kept[0]))
    context_grad = jnp.dot(attn_grad, out_full, preferred_element_type=full).astype(low)
    out_grad = contract(after(attn_grad, context_grad), context, 0, 0).astype(low)
    out_shard = lax.psum_scatter(out_grad, "dp", scatter_dimension=0, tiled=True).astype(full)
    outputs = {0: expert_own[:MOST]}
    part = after(expert_own[MOST : 2 * MOST], context_grad)
    outputs[2] = swap(part, "dp", 2 * group_count)
    context_grad = after(context_grad, out_grad)
    qkv_grad_rows = attention_back(query, keys, values, logs, context_grad, cosine, sine, scale)
    qkv_grad_rows = after(qkv_grad_rows, pair_sums[1])
    qkv_grad = contract(normed_in, qkv_grad_rows, 0, 0).astype(low)
    qkv_shard = lax.psum_scatter(qkv_grad, "dp", scatter_dimension=0, tiled=True).astype(full)
    pair_sums.append(group_send(pair_given[0][48 * unit :], pair_sums[1], qkv_grad))
    pair_last = group_send(pair_given[1], pair_sums[1], qkv_grad)
    for k in (2, 3):
        part = after(expert_own[k * MOST : (k + 1) * MOST], outputs[2])
        outputs[order[k]] = swap(part, "dp", order[k] * group_count)

    def keep(sent):
        kept.append(term(grad_rows, after(activation, sent))(mine_at, half))
        return (kept[1], outputs[2], pair_sums[2])

    parts = spread_dot(
        where, after(qkv_grad_rows, qkv_grad), first, 0, tensor_count
    )
    normed_grad = near_reduce(*parts, [], filler=keep)
    normed_one = inputs_own * scale_one
    scaled_in = normed_grad * gain_first_own
    attn_gain_grad = jnp.sum(normed_grad * normed_one, axis=0)
    mean_one = tensor_sum(jnp.sum(scaled_in * normed_one, axis=1)[None]) / width
    input_own = hidden_grad + scale_one * (scaled_in - normed_one * mean_one.reshape(rows, 1))
    mine = jnp.concatenate([router_grad, attn_gain_grad[None], moe_gain_grad[None]], 0)
    mine = lax.dynamic_update_slice_in_dim(
        jnp.zeros((mine.shape[0], width), full), mine, place * size, 1
    )
    mine = all_sum(mine)
    expert_grad = expert_grad_sum(
        group_finish(kept[0], [jnp.concatenate(pair_sums, 0), pair_last], member, group_count),
        group_finish(kept[1], [jnp.concatenate(down_sums, 0)], member, group_count),
        hidden_size,
    )
    input_grad = tensor_gather(input_own.astype(low), lambda sent: (mine, outputs[3], outputs[1]))
    input_grad = input_grad.astype(full)
    layer_own = hidden + unpacked([outputs[s] for s in range(EXPERTS)])
    layer_out = tensor_gather(layer_own.astype(low)).astype(full)
    share = width // dp_count
    mine = lax.dynamic_slice_in_dim(mine, index * share, share, 1)
    return (
        layer_out,
        input_grad,
        mine[EXPERTS],
        qkv_shard.reshape(share, 3, size),
        out_shard,
        mine[EXPERTS + 1],
        mine[:EXPERTS].T,
        expert_grad,
    )


def solution(mesh):
    placed = (
        P("dp", None),
        P("dp"),
        P("dp", None, "tensor"),
        P("dp", "tensor"),
        P("dp"),
        P("dp", None),
        P(None, "dp", "tensor"),
        P("dp", None),
        P("dp", None),
    )
    return jax.shard_map(
        body,
        mesh=mesh,
        in_specs=placed,
        out_specs=(
            P("dp", None),
            P("dp", None),
            P("dp"),
            P("dp", None, "tensor"),
            P("dp", "tensor"),
            P("dp"),
            P("dp", None),
            P(None, "dp", "tensor"),
        ),
        check_vma=False,
    )
```

```python
import functools
import math

import jax
import jax.numpy as jnp
from jax import lax
from jax.experimental import pallas as pl
from jax.experimental.pallas import tpu as pltpu
from jax.sharding import PartitionSpec as P

HEAD = 128
EXPERTS = 4
SEQ = 1024
BLOCK = 256
MOST = 768


epsilon = 1e-05
theta_base = 10000.0
masked_out = -1e30
low = jnp.bfloat16
full = jnp.float32


def swap(value, axis, distance):
    return lax.ppermute(value, axis, [(i, i ^ distance) for i in range(lax.axis_size(axis))])


def contract(left, right, left_dim, right_dim):
    return lax.dot_general(
        left, right, (((left_dim,), (right_dim,)), ((), ())), preferred_element_type=jnp.float32
    )


def levels_of(count):
    return count.bit_length() - 1


def side_of(index, bit):
    return (index >> bit) & 1 == 1


def tensor_sum(value):
    for bit in range(levels_of(lax.axis_size("tensor"))):
        value = value + swap(value, "tensor", 1 << bit)
    return value


def all_sum(value):
    for axis in ("tensor", "dp"):
        for bit in range(levels_of(lax.axis_size(axis))):
            value = value + swap(value, axis, 1 << bit)
    return value


def tensor_gather(own, filler=None):
    count = lax.axis_size("tensor")
    place = lax.axis_index("tensor")
    size = own.shape[1]
    held = own
    order = list(range(levels_of(count)))[::-1]
    for bit in order:
        came = swap(held, "tensor", 1 << bit)
        if filler is not None and bit == order[0]:
            came = after(came, *filler(held))
        upper = side_of(place, bit)
        number = held.shape[1] // size
        mine = [held[:, i * size : (i + 1) * size] for i in range(number)]
        theirs = [came[:, i * size : (i + 1) * size] for i in range(number)]
        pairs = []
        for a, b in zip(mine, theirs):
            pairs.append((jnp.where(upper, b, a), jnp.where(upper, a, b)))
        held = jnp.concatenate([v for pair in pairs for v in pair], 1)
    return held


def after(value, *others):
    return lax.optimization_barrier((value, *others))[0]


def rotary_tables():
    half = HEAD // 2
    freqs = theta_base ** (-(jnp.arange(half, dtype=full) * 2.0 / HEAD))
    angles = jnp.arange(SEQ, dtype=full)[:, None] * freqs[None, :]
    cosine = jnp.cos(angles)
    sine = jnp.sin(angles)
    return (jnp.concatenate([cosine, cosine], 1), jnp.concatenate([-sine, sine], 1))


def limits(mib):
    return pltpu.CompilerParams(vmem_limit_bytes=mib << 20)


def cost(flops, moved, powers=0):
    return pl.CostEstimate(flops=int(flops), bytes_accessed=int(moved), transcendentals=int(powers))


def dot_cols(a, b):
    return lax.dot_general(a, b, (((1,), (1,)), ((), ())), preferred_element_type=full)


def dot_rows(a, b):
    return lax.dot_general(a, b, (((0,), (0,)), ((), ())), preferred_element_type=full)


def attention_kernel(scale, q_in, k_in, v_in, cos, sin, out, q_out, k_out, v_out, logs):
    def turned(ref):
        x = ref[...]
        return (x * cos[...] + pltpu.roll(x, HEAD // 2, 1) * sin[...]).astype(low)

    q_out[...] = turned(q_in)
    k_out[...] = turned(k_in)
    v_out[...] = v_in[...].astype(low)
    for block in range(SEQ // BLOCK):
        mine = pl.ds(block * BLOCK, BLOCK)
        seen = pl.ds(0, (block + 1) * BLOCK)
        scores = dot_cols(q_out[mine, :], k_out[seen, :]) * scale
        peak = jnp.max(scores, axis=1, keepdims=True)
        expo = jnp.exp(scores - peak)
        total = jnp.sum(expo, axis=1, keepdims=True)
        probs = (expo / total).astype(low)
        out[mine, :] = jnp.dot(probs, v_out[seen, :], preferred_element_type=full).astype(low)
        logs[0, mine, :] = peak + jnp.log(total)


def attention(qkv, cosine, sine, scale):
    rows = qkv.shape[0]
    size = qkv.shape[1] // 3
    heads = size // HEAD
    block = (SEQ, HEAD)
    table = pl.BlockSpec(block, lambda s, h: (0, 0))
    spec = pl.BlockSpec(block, lambda s, h: (s, h))
    shape = jax.ShapeDtypeStruct((rows, size), low)
    pairs = rows * heads * SEQ * 5 // 8
    return pl.pallas_call(
        functools.partial(attention_kernel, scale),
        grid=(rows // SEQ, heads),
        in_specs=[
            pl.BlockSpec(block, lambda s, h: (s, h)),
            pl.BlockSpec(block, lambda s, h: (s, heads + h)),
            pl.BlockSpec(block, lambda s, h: (s, 2 * heads + h)),
            table,
            table,
        ],
        out_specs=[spec] * 4 + [pl.BlockSpec((1, SEQ, 1), lambda s, h: (h, s, 0))],
        out_shape=[shape] * 4 + [jax.ShapeDtypeStruct((heads, rows, 1), full)],
        compiler_params=limits(48),
        cost_estimate=cost(4 * pairs * HEAD, rows * size * 20, pairs),
        name="attention",
    )(qkv, qkv, qkv, cosine, sine)


def attention_back_kernel(scale, heads, q_in, k_in, v_in, logs, grad, cos, sin, out, dk, dv):
    head = pl.program_id(1)
    dk[...] = jnp.zeros_like(dk)
    dv[...] = jnp.zeros_like(dv)

    def columns(which):
        return pl.ds(pl.multiple_of((which * heads + head) * HEAD, HEAD), HEAD)

    def turned(x, at):
        return (x * cos[at, :] - pltpu.roll(x, HEAD // 2, 1) * sin[at, :]).astype(low)

    for block in range(SEQ // BLOCK):
        mine = pl.ds(block * BLOCK, BLOCK)
        seen = pl.ds(0, (block + 1) * BLOCK)
        query, keys, values, given = q_in[mine, :], k_in[seen, :], v_in[seen, :], grad[mine, :]
        probs = jnp.exp(dot_cols(query, keys) * scale - logs[0, mine, :])
        prob_grad = dot_cols(given, values)
        inner = jnp.sum(probs * prob_grad, axis=1, keepdims=True)
        score_grad = (probs * (prob_grad - inner)).astype(low)
        query_grad = jnp.dot(score_grad, keys, preferred_element_type=full) * scale
        out[mine, columns(0)] = turned(query_grad, mine)
        dk[seen, :] += dot_rows(score_grad, query)
        dv[seen, :] += dot_rows(probs.astype(low), given)
    whole = pl.ds(0, SEQ)
    out[:, columns(1)] = turned(dk[...] * scale, whole)
    out[:, columns(2)] = dv[...].astype(low)


def attention_back(query, keys, values, logs, grad, cosine, sine, scale):
    rows, size = query.shape
    heads = size // HEAD
    block = (SEQ, HEAD)
    table = pl.BlockSpec(block, lambda s, h: (0, 0))
    spec = pl.BlockSpec(block, lambda s, h: (s, h))
    pairs = rows * heads * SEQ * 5 // 8
    return pl.pallas_call(
        functools.partial(attention_back_kernel, scale, heads),
        grid=(rows // SEQ, heads),
        in_specs=[spec] * 3
        + [pl.BlockSpec((1, SEQ, 1), lambda s, h: (h, s, 0)), spec, table, table],
        out_specs=pl.BlockSpec((SEQ, 3 * size), lambda s, h: (s, 0)),
        out_shape=jax.ShapeDtypeStruct((rows, 3 * size), low),
        scratch_shapes=[pltpu.VMEM(block, full)] * 2,
        compiler_params=limits(48),
        cost_estimate=cost(10 * pairs * HEAD, rows * size * 16, pairs),
        name="attention_back",
    )(query, keys, values, logs, grad, cosine, sine)


def place_rows(pieces, held, sems, upper, first):
    copies = []
    for ref, start, number, mine, there, column in pieces:
        half = held.shape[0] // 2
        columns = ref.shape[1]
        side = upper if mine else 1 - upper
        copies.append(
            pltpu.make_async_copy(
                ref.at[pl.ds(start, number), :],
                held.at[
                    pl.ds(pl.multiple_of(side * half + there, 64), number),
                    pl.ds(column * columns, columns),
                ],
                sems.at[len(copies)],
            )
        )

    @pl.when(first)
    def _():
        for copy in copies:
            copy.start()
        for copy in copies:
            copy.wait()


def down_pieces(own, came):
    half = own.shape[0]
    return [(own, 0, half, True, 0, 0), (came, 0, half, False, 0, 0)]


cuts = (
    ((0, 0, 16),),
    ((0, 16, 40),),
    ((0, 40, 56),),
    ((0, 56, 108),),
    ((0, 108, 128), (1, 0, 128)),
)
order = (0, 2, 3, 1)


def pair_pieces(own_gate, own_up, *came):
    half = own_gate.shape[0]
    pieces = [(own_gate, 0, half, True, 0, 0), (own_up, 0, half, True, 0, 1)]
    for cut, ref in zip(cuts, came):
        at = 0
        for which, start, stop in cut:
            number = (stop - start) * half // 128
            pieces.append((ref, at, number, False, start * half // 128, which))
            at += number
    return pieces


def column_block(where, i, size):
    return pl.ds(pl.multiple_of((i ^ where[0]) * size, size), size)


def down_kernel(carried, where, rows, own, came, *refs):
    rows_out, raw, held, sems = refs[carried:]
    place_rows(down_pieces(own, came), held, sems, where[1], pl.program_id(0) == 0)
    rows_out[...] = rows[...]
    raw[...] = jnp.dot(rows[...], held[...], preferred_element_type=full).astype(low)


def down_pass(where, rows, own, came, start, total, carried):
    number, width = rows.shape
    hidden = own.shape[1]
    tile = 256
    first = start // tile
    anywhere = pl.BlockSpec(memory_space=pl.ANY)
    here = lambda columns: pl.BlockSpec((tile, columns), lambda i, where: (first + i, 0))
    return pl.pallas_call(
        functools.partial(down_kernel, len(carried)),
        grid_spec=pltpu.PrefetchScalarGridSpec(
            num_scalar_prefetch=1,
            grid=(number // tile,),
            in_specs=[pl.BlockSpec((tile, width), lambda i, where: (i, 0))]
            + [anywhere] * (2 + len(carried)),
            out_specs=[here(width), here(hidden)],
            scratch_shapes=[pltpu.VMEM((width, hidden), low), pltpu.SemaphoreType.DMA((2,))],
        ),
        out_shape=[
            jax.ShapeDtypeStruct((total, width), low),
            jax.ShapeDtypeStruct((total, hidden), low),
        ],
        input_output_aliases={4 + i: i for i in range(len(carried))},
        compiler_params=limits(48),
        cost_estimate=cost(
            2 * number * width * hidden, (number * (2 * width + hidden) + width * hidden) * 2
        ),
        name="down",
    )(where, rows, own, came, *carried)


def spread_kernel(count, where, left, right, even, odd, part):
    size = part.shape[1] // count
    part[...] = dot_cols(left[...], right[...]).astype(low)
    for i in range(count):
        (odd if i % 2 else even)[:, i // 2 * size : (i // 2 + 1) * size] = part[
            :, column_block(where, i, size)
        ]


def spread_dot(where, left, right, column, count):
    rows, depth = left.shape
    width = right.shape[0]
    tile = 256
    spec = lambda columns: pl.BlockSpec((tile, columns), lambda i, where: (i, 0))
    half = jax.ShapeDtypeStruct((rows, width // 2), low)
    return pl.pallas_call(
        functools.partial(spread_kernel, count),
        grid_spec=pltpu.PrefetchScalarGridSpec(
            num_scalar_prefetch=1,
            grid=(rows // tile,),
            in_specs=[
                spec(depth),
                pl.BlockSpec((width, depth), lambda i, where: (0, column)),
            ],
            out_specs=[spec(width // 2)] * 2,
            scratch_shapes=[pltpu.VMEM((tile, width), low)],
        ),
        out_shape=[half, half],
        compiler_params=limits(48),
        cost_estimate=cost(2 * rows * width * depth, (rows * (width + depth) + width * depth) * 2),
        name="spread",
    )(where, left, right)


def up_kernel(where, act, own, came, out, held, sems):
    place_rows(down_pieces(own, came), held, sems, where[1], pl.program_id(0) == 0)
    out[...] = dot_cols(act[...], held[...]).astype(low)


def up_pass(where, act, own, came):
    total, hidden = act.shape
    width = 2 * own.shape[0]
    tile = 256
    spec = lambda columns: pl.BlockSpec((tile, columns), lambda i, where: (i, 0))
    return pl.pallas_call(
        up_kernel,
        grid_spec=pltpu.PrefetchScalarGridSpec(
            num_scalar_prefetch=1,
            grid=(total // tile,),
            in_specs=[spec(hidden)] + [pl.BlockSpec(memory_space=pl.ANY)] * 2,
            out_specs=spec(width),
            scratch_shapes=[pltpu.VMEM((width, hidden), low), pltpu.SemaphoreType.DMA((2,))],
        ),
        out_shape=jax.ShapeDtypeStruct((total, width), low),
        compiler_params=limits(48),
        cost_estimate=cost(
            2 * total * width * hidden, (total * (width + hidden) + width * hidden) * 2
        ),
        name="up",
    )(where, act, own, came)


def expert_kernel(count, carried, where, *refs):
    blocks, refs = refs[:count], refs[count:]
    number = 2 + len(cuts)
    weights, (raw, routed, router) = refs[:number], refs[number : number + 3]
    rows_out, act_out, grad_out, even, odd, gate_grad, pair, part, sems = refs[
        number + 3 + carried :
    ]
    size = blocks[0].shape[1]
    hidden = raw.shape[1]
    place_rows(pair_pieces(*weights), pair, sems, where[1], pl.program_id(0) == 0)
    for i, ref in enumerate(blocks):
        rows_out[:, column_block(where, i, size)] = ref[...]
    both = jnp.dot(rows_out[...], pair[...], preferred_element_type=full)
    pre_gate = both[:, :hidden]
    pre_up = both[:, hidden:]
    sigma = 1.0 / (1.0 + jnp.exp(-pre_gate))
    silu = pre_gate * sigma
    act = silu * pre_up
    back = raw[...].astype(full)
    tile = back.shape[0]
    own = where[2].astype(full)
    other = jnp.broadcast_to(routed[...], (128, tile)).T - own
    logits = jnp.dot(rows_out[...], router[...], preferred_element_type=full)
    lane = lax.broadcasted_iota(jnp.int32, (tile, 128), 1).astype(full)
    ahead = jnp.where(lane == other, logits, 0.0) - jnp.where(lane == own, logits, 0.0)
    gate = 1.0 / (1.0 + jnp.exp(jnp.sum(ahead, axis=1, keepdims=True)))
    gate_sum = jnp.sum(act * back, axis=1, keepdims=True)
    gate_grad[...] = jnp.broadcast_to(gate_sum, (tile, 128)).T[:1]
    act_out[...] = (act * gate).astype(low)
    back = back * gate
    grad_out[:, :hidden] = (back * pre_up * sigma * (1.0 + pre_gate * (1.0 - sigma))).astype(low)
    grad_out[:, hidden:] = (back * silu).astype(low)
    part[...] = dot_cols(grad_out[...], pair[...]).astype(low)
    for i in range(count):
        (odd if i % 2 else even)[:, i // 2 * size : (i // 2 + 1) * size] = part[
            :, column_block(where, i, size)
        ]


def expert_pass(step, where, blocks, weights, raw, routed, router, carried):
    count = len(blocks)
    size = blocks[0].shape[1]
    width, hidden = 2 * weights[0].shape[0], weights[0].shape[1]
    both = 2 * hidden
    total = raw.shape[0]
    tile = 256
    steps = MOST // tile
    here = lambda i, where: (step * steps + i, 0)
    near = lambda i, where: (i, 0)
    near_spec = lambda columns: pl.BlockSpec((tile, columns), near)
    here_spec = lambda columns: pl.BlockSpec((tile, columns), here)
    row_spec = pl.BlockSpec((1, tile), lambda i, where: (0, i))
    anywhere = pl.BlockSpec(memory_space=pl.ANY)
    shape = lambda r, c, t=low: jax.ShapeDtypeStruct((r, c), t)
    return pl.pallas_call(
        functools.partial(expert_kernel, count, len(carried)),
        grid_spec=pltpu.PrefetchScalarGridSpec(
            num_scalar_prefetch=1,
            grid=(steps,),
            in_specs=[near_spec(size)] * count
            + [anywhere] * len(weights)
            + [
                here_spec(hidden),
                row_spec,
                pl.BlockSpec((width, 128), lambda i, where: (0, 0)),
            ]
            + [anywhere] * len(carried),
            out_specs=[
                here_spec(width),
                here_spec(hidden),
                here_spec(both),
                near_spec(width // 2),
                near_spec(width // 2),
                row_spec,
            ],
            scratch_shapes=[
                pltpu.VMEM((width, both), low),
                pltpu.VMEM((tile, width), low),
                pltpu.SemaphoreType.DMA((2 + sum(len(cut) for cut in cuts),)),
            ],
        ),
        out_shape=[
            shape(total, width),
            shape(total, hidden),
            shape(total, both),
            shape(MOST, width // 2),
            shape(MOST, width // 2),
            shape(1, MOST, full),
        ],
        input_output_aliases={
            count + len(weights) + 4 + i: i for i in range(len(carried))
        },
        compiler_params=limits(60),
        cost_estimate=cost(
            4 * MOST * width * both, width * both * 2 + MOST * (width * 8 + hidden * 8), MOST * hidden
        ),
        name="expert",
    )(where, *blocks, *weights, raw, routed, router, *carried)


def expert_grad_kernel(hidden, pieces, per, *refs):
    out = refs[-1]
    which, at = pl.program_id(0), pl.program_id(1)

    def add(ref, other):
        out[0] = (ref[...].astype(full) + other[...].astype(full))[:, :hidden]

    for k in range(pieces):

        @pl.when((which < 2) & (at // per == k))
        def _():
            add(refs[0], refs[1 + k])

    @pl.when(which == 2)
    def _():
        add(refs[1 + pieces], refs[2 + pieces])


def expert_grad_sum(pair, down, hidden):
    rows, padded = down[0].shape
    tile = min(256, rows)
    pieces = len(pair) - 1
    per = rows // tile // pieces
    last = rows // tile - 1

    def piece_spec(k):
        return pl.BlockSpec(
            (tile, padded),
            lambda w, i: (
                jnp.where(w == 2, per - 1, jnp.clip(i - k * per, 0, per - 1)),
                jnp.minimum(w, 1),
            ),
        )

    pair_spec = pl.BlockSpec(
        (tile, padded), lambda w, i: (jnp.where(w == 2, last, i), jnp.minimum(w, 1))
    )
    down_spec = pl.BlockSpec((tile, padded), lambda w, i: (jnp.where(w == 2, i, 0), 0))
    return pl.pallas_call(
        functools.partial(expert_grad_kernel, hidden, pieces, per),
        grid=(3, rows // tile),
        in_specs=[pair_spec] + [piece_spec(k) for k in range(pieces)] + [down_spec] * 2,
        out_specs=pl.BlockSpec((1, tile, hidden), lambda w, i: (w, i, 0)),
        out_shape=jax.ShapeDtypeStruct((3, rows, hidden), full),
        compiler_params=limits(40),
        cost_estimate=cost(rows * padded * 3, rows * padded * 24),
        name="expert_grad_sum",
    )(*pair, *down)


def near_blocks(own, *others):
    held = [own]
    for bit in range(levels_of(lax.axis_size("tensor")))[::-1]:
        theirs = [swap(v, "tensor", 1 << bit) for v in held]
        if bit and others:
            theirs = [after(v, *others) for v in theirs]
        held = [v for pair in zip(held, theirs) for v in pair]
    return held


def near_reduce(even, odd, meet, *others, filler=None):
    count = lax.axis_size("tensor")
    number = count // 2
    size = even.shape[1] // number
    came = swap(odd, "tensor", 1)
    for bit in range(1, levels_of(count)):
        blocks = [
            even[:, i * size : (i + 1) * size].astype(full)
            + came[:, i * size : (i + 1) * size].astype(full)
            for i in range(number)
        ]
        sent = jnp.concatenate([v.astype(low) for v in blocks[1::2]], 1)
        if bit == levels_of(count) - 1:
            sent = after(sent, *others)
            meet.append(sent)
        even = jnp.concatenate(blocks[::2], 1)
        came = swap(sent, "tensor", 1 << bit)
        if filler is not None and bit == levels_of(count) - 1:
            came = after(came, *filler(sent))
        number //= 2
    return even.astype(full) + came.astype(full)


def half_gather(local, group_count):
    held = local
    place = lax.axis_index("dp") % group_count
    for bit in range(levels_of(group_count) - 1):
        came = swap(held, "dp", 1 << bit)
        upper = side_of(place, bit)
        held = jnp.concatenate([jnp.where(upper, came, held), jnp.where(upper, held, came)], 0)
    return held


def group_finish(kept, came, position, group_count):
    if group_count > 2:
        came = jnp.concatenate(came, 0)
    for bit in range(levels_of(group_count) - 1)[::-1]:
        current = kept.astype(full) + came.astype(full)
        middle = current.shape[0] // 2
        upper = (position >> bit) & 1
        kept = lax.dynamic_slice_in_dim(current, upper * middle, middle, 0)
        given = lax.dynamic_slice_in_dim(current, (1 - upper) * middle, middle, 0)
        came = swap(given.astype(low), "dp", 1 << bit)
    return [kept, *came] if isinstance(came, list) else [kept, came]


def body(
    tokens,
    attn_gain,
    qkv_weight,
    out_weight,
    moe_gain,
    router_weight,
    expert_weight,
    routes,
    cotangent,
):
    rows = tokens.shape[0]
    width = tokens.shape[1]
    tensor_count = lax.axis_size("tensor")
    dp_count = lax.axis_size("dp")
    group_count = dp_count // EXPERTS
    size = width // tensor_count
    hidden_size = expert_weight.shape[2]
    padded = -(-hidden_size // 128) * 128
    scale = 1.0 / math.sqrt(HEAD)
    place = lax.axis_index("tensor")
    index = lax.axis_index("dp")
    expert = index // group_count
    member = index % group_count
    top_half = member >> (levels_of(group_count) - 1)
    where = jnp.stack([place, top_half, expert]).astype(jnp.int32)

    def own_columns(value):
        return lax.dynamic_slice_in_dim(value, place * size, size, 1)

    extras = jnp.concatenate([router_weight, attn_gain[:, None], moe_gain[:, None]], 1)
    extras = jnp.pad(extras, ((0, 0), (0, 128 - extras.shape[1])))
    first = lax.all_gather(
        jnp.concatenate([qkv_weight.reshape(-1, 3 * size), out_weight, extras], 1),
        "dp",
        axis=0,
        tiled=True,
    )
    qkv_flat = first[:, : 3 * size]
    out_full = first[:, 3 * size : 4 * size]
    small = first[:, 4 * size :].T
    router_full = small[:EXPERTS]
    gain_first = small[EXPERTS : EXPERTS + 1].astype(full)
    gain_second = small[EXPERTS + 1 : EXPERTS + 2].astype(full)
    gain_first_own = own_columns(gain_first)
    gain_second_own = own_columns(gain_second)
    router_own = own_columns(router_full)

    near = jnp.arange(EXPERTS, dtype=jnp.int32) ^ expert
    names = jnp.arange(EXPERTS, dtype=jnp.int32)
    hits = jnp.sum((routes.T[None] == names[:, None, None]).astype(jnp.int32), 1)
    rank = jnp.cumsum(hits, axis=1) - hits
    slot_near = jnp.take(jnp.where(hits > 0, rank, -1), near, axis=0)
    places = jnp.arange(MOST, dtype=jnp.int32)[:, None]
    chosen = [(places == slot_near[s][None, :]).astype(low) for s in range(EXPERTS)]

    def packed(own):
        return [jnp.dot(c, own, preferred_element_type=full).astype(low) for c in chosen]

    def exchange(parts):
        return [parts[0]] + [swap(parts[s], "dp", s * group_count) for s in range(1, EXPERTS)]

    def unpacked(parts):
        total = contract(chosen[0], parts[0], 0, 0)
        for c, part in zip(chosen[1:], parts[1:]):
            total = total + contract(c, part, 0, 0)
        return total

    def widened(value):
        return jnp.pad(value, ((0, 0), (0, padded - hidden_size)))

    gate_mine, up_mine, down_mine = [
        half_gather(widened(expert_weight[k]), group_count) for k in range(3)
    ]
    half = width // 2
    mine_at, given_at = top_half * half, (1 - top_half) * half
    reach = group_count // 2

    def group_send(given, *others):
        return swap(after(given, *others), "dp", reach)

    down = (down_mine, group_send(down_mine))
    crossing = []

    def cross(*others):
        pieces = [
            (gate_mine, up_mine)[which][start * half // 128 : stop * half // 128]
            for which, start, stop in cuts[len(crossing)]
        ]
        crossing.append(group_send(jnp.concatenate(pieces, 0), *crossing[-1:], *others))

    cross(first)

    grad_own = own_columns(cotangent)
    grad_mine = jnp.dot(chosen[0], cotangent, preferred_element_type=full).astype(low)
    planes = [
        [m + g * group_count for g in range(EXPERTS)] for m in range(group_count)
    ]
    grad_planes = lax.all_gather(
        after(grad_own, first), "dp", axis=0, tiled=True, axis_index_groups=planes
    )
    slots_came = exchange([slot_near[s][None].astype(full) for s in range(EXPERTS)])
    route_sums = jnp.sum(routes, axis=1)[None].astype(low)
    routed = exchange([contract(route_sums, c, 1, 1) for c in chosen])

    inputs = tokens.astype(full)
    scale_one = lax.rsqrt(jnp.mean(inputs * inputs, axis=1, keepdims=True) + epsilon)
    normed_in = (inputs * scale_one * gain_first).astype(low)
    inputs_own = own_columns(tokens).astype(full)
    normed_in = after(normed_in, down[1], grad_mine, *slots_came, *routed)
    qkv = jnp.dot(normed_in, qkv_flat, preferred_element_type=full)
    cross(qkv)
    cosine, sine = rotary_tables()
    context, query, keys, values, logs = attention(qkv, cosine, sine, scale)
    context = after(context, crossing[1])
    cross(context)
    attn_parts = spread_dot(where, context, first, 3, tensor_count)
    rows_raw = []

    total = EXPERTS * MOST

    def down_filler(sent):
        cross(sent)
        rows_raw.extend(down_pass(where, after(grad_mine, sent), *down, 0, total, ()))
        return (rows_raw[1], crossing[3])

    hidden = inputs_own + near_reduce(*attn_parts, [], crossing[2], filler=down_filler)
    cross(rows_raw[1])
    grad_planes = after(grad_planes, hidden)
    grad_packed = []
    for s in order[1:]:
        source = lax.dynamic_slice_in_dim(grad_planes, (expert ^ s) * rows, rows, 0)
        taken = (places.astype(full) == slots_came[s]).astype(low)
        grad_packed.append(jnp.dot(taken, source, preferred_element_type=full).astype(low))
    grad_rest = lax.all_gather(jnp.concatenate(grad_packed, 0), "tensor", axis=1, tiled=True)

    scaled_hidden = (hidden * gain_second_own).astype(low)
    sums = tensor_sum(
        jnp.concatenate(
            [contract(router_own, scaled_hidden, 1, 1), jnp.sum(hidden * hidden, 1)[None]], 0
        )
    )
    scale_two_row = lax.rsqrt(sums[EXPERTS:] / width + epsilon)
    scale_two = scale_two_row.reshape(rows, 1)
    logits = sums[:EXPERTS] * scale_two_row
    normed_two = hidden * scale_two
    moe_in = (normed_two * gain_second_own).astype(low)
    named = hits > 0
    top = jnp.max(jnp.where(named, logits, masked_out), axis=0, keepdims=True)
    weight = jnp.where(named, jnp.exp(logits - top), 0.0)
    gates = weight / jnp.sum(weight, axis=0, keepdims=True)

    def three_parts(value):
        a = value.astype(low)
        b = (value - a.astype(full)).astype(low)
        return jnp.stack([a, b, (value - a.astype(full) - b.astype(full)).astype(low)])

    moe_packed = packed(moe_in)
    pair = (gate_mine, up_mine, *crossing)
    crossed = {2: swap(moe_packed[2], "dp", 2 * group_count)}
    crossed[3] = swap(after(moe_packed[3], crossed[2]), "dp", 3 * group_count)
    arrived = [near_blocks(moe_packed[0])]

    carried = ()
    sums_sent = []
    came_home = {}
    returned = []
    gate_grads = []
    router_block = first[:, 4 * size :]
    for step in range(EXPERTS):
        named_sum = routed[order[step]]
        if step == 1:
            rows_raw = down_pass(where, after(grad_rest, even), *down, MOST, total, rows_raw)
            named_sum = after(named_sum, crossed[3])
        if step == 2:
            named_sum = after(named_sum, crossed[1], sums_sent[0])
        if step == 3:
            named_sum = after(named_sum, sums_sent[1])
        moe_rows, activation, pre_grad, even, odd, gate_grad = expert_pass(
            step, where, arrived[step], pair, rows_raw[1], named_sum, router_block, carried
        )
        carried = (moe_rows, activation, pre_grad)
        if step == 0:
            arrived.append(near_blocks(crossed[2], even))
            crossed[3] = after(crossed[3], even)
            crossed[1] = swap(after(moe_packed[1], crossed[3]), "dp", group_count)
        if step == 1:
            arrived.append(near_blocks(crossed[3], even))
            odd = after(odd, crossed[1], arrived[2][tensor_count // 2])
        if step == 2:
            arrived.append(near_blocks(crossed[1], even))
        if step == 2:
            odd = after(odd, *returned, arrived[3][tensor_count // 2])
        if step == 3:
            came_home[2] = swap(returned[0], "dp", 2 * group_count)
            odd = after(odd, returned[1], came_home[2])
        if step == 0:
            own_parts = (even, odd)
        else:
            returned.append(near_reduce(even, odd, sums_sent).astype(low))
        gate_grads.append(gate_grad)

    def home(parts):
        return {
            s: swap(v, "dp", s * group_count) if s else v for s, v in zip(order, parts)
        }

    came_home[3] = swap(returned[1], "dp", 3 * group_count)
    came_home[1] = swap(returned[2], "dp", group_count)
    own_even, own_odd = own_parts
    came_home[0] = near_reduce(own_even, after(own_odd, sums_sent[2]), []).astype(low)
    gate_grad_near = home([gate_grads[0]] + [after(v, even) for v in gate_grads[1:]])
    grad_rows = rows_raw[0]

    def term(left, right):
        def part(start, number):
            taken = lax.dynamic_slice_in_dim(left, start, number, 1)
            return contract(taken, right, 0, 0).astype(low)

        return part

    unit = half // 128
    quarter = half // 2
    act_late = after(activation, sums_sent[2], returned[1])
    down_given = term(grad_rows, act_late)(given_at, half)
    down_sums = [group_send(down_given[: 40 * unit])]
    expert_part = up_pass(
        where, after(activation, down_given, returned[2], *gate_grad_near.values()), *down
    )
    expert_part = after(expert_part, down_sums[0], *came_home.values())
    expert_own = lax.psum_scatter(expert_part, "tensor", scatter_dimension=1, tiled=True)
    down_sums.append(group_send(down_given[40 * unit : 80 * unit], down_sums[0]))
    came_home = {s: after(v, expert_part) for s, v in came_home.items()}
    back = unpacked([came_home[s] for s in range(EXPERTS)])

    gate_grad = jnp.concatenate(
        [
            jnp.sum(contract(three_parts(gate_grad_near[s][0]), chosen[s], 1, 0), 0, keepdims=True)
            for s in range(EXPERTS)
        ],
        0,
    )
    scaled_back = back * gain_second_own
    sums = tensor_sum(
        jnp.concatenate([gate_grad, jnp.sum(scaled_back * normed_two, axis=1)[None]], 0)
    )
    gate_grad = jnp.take(sums[:EXPERTS], near, axis=0)
    weighted = jnp.sum(gates * gate_grad, axis=0, keepdims=True)
    logit_grad = (gates * (gate_grad - weighted)).astype(low)
    mean_two = (
        sums[EXPERTS:] + jnp.sum(logit_grad.astype(full) * logits, axis=0, keepdims=True)
    ) / width
    moe_grad = contract(logit_grad, router_own, 0, 0) + back

    grad_out = grad_own.astype(full)
    hidden_grad = grad_out + scale_two * (
        moe_grad * gain_second_own - normed_two * mean_two.reshape(rows, 1)
    )
    router_grad = jnp.dot(logit_grad, moe_in, preferred_element_type=full)
    moe_gain_grad = jnp.sum(moe_grad * normed_two, axis=0)
    pair_given = []
    kept = []

    def give_pair(sent):
        down_sums.append(group_send(down_given[80 * unit :], down_sums[1], sent))
        pair_term = term(moe_rows, after(pre_grad, sent, down_sums[1]))
        pair_given.extend(pair_term(given_at + k * quarter, quarter) for k in range(2))
        return (*pair_given, down_sums[2])

    attn_grad = tensor_gather(hidden_grad.astype(low), give_pair)
    pair_sums = [group_send(pair_given[0][: 16 * unit], down_sums[2])]
    context_grad = jnp.dot(attn_grad, out_full, preferred_element_type=full).astype(low)
    out_grad = contract(after(attn_grad, context_grad), context, 0, 0).astype(low)
    qkv_grad_rows = attention_back(query, keys, values, logs, context_grad, cosine, sine, scale)
    qkv_grad_rows = after(qkv_grad_rows, pair_sums[0], out_grad)
    qkv_grad = contract(normed_in, qkv_grad_rows, 0, 0).astype(low)
    grads_both = jnp.concatenate([qkv_grad, out_grad], 1)
    shards = lax.psum_scatter(grads_both, "dp", scatter_dimension=0, tiled=True)
    pair_sums.append(group_send(pair_given[0][16 * unit :], pair_sums[0], grads_both))
    pair_last = group_send(pair_given[1], pair_sums[0], grads_both)
    outputs = {0: expert_own[:MOST]}
    part = after(expert_own[MOST : 2 * MOST], grads_both)
    outputs[2] = swap(part, "dp", 2 * group_count)

    def keep(sent):
        late = after(pre_grad, sent, expert_own)
        kept.append(term(moe_rows, late)(mine_at, half))
        kept.append(term(grad_rows, after(activation, kept[0]))(mine_at, half))
        return kept

    parts = spread_dot(where, after(qkv_grad_rows, grads_both), first, 0, tensor_count)
    normed_grad = near_reduce(*parts, [], outputs[2], filler=keep)
    for k in (2, 3):
        part = after(expert_own[k * MOST : (k + 1) * MOST], outputs[2])
        outputs[order[k]] = swap(part, "dp", order[k] * group_count)
    normed_one = inputs_own * scale_one
    scaled_in = normed_grad * gain_first_own
    attn_gain_grad = jnp.sum(normed_grad * normed_one, axis=0)
    mean_one = tensor_sum(jnp.sum(scaled_in * normed_one, axis=1)[None]) / width
    input_own = hidden_grad + scale_one * (scaled_in - normed_one * mean_one.reshape(rows, 1))
    mine = jnp.concatenate([router_grad, attn_gain_grad[None], moe_gain_grad[None]], 0)
    mine = lax.dynamic_update_slice_in_dim(
        jnp.zeros((mine.shape[0], width), full), mine, place * size, 1
    )
    mine = all_sum(mine)
    expert_grad = expert_grad_sum(
        group_finish(kept[0], [jnp.concatenate(pair_sums, 0), pair_last], member, group_count),
        group_finish(kept[1], [jnp.concatenate(down_sums, 0)], member, group_count),
        hidden_size,
    )
    input_grad = tensor_gather(input_own.astype(low), lambda sent: (mine, outputs[3], outputs[1]))
    input_grad = input_grad.astype(full)
    layer_own = hidden + unpacked([outputs[s] for s in range(EXPERTS)])
    layer_out = tensor_gather(layer_own.astype(low)).astype(full)
    share = width // dp_count
    mine = lax.dynamic_slice_in_dim(mine, index * share, share, 1)
    shards = shards.astype(full)
    qkv_shard, out_shard = shards[:, : 3 * size], shards[:, 3 * size :]
    return (
        layer_out,
        input_grad,
        mine[EXPERTS],
        qkv_shard.reshape(share, 3, size),
        out_shard,
        mine[EXPERTS + 1],
        mine[:EXPERTS].T,
        expert_grad,
    )


def solution(mesh):
    placed = (
        P("dp", None),
        P("dp"),
        P("dp", None, "tensor"),
        P("dp", "tensor"),
        P("dp"),
        P("dp", None),
        P(None, "dp", "tensor"),
        P("dp", None),
        P("dp", None),
    )
    return jax.shard_map(
        body,
        mesh=mesh,
        in_specs=placed,
        out_specs=(
            P("dp", None),
            P("dp", None),
            P("dp"),
            P("dp", None, "tensor"),
            P("dp", "tensor"),
            P("dp"),
            P("dp", None),
            P(None, "dp", "tensor"),
        ),
        check_vma=False,
    )
```

```python
import functools
import math

import jax
import jax.numpy as jnp
from jax import lax
from jax.experimental import pallas as pl
from jax.experimental.pallas import tpu as pltpu
from jax.sharding import PartitionSpec as P

HEAD = 128
EXPERTS = 4
SEQ = 1024
BLOCK = 256
MOST = 768


epsilon = 1e-05
theta_base = 10000.0
masked_out = -1e30
low = jnp.bfloat16
full = jnp.float32


def swap(value, axis, distance):
    return lax.ppermute(value, axis, [(i, i ^ distance) for i in range(lax.axis_size(axis))])


def contract(left, right, left_dim, right_dim):
    return lax.dot_general(
        left, right, (((left_dim,), (right_dim,)), ((), ())), preferred_element_type=jnp.float32
    )


def levels_of(count):
    return count.bit_length() - 1


def side_of(index, bit):
    return (index >> bit) & 1 == 1


def tensor_sum(value):
    for bit in range(levels_of(lax.axis_size("tensor"))):
        value = value + swap(value, "tensor", 1 << bit)
    return value


def all_sum(value):
    for axis in ("tensor", "dp"):
        for bit in range(levels_of(lax.axis_size(axis))):
            value = value + swap(value, axis, 1 << bit)
    return value


def tensor_gather(own, filler=None):
    count = lax.axis_size("tensor")
    place = lax.axis_index("tensor")
    size = own.shape[1]
    held = own
    order = list(range(levels_of(count)))[::-1]
    for bit in order:
        came = swap(held, "tensor", 1 << bit)
        if filler is not None and bit == order[0]:
            came = after(came, *filler(held))
        upper = side_of(place, bit)
        number = held.shape[1] // size
        mine = [held[:, i * size : (i + 1) * size] for i in range(number)]
        theirs = [came[:, i * size : (i + 1) * size] for i in range(number)]
        pairs = []
        for a, b in zip(mine, theirs):
            pairs.append((jnp.where(upper, b, a), jnp.where(upper, a, b)))
        held = jnp.concatenate([v for pair in pairs for v in pair], 1)
    return held


def after(value, *others):
    return lax.optimization_barrier((value, *others))[0]


def rotary_tables():
    half = HEAD // 2
    freqs = theta_base ** (-(jnp.arange(half, dtype=full) * 2.0 / HEAD))
    angles = jnp.arange(SEQ, dtype=full)[:, None] * freqs[None, :]
    cosine = jnp.cos(angles)
    sine = jnp.sin(angles)
    return (jnp.concatenate([cosine, cosine], 1), jnp.concatenate([-sine, sine], 1))


def limits(mib):
    return pltpu.CompilerParams(vmem_limit_bytes=mib << 20)


def cost(flops, moved, powers=0):
    return pl.CostEstimate(flops=int(flops), bytes_accessed=int(moved), transcendentals=int(powers))


def dot_cols(a, b):
    return lax.dot_general(a, b, (((1,), (1,)), ((), ())), preferred_element_type=full)


def dot_rows(a, b):
    return lax.dot_general(a, b, (((0,), (0,)), ((), ())), preferred_element_type=full)


def attention_kernel(scale, q_in, k_in, v_in, cos, sin, out, q_out, k_out, v_out, logs):
    def turned(ref):
        x = ref[...]
        return (x * cos[...] + pltpu.roll(x, HEAD // 2, 1) * sin[...]).astype(low)

    q_out[...] = turned(q_in)
    k_out[...] = turned(k_in)
    v_out[...] = v_in[...].astype(low)
    for block in range(SEQ // BLOCK):
        mine = pl.ds(block * BLOCK, BLOCK)
        seen = pl.ds(0, (block + 1) * BLOCK)
        scores = dot_cols(q_out[mine, :], k_out[seen, :]) * scale
        peak = jnp.max(scores, axis=1, keepdims=True)
        expo = jnp.exp(scores - peak)
        total = jnp.sum(expo, axis=1, keepdims=True)
        probs = (expo / total).astype(low)
        out[mine, :] = jnp.dot(probs, v_out[seen, :], preferred_element_type=full).astype(low)
        logs[0, mine, :] = peak + jnp.log(total)


def attention(qkv, cosine, sine, scale):
    rows = qkv.shape[0]
    size = qkv.shape[1] // 3
    heads = size // HEAD
    block = (SEQ, HEAD)
    table = pl.BlockSpec(block, lambda s, h: (0, 0))
    spec = pl.BlockSpec(block, lambda s, h: (s, h))
    shape = jax.ShapeDtypeStruct((rows, size), low)
    pairs = rows * heads * SEQ * 5 // 8
    return pl.pallas_call(
        functools.partial(attention_kernel, scale),
        grid=(rows // SEQ, heads),
        in_specs=[
            pl.BlockSpec(block, lambda s, h: (s, h)),
            pl.BlockSpec(block, lambda s, h: (s, heads + h)),
            pl.BlockSpec(block, lambda s, h: (s, 2 * heads + h)),
            table,
            table,
        ],
        out_specs=[spec] * 4 + [pl.BlockSpec((1, SEQ, 1), lambda s, h: (h, s, 0))],
        out_shape=[shape] * 4 + [jax.ShapeDtypeStruct((heads, rows, 1), full)],
        compiler_params=limits(48),
        cost_estimate=cost(4 * pairs * HEAD, rows * size * 20, pairs),
        name="attention",
    )(qkv, qkv, qkv, cosine, sine)


def attention_back_kernel(scale, heads, q_in, k_in, v_in, logs, grad, cos, sin, out, dk, dv):
    head = pl.program_id(1)
    dk[...] = jnp.zeros_like(dk)
    dv[...] = jnp.zeros_like(dv)

    def columns(which):
        return pl.ds(pl.multiple_of((which * heads + head) * HEAD, HEAD), HEAD)

    def turned(x, at):
        return (x * cos[at, :] - pltpu.roll(x, HEAD // 2, 1) * sin[at, :]).astype(low)

    for block in range(SEQ // BLOCK):
        mine = pl.ds(block * BLOCK, BLOCK)
        seen = pl.ds(0, (block + 1) * BLOCK)
        query, keys, values, given = q_in[mine, :], k_in[seen, :], v_in[seen, :], grad[mine, :]
        probs = jnp.exp(dot_cols(query, keys) * scale - logs[0, mine, :])
        prob_grad = dot_cols(given, values)
        inner = jnp.sum(probs * prob_grad, axis=1, keepdims=True)
        score_grad = (probs * (prob_grad - inner)).astype(low)
        query_grad = jnp.dot(score_grad, keys, preferred_element_type=full) * scale
        out[mine, columns(0)] = turned(query_grad, mine)
        dk[seen, :] += dot_rows(score_grad, query)
        dv[seen, :] += dot_rows(probs.astype(low), given)
    whole = pl.ds(0, SEQ)
    out[:, columns(1)] = turned(dk[...] * scale, whole)
    out[:, columns(2)] = dv[...].astype(low)


def attention_back(query, keys, values, logs, grad, cosine, sine, scale):
    rows, size = query.shape
    heads = size // HEAD
    block = (SEQ, HEAD)
    table = pl.BlockSpec(block, lambda s, h: (0, 0))
    spec = pl.BlockSpec(block, lambda s, h: (s, h))
    pairs = rows * heads * SEQ * 5 // 8
    return pl.pallas_call(
        functools.partial(attention_back_kernel, scale, heads),
        grid=(rows // SEQ, heads),
        in_specs=[spec] * 3
        + [pl.BlockSpec((1, SEQ, 1), lambda s, h: (h, s, 0)), spec, table, table],
        out_specs=pl.BlockSpec((SEQ, 3 * size), lambda s, h: (s, 0)),
        out_shape=jax.ShapeDtypeStruct((rows, 3 * size), low),
        scratch_shapes=[pltpu.VMEM(block, full)] * 2,
        compiler_params=limits(48),
        cost_estimate=cost(10 * pairs * HEAD, rows * size * 16, pairs),
        name="attention_back",
    )(query, keys, values, logs, grad, cosine, sine)


def place_rows(pieces, held, sems, upper, first):
    copies = []
    for ref, start, number, mine, there, column in pieces:
        half = held.shape[0] // 2
        columns = ref.shape[1]
        side = upper if mine else 1 - upper
        copies.append(
            pltpu.make_async_copy(
                ref.at[pl.ds(start, number), :],
                held.at[
                    pl.ds(pl.multiple_of(side * half + there, 64), number),
                    pl.ds(column * columns, columns),
                ],
                sems.at[len(copies)],
            )
        )

    @pl.when(first)
    def _():
        for copy in copies:
            copy.start()
        for copy in copies:
            copy.wait()


def down_pieces(own, came):
    half = own.shape[0]
    return [(own, 0, half, True, 0, 0), (came, 0, half, False, 0, 0)]


cuts = (
    ((0, 0, 16),),
    ((0, 16, 40),),
    ((0, 40, 56),),
    ((0, 56, 108),),
    ((0, 108, 128), (1, 0, 128)),
)
order = (0, 2, 3, 1)


def pair_pieces(own_gate, own_up, *came):
    half = own_gate.shape[0]
    pieces = [(own_gate, 0, half, True, 0, 0), (own_up, 0, half, True, 0, 1)]
    for cut, ref in zip(cuts, came):
        at = 0
        for which, start, stop in cut:
            number = (stop - start) * half // 128
            pieces.append((ref, at, number, False, start * half // 128, which))
            at += number
    return pieces


def column_block(where, i, size):
    return pl.ds(pl.multiple_of((i ^ where[0]) * size, size), size)


def down_kernel(carried, where, rows, own, came, *refs):
    rows_out, raw, held, sems = refs[carried:]
    place_rows(down_pieces(own, came), held, sems, where[1], pl.program_id(0) == 0)
    rows_out[...] = rows[...]
    raw[...] = jnp.dot(rows[...], held[...], preferred_element_type=full).astype(low)


def down_pass(where, rows, own, came, start, total, carried):
    number, width = rows.shape
    hidden = own.shape[1]
    tile = 256
    first = start // tile
    anywhere = pl.BlockSpec(memory_space=pl.ANY)
    here = lambda columns: pl.BlockSpec((tile, columns), lambda i, where: (first + i, 0))
    return pl.pallas_call(
        functools.partial(down_kernel, len(carried)),
        grid_spec=pltpu.PrefetchScalarGridSpec(
            num_scalar_prefetch=1,
            grid=(number // tile,),
            in_specs=[pl.BlockSpec((tile, width), lambda i, where: (i, 0))]
            + [anywhere] * (2 + len(carried)),
            out_specs=[here(width), here(hidden)],
            scratch_shapes=[pltpu.VMEM((width, hidden), low), pltpu.SemaphoreType.DMA((2,))],
        ),
        out_shape=[
            jax.ShapeDtypeStruct((total, width), low),
            jax.ShapeDtypeStruct((total, hidden), low),
        ],
        input_output_aliases={4 + i: i for i in range(len(carried))},
        compiler_params=limits(48),
        cost_estimate=cost(
            2 * number * width * hidden, (number * (2 * width + hidden) + width * hidden) * 2
        ),
        name="down",
    )(where, rows, own, came, *carried)


def spread_kernel(count, where, left, right, even, odd, part):
    size = part.shape[1] // count
    part[...] = dot_cols(left[...], right[...]).astype(low)
    for i in range(count):
        (odd if i % 2 else even)[:, i // 2 * size : (i // 2 + 1) * size] = part[
            :, column_block(where, i, size)
        ]


def spread_dot(where, left, right, column, count):
    rows, depth = left.shape
    width = right.shape[0]
    tile = 256
    spec = lambda columns: pl.BlockSpec((tile, columns), lambda i, where: (i, 0))
    half = jax.ShapeDtypeStruct((rows, width // 2), low)
    return pl.pallas_call(
        functools.partial(spread_kernel, count),
        grid_spec=pltpu.PrefetchScalarGridSpec(
            num_scalar_prefetch=1,
            grid=(rows // tile,),
            in_specs=[
                spec(depth),
                pl.BlockSpec((width, depth), lambda i, where: (0, column)),
            ],
            out_specs=[spec(width // 2)] * 2,
            scratch_shapes=[pltpu.VMEM((tile, width), low)],
        ),
        out_shape=[half, half],
        compiler_params=limits(48),
        cost_estimate=cost(2 * rows * width * depth, (rows * (width + depth) + width * depth) * 2),
        name="spread",
    )(where, left, right)


def up_kernel(where, act, own, came, out, held, sems):
    place_rows(down_pieces(own, came), held, sems, where[1], pl.program_id(0) == 0)
    out[...] = dot_cols(act[...], held[...]).astype(low)


def up_pass(where, act, own, came):
    total, hidden = act.shape
    width = 2 * own.shape[0]
    tile = 256
    spec = lambda columns: pl.BlockSpec((tile, columns), lambda i, where: (i, 0))
    return pl.pallas_call(
        up_kernel,
        grid_spec=pltpu.PrefetchScalarGridSpec(
            num_scalar_prefetch=1,
            grid=(total // tile,),
            in_specs=[spec(hidden)] + [pl.BlockSpec(memory_space=pl.ANY)] * 2,
            out_specs=spec(width),
            scratch_shapes=[pltpu.VMEM((width, hidden), low), pltpu.SemaphoreType.DMA((2,))],
        ),
        out_shape=jax.ShapeDtypeStruct((total, width), low),
        compiler_params=limits(48),
        cost_estimate=cost(
            2 * total * width * hidden, (total * (width + hidden) + width * hidden) * 2
        ),
        name="up",
    )(where, act, own, came)


def expert_kernel(count, carried, where, *refs):
    blocks, refs = refs[:count], refs[count:]
    number = 2 + len(cuts)
    weights, (raw, routed, router) = refs[:number], refs[number : number + 3]
    rows_out, act_out, grad_out, even, odd, gate_grad, pair, part, sems = refs[
        number + 3 + carried :
    ]
    size = blocks[0].shape[1]
    hidden = raw.shape[1]
    place_rows(pair_pieces(*weights), pair, sems, where[1], pl.program_id(0) == 0)
    for i, ref in enumerate(blocks):
        rows_out[:, column_block(where, i, size)] = ref[...]
    both = jnp.dot(rows_out[...], pair[...], preferred_element_type=full)
    pre_gate = both[:, :hidden]
    pre_up = both[:, hidden:]
    sigma = 1.0 / (1.0 + jnp.exp(-pre_gate))
    silu = pre_gate * sigma
    act = silu * pre_up
    back = raw[...].astype(full)
    tile = back.shape[0]
    own = where[2].astype(full)
    other = jnp.broadcast_to(routed[...], (128, tile)).T - own
    logits = jnp.dot(rows_out[...], router[...], preferred_element_type=full)
    lane = lax.broadcasted_iota(jnp.int32, (tile, 128), 1).astype(full)
    ahead = jnp.where(lane == other, logits, 0.0) - jnp.where(lane == own, logits, 0.0)
    gate = 1.0 / (1.0 + jnp.exp(jnp.sum(ahead, axis=1, keepdims=True)))
    gate_sum = jnp.sum(act * back, axis=1, keepdims=True)
    gate_grad[...] = jnp.broadcast_to(gate_sum, (tile, 128)).T[:1]
    act_out[...] = (act * gate).astype(low)
    back = back * gate
    grad_out[:, :hidden] = (back * pre_up * sigma * (1.0 + pre_gate * (1.0 - sigma))).astype(low)
    grad_out[:, hidden:] = (back * silu).astype(low)
    part[...] = dot_cols(grad_out[...], pair[...]).astype(low)
    for i in range(count):
        (odd if i % 2 else even)[:, i // 2 * size : (i // 2 + 1) * size] = part[
            :, column_block(where, i, size)
        ]


def expert_pass(step, where, blocks, weights, raw, routed, router, carried):
    count = len(blocks)
    size = blocks[0].shape[1]
    width, hidden = 2 * weights[0].shape[0], weights[0].shape[1]
    both = 2 * hidden
    total = raw.shape[0]
    tile = 256
    steps = MOST // tile
    here = lambda i, where: (step * steps + i, 0)
    near = lambda i, where: (i, 0)
    near_spec = lambda columns: pl.BlockSpec((tile, columns), near)
    here_spec = lambda columns: pl.BlockSpec((tile, columns), here)
    row_spec = pl.BlockSpec((1, tile), lambda i, where: (0, i))
    anywhere = pl.BlockSpec(memory_space=pl.ANY)
    shape = lambda r, c, t=low: jax.ShapeDtypeStruct((r, c), t)
    return pl.pallas_call(
        functools.partial(expert_kernel, count, len(carried)),
        grid_spec=pltpu.PrefetchScalarGridSpec(
            num_scalar_prefetch=1,
            grid=(steps,),
            in_specs=[near_spec(size)] * count
            + [anywhere] * len(weights)
            + [
                here_spec(hidden),
                row_spec,
                pl.BlockSpec((width, 128), lambda i, where: (0, 0)),
            ]
            + [anywhere] * len(carried),
            out_specs=[
                here_spec(width),
                here_spec(hidden),
                here_spec(both),
                near_spec(width // 2),
                near_spec(width // 2),
                row_spec,
            ],
            scratch_shapes=[
                pltpu.VMEM((width, both), low),
                pltpu.VMEM((tile, width), low),
                pltpu.SemaphoreType.DMA((2 + sum(len(cut) for cut in cuts),)),
            ],
        ),
        out_shape=[
            shape(total, width),
            shape(total, hidden),
            shape(total, both),
            shape(MOST, width // 2),
            shape(MOST, width // 2),
            shape(1, MOST, full),
        ],
        input_output_aliases={
            count + len(weights) + 4 + i: i for i in range(len(carried))
        },
        compiler_params=limits(60),
        cost_estimate=cost(
            4 * MOST * width * both, width * both * 2 + MOST * (width * 8 + hidden * 8), MOST * hidden
        ),
        name="expert",
    )(where, *blocks, *weights, raw, routed, router, *carried)


def expert_grad_kernel(hidden, pieces, per, *refs):
    out = refs[-1]
    which, at = pl.program_id(0), pl.program_id(1)

    def add(ref, other):
        out[0] = (ref[...].astype(full) + other[...].astype(full))[:, :hidden]

    for k in range(pieces):

        @pl.when((which < 2) & (at // per == k))
        def _():
            add(refs[0], refs[1 + k])

    @pl.when(which == 2)
    def _():
        add(refs[1 + pieces], refs[2 + pieces])


def expert_grad_sum(pair, down, hidden):
    rows, padded = down[0].shape
    tile = min(256, rows)
    pieces = len(pair) - 1
    per = rows // tile // pieces
    last = rows // tile - 1

    def piece_spec(k):
        return pl.BlockSpec(
            (tile, padded),
            lambda w, i: (
                jnp.where(w == 2, per - 1, jnp.clip(i - k * per, 0, per - 1)),
                jnp.minimum(w, 1),
            ),
        )

    pair_spec = pl.BlockSpec(
        (tile, padded), lambda w, i: (jnp.where(w == 2, last, i), jnp.minimum(w, 1))
    )
    down_spec = pl.BlockSpec((tile, padded), lambda w, i: (jnp.where(w == 2, i, 0), 0))
    return pl.pallas_call(
        functools.partial(expert_grad_kernel, hidden, pieces, per),
        grid=(3, rows // tile),
        in_specs=[pair_spec] + [piece_spec(k) for k in range(pieces)] + [down_spec] * 2,
        out_specs=pl.BlockSpec((1, tile, hidden), lambda w, i: (w, i, 0)),
        out_shape=jax.ShapeDtypeStruct((3, rows, hidden), full),
        compiler_params=limits(40),
        cost_estimate=cost(rows * padded * 3, rows * padded * 24),
        name="expert_grad_sum",
    )(*pair, *down)


def near_blocks(own, *others):
    held = [own]
    for bit in range(levels_of(lax.axis_size("tensor")))[::-1]:
        theirs = [swap(v, "tensor", 1 << bit) for v in held]
        if bit and others:
            theirs = [after(v, *others) for v in theirs]
        held = [v for pair in zip(held, theirs) for v in pair]
    return held


def near_reduce(even, odd, meet, *others, filler=None):
    count = lax.axis_size("tensor")
    number = count // 2
    size = even.shape[1] // number
    came = swap(odd, "tensor", 1)
    for bit in range(1, levels_of(count)):
        blocks = [
            even[:, i * size : (i + 1) * size].astype(full)
            + came[:, i * size : (i + 1) * size].astype(full)
            for i in range(number)
        ]
        sent = jnp.concatenate([v.astype(low) for v in blocks[1::2]], 1)
        if bit == levels_of(count) - 1:
            sent = after(sent, *others)
            meet.append(sent)
        even = jnp.concatenate(blocks[::2], 1)
        came = swap(sent, "tensor", 1 << bit)
        if filler is not None and bit == levels_of(count) - 1:
            came = after(came, *filler(sent))
        number //= 2
    return even.astype(full) + came.astype(full)


def half_gather(local, group_count):
    held = local
    place = lax.axis_index("dp") % group_count
    for bit in range(levels_of(group_count) - 1):
        came = swap(held, "dp", 1 << bit)
        upper = side_of(place, bit)
        held = jnp.concatenate([jnp.where(upper, came, held), jnp.where(upper, held, came)], 0)
    return held


def group_finish(kept, came, position, group_count):
    if group_count > 2:
        came = jnp.concatenate(came, 0)
    for bit in range(levels_of(group_count) - 1)[::-1]:
        current = kept.astype(full) + came.astype(full)
        middle = current.shape[0] // 2
        upper = (position >> bit) & 1
        kept = lax.dynamic_slice_in_dim(current, upper * middle, middle, 0)
        given = lax.dynamic_slice_in_dim(current, (1 - upper) * middle, middle, 0)
        came = swap(given.astype(low), "dp", 1 << bit)
    return [kept, *came] if isinstance(came, list) else [kept, came]


def body(
    tokens,
    attn_gain,
    qkv_weight,
    out_weight,
    moe_gain,
    router_weight,
    expert_weight,
    routes,
    cotangent,
):
    rows = tokens.shape[0]
    width = tokens.shape[1]
    tensor_count = lax.axis_size("tensor")
    dp_count = lax.axis_size("dp")
    group_count = dp_count // EXPERTS
    size = width // tensor_count
    hidden_size = expert_weight.shape[2]
    padded = -(-hidden_size // 128) * 128
    scale = 1.0 / math.sqrt(HEAD)
    place = lax.axis_index("tensor")
    index = lax.axis_index("dp")
    expert = index // group_count
    member = index % group_count
    top_half = member >> (levels_of(group_count) - 1)
    where = jnp.stack([place, top_half, expert]).astype(jnp.int32)

    def own_columns(value):
        return lax.dynamic_slice_in_dim(value, place * size, size, 1)

    extras = jnp.concatenate([router_weight, attn_gain[:, None], moe_gain[:, None]], 1)
    extras = jnp.pad(extras, ((0, 0), (0, 128 - extras.shape[1])))
    first = lax.all_gather(
        jnp.concatenate([qkv_weight.reshape(-1, 3 * size), out_weight, extras], 1),
        "dp",
        axis=0,
        tiled=True,
    )
    qkv_flat = first[:, : 3 * size]
    out_full = first[:, 3 * size : 4 * size]
    small = first[:, 4 * size :].T
    router_full = small[:EXPERTS]
    gain_first = small[EXPERTS : EXPERTS + 1].astype(full)
    gain_second = small[EXPERTS + 1 : EXPERTS + 2].astype(full)
    gain_first_own = own_columns(gain_first)
    gain_second_own = own_columns(gain_second)
    router_own = own_columns(router_full)

    near = jnp.arange(EXPERTS, dtype=jnp.int32) ^ expert
    names = jnp.arange(EXPERTS, dtype=jnp.int32)
    hits = jnp.sum((routes.T[None] == names[:, None, None]).astype(jnp.int32), 1)
    rank = jnp.cumsum(hits, axis=1) - hits
    slot_near = jnp.take(jnp.where(hits > 0, rank, -1), near, axis=0)
    places = jnp.arange(MOST, dtype=jnp.int32)[:, None]
    chosen = [(places == slot_near[s][None, :]).astype(low) for s in range(EXPERTS)]

    def packed(own):
        return [jnp.dot(c, own, preferred_element_type=full).astype(low) for c in chosen]

    def exchange(parts):
        return [parts[0]] + [swap(parts[s], "dp", s * group_count) for s in range(1, EXPERTS)]

    def unpacked(parts):
        total = contract(chosen[0], parts[0], 0, 0)
        for c, part in zip(chosen[1:], parts[1:]):
            total = total + contract(c, part, 0, 0)
        return total

    def widened(value):
        return jnp.pad(value, ((0, 0), (0, padded - hidden_size)))

    gate_mine, up_mine, down_mine = [
        half_gather(widened(expert_weight[k]), group_count) for k in range(3)
    ]
    half = width // 2
    mine_at, given_at = top_half * half, (1 - top_half) * half
    reach = group_count // 2

    def group_send(given, *others):
        return swap(after(given, *others), "dp", reach)

    down = (down_mine, group_send(down_mine))
    crossing = []

    def cross(*others):
        pieces = [
            (gate_mine, up_mine)[which][start * half // 128 : stop * half // 128]
            for which, start, stop in cuts[len(crossing)]
        ]
        crossing.append(group_send(jnp.concatenate(pieces, 0), *crossing[-1:], *others))

    cross(first)

    grad_own = own_columns(cotangent)
    grad_mine = jnp.dot(chosen[0], cotangent, preferred_element_type=full).astype(low)
    planes = [
        [m + g * group_count for g in range(EXPERTS)] for m in range(group_count)
    ]
    grad_planes = lax.all_gather(
        after(grad_own, first), "dp", axis=0, tiled=True, axis_index_groups=planes
    )
    slots_came = exchange([slot_near[s][None].astype(full) for s in range(EXPERTS)])
    route_sums = jnp.sum(routes, axis=1)[None].astype(low)
    routed = exchange([contract(route_sums, c, 1, 1) for c in chosen])

    inputs = tokens.astype(full)
    scale_one = lax.rsqrt(jnp.mean(inputs * inputs, axis=1, keepdims=True) + epsilon)
    normed_in = (inputs * scale_one * gain_first).astype(low)
    inputs_own = own_columns(tokens).astype(full)
    normed_in = after(normed_in, down[1], grad_mine, *slots_came, *routed)
    qkv = jnp.dot(normed_in, qkv_flat, preferred_element_type=full)
    cross(qkv)
    cosine, sine = rotary_tables()
    context, query, keys, values, logs = attention(qkv, cosine, sine, scale)
    context = after(context, crossing[1])
    cross(context)
    attn_parts = spread_dot(where, context, first, 3, tensor_count)
    rows_raw = []

    total = EXPERTS * MOST

    def down_filler(sent):
        cross(sent)
        rows_raw.extend(down_pass(where, after(grad_mine, sent), *down, 0, total, ()))
        return (rows_raw[1], crossing[3])

    hidden = inputs_own + near_reduce(*attn_parts, [], crossing[2], filler=down_filler)
    cross(rows_raw[1])
    grad_planes = after(grad_planes, hidden)
    grad_packed = []
    for s in order[1:]:
        source = lax.dynamic_slice_in_dim(grad_planes, (expert ^ s) * rows, rows, 0)
        taken = (places.astype(full) == slots_came[s]).astype(low)
        grad_packed.append(jnp.dot(taken, source, preferred_element_type=full).astype(low))
    grad_rest = lax.all_gather(jnp.concatenate(grad_packed, 0), "tensor", axis=1, tiled=True)

    scaled_hidden = (hidden * gain_second_own).astype(low)
    sums = tensor_sum(
        jnp.concatenate(
            [contract(router_own, scaled_hidden, 1, 1), jnp.sum(hidden * hidden, 1)[None]], 0
        )
    )
    scale_two_row = lax.rsqrt(sums[EXPERTS:] / width + epsilon)
    scale_two = scale_two_row.reshape(rows, 1)
    logits = sums[:EXPERTS] * scale_two_row
    normed_two = hidden * scale_two
    moe_in = (normed_two * gain_second_own).astype(low)
    named = hits > 0
    top = jnp.max(jnp.where(named, logits, masked_out), axis=0, keepdims=True)
    weight = jnp.where(named, jnp.exp(logits - top), 0.0)
    gates = weight / jnp.sum(weight, axis=0, keepdims=True)

    def three_parts(value):
        a = value.astype(low)
        b = (value - a.astype(full)).astype(low)
        return jnp.stack([a, b, (value - a.astype(full) - b.astype(full)).astype(low)])

    moe_packed = packed(moe_in)
    pair = (gate_mine, up_mine, *crossing)
    crossed = {2: swap(moe_packed[2], "dp", 2 * group_count)}
    crossed[3] = swap(after(moe_packed[3], crossed[2]), "dp", 3 * group_count)
    arrived = [near_blocks(moe_packed[0])]

    carried = ()
    sums_sent = []
    came_home = {}
    returned = []
    gate_grads = []
    router_block = first[:, 4 * size :]
    for step in range(EXPERTS):
        named_sum = routed[order[step]]
        if step == 1:
            rows_raw = down_pass(where, after(grad_rest, even), *down, MOST, total, rows_raw)
            named_sum = after(named_sum, crossed[3])
        if step == 2:
            named_sum = after(named_sum, crossed[1], sums_sent[0])
        if step == 3:
            named_sum = after(named_sum, sums_sent[1])
        moe_rows, activation, pre_grad, even, odd, gate_grad = expert_pass(
            step, where, arrived[step], pair, rows_raw[1], named_sum, router_block, carried
        )
        carried = (moe_rows, activation, pre_grad)
        if step == 0:
            arrived.append(near_blocks(crossed[2], even))
            crossed[3] = after(crossed[3], even)
            crossed[1] = swap(after(moe_packed[1], crossed[3]), "dp", group_count)
        if step == 1:
            arrived.append(near_blocks(crossed[3], even))
            odd = after(odd, crossed[1], arrived[2][tensor_count // 2])
        if step == 2:
            arrived.append(near_blocks(crossed[1], even))
        if step == 2:
            odd = after(odd, *returned, arrived[3][tensor_count // 2])
        if step == 3:
            came_home[2] = swap(returned[0], "dp", 2 * group_count)
            odd = after(odd, returned[1], came_home[2])
        if step == 0:
            own_parts = (even, odd)
        else:
            returned.append(near_reduce(even, odd, sums_sent).astype(low))
        gate_grads.append(gate_grad)

    def home(parts):
        return {
            s: swap(v, "dp", s * group_count) if s else v for s, v in zip(order, parts)
        }

    came_home[3] = swap(returned[1], "dp", 3 * group_count)
    came_home[1] = swap(returned[2], "dp", group_count)
    own_even, own_odd = own_parts
    came_home[0] = near_reduce(own_even, after(own_odd, sums_sent[2]), []).astype(low)
    gate_grad_near = home([gate_grads[0]] + [after(v, even) for v in gate_grads[1:]])
    grad_rows = rows_raw[0]

    def term(left, right):
        def part(start, number):
            taken = lax.dynamic_slice_in_dim(left, start, number, 1)
            return contract(taken, right, 0, 0).astype(low)

        return part

    unit = half // 128
    quarter = half // 2
    act_late = after(activation, sums_sent[2], returned[1])
    down_given = term(grad_rows, act_late)(given_at, half)
    down_sums = [group_send(down_given[: 56 * unit])]
    expert_part = up_pass(
        where, after(activation, down_given, returned[2], *gate_grad_near.values()), *down
    )
    expert_part = after(expert_part, down_sums[0], *came_home.values())
    expert_own = lax.psum_scatter(expert_part, "tensor", scatter_dimension=1, tiled=True)
    came_home = {s: after(v, expert_part) for s, v in came_home.items()}
    back = unpacked([came_home[s] for s in range(EXPERTS)])

    gate_grad = jnp.concatenate(
        [
            jnp.sum(contract(three_parts(gate_grad_near[s][0]), chosen[s], 1, 0), 0, keepdims=True)
            for s in range(EXPERTS)
        ],
        0,
    )
    scaled_back = back * gain_second_own
    sums = tensor_sum(
        jnp.concatenate([gate_grad, jnp.sum(scaled_back * normed_two, axis=1)[None]], 0)
    )
    gate_grad = jnp.take(sums[:EXPERTS], near, axis=0)
    weighted = jnp.sum(gates * gate_grad, axis=0, keepdims=True)
    logit_grad = (gates * (gate_grad - weighted)).astype(low)
    mean_two = (
        sums[EXPERTS:] + jnp.sum(logit_grad.astype(full) * logits, axis=0, keepdims=True)
    ) / width
    moe_grad = contract(logit_grad, router_own, 0, 0) + back

    grad_out = grad_own.astype(full)
    hidden_grad = grad_out + scale_two * (
        moe_grad * gain_second_own - normed_two * mean_two.reshape(rows, 1)
    )
    router_grad = jnp.dot(logit_grad, moe_in, preferred_element_type=full)
    moe_gain_grad = jnp.sum(moe_grad * normed_two, axis=0)
    pair_given = []
    kept = []

    def give_pair(sent):
        down_sums.append(group_send(down_given[56 * unit : 112 * unit], down_sums[0], sent))
        pair_term = term(moe_rows, after(pre_grad, sent))
        pair_given.extend(pair_term(given_at + k * quarter, quarter) for k in range(2))
        return (*pair_given, down_sums[1])

    attn_grad = tensor_gather(hidden_grad.astype(low), give_pair)
    down_sums.append(group_send(down_given[112 * unit :], down_sums[1]))
    pair_sums = [group_send(pair_given[0][: 12 * unit], down_sums[1])]
    context_grad = jnp.dot(attn_grad, out_full, preferred_element_type=full).astype(low)
    out_grad = contract(after(attn_grad, context_grad), context, 0, 0).astype(low)
    qkv_grad_rows = attention_back(query, keys, values, logs, context_grad, cosine, sine, scale)
    qkv_grad_rows = after(qkv_grad_rows, pair_sums[0], down_sums[2], out_grad)
    qkv_grad = contract(normed_in, qkv_grad_rows, 0, 0).astype(low)
    grads_both = jnp.concatenate([qkv_grad, out_grad], 1)
    shards = lax.psum_scatter(grads_both, "dp", scatter_dimension=0, tiled=True)
    pair_sums.append(group_send(pair_given[0][12 * unit :], pair_sums[0], grads_both))
    pair_last = group_send(pair_given[1], pair_sums[0], grads_both)
    outputs = {0: expert_own[:MOST]}
    part = after(expert_own[MOST : 2 * MOST], grads_both)
    outputs[2] = swap(part, "dp", 2 * group_count)

    def keep(sent):
        late = after(pre_grad, sent, expert_own)
        kept.append(term(moe_rows, late)(mine_at, half))
        kept.append(term(grad_rows, after(activation, kept[0], outputs[2]))(mine_at, half))
        return kept

    parts = spread_dot(where, after(qkv_grad_rows, grads_both), first, 0, tensor_count)
    normed_grad = near_reduce(*parts, [], filler=keep)
    for k in (2, 3):
        part = after(expert_own[k * MOST : (k + 1) * MOST], outputs[2])
        outputs[order[k]] = swap(part, "dp", order[k] * group_count)
    normed_one = inputs_own * scale_one
    scaled_in = normed_grad * gain_first_own
    attn_gain_grad = jnp.sum(normed_grad * normed_one, axis=0)
    mean_one = tensor_sum(jnp.sum(scaled_in * normed_one, axis=1)[None]) / width
    input_own = hidden_grad + scale_one * (scaled_in - normed_one * mean_one.reshape(rows, 1))
    mine = jnp.concatenate([router_grad, attn_gain_grad[None], moe_gain_grad[None]], 0)
    mine = lax.dynamic_update_slice_in_dim(
        jnp.zeros((mine.shape[0], width), full), mine, place * size, 1
    )
    mine = all_sum(mine)
    expert_grad = expert_grad_sum(
        group_finish(kept[0], [jnp.concatenate(pair_sums, 0), pair_last], member, group_count),
        group_finish(kept[1], [jnp.concatenate(down_sums, 0)], member, group_count),
        hidden_size,
    )
    input_grad = tensor_gather(input_own.astype(low), lambda sent: (mine, outputs[3], outputs[1]))
    input_grad = input_grad.astype(full)
    layer_own = hidden + unpacked([outputs[s] for s in range(EXPERTS)])
    layer_out = tensor_gather(layer_own.astype(low)).astype(full)
    share = width // dp_count
    mine = lax.dynamic_slice_in_dim(mine, index * share, share, 1)
    shards = shards.astype(full)
    qkv_shard, out_shard = shards[:, : 3 * size], shards[:, 3 * size :]
    return (
        layer_out,
        input_grad,
        mine[EXPERTS],
        qkv_shard.reshape(share, 3, size),
        out_shard,
        mine[EXPERTS + 1],
        mine[:EXPERTS].T,
        expert_grad,
    )


def solution(mesh):
    placed = (
        P("dp", None),
        P("dp"),
        P("dp", None, "tensor"),
        P("dp", "tensor"),
        P("dp"),
        P("dp", None),
        P(None, "dp", "tensor"),
        P("dp", None),
        P("dp", None),
    )
    return jax.shard_map(
        body,
        mesh=mesh,
        in_specs=placed,
        out_specs=(
            P("dp", None),
            P("dp", None),
            P("dp"),
            P("dp", None, "tensor"),
            P("dp", "tensor"),
            P("dp"),
            P("dp", None),
            P(None, "dp", "tensor"),
        ),
        check_vma=False,
    )
```

```python
import functools
import math

import jax
import jax.numpy as jnp
from jax import lax
from jax.experimental import pallas as pl
from jax.experimental.pallas import tpu as pltpu
from jax.sharding import PartitionSpec as P

HEAD = 128
EXPERTS = 4
SEQ = 1024
BLOCK = 256
MOST = 768


epsilon = 1e-05
theta_base = 10000.0
masked_out = -1e30
low = jnp.bfloat16
full = jnp.float32


def swap(value, axis, distance):
    return lax.ppermute(value, axis, [(i, i ^ distance) for i in range(lax.axis_size(axis))])


def contract(left, right, left_dim, right_dim):
    return lax.dot_general(
        left, right, (((left_dim,), (right_dim,)), ((), ())), preferred_element_type=jnp.float32
    )


def levels_of(count):
    return count.bit_length() - 1


def side_of(index, bit):
    return (index >> bit) & 1 == 1


def tensor_sum(value):
    for bit in range(levels_of(lax.axis_size("tensor"))):
        value = value + swap(value, "tensor", 1 << bit)
    return value


def all_sum(value):
    for axis in ("tensor", "dp"):
        for bit in range(levels_of(lax.axis_size(axis))):
            value = value + swap(value, axis, 1 << bit)
    return value


def tensor_gather(own, filler=None):
    count = lax.axis_size("tensor")
    place = lax.axis_index("tensor")
    size = own.shape[1]
    held = own
    order = list(range(levels_of(count)))[::-1]
    for bit in order:
        came = swap(held, "tensor", 1 << bit)
        if filler is not None and bit == order[0]:
            came = after(came, *filler(held))
        upper = side_of(place, bit)
        number = held.shape[1] // size
        mine = [held[:, i * size : (i + 1) * size] for i in range(number)]
        theirs = [came[:, i * size : (i + 1) * size] for i in range(number)]
        pairs = []
        for a, b in zip(mine, theirs):
            pairs.append((jnp.where(upper, b, a), jnp.where(upper, a, b)))
        held = jnp.concatenate([v for pair in pairs for v in pair], 1)
    return held


def after(value, *others):
    return lax.optimization_barrier((value, *others))[0]


def rotary_tables():
    half = HEAD // 2
    freqs = theta_base ** (-(jnp.arange(half, dtype=full) * 2.0 / HEAD))
    angles = jnp.arange(SEQ, dtype=full)[:, None] * freqs[None, :]
    cosine = jnp.cos(angles)
    sine = jnp.sin(angles)
    return (jnp.concatenate([cosine, cosine], 1), jnp.concatenate([-sine, sine], 1))


def limits(mib):
    return pltpu.CompilerParams(vmem_limit_bytes=mib << 20)


def cost(flops, moved, powers=0):
    return pl.CostEstimate(flops=int(flops), bytes_accessed=int(moved), transcendentals=int(powers))


def dot_cols(a, b):
    return lax.dot_general(a, b, (((1,), (1,)), ((), ())), preferred_element_type=full)


def dot_rows(a, b):
    return lax.dot_general(a, b, (((0,), (0,)), ((), ())), preferred_element_type=full)


def attention_kernel(scale, q_in, k_in, v_in, cos, sin, out, q_out, k_out, v_out, logs):
    def turned(ref):
        x = ref[...]
        return (x * cos[...] + pltpu.roll(x, HEAD // 2, 1) * sin[...]).astype(low)

    q_out[...] = turned(q_in)
    k_out[...] = turned(k_in)
    v_out[...] = v_in[...].astype(low)
    for block in range(SEQ // BLOCK):
        mine = pl.ds(block * BLOCK, BLOCK)
        seen = pl.ds(0, (block + 1) * BLOCK)
        scores = dot_cols(q_out[mine, :], k_out[seen, :]) * scale
        peak = jnp.max(scores, axis=1, keepdims=True)
        expo = jnp.exp(scores - peak)
        total = jnp.sum(expo, axis=1, keepdims=True)
        probs = (expo / total).astype(low)
        out[mine, :] = jnp.dot(probs, v_out[seen, :], preferred_element_type=full).astype(low)
        logs[0, mine, :] = peak + jnp.log(total)


def attention(qkv, cosine, sine, scale):
    rows = qkv.shape[0]
    size = qkv.shape[1] // 3
    heads = size // HEAD
    block = (SEQ, HEAD)
    table = pl.BlockSpec(block, lambda s, h: (0, 0))
    spec = pl.BlockSpec(block, lambda s, h: (s, h))
    shape = jax.ShapeDtypeStruct((rows, size), low)
    pairs = rows * heads * SEQ * 5 // 8
    return pl.pallas_call(
        functools.partial(attention_kernel, scale),
        grid=(rows // SEQ, heads),
        in_specs=[
            pl.BlockSpec(block, lambda s, h: (s, h)),
            pl.BlockSpec(block, lambda s, h: (s, heads + h)),
            pl.BlockSpec(block, lambda s, h: (s, 2 * heads + h)),
            table,
            table,
        ],
        out_specs=[spec] * 4 + [pl.BlockSpec((1, SEQ, 1), lambda s, h: (h, s, 0))],
        out_shape=[shape] * 4 + [jax.ShapeDtypeStruct((heads, rows, 1), full)],
        compiler_params=limits(48),
        cost_estimate=cost(4 * pairs * HEAD, rows * size * 20, pairs),
        name="attention",
    )(qkv, qkv, qkv, cosine, sine)


def attention_back_kernel(scale, heads, q_in, k_in, v_in, logs, grad, cos, sin, out, dk, dv):
    head = pl.program_id(1)
    dk[...] = jnp.zeros_like(dk)
    dv[...] = jnp.zeros_like(dv)

    def columns(which):
        return pl.ds(pl.multiple_of((which * heads + head) * HEAD, HEAD), HEAD)

    def turned(x, at):
        return (x * cos[at, :] - pltpu.roll(x, HEAD // 2, 1) * sin[at, :]).astype(low)

    for block in range(SEQ // BLOCK):
        mine = pl.ds(block * BLOCK, BLOCK)
        seen = pl.ds(0, (block + 1) * BLOCK)
        query, keys, values, given = q_in[mine, :], k_in[seen, :], v_in[seen, :], grad[mine, :]
        probs = jnp.exp(dot_cols(query, keys) * scale - logs[0, mine, :])
        prob_grad = dot_cols(given, values)
        inner = jnp.sum(probs * prob_grad, axis=1, keepdims=True)
        score_grad = (probs * (prob_grad - inner)).astype(low)
        query_grad = jnp.dot(score_grad, keys, preferred_element_type=full) * scale
        out[mine, columns(0)] = turned(query_grad, mine)
        dk[seen, :] += dot_rows(score_grad, query)
        dv[seen, :] += dot_rows(probs.astype(low), given)
    whole = pl.ds(0, SEQ)
    out[:, columns(1)] = turned(dk[...] * scale, whole)
    out[:, columns(2)] = dv[...].astype(low)


def attention_back(query, keys, values, logs, grad, cosine, sine, scale):
    rows, size = query.shape
    heads = size // HEAD
    block = (SEQ, HEAD)
    table = pl.BlockSpec(block, lambda s, h: (0, 0))
    spec = pl.BlockSpec(block, lambda s, h: (s, h))
    pairs = rows * heads * SEQ * 5 // 8
    return pl.pallas_call(
        functools.partial(attention_back_kernel, scale, heads),
        grid=(rows // SEQ, heads),
        in_specs=[spec] * 3
        + [pl.BlockSpec((1, SEQ, 1), lambda s, h: (h, s, 0)), spec, table, table],
        out_specs=pl.BlockSpec((SEQ, 3 * size), lambda s, h: (s, 0)),
        out_shape=jax.ShapeDtypeStruct((rows, 3 * size), low),
        scratch_shapes=[pltpu.VMEM(block, full)] * 2,
        compiler_params=limits(48),
        cost_estimate=cost(10 * pairs * HEAD, rows * size * 16, pairs),
        name="attention_back",
    )(query, keys, values, logs, grad, cosine, sine)


def place_rows(pieces, held, sems, upper, first):
    copies = []
    for ref, start, number, mine, there, column in pieces:
        half = held.shape[0] // 2
        columns = ref.shape[1]
        side = upper if mine else 1 - upper
        copies.append(
            pltpu.make_async_copy(
                ref.at[pl.ds(start, number), :],
                held.at[
                    pl.ds(pl.multiple_of(side * half + there, 64), number),
                    pl.ds(column * columns, columns),
                ],
                sems.at[len(copies)],
            )
        )

    @pl.when(first)
    def _():
        for copy in copies:
            copy.start()
        for copy in copies:
            copy.wait()


def down_pieces(own, came):
    half = own.shape[0]
    return [(own, 0, half, True, 0, 0), (came, 0, half, False, 0, 0)]


cuts = (
    ((0, 0, 16),),
    ((0, 16, 40),),
    ((0, 40, 56),),
    ((0, 56, 108),),
    ((0, 108, 128), (1, 0, 128)),
)
order = (0, 2, 3, 1)


def pair_pieces(own_gate, own_up, *came):
    half = own_gate.shape[0]
    pieces = [(own_gate, 0, half, True, 0, 0), (own_up, 0, half, True, 0, 1)]
    for cut, ref in zip(cuts, came):
        at = 0
        for which, start, stop in cut:
            number = (stop - start) * half // 128
            pieces.append((ref, at, number, False, start * half // 128, which))
            at += number
    return pieces


def column_block(where, i, size):
    return pl.ds(pl.multiple_of((i ^ where[0]) * size, size), size)


def down_kernel(carried, where, rows, own, came, *refs):
    rows_out, raw, held, sems = refs[carried:]
    place_rows(down_pieces(own, came), held, sems, where[1], pl.program_id(0) == 0)
    rows_out[...] = rows[...]
    raw[...] = jnp.dot(rows[...], held[...], preferred_element_type=full).astype(low)


def down_pass(where, rows, own, came, start, total, carried):
    number, width = rows.shape
    hidden = own.shape[1]
    tile = 256
    first = start // tile
    anywhere = pl.BlockSpec(memory_space=pl.ANY)
    here = lambda columns: pl.BlockSpec((tile, columns), lambda i, where: (first + i, 0))
    return pl.pallas_call(
        functools.partial(down_kernel, len(carried)),
        grid_spec=pltpu.PrefetchScalarGridSpec(
            num_scalar_prefetch=1,
            grid=(number // tile,),
            in_specs=[pl.BlockSpec((tile, width), lambda i, where: (i, 0))]
            + [anywhere] * (2 + len(carried)),
            out_specs=[here(width), here(hidden)],
            scratch_shapes=[pltpu.VMEM((width, hidden), low), pltpu.SemaphoreType.DMA((2,))],
        ),
        out_shape=[
            jax.ShapeDtypeStruct((total, width), low),
            jax.ShapeDtypeStruct((total, hidden), low),
        ],
        input_output_aliases={4 + i: i for i in range(len(carried))},
        compiler_params=limits(48),
        cost_estimate=cost(
            2 * number * width * hidden, (number * (2 * width + hidden) + width * hidden) * 2
        ),
        name="down",
    )(where, rows, own, came, *carried)


def spread_kernel(count, where, left, right, even, odd, part):
    size = part.shape[1] // count
    part[...] = dot_cols(left[...], right[...]).astype(low)
    for i in range(count):
        (odd if i % 2 else even)[:, i // 2 * size : (i // 2 + 1) * size] = part[
            :, column_block(where, i, size)
        ]


def spread_dot(where, left, right, column, count):
    rows, depth = left.shape
    width = right.shape[0]
    tile = 256
    spec = lambda columns: pl.BlockSpec((tile, columns), lambda i, where: (i, 0))
    half = jax.ShapeDtypeStruct((rows, width // 2), low)
    return pl.pallas_call(
        functools.partial(spread_kernel, count),
        grid_spec=pltpu.PrefetchScalarGridSpec(
            num_scalar_prefetch=1,
            grid=(rows // tile,),
            in_specs=[
                spec(depth),
                pl.BlockSpec((width, depth), lambda i, where: (0, column)),
            ],
            out_specs=[spec(width // 2)] * 2,
            scratch_shapes=[pltpu.VMEM((tile, width), low)],
        ),
        out_shape=[half, half],
        compiler_params=limits(48),
        cost_estimate=cost(2 * rows * width * depth, (rows * (width + depth) + width * depth) * 2),
        name="spread",
    )(where, left, right)


def up_kernel(where, act, own, came, out, held, sems):
    place_rows(down_pieces(own, came), held, sems, where[1], pl.program_id(0) == 0)
    out[...] = dot_cols(act[...], held[...]).astype(low)


def up_pass(where, act, own, came):
    total, hidden = act.shape
    width = 2 * own.shape[0]
    tile = 256
    spec = lambda columns: pl.BlockSpec((tile, columns), lambda i, where: (i, 0))
    return pl.pallas_call(
        up_kernel,
        grid_spec=pltpu.PrefetchScalarGridSpec(
            num_scalar_prefetch=1,
            grid=(total // tile,),
            in_specs=[spec(hidden)] + [pl.BlockSpec(memory_space=pl.ANY)] * 2,
            out_specs=spec(width),
            scratch_shapes=[pltpu.VMEM((width, hidden), low), pltpu.SemaphoreType.DMA((2,))],
        ),
        out_shape=jax.ShapeDtypeStruct((total, width), low),
        compiler_params=limits(48),
        cost_estimate=cost(
            2 * total * width * hidden, (total * (width + hidden) + width * hidden) * 2
        ),
        name="up",
    )(where, act, own, came)


def expert_kernel(count, carried, where, *refs):
    blocks, refs = refs[:count], refs[count:]
    number = 2 + len(cuts)
    weights, (raw, routed, router) = refs[:number], refs[number : number + 3]
    rows_out, act_out, grad_out, even, odd, gate_grad, pair, part, sems = refs[
        number + 3 + carried :
    ]
    size = blocks[0].shape[1]
    hidden = raw.shape[1]
    place_rows(pair_pieces(*weights), pair, sems, where[1], pl.program_id(0) == 0)
    for i, ref in enumerate(blocks):
        rows_out[:, column_block(where, i, size)] = ref[...]
    both = jnp.dot(rows_out[...], pair[...], preferred_element_type=full)
    pre_gate = both[:, :hidden]
    pre_up = both[:, hidden:]
    sigma = 1.0 / (1.0 + jnp.exp(-pre_gate))
    silu = pre_gate * sigma
    act = silu * pre_up
    back = raw[...].astype(full)
    tile = back.shape[0]
    own = where[2].astype(full)
    other = jnp.broadcast_to(routed[...], (128, tile)).T - own
    logits = jnp.dot(rows_out[...], router[...], preferred_element_type=full)
    lane = lax.broadcasted_iota(jnp.int32, (tile, 128), 1).astype(full)
    ahead = jnp.where(lane == other, logits, 0.0) - jnp.where(lane == own, logits, 0.0)
    gate = 1.0 / (1.0 + jnp.exp(jnp.sum(ahead, axis=1, keepdims=True)))
    gate_sum = jnp.sum(act * back, axis=1, keepdims=True)
    gate_grad[...] = jnp.broadcast_to(gate_sum, (tile, 128)).T[:1]
    act_out[...] = (act * gate).astype(low)
    back = back * gate
    grad_out[:, :hidden] = (back * pre_up * sigma * (1.0 + pre_gate * (1.0 - sigma))).astype(low)
    grad_out[:, hidden:] = (back * silu).astype(low)
    part[...] = dot_cols(grad_out[...], pair[...]).astype(low)
    for i in range(count):
        (odd if i % 2 else even)[:, i // 2 * size : (i // 2 + 1) * size] = part[
            :, column_block(where, i, size)
        ]


def expert_pass(step, where, blocks, weights, raw, routed, router, carried):
    count = len(blocks)
    size = blocks[0].shape[1]
    width, hidden = 2 * weights[0].shape[0], weights[0].shape[1]
    both = 2 * hidden
    total = raw.shape[0]
    tile = 256
    steps = MOST // tile
    here = lambda i, where: (step * steps + i, 0)
    near = lambda i, where: (i, 0)
    near_spec = lambda columns: pl.BlockSpec((tile, columns), near)
    here_spec = lambda columns: pl.BlockSpec((tile, columns), here)
    row_spec = pl.BlockSpec((1, tile), lambda i, where: (0, i))
    anywhere = pl.BlockSpec(memory_space=pl.ANY)
    shape = lambda r, c, t=low: jax.ShapeDtypeStruct((r, c), t)
    return pl.pallas_call(
        functools.partial(expert_kernel, count, len(carried)),
        grid_spec=pltpu.PrefetchScalarGridSpec(
            num_scalar_prefetch=1,
            grid=(steps,),
            in_specs=[near_spec(size)] * count
            + [anywhere] * len(weights)
            + [
                here_spec(hidden),
                row_spec,
                pl.BlockSpec((width, 128), lambda i, where: (0, 0)),
            ]
            + [anywhere] * len(carried),
            out_specs=[
                here_spec(width),
                here_spec(hidden),
                here_spec(both),
                near_spec(width // 2),
                near_spec(width // 2),
                row_spec,
            ],
            scratch_shapes=[
                pltpu.VMEM((width, both), low),
                pltpu.VMEM((tile, width), low),
                pltpu.SemaphoreType.DMA((2 + sum(len(cut) for cut in cuts),)),
            ],
        ),
        out_shape=[
            shape(total, width),
            shape(total, hidden),
            shape(total, both),
            shape(MOST, width // 2),
            shape(MOST, width // 2),
            shape(1, MOST, full),
        ],
        input_output_aliases={
            count + len(weights) + 4 + i: i for i in range(len(carried))
        },
        compiler_params=limits(60),
        cost_estimate=cost(
            4 * MOST * width * both, width * both * 2 + MOST * (width * 8 + hidden * 8), MOST * hidden
        ),
        name="expert",
    )(where, *blocks, *weights, raw, routed, router, *carried)


def expert_grad_kernel(hidden, pieces, per, *refs):
    out = refs[-1]
    which, at = pl.program_id(0), pl.program_id(1)

    def add(ref, other):
        out[0] = (ref[...].astype(full) + other[...].astype(full))[:, :hidden]

    for k in range(pieces):

        @pl.when((which < 2) & (at // per == k))
        def _():
            add(refs[0], refs[1 + k])

    @pl.when(which == 2)
    def _():
        add(refs[1 + pieces], refs[2 + pieces])


def expert_grad_sum(pair, down, hidden):
    rows, padded = down[0].shape
    tile = min(256, rows)
    pieces = len(pair) - 1
    per = rows // tile // pieces
    last = rows // tile - 1

    def piece_spec(k):
        return pl.BlockSpec(
            (tile, padded),
            lambda w, i: (
                jnp.where(w == 2, per - 1, jnp.clip(i - k * per, 0, per - 1)),
                jnp.minimum(w, 1),
            ),
        )

    pair_spec = pl.BlockSpec(
        (tile, padded), lambda w, i: (jnp.where(w == 2, last, i), jnp.minimum(w, 1))
    )
    down_spec = pl.BlockSpec((tile, padded), lambda w, i: (jnp.where(w == 2, i, 0), 0))
    return pl.pallas_call(
        functools.partial(expert_grad_kernel, hidden, pieces, per),
        grid=(3, rows // tile),
        in_specs=[pair_spec] + [piece_spec(k) for k in range(pieces)] + [down_spec] * 2,
        out_specs=pl.BlockSpec((1, tile, hidden), lambda w, i: (w, i, 0)),
        out_shape=jax.ShapeDtypeStruct((3, rows, hidden), full),
        compiler_params=limits(40),
        cost_estimate=cost(rows * padded * 3, rows * padded * 24),
        name="expert_grad_sum",
    )(*pair, *down)


def near_blocks(own, *others):
    held = [own]
    for bit in range(levels_of(lax.axis_size("tensor")))[::-1]:
        theirs = [swap(v, "tensor", 1 << bit) for v in held]
        if bit and others:
            theirs = [after(v, *others) for v in theirs]
        held = [v for pair in zip(held, theirs) for v in pair]
    return held


def near_reduce(even, odd, meet, *others, filler=None):
    count = lax.axis_size("tensor")
    number = count // 2
    size = even.shape[1] // number
    came = swap(odd, "tensor", 1)
    for bit in range(1, levels_of(count)):
        blocks = [
            even[:, i * size : (i + 1) * size].astype(full)
            + came[:, i * size : (i + 1) * size].astype(full)
            for i in range(number)
        ]
        sent = jnp.concatenate([v.astype(low) for v in blocks[1::2]], 1)
        if bit == levels_of(count) - 1:
            sent = after(sent, *others)
            meet.append(sent)
        even = jnp.concatenate(blocks[::2], 1)
        came = swap(sent, "tensor", 1 << bit)
        if filler is not None and bit == levels_of(count) - 1:
            came = after(came, *filler(sent))
        number //= 2
    return even.astype(full) + came.astype(full)


def half_gather(local, group_count):
    held = local
    place = lax.axis_index("dp") % group_count
    for bit in range(levels_of(group_count) - 1):
        came = swap(held, "dp", 1 << bit)
        upper = side_of(place, bit)
        held = jnp.concatenate([jnp.where(upper, came, held), jnp.where(upper, held, came)], 0)
    return held


def group_finish(kept, came, position, group_count):
    if group_count > 2:
        came = jnp.concatenate(came, 0)
    for bit in range(levels_of(group_count) - 1)[::-1]:
        current = kept.astype(full) + came.astype(full)
        middle = current.shape[0] // 2
        upper = (position >> bit) & 1
        kept = lax.dynamic_slice_in_dim(current, upper * middle, middle, 0)
        given = lax.dynamic_slice_in_dim(current, (1 - upper) * middle, middle, 0)
        came = swap(given.astype(low), "dp", 1 << bit)
    return [kept, *came] if isinstance(came, list) else [kept, came]


def body(
    tokens,
    attn_gain,
    qkv_weight,
    out_weight,
    moe_gain,
    router_weight,
    expert_weight,
    routes,
    cotangent,
):
    rows = tokens.shape[0]
    width = tokens.shape[1]
    tensor_count = lax.axis_size("tensor")
    dp_count = lax.axis_size("dp")
    group_count = dp_count // EXPERTS
    size = width // tensor_count
    hidden_size = expert_weight.shape[2]
    padded = -(-hidden_size // 128) * 128
    scale = 1.0 / math.sqrt(HEAD)
    place = lax.axis_index("tensor")
    index = lax.axis_index("dp")
    expert = index // group_count
    member = index % group_count
    top_half = member >> (levels_of(group_count) - 1)
    where = jnp.stack([place, top_half, expert]).astype(jnp.int32)

    def own_columns(value):
        return lax.dynamic_slice_in_dim(value, place * size, size, 1)

    extras = jnp.concatenate([router_weight, attn_gain[:, None], moe_gain[:, None]], 1)
    extras = jnp.pad(extras, ((0, 0), (0, 128 - extras.shape[1])))
    first = lax.all_gather(
        jnp.concatenate([qkv_weight.reshape(-1, 3 * size), out_weight, extras], 1),
        "dp",
        axis=0,
        tiled=True,
    )
    qkv_flat = first[:, : 3 * size]
    out_full = first[:, 3 * size : 4 * size]
    small = first[:, 4 * size :].T
    router_full = small[:EXPERTS]
    gain_first = small[EXPERTS : EXPERTS + 1].astype(full)
    gain_second = small[EXPERTS + 1 : EXPERTS + 2].astype(full)
    gain_first_own = own_columns(gain_first)
    gain_second_own = own_columns(gain_second)
    router_own = own_columns(router_full)

    near = jnp.arange(EXPERTS, dtype=jnp.int32) ^ expert
    names = jnp.arange(EXPERTS, dtype=jnp.int32)
    hits = jnp.sum((routes.T[None] == names[:, None, None]).astype(jnp.int32), 1)
    rank = jnp.cumsum(hits, axis=1) - hits
    slot_near = jnp.take(jnp.where(hits > 0, rank, -1), near, axis=0)
    places = jnp.arange(MOST, dtype=jnp.int32)[:, None]
    chosen = [(places == slot_near[s][None, :]).astype(low) for s in range(EXPERTS)]

    def packed(own):
        return [jnp.dot(c, own, preferred_element_type=full).astype(low) for c in chosen]

    def exchange(parts):
        return [parts[0]] + [swap(parts[s], "dp", s * group_count) for s in range(1, EXPERTS)]

    def unpacked(parts):
        total = contract(chosen[0], parts[0], 0, 0)
        for c, part in zip(chosen[1:], parts[1:]):
            total = total + contract(c, part, 0, 0)
        return total

    def widened(value):
        return jnp.pad(value, ((0, 0), (0, padded - hidden_size)))

    gate_mine, up_mine, down_mine = [
        half_gather(widened(expert_weight[k]), group_count) for k in range(3)
    ]
    half = width // 2
    mine_at, given_at = top_half * half, (1 - top_half) * half
    reach = group_count // 2

    def group_send(given, *others):
        return swap(after(given, *others), "dp", reach)

    down = (down_mine, group_send(down_mine))
    crossing = []

    def cross(*others):
        pieces = [
            (gate_mine, up_mine)[which][start * half // 128 : stop * half // 128]
            for which, start, stop in cuts[len(crossing)]
        ]
        crossing.append(group_send(jnp.concatenate(pieces, 0), *crossing[-1:], *others))

    cross(first)

    grad_own = own_columns(cotangent)
    grad_mine = jnp.dot(chosen[0], cotangent, preferred_element_type=full).astype(low)
    planes = [
        [m + g * group_count for g in range(EXPERTS)] for m in range(group_count)
    ]
    grad_planes = lax.all_gather(
        after(grad_own, first), "dp", axis=0, tiled=True, axis_index_groups=planes
    )
    slots_came = exchange([slot_near[s][None].astype(full) for s in range(EXPERTS)])
    route_sums = jnp.sum(routes, axis=1)[None].astype(low)
    routed = exchange([contract(route_sums, c, 1, 1) for c in chosen])

    inputs = tokens.astype(full)
    scale_one = lax.rsqrt(jnp.mean(inputs * inputs, axis=1, keepdims=True) + epsilon)
    normed_in = (inputs * scale_one * gain_first).astype(low)
    inputs_own = own_columns(tokens).astype(full)
    normed_in = after(normed_in, down[1], grad_mine, *slots_came, *routed)
    qkv = jnp.dot(normed_in, qkv_flat, preferred_element_type=full)
    cross(qkv)
    cosine, sine = rotary_tables()
    context, query, keys, values, logs = attention(qkv, cosine, sine, scale)
    context = after(context, crossing[1])
    cross(context)
    attn_parts = spread_dot(where, context, first, 3, tensor_count)
    rows_raw = []

    total = EXPERTS * MOST

    def down_filler(sent):
        cross(sent)
        rows_raw.extend(down_pass(where, after(grad_mine, sent), *down, 0, total, ()))
        return (rows_raw[1], crossing[3])

    hidden = inputs_own + near_reduce(*attn_parts, [], crossing[2], filler=down_filler)
    cross(rows_raw[1])
    grad_planes = after(grad_planes, hidden)
    grad_packed = []
    for s in order[1:]:
        source = lax.dynamic_slice_in_dim(grad_planes, (expert ^ s) * rows, rows, 0)
        taken = (places.astype(full) == slots_came[s]).astype(low)
        grad_packed.append(jnp.dot(taken, source, preferred_element_type=full).astype(low))
    grad_rest = lax.all_gather(jnp.concatenate(grad_packed, 0), "tensor", axis=1, tiled=True)

    scaled_hidden = (hidden * gain_second_own).astype(low)
    sums = tensor_sum(
        jnp.concatenate(
            [contract(router_own, scaled_hidden, 1, 1), jnp.sum(hidden * hidden, 1)[None]], 0
        )
    )
    scale_two_row = lax.rsqrt(sums[EXPERTS:] / width + epsilon)
    scale_two = scale_two_row.reshape(rows, 1)
    logits = sums[:EXPERTS] * scale_two_row
    normed_two = hidden * scale_two
    moe_in = (normed_two * gain_second_own).astype(low)
    named = hits > 0
    top = jnp.max(jnp.where(named, logits, masked_out), axis=0, keepdims=True)
    weight = jnp.where(named, jnp.exp(logits - top), 0.0)
    gates = weight / jnp.sum(weight, axis=0, keepdims=True)

    def three_parts(value):
        a = value.astype(low)
        b = (value - a.astype(full)).astype(low)
        return jnp.stack([a, b, (value - a.astype(full) - b.astype(full)).astype(low)])

    moe_packed = packed(moe_in)
    pair = (gate_mine, up_mine, *crossing)
    crossed = {2: swap(moe_packed[2], "dp", 2 * group_count)}
    crossed[3] = swap(after(moe_packed[3], crossed[2]), "dp", 3 * group_count)
    arrived = [near_blocks(moe_packed[0])]

    carried = ()
    sums_sent = []
    came_home = {}
    returned = []
    gate_grads = []
    router_block = first[:, 4 * size :]
    for step in range(EXPERTS):
        named_sum = routed[order[step]]
        if step == 1:
            rows_raw = down_pass(where, after(grad_rest, even), *down, MOST, total, rows_raw)
            named_sum = after(named_sum, crossed[3])
        if step == 2:
            named_sum = after(named_sum, crossed[1], sums_sent[0])
        if step == 3:
            named_sum = after(named_sum, sums_sent[1])
        moe_rows, activation, pre_grad, even, odd, gate_grad = expert_pass(
            step, where, arrived[step], pair, rows_raw[1], named_sum, router_block, carried
        )
        carried = (moe_rows, activation, pre_grad)
        if step == 0:
            arrived.append(near_blocks(crossed[2], even))
            crossed[3] = after(crossed[3], even)
            crossed[1] = swap(after(moe_packed[1], crossed[3]), "dp", group_count)
        if step == 1:
            arrived.append(near_blocks(crossed[3], even))
            odd = after(odd, crossed[1], arrived[2][tensor_count // 2])
        if step == 2:
            arrived.append(near_blocks(crossed[1], even))
        if step == 2:
            odd = after(odd, *returned, arrived[3][tensor_count // 2])
        if step == 3:
            came_home[2] = swap(returned[0], "dp", 2 * group_count)
            odd = after(odd, returned[1], came_home[2])
        if step == 0:
            own_parts = (even, odd)
        else:
            returned.append(near_reduce(even, odd, sums_sent).astype(low))
        gate_grads.append(gate_grad)

    def home(parts):
        return {
            s: swap(v, "dp", s * group_count) if s else v for s, v in zip(order, parts)
        }

    came_home[3] = swap(returned[1], "dp", 3 * group_count)
    came_home[1] = swap(returned[2], "dp", group_count)
    own_even, own_odd = own_parts
    came_home[0] = near_reduce(own_even, after(own_odd, sums_sent[2]), []).astype(low)
    gate_grad_near = home([gate_grads[0]] + [after(v, even) for v in gate_grads[1:]])
    grad_rows = rows_raw[0]

    def term(left, right):
        def part(start, number):
            taken = lax.dynamic_slice_in_dim(left, start, number, 1)
            return contract(taken, right, 0, 0).astype(low)

        return part

    unit = half // 128
    quarter = half // 2
    act_late = after(activation, sums_sent[2], returned[1])
    down_given = term(grad_rows, act_late)(given_at, half)
    down_sums = [group_send(down_given[: 56 * unit])]
    expert_part = up_pass(
        where, after(activation, down_given, returned[2], *gate_grad_near.values()), *down
    )
    expert_part = after(expert_part, down_sums[0], *came_home.values())
    expert_own = lax.psum_scatter(expert_part, "tensor", scatter_dimension=1, tiled=True)
    came_home = {s: after(v, expert_part) for s, v in came_home.items()}
    back = unpacked([came_home[s] for s in range(EXPERTS)])

    gate_grad = jnp.concatenate(
        [
            jnp.sum(contract(three_parts(gate_grad_near[s][0]), chosen[s], 1, 0), 0, keepdims=True)
            for s in range(EXPERTS)
        ],
        0,
    )
    scaled_back = back * gain_second_own
    sums = tensor_sum(
        jnp.concatenate([gate_grad, jnp.sum(scaled_back * normed_two, axis=1)[None]], 0)
    )
    gate_grad = jnp.take(sums[:EXPERTS], near, axis=0)
    weighted = jnp.sum(gates * gate_grad, axis=0, keepdims=True)
    logit_grad = (gates * (gate_grad - weighted)).astype(low)
    mean_two = (
        sums[EXPERTS:] + jnp.sum(logit_grad.astype(full) * logits, axis=0, keepdims=True)
    ) / width
    moe_grad = contract(logit_grad, router_own, 0, 0) + back

    grad_out = grad_own.astype(full)
    hidden_grad = grad_out + scale_two * (
        moe_grad * gain_second_own - normed_two * mean_two.reshape(rows, 1)
    )
    router_grad = jnp.dot(logit_grad, moe_in, preferred_element_type=full)
    moe_gain_grad = jnp.sum(moe_grad * normed_two, axis=0)
    pair_given = []
    kept = []

    def give_pair(sent):
        down_sums.append(group_send(down_given[56 * unit : 112 * unit], down_sums[0], sent))
        pair_term = term(moe_rows, after(pre_grad, sent))
        pair_given.extend(pair_term(given_at + k * quarter, quarter) for k in range(2))
        return (*pair_given, down_sums[1])

    attn_grad = tensor_gather(hidden_grad.astype(low), give_pair)
    down_sums.append(group_send(down_given[112 * unit :], down_sums[1]))
    pair_sums = [group_send(pair_given[0][: 12 * unit], down_sums[1])]
    context_grad = jnp.dot(attn_grad, out_full, preferred_element_type=full).astype(low)
    out_grad = contract(after(attn_grad, context_grad), context, 0, 0).astype(low)
    qkv_grad_rows = attention_back(query, keys, values, logs, context_grad, cosine, sine, scale)
    qkv_grad_rows = after(qkv_grad_rows, pair_sums[0], down_sums[2], out_grad)
    qkv_grad = contract(normed_in, qkv_grad_rows, 0, 0).astype(low)
    grads_both = jnp.concatenate([qkv_grad, out_grad], 1)
    shards = lax.psum_scatter(grads_both, "dp", scatter_dimension=0, tiled=True)
    pair_sums.append(group_send(pair_given[0][12 * unit :], pair_sums[0], grads_both))
    pair_last = group_send(pair_given[1], pair_sums[0], grads_both)
    outputs = {0: expert_own[:MOST]}
    part = after(expert_own[MOST : 2 * MOST], grads_both)
    outputs[2] = swap(part, "dp", 2 * group_count)

    def keep(sent):
        late = after(pre_grad, sent, expert_own)
        kept.append(term(moe_rows, late)(mine_at, half))
        kept.append(term(grad_rows, after(activation, kept[0], outputs[2]))(mine_at, half))
        return kept

    parts = spread_dot(where, after(qkv_grad_rows, grads_both), first, 0, tensor_count)
    normed_grad = near_reduce(*parts, [], filler=keep)
    for k in (2, 3):
        part = after(expert_own[k * MOST : (k + 1) * MOST], outputs[2])
        outputs[order[k]] = swap(part, "dp", order[k] * group_count)
    normed_one = inputs_own * scale_one
    scaled_in = normed_grad * gain_first_own
    attn_gain_grad = jnp.sum(normed_grad * normed_one, axis=0)
    mean_one = tensor_sum(jnp.sum(scaled_in * normed_one, axis=1)[None]) / width
    input_own = hidden_grad + scale_one * (scaled_in - normed_one * mean_one.reshape(rows, 1))
    mine = jnp.concatenate([router_grad, attn_gain_grad[None], moe_gain_grad[None]], 0)
    mine = lax.dynamic_update_slice_in_dim(
        jnp.zeros((mine.shape[0], width), full), mine, place * size, 1
    )
    expert_grad = expert_grad_sum(
        group_finish(kept[0], [jnp.concatenate(pair_sums, 0), pair_last], member, group_count),
        group_finish(kept[1], [jnp.concatenate(down_sums, 0)], member, group_count),
        hidden_size,
    )
    small_sums = []

    def sum_small(sent):
        small_sums.append(all_sum(after(mine, sent)))
        return (small_sums[0], outputs[3], outputs[1])

    input_grad = tensor_gather(input_own.astype(low), sum_small)
    input_grad = input_grad.astype(full)
    layer_own = hidden + unpacked([outputs[s] for s in range(EXPERTS)])
    layer_out = tensor_gather(layer_own.astype(low)).astype(full)
    share = width // dp_count
    mine = lax.dynamic_slice_in_dim(small_sums[0], index * share, share, 1)
    shards = shards.astype(full)
    qkv_shard, out_shard = shards[:, : 3 * size], shards[:, 3 * size :]
    return (
        layer_out,
        input_grad,
        mine[EXPERTS],
        qkv_shard.reshape(share, 3, size),
        out_shard,
        mine[EXPERTS + 1],
        mine[:EXPERTS].T,
        expert_grad,
    )


def solution(mesh):
    placed = (
        P("dp", None),
        P("dp"),
        P("dp", None, "tensor"),
        P("dp", "tensor"),
        P("dp"),
        P("dp", None),
        P(None, "dp", "tensor"),
        P("dp", None),
        P("dp", None),
    )
    return jax.shard_map(
        body,
        mesh=mesh,
        in_specs=placed,
        out_specs=(
            P("dp", None),
            P("dp", None),
            P("dp"),
            P("dp", None, "tensor"),
            P("dp", "tensor"),
            P("dp"),
            P("dp", None),
            P(None, "dp", "tensor"),
        ),
        check_vma=False,
    )
```

```python
import functools
import math

import jax
import jax.numpy as jnp
from jax import lax
from jax.experimental import pallas as pl
from jax.experimental.pallas import tpu as pltpu
from jax.sharding import PartitionSpec as P

HEAD = 128
EXPERTS = 4
SEQ = 1024
BLOCK = 256
MOST = 768


epsilon = 1e-05
theta_base = 10000.0
masked_out = -1e30
low = jnp.bfloat16
full = jnp.float32


def swap(value, axis, distance):
    return lax.ppermute(value, axis, [(i, i ^ distance) for i in range(lax.axis_size(axis))])


def contract(left, right, left_dim, right_dim):
    return lax.dot_general(
        left, right, (((left_dim,), (right_dim,)), ((), ())), preferred_element_type=jnp.float32
    )


def levels_of(count):
    return count.bit_length() - 1


def side_of(index, bit):
    return (index >> bit) & 1 == 1


def tensor_sum(value):
    for bit in range(levels_of(lax.axis_size("tensor"))):
        value = value + swap(value, "tensor", 1 << bit)
    return value


def all_sum(value):
    for axis in ("tensor", "dp"):
        for bit in range(levels_of(lax.axis_size(axis))):
            value = value + swap(value, axis, 1 << bit)
    return value


def tensor_gather(own, filler=None):
    count = lax.axis_size("tensor")
    place = lax.axis_index("tensor")
    size = own.shape[1]
    held = own
    order = list(range(levels_of(count)))[::-1]
    for bit in order:
        came = swap(held, "tensor", 1 << bit)
        if filler is not None and bit == order[0]:
            came = after(came, *filler(held))
        upper = side_of(place, bit)
        number = held.shape[1] // size
        mine = [held[:, i * size : (i + 1) * size] for i in range(number)]
        theirs = [came[:, i * size : (i + 1) * size] for i in range(number)]
        pairs = []
        for a, b in zip(mine, theirs):
            pairs.append((jnp.where(upper, b, a), jnp.where(upper, a, b)))
        held = jnp.concatenate([v for pair in pairs for v in pair], 1)
    return held


def after(value, *others):
    return lax.optimization_barrier((value, *others))[0]


def rotary_tables():
    half = HEAD // 2
    freqs = theta_base ** (-(jnp.arange(half, dtype=full) * 2.0 / HEAD))
    angles = jnp.arange(SEQ, dtype=full)[:, None] * freqs[None, :]
    cosine = jnp.cos(angles)
    sine = jnp.sin(angles)
    return (jnp.concatenate([cosine, cosine], 1), jnp.concatenate([-sine, sine], 1))


def limits(mib):
    return pltpu.CompilerParams(vmem_limit_bytes=mib << 20)


def cost(flops, moved, powers=0):
    return pl.CostEstimate(flops=int(flops), bytes_accessed=int(moved), transcendentals=int(powers))


def dot_cols(a, b):
    return lax.dot_general(a, b, (((1,), (1,)), ((), ())), preferred_element_type=full)


def dot_rows(a, b):
    return lax.dot_general(a, b, (((0,), (0,)), ((), ())), preferred_element_type=full)


def attention_kernel(scale, q_in, k_in, v_in, cos, sin, out, q_out, k_out, v_out, logs):
    def turned(ref):
        x = ref[...]
        return (x * cos[...] + pltpu.roll(x, HEAD // 2, 1) * sin[...]).astype(low)

    q_out[...] = turned(q_in)
    k_out[...] = turned(k_in)
    v_out[...] = v_in[...].astype(low)
    for block in range(SEQ // BLOCK):
        mine = pl.ds(block * BLOCK, BLOCK)
        seen = pl.ds(0, (block + 1) * BLOCK)
        scores = dot_cols(q_out[mine, :], k_out[seen, :]) * scale
        peak = jnp.max(scores, axis=1, keepdims=True)
        expo = jnp.exp(scores - peak)
        total = jnp.sum(expo, axis=1, keepdims=True)
        probs = (expo / total).astype(low)
        out[mine, :] = jnp.dot(probs, v_out[seen, :], preferred_element_type=full).astype(low)
        logs[0, mine, :] = peak + jnp.log(total)


def attention(qkv, cosine, sine, scale):
    rows = qkv.shape[0]
    size = qkv.shape[1] // 3
    heads = size // HEAD
    block = (SEQ, HEAD)
    table = pl.BlockSpec(block, lambda s, h: (0, 0))
    spec = pl.BlockSpec(block, lambda s, h: (s, h))
    shape = jax.ShapeDtypeStruct((rows, size), low)
    pairs = rows * heads * SEQ * 5 // 8
    return pl.pallas_call(
        functools.partial(attention_kernel, scale),
        grid=(rows // SEQ, heads),
        in_specs=[
            pl.BlockSpec(block, lambda s, h: (s, h)),
            pl.BlockSpec(block, lambda s, h: (s, heads + h)),
            pl.BlockSpec(block, lambda s, h: (s, 2 * heads + h)),
            table,
            table,
        ],
        out_specs=[spec] * 4 + [pl.BlockSpec((1, SEQ, 1), lambda s, h: (h, s, 0))],
        out_shape=[shape] * 4 + [jax.ShapeDtypeStruct((heads, rows, 1), full)],
        compiler_params=limits(48),
        cost_estimate=cost(4 * pairs * HEAD, rows * size * 20, pairs),
        name="attention",
    )(qkv, qkv, qkv, cosine, sine)


def attention_back_kernel(scale, heads, q_in, k_in, v_in, logs, grad, cos, sin, out, dk, dv):
    head = pl.program_id(1)
    dk[...] = jnp.zeros_like(dk)
    dv[...] = jnp.zeros_like(dv)

    def columns(which):
        return pl.ds(pl.multiple_of((which * heads + head) * HEAD, HEAD), HEAD)

    def turned(x, at):
        return (x * cos[at, :] - pltpu.roll(x, HEAD // 2, 1) * sin[at, :]).astype(low)

    for block in range(SEQ // BLOCK):
        mine = pl.ds(block * BLOCK, BLOCK)
        seen = pl.ds(0, (block + 1) * BLOCK)
        query, keys, values, given = q_in[mine, :], k_in[seen, :], v_in[seen, :], grad[mine, :]
        probs = jnp.exp(dot_cols(query, keys) * scale - logs[0, mine, :])
        prob_grad = dot_cols(given, values)
        inner = jnp.sum(probs * prob_grad, axis=1, keepdims=True)
        score_grad = (probs * (prob_grad - inner)).astype(low)
        query_grad = jnp.dot(score_grad, keys, preferred_element_type=full) * scale
        out[mine, columns(0)] = turned(query_grad, mine)
        dk[seen, :] += dot_rows(score_grad, query)
        dv[seen, :] += dot_rows(probs.astype(low), given)
    whole = pl.ds(0, SEQ)
    out[:, columns(1)] = turned(dk[...] * scale, whole)
    out[:, columns(2)] = dv[...].astype(low)


def attention_back(query, keys, values, logs, grad, cosine, sine, scale):
    rows, size = query.shape
    heads = size // HEAD
    block = (SEQ, HEAD)
    table = pl.BlockSpec(block, lambda s, h: (0, 0))
    spec = pl.BlockSpec(block, lambda s, h: (s, h))
    pairs = rows * heads * SEQ * 5 // 8
    return pl.pallas_call(
        functools.partial(attention_back_kernel, scale, heads),
        grid=(rows // SEQ, heads),
        in_specs=[spec] * 3
        + [pl.BlockSpec((1, SEQ, 1), lambda s, h: (h, s, 0)), spec, table, table],
        out_specs=pl.BlockSpec((SEQ, 3 * size), lambda s, h: (s, 0)),
        out_shape=jax.ShapeDtypeStruct((rows, 3 * size), low),
        scratch_shapes=[pltpu.VMEM(block, full)] * 2,
        compiler_params=limits(48),
        cost_estimate=cost(10 * pairs * HEAD, rows * size * 16, pairs),
        name="attention_back",
    )(query, keys, values, logs, grad, cosine, sine)


def place_rows(pieces, held, sems, upper, first):
    copies = []
    for ref, start, number, mine, there, column in pieces:
        half = held.shape[0] // 2
        columns = ref.shape[1]
        side = upper if mine else 1 - upper
        copies.append(
            pltpu.make_async_copy(
                ref.at[pl.ds(start, number), :],
                held.at[
                    pl.ds(pl.multiple_of(side * half + there, 64), number),
                    pl.ds(column * columns, columns),
                ],
                sems.at[len(copies)],
            )
        )

    @pl.when(first)
    def _():
        for copy in copies:
            copy.start()
        for copy in copies:
            copy.wait()


def down_pieces(own, came):
    half = own.shape[0]
    return [(own, 0, half, True, 0, 0), (came, 0, half, False, 0, 0)]


cuts = (
    ((0, 0, 16),),
    ((0, 16, 40),),
    ((0, 40, 56),),
    ((0, 56, 108),),
    ((0, 108, 128), (1, 0, 128)),
)
order = (0, 2, 3, 1)


def pair_pieces(own_gate, own_up, *came):
    half = own_gate.shape[0]
    pieces = [(own_gate, 0, half, True, 0, 0), (own_up, 0, half, True, 0, 1)]
    for cut, ref in zip(cuts, came):
        at = 0
        for which, start, stop in cut:
            number = (stop - start) * half // 128
            pieces.append((ref, at, number, False, start * half // 128, which))
            at += number
    return pieces


def column_block(where, i, size):
    return pl.ds(pl.multiple_of((i ^ where[0]) * size, size), size)


def down_kernel(carried, where, rows, own, came, *refs):
    rows_out, raw, held, sems = refs[carried:]
    place_rows(down_pieces(own, came), held, sems, where[1], pl.program_id(0) == 0)
    rows_out[...] = rows[...]
    raw[...] = jnp.dot(rows[...], held[...], preferred_element_type=full).astype(low)


def down_pass(where, rows, own, came, start, total, carried):
    number, width = rows.shape
    hidden = own.shape[1]
    tile = 256
    first = start // tile
    anywhere = pl.BlockSpec(memory_space=pl.ANY)
    here = lambda columns: pl.BlockSpec((tile, columns), lambda i, where: (first + i, 0))
    return pl.pallas_call(
        functools.partial(down_kernel, len(carried)),
        grid_spec=pltpu.PrefetchScalarGridSpec(
            num_scalar_prefetch=1,
            grid=(number // tile,),
            in_specs=[pl.BlockSpec((tile, width), lambda i, where: (i, 0))]
            + [anywhere] * (2 + len(carried)),
            out_specs=[here(width), here(hidden)],
            scratch_shapes=[pltpu.VMEM((width, hidden), low), pltpu.SemaphoreType.DMA((2,))],
        ),
        out_shape=[
            jax.ShapeDtypeStruct((total, width), low),
            jax.ShapeDtypeStruct((total, hidden), low),
        ],
        input_output_aliases={4 + i: i for i in range(len(carried))},
        compiler_params=limits(48),
        cost_estimate=cost(
            2 * number * width * hidden, (number * (2 * width + hidden) + width * hidden) * 2
        ),
        name="down",
    )(where, rows, own, came, *carried)


def spread_kernel(count, where, left, right, even, odd, part):
    size = part.shape[1] // count
    part[...] = dot_cols(left[...], right[...]).astype(low)
    for i in range(count):
        (odd if i % 2 else even)[:, i // 2 * size : (i // 2 + 1) * size] = part[
            :, column_block(where, i, size)
        ]


def spread_dot(where, left, right, column, count):
    rows, depth = left.shape
    width = right.shape[0]
    tile = 256
    spec = lambda columns: pl.BlockSpec((tile, columns), lambda i, where: (i, 0))
    half = jax.ShapeDtypeStruct((rows, width // 2), low)
    return pl.pallas_call(
        functools.partial(spread_kernel, count),
        grid_spec=pltpu.PrefetchScalarGridSpec(
            num_scalar_prefetch=1,
            grid=(rows // tile,),
            in_specs=[
                spec(depth),
                pl.BlockSpec((width, depth), lambda i, where: (0, column)),
            ],
            out_specs=[spec(width // 2)] * 2,
            scratch_shapes=[pltpu.VMEM((tile, width), low)],
        ),
        out_shape=[half, half],
        compiler_params=limits(48),
        cost_estimate=cost(2 * rows * width * depth, (rows * (width + depth) + width * depth) * 2),
        name="spread",
    )(where, left, right)


def up_kernel(where, act, own, came, out, held, sems):
    place_rows(down_pieces(own, came), held, sems, where[1], pl.program_id(0) == 0)
    out[...] = dot_cols(act[...], held[...]).astype(low)


def up_pass(where, act, own, came):
    total, hidden = act.shape
    width = 2 * own.shape[0]
    tile = 256
    spec = lambda columns: pl.BlockSpec((tile, columns), lambda i, where: (i, 0))
    return pl.pallas_call(
        up_kernel,
        grid_spec=pltpu.PrefetchScalarGridSpec(
            num_scalar_prefetch=1,
            grid=(total // tile,),
            in_specs=[spec(hidden)] + [pl.BlockSpec(memory_space=pl.ANY)] * 2,
            out_specs=spec(width),
            scratch_shapes=[pltpu.VMEM((width, hidden), low), pltpu.SemaphoreType.DMA((2,))],
        ),
        out_shape=jax.ShapeDtypeStruct((total, width), low),
        compiler_params=limits(48),
        cost_estimate=cost(
            2 * total * width * hidden, (total * (width + hidden) + width * hidden) * 2
        ),
        name="up",
    )(where, act, own, came)


def expert_kernel(count, carried, where, *refs):
    blocks, refs = refs[:count], refs[count:]
    number = 2 + len(cuts)
    weights, (raw, routed, router) = refs[:number], refs[number : number + 3]
    rows_out, act_out, grad_out, even, odd, gate_grad, pair, part, sems = refs[
        number + 3 + carried :
    ]
    size = blocks[0].shape[1]
    hidden = raw.shape[1]
    place_rows(pair_pieces(*weights), pair, sems, where[1], pl.program_id(0) == 0)
    for i, ref in enumerate(blocks):
        rows_out[:, column_block(where, i, size)] = ref[...]
    both = jnp.dot(rows_out[...], pair[...], preferred_element_type=full)
    pre_gate = both[:, :hidden]
    pre_up = both[:, hidden:]
    sigma = 1.0 / (1.0 + jnp.exp(-pre_gate))
    silu = pre_gate * sigma
    act = silu * pre_up
    back = raw[...].astype(full)
    tile = back.shape[0]
    own = where[2].astype(full)
    other = jnp.broadcast_to(routed[...], (128, tile)).T - own
    logits = jnp.dot(rows_out[...], router[...], preferred_element_type=full)
    lane = lax.broadcasted_iota(jnp.int32, (tile, 128), 1).astype(full)
    ahead = jnp.where(lane == other, logits, 0.0) - jnp.where(lane == own, logits, 0.0)
    gate = 1.0 / (1.0 + jnp.exp(jnp.sum(ahead, axis=1, keepdims=True)))
    gate_sum = jnp.sum(act * back, axis=1, keepdims=True)
    gate_grad[...] = jnp.broadcast_to(gate_sum, (tile, 128)).T[:1]
    act_out[...] = (act * gate).astype(low)
    back = back * gate
    grad_out[:, :hidden] = (back * pre_up * sigma * (1.0 + pre_gate * (1.0 - sigma))).astype(low)
    grad_out[:, hidden:] = (back * silu).astype(low)
    part[...] = dot_cols(grad_out[...], pair[...]).astype(low)
    for i in range(count):
        (odd if i % 2 else even)[:, i // 2 * size : (i // 2 + 1) * size] = part[
            :, column_block(where, i, size)
        ]


def expert_pass(step, where, blocks, weights, raw, routed, router, carried):
    count = len(blocks)
    size = blocks[0].shape[1]
    width, hidden = 2 * weights[0].shape[0], weights[0].shape[1]
    both = 2 * hidden
    total = raw.shape[0]
    tile = 256
    steps = MOST // tile
    here = lambda i, where: (step * steps + i, 0)
    near = lambda i, where: (i, 0)
    near_spec = lambda columns: pl.BlockSpec((tile, columns), near)
    here_spec = lambda columns: pl.BlockSpec((tile, columns), here)
    row_spec = pl.BlockSpec((1, tile), lambda i, where: (0, i))
    anywhere = pl.BlockSpec(memory_space=pl.ANY)
    shape = lambda r, c, t=low: jax.ShapeDtypeStruct((r, c), t)
    return pl.pallas_call(
        functools.partial(expert_kernel, count, len(carried)),
        grid_spec=pltpu.PrefetchScalarGridSpec(
            num_scalar_prefetch=1,
            grid=(steps,),
            in_specs=[near_spec(size)] * count
            + [anywhere] * len(weights)
            + [
                here_spec(hidden),
                row_spec,
                pl.BlockSpec((width, 128), lambda i, where: (0, 0)),
            ]
            + [anywhere] * len(carried),
            out_specs=[
                here_spec(width),
                here_spec(hidden),
                here_spec(both),
                near_spec(width // 2),
                near_spec(width // 2),
                row_spec,
            ],
            scratch_shapes=[
                pltpu.VMEM((width, both), low),
                pltpu.VMEM((tile, width), low),
                pltpu.SemaphoreType.DMA((2 + sum(len(cut) for cut in cuts),)),
            ],
        ),
        out_shape=[
            shape(total, width),
            shape(total, hidden),
            shape(total, both),
            shape(MOST, width // 2),
            shape(MOST, width // 2),
            shape(1, MOST, full),
        ],
        input_output_aliases={
            count + len(weights) + 4 + i: i for i in range(len(carried))
        },
        compiler_params=limits(60),
        cost_estimate=cost(
            4 * MOST * width * both, width * both * 2 + MOST * (width * 8 + hidden * 8), MOST * hidden
        ),
        name="expert",
    )(where, *blocks, *weights, raw, routed, router, *carried)


def expert_grad_kernel(hidden, pieces, per, *refs):
    out = refs[-1]
    which, at = pl.program_id(0), pl.program_id(1)

    def add(ref, other):
        out[0] = (ref[...].astype(full) + other[...].astype(full))[:, :hidden]

    for k in range(pieces):

        @pl.when((which < 2) & (at // per == k))
        def _():
            add(refs[0], refs[1 + k])

    @pl.when(which == 2)
    def _():
        add(refs[1 + pieces], refs[2 + pieces])


def expert_grad_sum(pair, down, hidden):
    rows, padded = down[0].shape
    tile = min(256, rows)
    pieces = len(pair) - 1
    per = rows // tile // pieces
    last = rows // tile - 1

    def piece_spec(k):
        return pl.BlockSpec(
            (tile, padded),
            lambda w, i: (
                jnp.where(w == 2, per - 1, jnp.clip(i - k * per, 0, per - 1)),
                jnp.minimum(w, 1),
            ),
        )

    pair_spec = pl.BlockSpec(
        (tile, padded), lambda w, i: (jnp.where(w == 2, last, i), jnp.minimum(w, 1))
    )
    down_spec = pl.BlockSpec((tile, padded), lambda w, i: (jnp.where(w == 2, i, 0), 0))
    return pl.pallas_call(
        functools.partial(expert_grad_kernel, hidden, pieces, per),
        grid=(3, rows // tile),
        in_specs=[pair_spec] + [piece_spec(k) for k in range(pieces)] + [down_spec] * 2,
        out_specs=pl.BlockSpec((1, tile, hidden), lambda w, i: (w, i, 0)),
        out_shape=jax.ShapeDtypeStruct((3, rows, hidden), full),
        compiler_params=limits(40),
        cost_estimate=cost(rows * padded * 3, rows * padded * 24),
        name="expert_grad_sum",
    )(*pair, *down)


def near_blocks(own, *others):
    held = [own]
    for bit in range(levels_of(lax.axis_size("tensor")))[::-1]:
        theirs = [swap(v, "tensor", 1 << bit) for v in held]
        if bit and others:
            theirs = [after(v, *others) for v in theirs]
        held = [v for pair in zip(held, theirs) for v in pair]
    return held


def near_reduce(even, odd, meet, *others, filler=None):
    count = lax.axis_size("tensor")
    number = count // 2
    size = even.shape[1] // number
    came = swap(odd, "tensor", 1)
    for bit in range(1, levels_of(count)):
        blocks = [
            even[:, i * size : (i + 1) * size].astype(full)
            + came[:, i * size : (i + 1) * size].astype(full)
            for i in range(number)
        ]
        sent = jnp.concatenate([v.astype(low) for v in blocks[1::2]], 1)
        if bit == levels_of(count) - 1:
            sent = after(sent, *others)
            meet.append(sent)
        even = jnp.concatenate(blocks[::2], 1)
        came = swap(sent, "tensor", 1 << bit)
        if filler is not None and bit == levels_of(count) - 1:
            came = after(came, *filler(sent))
        number //= 2
    return even.astype(full) + came.astype(full)


def half_gather(local, group_count):
    held = local
    place = lax.axis_index("dp") % group_count
    for bit in range(levels_of(group_count) - 1):
        came = swap(held, "dp", 1 << bit)
        upper = side_of(place, bit)
        held = jnp.concatenate([jnp.where(upper, came, held), jnp.where(upper, held, came)], 0)
    return held


def group_finish(kept, came, position, group_count):
    if group_count > 2:
        came = jnp.concatenate(came, 0)
    for bit in range(levels_of(group_count) - 1)[::-1]:
        current = kept.astype(full) + came.astype(full)
        middle = current.shape[0] // 2
        upper = (position >> bit) & 1
        kept = lax.dynamic_slice_in_dim(current, upper * middle, middle, 0)
        given = lax.dynamic_slice_in_dim(current, (1 - upper) * middle, middle, 0)
        came = swap(given.astype(low), "dp", 1 << bit)
    return [kept, *came] if isinstance(came, list) else [kept, came]


def body(
    tokens,
    attn_gain,
    qkv_weight,
    out_weight,
    moe_gain,
    router_weight,
    expert_weight,
    routes,
    cotangent,
):
    rows = tokens.shape[0]
    width = tokens.shape[1]
    tensor_count = lax.axis_size("tensor")
    dp_count = lax.axis_size("dp")
    group_count = dp_count // EXPERTS
    size = width // tensor_count
    hidden_size = expert_weight.shape[2]
    padded = -(-hidden_size // 128) * 128
    scale = 1.0 / math.sqrt(HEAD)
    place = lax.axis_index("tensor")
    index = lax.axis_index("dp")
    expert = index // group_count
    member = index % group_count
    top_half = member >> (levels_of(group_count) - 1)
    where = jnp.stack([place, top_half, expert]).astype(jnp.int32)

    def own_columns(value):
        return lax.dynamic_slice_in_dim(value, place * size, size, 1)

    extras = jnp.concatenate([router_weight, attn_gain[:, None], moe_gain[:, None]], 1)
    extras = jnp.pad(extras, ((0, 0), (0, 128 - extras.shape[1])))
    first = lax.all_gather(
        jnp.concatenate([qkv_weight.reshape(-1, 3 * size), out_weight, extras], 1),
        "dp",
        axis=0,
        tiled=True,
    )
    qkv_flat = first[:, : 3 * size]
    out_full = first[:, 3 * size : 4 * size]
    small = first[:, 4 * size :].T
    router_full = small[:EXPERTS]
    gain_first = small[EXPERTS : EXPERTS + 1].astype(full)
    gain_second = small[EXPERTS + 1 : EXPERTS + 2].astype(full)
    gain_first_own = own_columns(gain_first)
    gain_second_own = own_columns(gain_second)
    router_own = own_columns(router_full)

    near = jnp.arange(EXPERTS, dtype=jnp.int32) ^ expert
    names = jnp.arange(EXPERTS, dtype=jnp.int32)
    hits = jnp.sum((routes.T[None] == names[:, None, None]).astype(jnp.int32), 1)
    rank = jnp.cumsum(hits, axis=1) - hits
    slot_near = jnp.take(jnp.where(hits > 0, rank, -1), near, axis=0)
    places = jnp.arange(MOST, dtype=jnp.int32)[:, None]
    chosen = [(places == slot_near[s][None, :]).astype(low) for s in range(EXPERTS)]

    def packed(own):
        return [jnp.dot(c, own, preferred_element_type=full).astype(low) for c in chosen]

    def exchange(parts):
        return [parts[0]] + [swap(parts[s], "dp", s * group_count) for s in range(1, EXPERTS)]

    def unpacked(parts):
        total = contract(chosen[0], parts[0], 0, 0)
        for c, part in zip(chosen[1:], parts[1:]):
            total = total + contract(c, part, 0, 0)
        return total

    def widened(value):
        return jnp.pad(value, ((0, 0), (0, padded - hidden_size)))

    gate_mine, up_mine, down_mine = [
        half_gather(widened(expert_weight[k]), group_count) for k in range(3)
    ]
    half = width // 2
    mine_at, given_at = top_half * half, (1 - top_half) * half
    reach = group_count // 2

    def group_send(given, *others):
        return swap(after(given, *others), "dp", reach)

    down = (down_mine, group_send(down_mine))
    crossing = []

    def cross(*others):
        pieces = [
            (gate_mine, up_mine)[which][start * half // 128 : stop * half // 128]
            for which, start, stop in cuts[len(crossing)]
        ]
        crossing.append(group_send(jnp.concatenate(pieces, 0), *crossing[-1:], *others))

    cross(first)

    grad_own = own_columns(cotangent)
    grad_mine = jnp.dot(chosen[0], cotangent, preferred_element_type=full).astype(low)
    planes = [
        [m + g * group_count for g in range(EXPERTS)] for m in range(group_count)
    ]
    grad_planes = lax.all_gather(
        after(grad_own, first), "dp", axis=0, tiled=True, axis_index_groups=planes
    )
    slots_came = exchange([slot_near[s][None].astype(full) for s in range(EXPERTS)])
    route_sums = jnp.sum(routes, axis=1)[None].astype(low)
    routed = exchange([contract(route_sums, c, 1, 1) for c in chosen])

    inputs = tokens.astype(full)
    scale_one = lax.rsqrt(jnp.mean(inputs * inputs, axis=1, keepdims=True) + epsilon)
    normed_in = (inputs * scale_one * gain_first).astype(low)
    inputs_own = own_columns(tokens).astype(full)
    normed_in = after(normed_in, down[1], grad_mine, *slots_came, *routed)
    qkv = jnp.dot(normed_in, qkv_flat, preferred_element_type=full)
    cross(qkv)
    cosine, sine = rotary_tables()
    context, query, keys, values, logs = attention(qkv, cosine, sine, scale)
    context = after(context, crossing[1])
    cross(context)
    attn_parts = spread_dot(where, context, first, 3, tensor_count)
    rows_raw = []

    total = EXPERTS * MOST

    def down_filler(sent):
        cross(sent)
        rows_raw.extend(down_pass(where, after(grad_mine, sent), *down, 0, total, ()))
        return (rows_raw[1], crossing[3])

    hidden = inputs_own + near_reduce(*attn_parts, [], crossing[2], filler=down_filler)
    cross(rows_raw[1])
    grad_planes = after(grad_planes, hidden)
    grad_packed = []
    for s in order[1:]:
        source = lax.dynamic_slice_in_dim(grad_planes, (expert ^ s) * rows, rows, 0)
        taken = (places.astype(full) == slots_came[s]).astype(low)
        grad_packed.append(jnp.dot(taken, source, preferred_element_type=full).astype(low))
    grad_rest = lax.all_gather(jnp.concatenate(grad_packed, 0), "tensor", axis=1, tiled=True)

    scaled_hidden = (hidden * gain_second_own).astype(low)
    sums = tensor_sum(
        jnp.concatenate(
            [contract(router_own, scaled_hidden, 1, 1), jnp.sum(hidden * hidden, 1)[None]], 0
        )
    )
    scale_two_row = lax.rsqrt(sums[EXPERTS:] / width + epsilon)
    scale_two = scale_two_row.reshape(rows, 1)
    logits = sums[:EXPERTS] * scale_two_row
    normed_two = hidden * scale_two
    moe_in = (normed_two * gain_second_own).astype(low)
    named = hits > 0
    top = jnp.max(jnp.where(named, logits, masked_out), axis=0, keepdims=True)
    weight = jnp.where(named, jnp.exp(logits - top), 0.0)
    gates = weight / jnp.sum(weight, axis=0, keepdims=True)

    def three_parts(value):
        a = value.astype(low)
        b = (value - a.astype(full)).astype(low)
        return jnp.stack([a, b, (value - a.astype(full) - b.astype(full)).astype(low)])

    moe_packed = packed(moe_in)
    pair = (gate_mine, up_mine, *crossing)
    crossed = {2: swap(moe_packed[2], "dp", 2 * group_count)}
    crossed[3] = swap(after(moe_packed[3], crossed[2]), "dp", 3 * group_count)
    arrived = [near_blocks(moe_packed[0])]

    carried = ()
    sums_sent = []
    came_home = {}
    returned = []
    gate_grads = []
    router_block = first[:, 4 * size :]
    for step in range(EXPERTS):
        named_sum = routed[order[step]]
        if step == 1:
            rows_raw = down_pass(where, after(grad_rest, even), *down, MOST, total, rows_raw)
            named_sum = after(named_sum, crossed[3])
        if step == 2:
            named_sum = after(named_sum, crossed[1], sums_sent[0])
        if step == 3:
            named_sum = after(named_sum, sums_sent[1])
        moe_rows, activation, pre_grad, even, odd, gate_grad = expert_pass(
            step, where, arrived[step], pair, rows_raw[1], named_sum, router_block, carried
        )
        carried = (moe_rows, activation, pre_grad)
        if step == 0:
            arrived.append(near_blocks(crossed[2], even))
            crossed[3] = after(crossed[3], even)
            crossed[1] = swap(after(moe_packed[1], crossed[3]), "dp", group_count)
        if step == 1:
            arrived.append(near_blocks(crossed[3], even))
            odd = after(odd, crossed[1], arrived[2][tensor_count // 2])
        if step == 2:
            arrived.append(near_blocks(crossed[1], even))
        if step == 2:
            odd = after(odd, *returned, arrived[3][tensor_count // 2])
        if step == 3:
            came_home[2] = swap(returned[0], "dp", 2 * group_count)
            odd = after(odd, returned[1], came_home[2])
        if step == 0:
            own_parts = (even, odd)
        else:
            returned.append(near_reduce(even, odd, sums_sent).astype(low))
        gate_grads.append(gate_grad)

    def home(parts):
        return {
            s: swap(v, "dp", s * group_count) if s else v for s, v in zip(order, parts)
        }

    came_home[3] = swap(returned[1], "dp", 3 * group_count)
    came_home[1] = swap(returned[2], "dp", group_count)
    own_even, own_odd = own_parts
    came_home[0] = near_reduce(own_even, after(own_odd, sums_sent[2]), []).astype(low)
    gate_grad_near = home([gate_grads[0]] + [after(v, even) for v in gate_grads[1:]])
    grad_rows = rows_raw[0]

    def term(left, right):
        def part(start, number):
            taken = lax.dynamic_slice_in_dim(left, start, number, 1)
            return contract(taken, right, 0, 0).astype(low)

        return part

    unit = half // 128
    quarter = half // 2
    act_late = after(activation, sums_sent[2], returned[1])
    down_given = term(grad_rows, act_late)(given_at, half)
    down_sums = [group_send(down_given[: 56 * unit])]
    expert_part = up_pass(
        where, after(activation, down_given, returned[2], *gate_grad_near.values()), *down
    )
    expert_part = after(expert_part, down_sums[0], *came_home.values())
    expert_own = lax.psum_scatter(expert_part, "tensor", scatter_dimension=1, tiled=True)
    came_home = {s: after(v, expert_part) for s, v in came_home.items()}
    back = unpacked([came_home[s] for s in range(EXPERTS)])

    gate_grad = jnp.concatenate(
        [
            jnp.sum(contract(three_parts(gate_grad_near[s][0]), chosen[s], 1, 0), 0, keepdims=True)
            for s in range(EXPERTS)
        ],
        0,
    )
    scaled_back = back * gain_second_own
    sums = tensor_sum(
        jnp.concatenate([gate_grad, jnp.sum(scaled_back * normed_two, axis=1)[None]], 0)
    )
    gate_grad = jnp.take(sums[:EXPERTS], near, axis=0)
    weighted = jnp.sum(gates * gate_grad, axis=0, keepdims=True)
    logit_grad = (gates * (gate_grad - weighted)).astype(low)
    mean_two = (
        sums[EXPERTS:] + jnp.sum(logit_grad.astype(full) * logits, axis=0, keepdims=True)
    ) / width
    moe_grad = contract(logit_grad, router_own, 0, 0) + back

    grad_out = grad_own.astype(full)
    hidden_grad = grad_out + scale_two * (
        moe_grad * gain_second_own - normed_two * mean_two.reshape(rows, 1)
    )
    router_grad = jnp.dot(logit_grad, moe_in, preferred_element_type=full)
    moe_gain_grad = jnp.sum(moe_grad * normed_two, axis=0)
    pair_given = []
    kept = []

    def give_pair(sent):
        down_sums.append(group_send(down_given[56 * unit : 112 * unit], down_sums[0], sent))
        pair_term = term(moe_rows, after(pre_grad, sent))
        pair_given.extend(pair_term(given_at + k * quarter, quarter) for k in range(2))
        return (*pair_given, down_sums[1])

    attn_grad = tensor_gather(hidden_grad.astype(low), give_pair)
    down_sums.append(group_send(down_given[112 * unit :], down_sums[1]))
    pair_sums = [group_send(pair_given[0][: 12 * unit], down_sums[1])]
    context_grad = jnp.dot(attn_grad, out_full, preferred_element_type=full).astype(low)
    out_grad = contract(after(attn_grad, context_grad), context, 0, 0).astype(low)
    qkv_grad_rows = attention_back(query, keys, values, logs, context_grad, cosine, sine, scale)
    qkv_grad_rows = after(qkv_grad_rows, pair_sums[0], down_sums[2], out_grad)
    qkv_grad = contract(normed_in, qkv_grad_rows, 0, 0).astype(low)
    grads_both = jnp.concatenate([qkv_grad, out_grad], 1)
    shards = lax.psum_scatter(grads_both, "dp", scatter_dimension=0, tiled=True)
    pair_sums.append(group_send(pair_given[0][12 * unit :], pair_sums[0], grads_both))
    pair_last = group_send(pair_given[1], pair_sums[0], grads_both)
    outputs = {0: expert_own[:MOST]}
    part = after(expert_own[MOST : 2 * MOST], grads_both)
    outputs[2] = swap(part, "dp", 2 * group_count)

    def keep(sent):
        late = after(pre_grad, sent, expert_own)
        kept.append(term(moe_rows, late)(mine_at, half))
        kept.append(term(grad_rows, after(activation, kept[0], outputs[2]))(mine_at, half))
        return kept

    parts = spread_dot(where, after(qkv_grad_rows, grads_both), first, 0, tensor_count)
    normed_grad = near_reduce(*parts, [], filler=keep)
    for k in (2, 3):
        part = after(expert_own[k * MOST : (k + 1) * MOST], outputs[2])
        outputs[order[k]] = swap(part, "dp", order[k] * group_count)
    normed_one = inputs_own * scale_one
    scaled_in = normed_grad * gain_first_own
    attn_gain_grad = jnp.sum(normed_grad * normed_one, axis=0)
    mean_one = tensor_sum(jnp.sum(scaled_in * normed_one, axis=1)[None]) / width
    input_own = hidden_grad + scale_one * (scaled_in - normed_one * mean_one.reshape(rows, 1))
    mine = jnp.concatenate([router_grad, attn_gain_grad[None], moe_gain_grad[None]], 0)
    mine = lax.dynamic_update_slice_in_dim(
        jnp.zeros((mine.shape[0], width), full), mine, place * size, 1
    )
    expert_grad = expert_grad_sum(
        group_finish(kept[0], [jnp.concatenate(pair_sums, 0), pair_last], member, group_count),
        group_finish(kept[1], [jnp.concatenate(down_sums, 0)], member, group_count),
        hidden_size,
    )
    small_sums = []

    def sum_small(sent):
        small_sums.append(all_sum(after(mine, sent)))
        return (small_sums[0], outputs[3], outputs[1])

    input_grad = tensor_gather(input_own.astype(low), sum_small)
    input_grad = input_grad.astype(full)
    layer_own = hidden + unpacked([outputs[s] for s in range(EXPERTS)])
    layer_out = tensor_gather(layer_own.astype(low)).astype(full)
    share = width // dp_count
    mine = lax.dynamic_slice_in_dim(small_sums[0], index * share, share, 1)
    shards = after(shards, expert_grad).astype(full)
    qkv_shard, out_shard = shards[:, : 3 * size], shards[:, 3 * size :]
    return (
        layer_out,
        input_grad,
        mine[EXPERTS],
        qkv_shard.reshape(share, 3, size),
        out_shard,
        mine[EXPERTS + 1],
        mine[:EXPERTS].T,
        expert_grad,
    )


def solution(mesh):
    placed = (
        P("dp", None),
        P("dp"),
        P("dp", None, "tensor"),
        P("dp", "tensor"),
        P("dp"),
        P("dp", None),
        P(None, "dp", "tensor"),
        P("dp", None),
        P("dp", None),
    )
    return jax.shard_map(
        body,
        mesh=mesh,
        in_specs=placed,
        out_specs=(
            P("dp", None),
            P("dp", None),
            P("dp"),
            P("dp", None, "tensor"),
            P("dp", "tensor"),
            P("dp"),
            P("dp", None),
            P(None, "dp", "tensor"),
        ),
        check_vma=False,
    )
```
